32 devices in a mesh: dp: 16 (over z, x, core), tensor: 2 (over y).
Axes of the slice: x: 2, y: 2, z: 4, core: 2. Of those that a mesh axis runs over, the one named last changes fastest.
Arguments:
- tokens: bfloat16 [18944, 768], P('dp'), may hold values from -6 to 6
- w_qkv: bfloat16 [3, 768, 768], P(None, None, 'tensor'), may hold values from -0.21875 to 0.21875
- bias_qv: float32 [2, 768], P(None, 'tensor'), may hold values from -2 to 2
- w_out: bfloat16 [768, 768], P('tensor'), may hold values from -2.5 to 2.5
- bias_out: float32 [768], replicated, may hold values from -2 to 2
- gain_one: float32 [768], replicated, may hold values from 0.25 to 1.75
- shift_one: float32 [768], replicated, may hold values from -2 to 2
- w_up: bfloat16 [768, 3072], P(None, 'tensor'), may hold values from -0.21875 to 0.21875
- bias_up: float32 [3072], P('tensor'), may hold values from -2 to 2
- w_down: bfloat16 [3072, 768], P('tensor'), may hold values from -0.15625 to 0.15625
- bias_down: float32 [768], replicated, may hold values from -2 to 2
- gain_two: float32 [768], replicated, may hold values from 0.25 to 1.75
- shift_two: float32 [768], replicated, may hold values from -2 to 2
- grad_out: bfloat16 [18944, 768], P('dp'), may hold values from -6 to 6
- parent: int32 [128], P('dp'), may hold values from -1 to 126, as said below
- mem_slots: int32 [128, 10], P('dp'), may hold values from 0 to 147, as said below
Outputs:
- output: bfloat16 [18944, 768], P('dp')
- grad_tokens: bfloat16 [18944, 768], P('dp')
- grad_w_qkv: float32 [3, 768, 768], P(None, None, 'tensor')
- grad_bias_qv: float32 [2, 768], P(None, 'tensor')
- grad_w_out: float32 [768, 768], P('tensor')
- grad_bias_out: float32 [768], replicated
- grad_gain_one: float32 [768], replicated
- grad_shift_one: float32 [768], replicated
- grad_w_up: float32 [768, 3072], P(None, 'tensor')
- grad_bias_up: float32 [3072], P('tensor')
- grad_w_down: float32 [3072, 768], P('tensor')
- grad_bias_down: float32 [768], replicated
- grad_gain_two: float32 [768], replicated
- grad_shift_two: float32 [768], replicated
The draws below stay inside these ranges and needn't reach their ends.
Inputs may be any that keep to these rules, and one draw needn't show every extreme that they name: `parent`: segments 8 * t to 8 * t + 7 form tree t; its first segment has -1, every other segment an earlier segment of the same tree, and its last segment the segment just before it. `mem_slots`: the 10 offsets of one segment are distinct.
All inputs are finite; a program needn't handle non-finite values.
Results may differ from the reference program's by a relative error of at most 0.014.
Values sent between devices are 32-bit elements; how exact they have to be, the bound alone decides.
A program may use at most 320 MiB of HBM per device.

```python
import jax
import jax.numpy as jnp
from jax import lax

D = 768
HEADS = 12
HD = 64
FF = 3072
SEG = 148
MEMW = 10
TREE_SEGS = 8
TOK_DEV = 1184
TOKENS = 18944
SEGMENTS = 128


def draw_parent(key, part):
    indices = jnp.arange(SEGMENTS, dtype=jnp.int32)
    local_index = indices % TREE_SEGS
    picked = jax.random.randint(key, (SEGMENTS,), 0, jnp.maximum(local_index, 1), dtype=jnp.int32)
    picked = jnp.where(local_index == TREE_SEGS - 1, local_index - 1, picked).astype(jnp.int32)
    return jnp.where(local_index == 0, -1, indices - local_index + picked).astype(jnp.int32)


def draw_mem_slots(key, part):
    random_bits = jax.random.randint(key, (SEGMENTS, SEG), 0, 1 << 20, dtype=jnp.int32)
    ranked = random_bits * SEG + jnp.arange(SEG, dtype=jnp.int32)[None, :]
    ordering = jnp.argsort(ranked, axis=1)
    return ordering[:, :MEMW].astype(jnp.int32)


def with_spikes(values, stream_key, source, target, parts, factor):
    owner, partner = [(jnp.arange(values.shape[position]) // (values.shape[position] // parts)).reshape([-1 if axis == position else 1 for axis in range(values.ndim)]) for position in (source, target)]
    chosen = jax.random.permutation(stream_key, parts)[partner]
    strong = (owner == chosen) | (owner == (partner + parts // 2) % parts)
    return jnp.where(strong, factor * values, values)


def shard_levels(rng, extent, cuts, least, largest):
    level = 1.0
    for dim, parts in cuts:
        heights = jax.random.uniform(jax.random.fold_in(jax.random.fold_in(rng, 6), dim), (parts,), jnp.float32, least / len(cuts), largest / len(cuts))
        level = level * jnp.repeat(jnp.exp(heights), extent[dim] // parts).reshape((-1,) + (1,) * (len(extent) - 1 - dim))
    return level


def noise(own_key, extent, deviation, limit, shards=(), kind=jnp.bfloat16):
    drawn = deviation * jax.random.normal(own_key, extent, jnp.float32)
    if shards:
        drawn = drawn * shard_levels(own_key, extent, shards, -0.22, 0.18)
    return jnp.clip(drawn, -limit, limit).astype(kind)


def bell_draw_with(stream_key, extent, width, bound, pieces, heavy, held_as=jnp.bfloat16):
    values = width * jax.random.normal(stream_key, extent, jnp.float32)
    if pieces:
        values = values * shard_levels(stream_key, extent, pieces, -0.22, 0.18)
    return jnp.clip(with_spikes(values, jax.random.fold_in(stream_key, 3), *heavy), -bound, bound).astype(held_as)


def setup_inputs(seed: int = 0) -> dict:
    keys = jax.random.split(jax.random.key(seed), 17)
    tokens = noise(keys[0], (TOKENS, D), 1.0, 6.0, ((0, 16),))
    w_qkv = noise(keys[1], (3, D, D), D ** -0.5, 0.21875, ((2, 2),))
    bias_qv = noise(keys[2], (2, D), 0.3, 2.0, ((1, 2),), jnp.float32)
    w_out = noise(keys[3], (D, D), (D // 128) ** -0.5, 2.5, ((0, 2),))
    bias_out = noise(keys[4], (D,), 0.3, 2.0, (), jnp.float32)
    gain_one = jnp.clip(1.0 + 0.15 * jax.random.normal(keys[5], (D,), jnp.float32), 0.25, 1.75)
    shift_one = noise(keys[6], (D,), 0.3, 2.0, (), jnp.float32)
    w_up = noise(keys[7], (D, FF), D ** -0.5, 0.21875, ((1, 2),))
    bias_up = noise(keys[8], (FF,), 0.3, 2.0, ((0, 2),), jnp.float32)
    w_down = noise(keys[9], (FF, D), (FF // 2) ** -0.5, 0.15625, ((0, 2),))
    bias_down = noise(keys[10], (D,), 0.3, 2.0, (), jnp.float32)
    gain_two = jnp.clip(1.0 + 0.15 * jax.random.normal(keys[11], (D,), jnp.float32), 0.25, 1.75)
    shift_two = noise(keys[12], (D,), 0.3, 2.0, (), jnp.float32)
    grad_out = bell_draw_with(keys[13], (TOKENS, D), 1.0, 6.0, ((0, 16),), (0, 1, 16, 2.0))
    parent = draw_parent(jax.random.fold_in(keys[16], 71), 0)
    mem_slots = draw_mem_slots(jax.random.fold_in(keys[16], 71), 0)
    return {"tokens": tokens, "w_qkv": w_qkv, "bias_qv": bias_qv, "w_out": w_out, "bias_out": bias_out, "gain_one": gain_one, "shift_one": shift_one, "w_up": w_up, "bias_up": bias_up, "w_down": w_down, "bias_down": bias_down, "gain_two": gain_two, "shift_two": shift_two, "grad_out": grad_out, "parent": parent, "mem_slots": mem_slots}


EPSILON = 1e-12
MASKED = -1e+30

@jax.custom_vjp
def low(v):
    return lax.optimization_barrier(v.astype(jnp.bfloat16)).astype(jnp.float32)

@jax.custom_vjp
def low_back(v):
    return v

def low_keep(v):
    return (low(v), None)

def low_pass(kept, grad):
    return (grad,)

def back_keep(v):
    return (v, None)

def back_low(kept, grad):
    return (low(grad),)
low.defvjp(low_keep, low_pass)
low_back.defvjp(back_keep, back_low)

def normalize(values, gain, shift):
    average = lax.optimization_barrier(jnp.mean(values, axis=-1, keepdims=True))
    centered = values - average
    variance = lax.optimization_barrier(jnp.mean(centered * centered, axis=-1, keepdims=True))
    return centered * lax.rsqrt(variance + EPSILON) * gain + shift

def allowed_mask(local_parent, slot_ids):
    seg_count = local_parent.shape[0]
    seg_index = jnp.arange(seg_count, dtype=jnp.int32)
    ancestor = jnp.zeros((seg_count, seg_count), dtype=jnp.bool_)
    current = local_parent
    for hop in range(seg_count):
        matches = current[:, None] == seg_index[None, :]
        ancestor = jnp.logical_or(ancestor, matches)
        following = lax.optimization_barrier(jnp.sum(jnp.where(matches, local_parent[None, :], 0), axis=1)).astype(jnp.int32)
        current = jnp.where(jnp.any(matches, axis=1), following, -1).astype(jnp.int32)
    offsets = jnp.arange(SEG, dtype=jnp.int32)
    memory = jnp.any(slot_ids[:, :, None] == offsets[None, None, :], axis=1).reshape(seg_count * SEG)
    row_seg = jnp.arange(seg_count * SEG, dtype=jnp.int32) // SEG
    same_seg = row_seg[:, None] == row_seg[None, :]
    reach_all = jnp.repeat(jnp.repeat(ancestor, SEG, axis=0), SEG, axis=1)
    return jnp.logical_or(same_seg, jnp.logical_and(reach_all, memory[None, :]))

def block_forward(tokens_f, w_qkv, bias_qv, w_out, bias_out, gain_one, shift_one, w_up, bias_up, w_down, bias_down, gain_two, shift_two, allowed):
    highest = lax.Precision.HIGHEST
    row_count = tokens_f.shape[0]
    queries = low_back(low(jnp.dot(tokens_f, w_qkv[0], precision=highest) + bias_qv[0]))
    key_rows = low_back(low(jnp.dot(tokens_f, w_qkv[1], precision=highest)))
    value_rows = low_back(low(jnp.dot(tokens_f, w_qkv[2], precision=highest) + bias_qv[1]))
    head_shape = (row_count, HEADS, HD)
    scores = jnp.einsum('qhd,khd->hqk', queries.reshape(head_shape), key_rows.reshape(head_shape), precision=highest) * HD ** (-0.5)
    scores = low_back(jnp.where(allowed[None], scores, MASKED))
    row_max = lax.optimization_barrier(jnp.max(scores, axis=-1, keepdims=True))
    raised = jnp.exp(scores - row_max)
    chances = raised / lax.optimization_barrier(jnp.sum(raised, axis=-1, keepdims=True))
    mixed_heads = jnp.einsum('hqk,khd->qhd', low(chances), value_rows.reshape(head_shape), precision=highest)
    mixed_heads = low_back(low(mixed_heads.reshape(row_count, D)))
    attended = low_back(jnp.dot(mixed_heads, w_out, precision=highest) + bias_out)
    hidden = normalize(tokens_f + attended, gain_one, shift_one)
    inner_pre = low_back(jnp.dot(low(hidden), w_up, precision=highest) + bias_up)
    acted = low(jax.nn.gelu(inner_pre, approximate=False))
    ffn_out = low_back(jnp.dot(acted, w_down, precision=highest) + bias_down)
    return normalize(hidden + ffn_out, gain_two, shift_two)

def reference(tokens, w_qkv, bias_qv, w_out, bias_out, gain_one, shift_one, w_up, bias_up, w_down, bias_down, gain_two, shift_two, grad_out, parent, mem_slots):
    tree_count = tokens.shape[0] // TOK_DEV
    params = tuple((weight_arg.astype(jnp.float32) for weight_arg in (w_qkv, bias_qv, w_out, bias_out, gain_one, shift_one, w_up, bias_up, w_down, bias_down, gain_two, shift_two)))
    tree_tokens = tokens.astype(jnp.float32).reshape(tree_count, TOK_DEV, D)
    tree_grads = grad_out.astype(jnp.float32).reshape(tree_count, TOK_DEV, D)
    starts = jnp.arange(tree_count, dtype=jnp.int32)[:, None] * TREE_SEGS
    tree_parents = (parent.reshape(tree_count, TREE_SEGS) - starts).astype(jnp.int32)
    tree_slots = mem_slots.reshape(tree_count, TREE_SEGS, MEMW)

    def per_tree(running, tree_item):
        tokens_f, cotangent, local_parent, slot_ids = tree_item
        allowed = allowed_mask(local_parent, slot_ids)

        def forward_fn(inputs, *weights):
            return block_forward(inputs, *weights, allowed)
        result, pullback = jax.vjp(jax.checkpoint(forward_fn), tokens_f, *params)
        pulled = pullback(cotangent)
        running = tuple((running_sum + extra_term for running_sum, extra_term in zip(running, pulled[1:])))
        return (running, (result.astype(jnp.bfloat16), pulled[0].astype(jnp.bfloat16)))
    zeros_init = tuple((jnp.zeros_like(weight_arg) for weight_arg in params))
    summed, (outputs, grad_rows) = lax.scan(per_tree, zeros_init, (tree_tokens, tree_grads, tree_parents, tree_slots))
    return (outputs.reshape(tree_count * TOK_DEV, D), grad_rows.reshape(tree_count * TOK_DEV, D), summed[0], summed[1], summed[2], summed[3], summed[4], summed[5], summed[6], summed[7], summed[8], summed[9], summed[10], summed[11])
```

```python
import functools


import jax
import jax.numpy as jnp
from jax import lax
from jax.experimental import pallas as pl
from jax.experimental.pallas import tpu as pltpu
from jax.sharding import PartitionSpec as P


MESH = pl.DeviceIdType.MESH
BR, BC = 128, 384
SPREAD = 2
SLOTS = 16


class Place:
    def __init__(self):
        me = lax.axis_index("dp")
        self.core = lax.rem(me, 2)
        self.x = lax.rem(me // 2, 2)
        self.z = me // 4
        self.sib = me + 1 - 2 * self.core
        self.xn = me + 2 - 4 * self.x
        self.zp = me + 4 - 8 * lax.rem(self.z, 2)
        self.zm = me + 4 * (3 - 2 * self.z)
        self.end = (self.z == 0) | (self.z == 3)
        self.mid = (self.z == 1) | (self.z == 2)


def sum_barrier(pos):
    barrier = pltpu.get_barrier_semaphore()

    def greet(dev):
        pl.semaphore_signal(barrier, inc=1, device_id={"dp": dev}, device_id_type=MESH)

    greet(pos.sib)
    greet(pos.xn)
    greet(pos.zp)

    @pl.when(pos.mid)
    def _():
        greet(pos.zm)

    pl.semaphore_wait(barrier, jnp.where(pos.mid, 4, 3))


def make_tick(pos, grads, from_core, from_one, from_two, from_three, sent, got, credit, count, finish):
    half = BR // 2
    quarter = BR // 4

    def copy(stage, block, source, target, device):
        slot = lax.rem(block, SLOTS)
        return pltpu.make_async_remote_copy(
            src_ref=source,
            dst_ref=target,
            send_sem=sent.at[stage, slot],
            recv_sem=got.at[stage, slot],
            device_id={"dp": device},
            device_id_type=MESH,
        )

    def rows(block, start, size):
        return grads.at[block, pl.ds(pl.multiple_of(start, quarter), size)]

    def add(block, start, size, landed):
        where = pl.ds(pl.multiple_of(start, quarter), size)
        grads[block, where] = grads[block, where] + landed[...]

    def free(index, device):
        pl.semaphore_signal(credit.at[index], inc=1, device_id={"dp": device}, device_id_type=MESH)

    def claim(index):
        pl.semaphore_wait(credit.at[index], 1)

    x_first = pos.core == 0
    z_first = pos.core == 1
    mine = pos.core * half
    xrow = pos.x * quarter
    xrow_other = (1 - pos.x) * quarter
    far = lax.rem(pos.z, 2) == 0
    keep = half + jnp.where(far, quarter, 0)
    give = half + jnp.where(far, 0, quarter)

    def core_out(block):
        return copy(0, block, rows(block, (1 - pos.core) * half, half), from_core.at[lax.rem(block, SLOTS)], pos.sib)

    def x_one(block):
        return copy(1, block, rows(block, xrow_other, quarter), from_one.at[lax.rem(block, SLOTS), pl.ds(0, quarter)], pos.xn)

    def z_one(block):
        return copy(1, block, rows(block, half, half), from_one.at[lax.rem(block, SLOTS)], pos.zp)

    def x_two(block):
        return copy(2, block, rows(block, xrow, quarter), from_two.at[lax.rem(block, SLOTS)], pos.zp)

    def z_two(block):
        return copy(2, block, rows(block, give, quarter), from_two.at[lax.rem(block, SLOTS)], pos.zm)

    def x_three(block):
        return copy(3, block, rows(block, xrow, quarter), from_three.at[lax.rem(block, SLOTS)], pos.zm)

    def z_three(block):
        return copy(3, block, rows(block, keep, quarter), from_three.at[lax.rem(block, SLOTS)], pos.xn)

    def x_four(block):
        return copy(4, block, rows(block, xrow, quarter), rows(block, xrow, quarter), pos.zp)

    def z_four(block):
        return copy(4, block, rows(block, keep, quarter), rows(block, keep, quarter), pos.zm)

    def z_four_in(block):
        return copy(4, block, rows(block, give, quarter), rows(block, give, quarter), pos.zm)

    def x_five(block):
        return copy(5, block, rows(block, xrow, quarter), rows(block, xrow, quarter), pos.xn)

    def x_five_in(block):
        return copy(5, block, rows(block, xrow_other, quarter), rows(block, xrow_other, quarter), pos.xn)

    def z_five(block):
        return copy(5, block, rows(block, half, half), rows(block, half, half), pos.zp)

    def core_six(block):
        return copy(6, block, rows(block, mine, half), rows(block, mine, half), pos.sib)

    def core_six_in(block):
        return copy(6, block, rows(block, (1 - pos.core) * half, half), rows(block, (1 - pos.core) * half, half), pos.sib)

    def stage_zero(block):
        core_out(block).start()

    def stage_one(block):
        core_out(block).wait()
        free(2, pos.sib)
        add(block, mine, half, from_core.at[lax.rem(block, SLOTS)])

        @pl.when(x_first)
        def _():
            x_one(block).start()

        @pl.when(z_first & pos.end)
        def _():
            z_one(block).start()

    def stage_two(block):
        @pl.when(x_first)
        def _():
            x_one(block).wait()
            free(1, pos.xn)
            add(block, xrow, quarter, from_one.at[lax.rem(block, SLOTS), pl.ds(0, quarter)])

            @pl.when(pos.end)
            def _():
                x_two(block).start()

        @pl.when(z_first & pos.end)
        def _():
            z_one(block).wait_send()
            free(1, pos.zp)

        @pl.when(z_first & pos.mid)
        def _():
            z_one(block).wait_recv()
            add(block, half, half, from_one.at[lax.rem(block, SLOTS)])
            z_two(block).start()

    def stage_three(block):
        @pl.when(x_first & pos.end)
        def _():
            x_two(block).wait_send()
            free(0, pos.zp)

        @pl.when(x_first & pos.mid)
        def _():
            x_two(block).wait_recv()
            add(block, xrow, quarter, from_two.at[lax.rem(block, SLOTS)])
            x_three(block).start()

        @pl.when(z_first & pos.mid)
        def _():
            z_two(block).wait()
            free(0, pos.zm)
            add(block, keep, quarter, from_two.at[lax.rem(block, SLOTS)])
            z_three(block).start()

    def stage_four(block):
        @pl.when(x_first & pos.mid)
        def _():
            x_three(block).wait()
            add(block, xrow, quarter, from_three.at[lax.rem(block, SLOTS)])
            claim(0)
            x_four(block).start()

        @pl.when(z_first & pos.mid)
        def _():
            z_three(block).wait()
            add(block, keep, quarter, from_three.at[lax.rem(block, SLOTS)])
            claim(0)
            z_four(block).start()

    def stage_five(block):
        @pl.when(x_first)
        def _():
            @pl.when(pos.end)
            def _():
                x_four(block).wait_recv()

            @pl.when(pos.mid)
            def _():
                x_four(block).wait_send()

            claim(1)
            x_five(block).start()

        @pl.when(z_first & pos.mid)
        def _():
            z_four(block).wait_send()
            z_four_in(block).wait_recv()
            claim(1)
            z_five(block).start()

    def stage_six(block):
        @pl.when(x_first)
        def _():
            x_five(block).wait_send()
            x_five_in(block).wait_recv()

        @pl.when(z_first & pos.end)
        def _():
            z_five(block).wait_recv()

        @pl.when(z_first & pos.mid)
        def _():
            z_five(block).wait_send()

        claim(2)
        core_six(block).start()

    def stage_seven(block):
        core_six(block).wait_send()
        core_six_in(block).wait_recv()
        finish(block)

    stages = (stage_zero, stage_one, stage_two, stage_three, stage_four, stage_five, stage_six, stage_seven)

    def tick(step):
        for index in reversed(range(8)):
            block = step - SPREAD * index

            @pl.when((block >= 0) & (block < count))
            def _(index=index, block=block):
                stages[index](block)

    return tick


def sum_scratch():
    return [
        pltpu.VMEM((SLOTS, BR // 2, BC), jnp.float32),
        pltpu.VMEM((SLOTS, BR // 2, BC), jnp.float32),
        pltpu.VMEM((SLOTS, BR // 4, BC), jnp.float32),
        pltpu.VMEM((SLOTS, BR // 4, BC), jnp.float32),
        pltpu.SemaphoreType.DMA((7, SLOTS)),
        pltpu.SemaphoreType.DMA((7, SLOTS)),
        pltpu.SemaphoreType.REGULAR((3,)),
    ]


def sum_kernel(count, grads_in, out, grads, a, b, c, d, sent, got, credit, out_sem, in_sem):
    pos = Place()
    load = pltpu.make_async_copy(grads_in, grads, in_sem)
    load.start()
    sum_barrier(pos)
    load.wait()

    def put(block):
        return pltpu.make_async_copy(grads.at[block], out.at[block], out_sem.at[lax.rem(block, 4)])

    def finish(block):
        @pl.when(block >= 4)
        def _():
            put(block - 4).wait()

        put(block).start()

    tick = make_tick(pos, grads, a, b, c, d, sent, got, credit, count, finish)

    @pl.loop(0, count + 7 * SPREAD)
    def _(step):
        tick(step)

    for block in range(count - 4, count):
        put(block).wait()


def sum_blocks(blocks):
    count = blocks.shape[0]
    return pl.pallas_call(
        functools.partial(sum_kernel, count),
        out_shape=jax.ShapeDtypeStruct(blocks.shape, jnp.float32),
        in_specs=[pl.BlockSpec(memory_space=pl.ANY)],
        out_specs=pl.BlockSpec(memory_space=pl.ANY),
        scratch_shapes=[pltpu.VMEM(blocks.shape, jnp.float32)]
        + sum_scratch()
        + [pltpu.SemaphoreType.DMA((4,)), pltpu.SemaphoreType.DMA],
        compiler_params=pltpu.CompilerParams(collective_id=1, has_side_effects=True, vmem_limit_bytes=60 * 2**20),
        name="sum_blocks",
    )(blocks)


CR, CC = 64, 384
CHUNKS = 24
BF = jnp.bfloat16


def gather_barrier(pos, other):
    barrier = pltpu.get_barrier_semaphore()
    for where in ({"tensor": other}, {"dp": pos.xn}, {"dp": pos.zp}, {"dp": pos.sib}):
        pl.semaphore_signal(barrier, inc=1, device_id=where, device_id_type=MESH)
    pl.semaphore_wait(barrier, 4)


def chunk_parts(piece, chunk, kind):
    if kind == 0:
        return [(piece * 384 + chunk * 64, 64, 0, 0)]
    if kind == 1:
        return [(piece * 64 + (chunk - 6) * 32, 32, 384 * q, 32 * q) for q in range(2)]
    if kind == 2:
        return [(piece * 128 + (chunk - 8) * 16, 16, 384 * q, 16 * q) for q in range(4)]
    return [(piece * 256 + (chunk - 16) * 32, 32, 384 * q, 32 * q) for q in range(2)]


BOUNDS = ((0, 6), (6, 8), (8, 16), (16, 24))
UNIT = (64, 32, 16, 32)


def make_gather(pos, own, theirs, staged, landed, sent, got):
    other = 1 - lax.axis_index("tensor")
    odd = lax.rem(pos.z, 2)
    ky = jnp.where(pos.x == 0, odd, 2)
    kx = jnp.where(pos.x == 0, 2, odd)
    kz = 1 - odd
    piece_y = 2 * ky + pos.core
    piece_x = 2 * kx + pos.core
    piece_z = 2 * kz + pos.core
    sib_y = 2 * ky + 1 - pos.core
    sib_x = 2 * kx + 1 - pos.core
    sib_z = 2 * kz + 1 - pos.core

    def copy(lane, chunk, source, piece, where):
        return pltpu.make_async_remote_copy(
            src_ref=source,
            dst_ref=landed.at[piece, chunk],
            send_sem=sent.at[lane, chunk],
            recv_sem=got.at[lane, chunk],
            device_id=where,
            device_id_type=MESH,
        )

    def over_y(chunk):
        return copy(0, chunk, staged.at[chunk], piece_y, {"tensor": other})

    def over_x(chunk, piece):
        return copy(1, chunk, landed.at[piece, chunk], piece, {"dp": pos.xn})

    def over_z(chunk, piece):
        return copy(2, chunk, landed.at[piece, chunk], piece, {"dp": pos.zp})

    def over_core(lane, chunk, piece):
        return copy(lane, chunk, landed.at[piece, chunk], piece, {"dp": pos.sib})

    def stage_own():
        for kind in range(4):
            lo, hi = BOUNDS[kind]

            @pl.loop(lo, hi)
            def _(chunk, kind=kind):
                for row, rows, column, at in chunk_parts(piece_y, chunk, kind):
                    staged[chunk, pl.ds(at, rows)] = own[kind][
                        pl.ds(pl.multiple_of(row, UNIT[kind]), rows), pl.ds(column, CC)
                    ].astype(jnp.float32)

    def send_own():
        @pl.loop(0, CHUNKS)
        def _(chunk):
            over_y(chunk).start()

    def unpack(chunk):
        for kind in range(4):
            lo, hi = BOUNDS[kind]

            @pl.when((chunk >= lo) & (chunk < hi))
            def _(kind=kind):
                @pl.loop(0, 6)
                def _(piece):
                    for row, rows, column, at in chunk_parts(piece, chunk, kind):
                        theirs[kind][pl.ds(pl.multiple_of(row, UNIT[kind]), rows), pl.ds(column, CC)] = landed[
                            piece, chunk, pl.ds(at, rows)
                        ].astype(BF)

    def guarded(chunk, body):
        @pl.when((chunk >= 0) & (chunk < CHUNKS))
        def _():
            body(chunk)

    def first(chunk):
        over_y(chunk).wait_recv()
        over_x(chunk, piece_y).start()

        @pl.when(pos.x == 0)
        def _():
            over_z(chunk, piece_y).start()

        over_core(3, chunk, piece_y).start()

    def second(chunk):
        over_x(chunk, piece_x).wait_recv()

        @pl.when(pos.x == 1)
        def _():
            over_z(chunk, piece_x).start()

        over_core(4, chunk, piece_x).start()

    def third(chunk):
        over_z(chunk, piece_z).wait_recv()
        over_core(5, chunk, piece_z).start()

    def fourth(chunk):
        over_core(3, chunk, sib_y).wait_recv()
        over_core(4, chunk, sib_x).wait_recv()
        over_core(5, chunk, sib_z).wait_recv()
        over_y(chunk).wait_send()
        over_x(chunk, piece_y).wait_send()
        over_z(chunk, piece_y).wait_send()
        over_core(3, chunk, piece_y).wait_send()
        over_core(4, chunk, piece_x).wait_send()
        over_core(5, chunk, piece_z).wait_send()
        unpack(chunk)

    def tick(step):
        guarded(step - 6, fourth)
        guarded(step - 4, third)
        guarded(step - 2, second)
        guarded(step, first)

    return stage_own, send_own, tick


GATHER_TICKS = CHUNKS + 6


def gather_scratch():
    return [
        pltpu.VMEM((CHUNKS, CR, CC), jnp.float32),
        pltpu.VMEM((6, CHUNKS, CR, CC), jnp.float32),
        pltpu.SemaphoreType.DMA((6, CHUNKS)),
        pltpu.SemaphoreType.DMA((6, CHUNKS)),
    ]


def swap_small(small, small_out, sems):
    return pltpu.make_async_remote_copy(
        src_ref=small,
        dst_ref=small_out,
        send_sem=sems.at[0],
        recv_sem=sems.at[1],
        device_id={"tensor": 1 - lax.axis_index("tensor")},
        device_id_type=MESH,
    )


def gather_kernel(a, b, c, d, small, oa, ob, oc, od, small_out, staged, landed, sent, got, sems):
    pos = Place()
    stage_own, send_own, tick = make_gather(pos, (a, b, c, d), (oa, ob, oc, od), staged, landed, sent, got)
    stage_own()
    gather_barrier(pos, 1 - lax.axis_index("tensor"))
    swap = swap_small(small, small_out, sems)
    swap.start()
    send_own()

    @pl.loop(0, GATHER_TICKS)
    def _(step):
        tick(step)

    swap.wait()


def gather(ws):
    v = pl.BlockSpec(memory_space=pltpu.VMEM)
    return pl.pallas_call(
        gather_kernel,
        out_shape=[jax.ShapeDtypeStruct(w.shape, w.dtype) for w in ws],
        in_specs=[v] * 5,
        out_specs=[v] * 5,
        scratch_shapes=gather_scratch() + [pltpu.SemaphoreType.DMA((2,))],
        compiler_params=pltpu.CompilerParams(collective_id=0, has_side_effects=True, vmem_limit_bytes=60 * 2**20),
        name="gather_weights",
    )(*ws)


HD = 64
SEG = 148
MEMW = 10
F32 = jnp.float32
EPSILON = 1e-12
MASKED = -1e30
WIN = 160
MEMP = 96
SEGS = 8
PAIR = 2 * HD

CONTRACT_LAST = (((1,), (1,)), ((), ()))
CONTRACT_FIRST = (((0,), (0,)), ((), ()))


def mm(a, b):
    return jnp.dot(a, b, preferred_element_type=F32)


def mm_t(a, b):
    return lax.dot_general(a, b, CONTRACT_LAST, preferred_element_type=F32)


def t_mm(a, b):
    return lax.dot_general(a, b, CONTRACT_FIRST, preferred_element_type=F32)


def build_masks(parent, base, colbias):
    lane = lax.broadcasted_iota(jnp.int32, (1, WIN + MEMP), 1)
    in_mem = [
        ((lane >= WIN + MEMW * t) & (lane < WIN + MEMW * (t + 1))).astype(F32) for t in range(SEGS)
    ]
    reach = [jnp.zeros((1, WIN + MEMP), F32)]
    for s in range(1, SEGS):
        row = jnp.zeros((1, WIN + MEMP), F32)
        for t in range(s):
            hit = jnp.where(parent[s] - base == t, 1.0, 0.0)
            row = row + hit * jnp.maximum(reach[t], in_mem[t])
        reach.append(row)
    for s in range(SEGS):
        off = 4 * (s % 4)
        inside = ((lane >= off) & (lane < off + SEG)).astype(F32)
        colbias[s : s + 1, :] = jnp.where(jnp.maximum(inside, reach[s]) > 0.0, 0.0, MASKED)


def build_select(slot_rows, select):
    place = lax.broadcasted_iota(jnp.int32, select.shape, 1)
    select[...] = (slot_rows[...] == place).astype(F32).astype(BF)


def window(s):
    return pl.multiple_of(144 * s + 16 * (s // 4), 16), 4 * lax.rem(s, 4)


def lane_halves():
    lane = lax.broadcasted_iota(jnp.int32, (1, PAIR), 1)
    left = (lane < HD).astype(F32)
    return left.astype(BF), (1.0 - left).astype(BF), lane < HD


def valid_rows(off):
    row = lax.broadcasted_iota(jnp.int32, (WIN, 1), 0)
    return row, (row >= off) & (row < off + SEG)


def softmax_parts(qs, kk, bias):
    scores = mm_t(qs, kk) * HD ** (-0.5) + bias
    top = jnp.max(scores, axis=-1, keepdims=True)
    raised = jnp.exp(scores - top)
    return raised, 1.0 / jnp.sum(raised, axis=-1, keepdims=True)


def attend_pair(q, k, v, kmem, vmem, colbias, mixed, s, columns):
    left, right, is_left = lane_halves()
    at, off = window(s)
    rows = pl.ds(at, WIN)
    qw = q[rows, columns]
    qs = jnp.concatenate([qw * left, qw * right], axis=0)
    kk = jnp.concatenate([k[rows, columns], kmem[:, columns]], axis=0)
    vv = jnp.concatenate([v[rows, columns], vmem[:, columns]], axis=0)
    raised, scale = softmax_parts(qs, kk, colbias[pl.ds(s, 1), :])
    both = mm((raised * scale).astype(BF), vv)
    out = jnp.where(is_left, both[:WIN], both[WIN:])
    row, valid = valid_rows(off)
    old = mixed[rows, columns].astype(F32)
    mixed[rows, columns] = jnp.where(row >= off, out, old).astype(BF)


def attend_back_pair(q, k, v, kmem, vmem, colbias, dmix, dq, dk, dv, dkmem, dvmem, s, columns, acc):
    left, right, is_left = lane_halves()
    at, off = window(s)
    rows = pl.ds(at, WIN)
    qw = q[rows, columns]
    qs = jnp.concatenate([qw * left, qw * right], axis=0)
    kk = jnp.concatenate([k[rows, columns], kmem[:, columns]], axis=0)
    vv = jnp.concatenate([v[rows, columns], vmem[:, columns]], axis=0)
    dw = dmix[rows, columns]
    ds_in = jnp.concatenate([dw * left, dw * right], axis=0)
    raised, scale = softmax_parts(qs, kk, colbias[pl.ds(s, 1), :])
    row, valid = valid_rows(off)
    keep = jnp.where(valid, 1.0, 0.0)
    chances = raised * (scale * jnp.concatenate([keep, keep], axis=0))
    dp = mm_t(ds_in, vv)
    inner = jnp.sum(chances * dp, axis=-1, keepdims=True)
    ds = (chances * (dp - inner)).astype(BF)
    pb = chances.astype(BF)
    dqs = mm(ds, kk)
    new = jnp.where(is_left, dqs[:WIN], dqs[WIN:]) * HD ** (-0.5)
    old = dq[rows, columns].astype(F32)
    dq[rows, columns] = jnp.where(row >= off, new, old).astype(BF)
    dks = t_mm(ds, qs)
    dvs = t_mm(pb, ds_in)
    dk[rows, acc] = dk[rows, acc] + dks[:WIN]
    dv[rows, acc] = dv[rows, acc] + dvs[:WIN]
    dkmem[:, acc] = dkmem[:, acc] + dks[WIN:]
    dvmem[:, acc] = dvmem[:, acc] + dvs[WIN:]


def spread(select, part):
    high = part.astype(BF)
    low = (part - high.astype(F32)).astype(BF)
    return t_mm(select, high) + t_mm(select, low)


def forward_attention_kernel(parent, slot_rows, q, k, v, mixed, colbias, select, kmem, vmem):
    base = lax.axis_index("dp") * SEGS
    build_masks(parent, base, colbias)
    build_select(slot_rows, select)
    kmem[...] = mm(select[...], k[...]).astype(BF)
    vmem[...] = mm(select[...], v[...]).astype(BF)
    pairs = q.shape[1] // PAIR

    @pl.loop(0, SEGS)
    def _(s):
        for pair in range(pairs):
            attend_pair(q, k, v, kmem, vmem, colbias, mixed, s, pl.ds(pair * PAIR, PAIR))


def backward_attention_kernel(
    parent, slot_rows, q, k, v, dmix, dq, dk, dv, colbias, select, kmem, vmem, dka, dva, dkm, dvm
):
    base = lax.axis_index("dp") * SEGS
    build_masks(parent, base, colbias)
    build_select(slot_rows, select)
    kmem[...] = mm(select[...], k[...]).astype(BF)
    vmem[...] = mm(select[...], v[...]).astype(BF)
    pairs = q.shape[1] // PAIR
    for ref in (dka, dva, dkm, dvm):
        ref[...] = jnp.zeros(ref.shape, F32)

    @pl.loop(0, SEGS)
    def _(s):
        for pair in range(pairs):
            columns = pl.ds(pair * PAIR, PAIR)
            attend_back_pair(
                q, k, v, kmem, vmem, colbias, dmix, dq, dka, dva, dkm, dvm, s, columns, columns
            )

    for pair in range(pairs):
        columns = pl.ds(pair * PAIR, PAIR)
        dk[:, columns] = ((dka[:, columns] + spread(select[...], dkm[:, columns])) * HD ** (-0.5)).astype(BF)
        dv[:, columns] = (dva[:, columns] + spread(select[...], dvm[:, columns])).astype(BF)


def attention_call(kernel, outs, parent, slot_rows, arrays, scratch, name):
    rows, width = arrays[0].shape
    vm = pl.BlockSpec(memory_space=pltpu.VMEM)
    return pl.pallas_call(
        kernel,
        out_shape=[jax.ShapeDtypeStruct((rows, width), BF)] * outs,
        in_specs=[pl.BlockSpec(memory_space=pltpu.SMEM), vm] + [vm] * len(arrays),
        out_specs=[vm] * outs,
        scratch_shapes=[
            pltpu.VMEM((SEGS, WIN + MEMP), F32),
            pltpu.VMEM((MEMP, rows), BF),
            pltpu.VMEM((MEMP, width), BF),
            pltpu.VMEM((MEMP, width), BF),
        ]
        + scratch,
        compiler_params=pltpu.CompilerParams(vmem_limit_bytes=60 * 2**20),
        name=name,
    )(parent, slot_rows, *arrays)


def forward_attention(parent, slot_rows, q, k, v):
    return attention_call(forward_attention_kernel, 1, parent, slot_rows, (q, k, v), [], "attend")[0]


def backward_attention(parent, slot_rows, q, k, v, dmix):
    rows, width = q.shape
    scratch = [pltpu.VMEM((rows, width), F32)] * 2 + [pltpu.VMEM((MEMP, width), F32)] * 2
    return attention_call(
        backward_attention_kernel, 3, parent, slot_rows, (q, k, v, dmix), scratch, "attend_back"
    )


def halves_swap(own, small):
    unit = (lax.axis_index("dp") >= 0).astype(F32)

    def other(array):
        arrived = lax.ppermute(array.astype(F32), "tensor", [(0, 1), (1, 0)])
        return (arrived * unit).astype(array.dtype)

    return tuple(other(array) for array in own) + (other(small),)


def norm_stats(values):
    centered = values - jnp.mean(values, axis=-1, keepdims=True)
    inverse = lax.rsqrt(jnp.mean(centered * centered, axis=-1, keepdims=True) + EPSILON)
    return centered * inverse, inverse


def norm_back(grad, normed, inverse, gain):
    scaled = grad * gain
    return inverse * (
        scaled
        - jnp.mean(scaled, axis=-1, keepdims=True)
        - normed * jnp.mean(scaled * normed, axis=-1, keepdims=True)
    )


def gelu_parts(inner):
    phi = 0.5 * (1.0 + lax.erf(inner * (0.5**0.5)))
    density = jnp.exp(-0.5 * inner * inner) * (2.0 * jnp.pi) ** -0.5
    return (inner * phi).astype(BF), phi + inner * density


def split_blocks(array, rows, columns):
    height, width = array.shape
    return (
        array.reshape(height // rows, rows, width // columns, columns)
        .transpose(0, 2, 1, 3)
        .reshape(-1, rows, columns)
    )


def join_blocks(blocks, height, width):
    count, rows, columns = blocks.shape
    return (
        blocks.reshape(height // rows, width // columns, rows, columns)
        .transpose(0, 2, 1, 3)
        .reshape(height, width)
    )


def shards(
    fast,
    tokens,
    w_qkv,
    bias_qv,
    w_out,
    bias_out,
    gain_one,
    shift_one,
    w_up,
    bias_up,
    w_down,
    bias_down,
    gain_two,
    shift_two,
    grad_out,
    parent,
    mem_slots,
):
    depth, width = w_qkv.shape[1:]
    hidden_units = w_up.shape[1]
    own = (w_qkv.reshape(3 * depth, width), w_out, w_up, w_down)
    small = jnp.concatenate(
        [bias_qv, bias_up.reshape(-1, width), jnp.zeros((8 - 2 - hidden_units // width, width), F32)]
    )
    if fast:
        theirs = gather((*own, small))
    else:
        theirs = halves_swap(own, small)
    *theirs, small_theirs = theirs
    w_qkv_both = [own[0].reshape(w_qkv.shape), theirs[0].reshape(w_qkv.shape)]
    w_out_both, w_up_both, w_down_both = ([own[i], theirs[i]] for i in (1, 2, 3))
    bias_qv_both = [bias_qv, small_theirs[:2]]
    bias_up_both = [bias_up, small_theirs[2 : 2 + hidden_units // width].reshape(-1)]

    offsets = jnp.arange(SEGS, dtype=jnp.int32)[:, None] * SEG
    slot_rows = (mem_slots + offsets).reshape(-1, 1)
    slot_rows = jnp.concatenate([slot_rows, jnp.full((MEMP - slot_rows.shape[0], 1), -1, jnp.int32)])

    def project(index, bias):
        parts = []
        for half in range(2):
            part = mm(tokens, w_qkv_both[half][index])
            if bias is not None:
                part = part + bias_qv_both[half][bias]
            parts.append(part.astype(BF))
        return jnp.concatenate(parts, axis=1)

    queries, keys, values = project(0, 0), project(1, None), project(2, 1)
    mixed = forward_attention(parent, slot_rows, queries, keys, values)
    attended = mm(mixed[:, :width], w_out_both[0]) + mm(mixed[:, width:], w_out_both[1])
    resid_one = tokens.astype(F32) + (attended + bias_out)
    normed_one, inverse_one = norm_stats(resid_one)
    hidden = normed_one * gain_one + shift_one
    hidden_low = hidden.astype(BF)
    acted, slope, summed = [], [], []
    for half in range(2):
        inner = mm(hidden_low, w_up_both[half]) + bias_up_both[half]
        act, steep = gelu_parts(inner)
        acted.append(act)
        slope.append(steep)
        summed.append(mm(act, w_down_both[half]))
    resid_two = hidden + ((summed[0] + summed[1]) + bias_down)
    normed_two, inverse_two = norm_stats(resid_two)
    output = (normed_two * gain_two + shift_two).astype(BF)

    cotangent = grad_out.astype(F32)
    d_two = norm_back(cotangent, normed_two, inverse_two, gain_two)
    d_gain_two = jnp.sum(cotangent * normed_two, axis=0)
    d_shift_two = jnp.sum(cotangent, axis=0)
    d_ffn = d_two.astype(BF)
    d_w_down = t_mm(acted[0], d_ffn)
    d_bias_down = jnp.sum(d_ffn.astype(F32), axis=0)
    d_inner = [(mm_t(d_ffn, w_down_both[half]) * slope[half]).astype(BF) for half in range(2)]
    d_w_up = t_mm(hidden_low, d_inner[0])
    d_bias_up = jnp.sum(d_inner[0].astype(F32), axis=0)
    d_hidden = d_two + (mm_t(d_inner[0], w_up_both[0]) + mm_t(d_inner[1], w_up_both[1]))
    d_one = norm_back(d_hidden, normed_one, inverse_one, gain_one)
    d_gain_one = jnp.sum(d_hidden * normed_one, axis=0)
    d_shift_one = jnp.sum(d_hidden, axis=0)
    d_attn = d_one.astype(BF)
    d_w_out = t_mm(mixed[:, :width], d_attn)
    d_bias_out = jnp.sum(d_attn.astype(F32), axis=0)
    d_mixed = jnp.concatenate([mm_t(d_attn, w_out_both[half]).astype(BF) for half in range(2)], axis=1)
    d_qkv = backward_attention(parent, slot_rows, queries, keys, values, d_mixed)
    d_w_qkv = [t_mm(tokens, part[:, :width]) for part in d_qkv]
    d_bias_qv = [jnp.sum(d_qkv[i][:, :width].astype(F32), axis=0) for i in (0, 2)]
    parts = []
    for half in range(2):
        columns = slice(half * width, (half + 1) * width)
        parts.append(sum(mm_t(d_qkv[i][:, columns], w_qkv_both[half][i]) for i in range(3)))
    grad_tokens = ((parts[0] + parts[1]) + d_one).astype(BF)

    vectors = [*d_bias_qv, d_bias_up, d_bias_out, d_gain_one, d_shift_one, d_bias_down, d_gain_two, d_shift_two]
    if fast:
        flat = jnp.concatenate([v.reshape(-1, width) for v in vectors])
        flat = jnp.concatenate([flat, jnp.zeros((BR - flat.shape[0], width), F32)])
        blocks = jnp.concatenate(
            [
                split_blocks(d_w_down, BR, BC),
                split_blocks(d_w_up, BR, BC),
                split_blocks(d_w_out, BR, BC),
                *[split_blocks(part, BR, BC) for part in d_w_qkv],
                flat[None],
            ]
        )
        blocks = sum_blocks(blocks)
        g_w_down = join_blocks(blocks[:24], *w_down.shape)
        g_w_up = join_blocks(blocks[24:48], *w_up.shape)
        g_w_out = join_blocks(blocks[48:54], *w_out.shape)
        g_w_qkv = blocks[54:72].reshape(w_qkv.shape)
        flat = blocks[72]
        sums, row = [], 0
        for v in vectors:
            sums.append(flat[row : row + v.size // width].reshape(-1))
            row += v.size // width
    else:
        g_w_down, g_w_up, g_w_out, g_w_qkv, *sums = lax.psum(
            (d_w_down, d_w_up, d_w_out, jnp.stack(d_w_qkv), *vectors), "dp"
        )
    g_bias_q, g_bias_v, g_bias_up, g_bias_out, g_gain_one, g_shift_one, g_bias_down, g_gain_two, g_shift_two = sums
    return (
        output,
        grad_tokens,
        g_w_qkv,
        jnp.stack([g_bias_q, g_bias_v]),
        g_w_out,
        g_bias_out,
        g_gain_one,
        g_shift_one,
        g_w_up,
        g_bias_up,
        g_w_down,
        g_bias_down,
        g_gain_two,
        g_shift_two,
    )


def solution(mesh):
    fast = mesh.shape["dp"] == 16 and mesh.shape["tensor"] == 2
    rows, whole = P("dp", None), P()
    return jax.shard_map(
        functools.partial(shards, fast),
        mesh=mesh,
        in_specs=(
            rows,
            P(None, None, "tensor"),
            P(None, "tensor"),
            P("tensor", None),
            whole,
            whole,
            whole,
            P(None, "tensor"),
            P("tensor"),
            P("tensor", None),
            whole,
            whole,
            whole,
            rows,
            P("dp"),
            rows,
        ),
        out_specs=(
            rows,
            rows,
            P(None, None, "tensor"),
            P(None, "tensor"),
            P("tensor", None),
            whole,
            whole,
            whole,
            P(None, "tensor"),
            P("tensor"),
            P("tensor", None),
            whole,
            whole,
            whole,
        ),
        check_vma=False,
    )
```

```python
import functools


import jax
import jax.numpy as jnp
from jax import lax
from jax.experimental import pallas as pl
from jax.experimental.pallas import tpu as pltpu
from jax.sharding import PartitionSpec as P


MESH = pl.DeviceIdType.MESH
BR, BC = 384, 128
SPREAD = 2
SLOTS = 16


class Place:
    def __init__(self):
        me = lax.axis_index("dp")
        self.core = lax.rem(me, 2)
        self.x = lax.rem(me // 2, 2)
        self.z = me // 4
        self.sib = me + 1 - 2 * self.core
        self.xn = me + 2 - 4 * self.x
        self.zp = me + 4 - 8 * lax.rem(self.z, 2)
        self.zm = me + 4 * (3 - 2 * self.z)
        self.end = (self.z == 0) | (self.z == 3)
        self.mid = (self.z == 1) | (self.z == 2)


def sum_barrier(pos):
    barrier = pltpu.get_barrier_semaphore()

    def greet(dev):
        pl.semaphore_signal(barrier, inc=1, device_id={"dp": dev}, device_id_type=MESH)

    greet(pos.sib)
    greet(pos.xn)
    greet(pos.zp)

    @pl.when(pos.mid)
    def _():
        greet(pos.zm)

    pl.semaphore_wait(barrier, jnp.where(pos.mid, 4, 3))


def make_tick(pos, grads, from_core, from_one, from_two, from_three, sent, got, credit, count, finish):
    half = BR // 2
    quarter = BR // 4

    def copy(stage, block, source, target, device):
        slot = lax.rem(block, SLOTS)
        return pltpu.make_async_remote_copy(
            src_ref=source,
            dst_ref=target,
            send_sem=sent.at[stage, slot],
            recv_sem=got.at[stage, slot],
            device_id={"dp": device},
            device_id_type=MESH,
        )

    def rows(block, start, size):
        return grads.at[block, pl.ds(pl.multiple_of(start, quarter), size)]

    def add(block, start, size, landed):
        where = pl.ds(pl.multiple_of(start, quarter), size)
        grads[block, where] = grads[block, where] + landed[...]

    def free(index, device):
        pl.semaphore_signal(credit.at[index], inc=1, device_id={"dp": device}, device_id_type=MESH)

    def claim(index):
        pl.semaphore_wait(credit.at[index], 1)

    x_first = pos.core == 0
    z_first = pos.core == 1
    mine = pos.core * half
    xrow = pos.x * quarter
    xrow_other = (1 - pos.x) * quarter
    far = lax.rem(pos.z, 2) == 0
    keep = half + jnp.where(far, quarter, 0)
    give = half + jnp.where(far, 0, quarter)

    def core_out(block):
        return copy(0, block, rows(block, (1 - pos.core) * half, half), from_core.at[lax.rem(block, SLOTS)], pos.sib)

    def x_one(block):
        return copy(1, block, rows(block, xrow_other, quarter), from_one.at[lax.rem(block, SLOTS), pl.ds(0, quarter)], pos.xn)

    def z_one(block):
        return copy(1, block, rows(block, half, half), from_one.at[lax.rem(block, SLOTS)], pos.zp)

    def x_two(block):
        return copy(2, block, rows(block, xrow, quarter), from_two.at[lax.rem(block, SLOTS)], pos.zp)

    def z_two(block):
        return copy(2, block, rows(block, give, quarter), from_two.at[lax.rem(block, SLOTS)], pos.zm)

    def x_three(block):
        return copy(3, block, rows(block, xrow, quarter), from_three.at[lax.rem(block, SLOTS)], pos.zm)

    def z_three(block):
        return copy(3, block, rows(block, keep, quarter), from_three.at[lax.rem(block, SLOTS)], pos.xn)

    def x_four(block):
        return copy(4, block, rows(block, xrow, quarter), rows(block, xrow, quarter), pos.zp)

    def z_four(block):
        return copy(4, block, rows(block, keep, quarter), rows(block, keep, quarter), pos.zm)

    def z_four_in(block):
        return copy(4, block, rows(block, give, quarter), rows(block, give, quarter), pos.zm)

    def x_five(block):
        return copy(5, block, rows(block, xrow, quarter), rows(block, xrow, quarter), pos.xn)

    def x_five_in(block):
        return copy(5, block, rows(block, xrow_other, quarter), rows(block, xrow_other, quarter), pos.xn)

    def z_five(block):
        return copy(5, block, rows(block, half, half), rows(block, half, half), pos.zp)

    def core_six(block):
        return copy(6, block, rows(block, mine, half), rows(block, mine, half), pos.sib)

    def core_six_in(block):
        return copy(6, block, rows(block, (1 - pos.core) * half, half), rows(block, (1 - pos.core) * half, half), pos.sib)

    def stage_zero(block):
        core_out(block).start()

    def stage_one(block):
        core_out(block).wait()
        free(2, pos.sib)
        add(block, mine, half, from_core.at[lax.rem(block, SLOTS)])

        @pl.when(x_first)
        def _():
            x_one(block).start()

        @pl.when(z_first & pos.end)
        def _():
            z_one(block).start()

    def stage_two(block):
        @pl.when(x_first)
        def _():
            x_one(block).wait()
            free(1, pos.xn)
            add(block, xrow, quarter, from_one.at[lax.rem(block, SLOTS), pl.ds(0, quarter)])

            @pl.when(pos.end)
            def _():
                x_two(block).start()

        @pl.when(z_first & pos.end)
        def _():
            z_one(block).wait_send()
            free(1, pos.zp)

        @pl.when(z_first & pos.mid)
        def _():
            z_one(block).wait_recv()
            add(block, half, half, from_one.at[lax.rem(block, SLOTS)])
            z_two(block).start()

    def stage_three(block):
        @pl.when(x_first & pos.end)
        def _():
            x_two(block).wait_send()
            free(0, pos.zp)

        @pl.when(x_first & pos.mid)
        def _():
            x_two(block).wait_recv()
            add(block, xrow, quarter, from_two.at[lax.rem(block, SLOTS)])
            x_three(block).start()

        @pl.when(z_first & pos.mid)
        def _():
            z_two(block).wait()
            free(0, pos.zm)
            add(block, keep, quarter, from_two.at[lax.rem(block, SLOTS)])
            z_three(block).start()

    def stage_four(block):
        @pl.when(x_first & pos.mid)
        def _():
            x_three(block).wait()
            add(block, xrow, quarter, from_three.at[lax.rem(block, SLOTS)])
            claim(0)
            x_four(block).start()

        @pl.when(z_first & pos.mid)
        def _():
            z_three(block).wait()
            add(block, keep, quarter, from_three.at[lax.rem(block, SLOTS)])
            claim(0)
            z_four(block).start()

    def stage_five(block):
        @pl.when(x_first)
        def _():
            @pl.when(pos.end)
            def _():
                x_four(block).wait_recv()

            @pl.when(pos.mid)
            def _():
                x_four(block).wait_send()

            claim(1)
            x_five(block).start()

        @pl.when(z_first & pos.mid)
        def _():
            z_four(block).wait_send()
            z_four_in(block).wait_recv()
            claim(1)
            z_five(block).start()

    def stage_six(block):
        @pl.when(x_first)
        def _():
            x_five(block).wait_send()
            x_five_in(block).wait_recv()

        @pl.when(z_first & pos.end)
        def _():
            z_five(block).wait_recv()

        @pl.when(z_first & pos.mid)
        def _():
            z_five(block).wait_send()

        claim(2)
        core_six(block).start()

    def stage_seven(block):
        core_six(block).wait_send()
        core_six_in(block).wait_recv()
        finish(block)

    stages = (stage_zero, stage_one, stage_two, stage_three, stage_four, stage_five, stage_six, stage_seven)

    def tick(step):
        for index in reversed(range(8)):
            block = step - SPREAD * index

            @pl.when((block >= 0) & (block < count))
            def _(index=index, block=block):
                stages[index](block)

    return tick


def sum_scratch():
    return [
        pltpu.VMEM((SLOTS, BR // 2, BC), jnp.float32),
        pltpu.VMEM((SLOTS, BR // 2, BC), jnp.float32),
        pltpu.VMEM((SLOTS, BR // 4, BC), jnp.float32),
        pltpu.VMEM((SLOTS, BR // 4, BC), jnp.float32),
        pltpu.SemaphoreType.DMA((7, SLOTS)),
        pltpu.SemaphoreType.DMA((7, SLOTS)),
        pltpu.SemaphoreType.REGULAR((3,)),
    ]


CR, CC = 64, 384
CHUNKS = 24
BF = jnp.bfloat16


def gather_barrier(pos, other):
    barrier = pltpu.get_barrier_semaphore()
    for where in ({"tensor": other}, {"dp": pos.xn}, {"dp": pos.zp}, {"dp": pos.sib}):
        pl.semaphore_signal(barrier, inc=1, device_id=where, device_id_type=MESH)
    pl.semaphore_wait(barrier, 4)


def chunk_parts(piece, chunk, kind):
    if kind == 0:
        return [(piece * 384 + chunk * 64, 64, 0, 0)]
    if kind == 1:
        return [(piece * 64 + (chunk - 6) * 32, 32, 384 * q, 32 * q) for q in range(2)]
    if kind == 2:
        return [(piece * 128 + (chunk - 8) * 16, 16, 384 * q, 16 * q) for q in range(4)]
    return [(piece * 256 + (chunk - 16) * 32, 32, 384 * q, 32 * q) for q in range(2)]


BOUNDS = ((0, 6), (6, 8), (8, 16), (16, 24))
UNIT = (64, 32, 16, 32)


def make_gather(pos, own, theirs, staged, landed, sent, got):
    other = 1 - lax.axis_index("tensor")
    odd = lax.rem(pos.z, 2)
    ky = jnp.where(pos.x == 0, odd, 2)
    kx = jnp.where(pos.x == 0, 2, odd)
    kz = 1 - odd
    piece_y = 2 * ky + pos.core
    piece_x = 2 * kx + pos.core
    piece_z = 2 * kz + pos.core
    sib_y = 2 * ky + 1 - pos.core
    sib_x = 2 * kx + 1 - pos.core
    sib_z = 2 * kz + 1 - pos.core

    def copy(lane, chunk, source, piece, where):
        return pltpu.make_async_remote_copy(
            src_ref=source,
            dst_ref=landed.at[piece, chunk],
            send_sem=sent.at[lane, chunk],
            recv_sem=got.at[lane, chunk],
            device_id=where,
            device_id_type=MESH,
        )

    def over_y(chunk):
        return copy(0, chunk, staged.at[chunk], piece_y, {"tensor": other})

    def over_x(chunk, piece):
        return copy(1, chunk, landed.at[piece, chunk], piece, {"dp": pos.xn})

    def over_z(chunk, piece):
        return copy(2, chunk, landed.at[piece, chunk], piece, {"dp": pos.zp})

    def over_core(lane, chunk, piece):
        return copy(lane, chunk, landed.at[piece, chunk], piece, {"dp": pos.sib})

    def stage_own():
        for kind in range(4):
            lo, hi = BOUNDS[kind]

            @pl.loop(lo, hi)
            def _(chunk, kind=kind):
                for row, rows, column, at in chunk_parts(piece_y, chunk, kind):
                    staged[chunk, pl.ds(at, rows)] = own[kind][
                        pl.ds(pl.multiple_of(row, UNIT[kind]), rows), pl.ds(column, CC)
                    ].astype(jnp.float32)

    def send_own():
        @pl.loop(0, CHUNKS)
        def _(chunk):
            over_y(chunk).start()

    def unpack(chunk):
        for kind in range(4):
            lo, hi = BOUNDS[kind]

            @pl.when((chunk >= lo) & (chunk < hi))
            def _(kind=kind):
                @pl.loop(0, 6)
                def _(piece):
                    for row, rows, column, at in chunk_parts(piece, chunk, kind):
                        theirs[kind][pl.ds(pl.multiple_of(row, UNIT[kind]), rows), pl.ds(column, CC)] = landed[
                            piece, chunk, pl.ds(at, rows)
                        ].astype(BF)

    def guarded(chunk, body):
        @pl.when((chunk >= 0) & (chunk < CHUNKS))
        def _():
            body(chunk)

    def first(chunk):
        over_y(chunk).wait_recv()
        over_x(chunk, piece_y).start()

        @pl.when(pos.x == 0)
        def _():
            over_z(chunk, piece_y).start()

        over_core(3, chunk, piece_y).start()

    def second(chunk):
        over_x(chunk, piece_x).wait_recv()

        @pl.when(pos.x == 1)
        def _():
            over_z(chunk, piece_x).start()

        over_core(4, chunk, piece_x).start()

    def third(chunk):
        over_z(chunk, piece_z).wait_recv()
        over_core(5, chunk, piece_z).start()

    def fourth(chunk):
        over_core(3, chunk, sib_y).wait_recv()
        over_core(4, chunk, sib_x).wait_recv()
        over_core(5, chunk, sib_z).wait_recv()
        over_y(chunk).wait_send()
        over_x(chunk, piece_y).wait_send()
        over_z(chunk, piece_y).wait_send()
        over_core(3, chunk, piece_y).wait_send()
        over_core(4, chunk, piece_x).wait_send()
        over_core(5, chunk, piece_z).wait_send()
        unpack(chunk)

    def tick(step):
        guarded(step - 6, fourth)
        guarded(step - 4, third)
        guarded(step - 2, second)
        guarded(step, first)

    return stage_own, send_own, tick


GATHER_TICKS = CHUNKS + 6


def gather_scratch():
    return [
        pltpu.VMEM((CHUNKS, CR, CC), jnp.float32),
        pltpu.VMEM((6, CHUNKS, CR, CC), jnp.float32),
        pltpu.SemaphoreType.DMA((6, CHUNKS)),
        pltpu.SemaphoreType.DMA((6, CHUNKS)),
    ]


def swap_small(small, small_out, sems):
    return pltpu.make_async_remote_copy(
        src_ref=small,
        dst_ref=small_out,
        send_sem=sems.at[0],
        recv_sem=sems.at[1],
        device_id={"tensor": 1 - lax.axis_index("tensor")},
        device_id_type=MESH,
    )


def gather_kernel(a, b, c, d, small, oa, ob, oc, od, small_out, staged, landed, sent, got, sems):
    pos = Place()
    stage_own, send_own, tick = make_gather(pos, (a, b, c, d), (oa, ob, oc, od), staged, landed, sent, got)
    stage_own()
    gather_barrier(pos, 1 - lax.axis_index("tensor"))
    swap = swap_small(small, small_out, sems)
    swap.start()
    send_own()

    @pl.loop(0, GATHER_TICKS)
    def _(step):
        tick(step)

    swap.wait()


def gather(ws):
    v = pl.BlockSpec(memory_space=pltpu.VMEM)
    return pl.pallas_call(
        gather_kernel,
        out_shape=[jax.ShapeDtypeStruct(w.shape, w.dtype) for w in ws],
        in_specs=[v] * 5,
        out_specs=[v] * 5,
        scratch_shapes=gather_scratch() + [pltpu.SemaphoreType.DMA((2,))],
        compiler_params=pltpu.CompilerParams(collective_id=0, has_side_effects=True, vmem_limit_bytes=60 * 2**20),
        name="gather_weights",
    )(*ws)


HD = 64
SEG = 148
MEMW = 10
F32 = jnp.float32
EPSILON = 1e-12
MASKED = -1e30
WIN = 160
MEMP = 96
SEGS = 8
PAIR = 2 * HD

CONTRACT_LAST = (((1,), (1,)), ((), ()))
CONTRACT_FIRST = (((0,), (0,)), ((), ()))


def mm(a, b):
    return jnp.dot(a, b, preferred_element_type=F32)


def mm_t(a, b):
    return lax.dot_general(a, b, CONTRACT_LAST, preferred_element_type=F32)


def t_mm(a, b):
    return lax.dot_general(a, b, CONTRACT_FIRST, preferred_element_type=F32)


def build_masks(parent, base, colbias):
    lane = lax.broadcasted_iota(jnp.int32, (1, WIN + MEMP), 1)
    in_mem = [
        ((lane >= WIN + MEMW * t) & (lane < WIN + MEMW * (t + 1))).astype(F32) for t in range(SEGS)
    ]
    reach = [jnp.zeros((1, WIN + MEMP), F32)]
    for s in range(1, SEGS):
        row = jnp.zeros((1, WIN + MEMP), F32)
        for t in range(s):
            hit = jnp.where(parent[s] - base == t, 1.0, 0.0)
            row = row + hit * jnp.maximum(reach[t], in_mem[t])
        reach.append(row)
    for s in range(SEGS):
        off = 4 * (s % 4)
        inside = ((lane >= off) & (lane < off + SEG)).astype(F32)
        colbias[s : s + 1, :] = jnp.where(jnp.maximum(inside, reach[s]) > 0.0, 0.0, MASKED)


def build_select(slot_rows, select):
    place = lax.broadcasted_iota(jnp.int32, select.shape, 1)
    select[...] = (slot_rows[...] == place).astype(F32).astype(BF)


def window(s):
    return pl.multiple_of(144 * s + 16 * (s // 4), 16), 4 * lax.rem(s, 4)


def lane_halves():
    lane = lax.broadcasted_iota(jnp.int32, (1, PAIR), 1)
    left = (lane < HD).astype(F32)
    return left.astype(BF), (1.0 - left).astype(BF), lane < HD


def valid_rows(off):
    row = lax.broadcasted_iota(jnp.int32, (WIN, 1), 0)
    return row, (row >= off) & (row < off + SEG)


def softmax_parts(qs, kk, bias):
    scores = mm_t(qs, kk) * HD ** (-0.5) + bias
    top = jnp.max(scores, axis=-1, keepdims=True)
    raised = jnp.exp(scores - top)
    return raised, 1.0 / jnp.sum(raised, axis=-1, keepdims=True)


def attend_pair(q, k, v, kmem, vmem, colbias, mixed, s, columns):
    left, right, is_left = lane_halves()
    at, off = window(s)
    rows = pl.ds(at, WIN)
    qw = q[rows, columns]
    qs = jnp.concatenate([qw * left, qw * right], axis=0)
    kk = jnp.concatenate([k[rows, columns], kmem[:, columns]], axis=0)
    vv = jnp.concatenate([v[rows, columns], vmem[:, columns]], axis=0)
    raised, scale = softmax_parts(qs, kk, colbias[pl.ds(s, 1), :])
    both = mm((raised * scale).astype(BF), vv)
    out = jnp.where(is_left, both[:WIN], both[WIN:])
    row, valid = valid_rows(off)
    old = mixed[rows, columns].astype(F32)
    mixed[rows, columns] = jnp.where(row >= off, out, old).astype(BF)


def attend_back_pair(q, k, v, kmem, vmem, colbias, dmix, dq, dk, dv, dkmem, dvmem, s, columns, acc):
    left, right, is_left = lane_halves()
    at, off = window(s)
    rows = pl.ds(at, WIN)
    qw = q[rows, columns]
    qs = jnp.concatenate([qw * left, qw * right], axis=0)
    kk = jnp.concatenate([k[rows, columns], kmem[:, columns]], axis=0)
    vv = jnp.concatenate([v[rows, columns], vmem[:, columns]], axis=0)
    dw = dmix[rows, columns]
    ds_in = jnp.concatenate([dw * left, dw * right], axis=0)
    raised, scale = softmax_parts(qs, kk, colbias[pl.ds(s, 1), :])
    row, valid = valid_rows(off)
    keep = jnp.where(valid, 1.0, 0.0)
    chances = raised * (scale * jnp.concatenate([keep, keep], axis=0))
    dp = mm_t(ds_in, vv)
    inner = jnp.sum(chances * dp, axis=-1, keepdims=True)
    ds = (chances * (dp - inner)).astype(BF)
    pb = chances.astype(BF)
    dqs = mm(ds, kk)
    new = jnp.where(is_left, dqs[:WIN], dqs[WIN:]) * HD ** (-0.5)
    old = dq[rows, columns].astype(F32)
    dq[rows, columns] = jnp.where(row >= off, new, old).astype(BF)
    dks = t_mm(ds, qs)
    dvs = t_mm(pb, ds_in)
    dk[rows, acc] = dk[rows, acc] + dks[:WIN]
    dv[rows, acc] = dv[rows, acc] + dvs[:WIN]
    dkmem[:, acc] = dkmem[:, acc] + dks[WIN:]
    dvmem[:, acc] = dvmem[:, acc] + dvs[WIN:]


def spread(select, part):
    high = part.astype(BF)
    low = (part - high.astype(F32)).astype(BF)
    return t_mm(select, high) + t_mm(select, low)


def forward_attention_kernel(parent, slot_rows, q, k, v, mixed, colbias, select, kmem, vmem):
    base = lax.axis_index("dp") * SEGS
    build_masks(parent, base, colbias)
    build_select(slot_rows, select)
    kmem[...] = mm(select[...], k[...]).astype(BF)
    vmem[...] = mm(select[...], v[...]).astype(BF)
    pairs = q.shape[1] // PAIR

    @pl.loop(0, SEGS)
    def _(s):
        for pair in range(pairs):
            attend_pair(q, k, v, kmem, vmem, colbias, mixed, s, pl.ds(pair * PAIR, PAIR))


def backward_attention_kernel(
    parent, slot_rows, q, k, v, dmix, dq, dk, dv, colbias, select, kmem, vmem, dka, dva, dkm, dvm
):
    base = lax.axis_index("dp") * SEGS
    build_masks(parent, base, colbias)
    build_select(slot_rows, select)
    kmem[...] = mm(select[...], k[...]).astype(BF)
    vmem[...] = mm(select[...], v[...]).astype(BF)
    pairs = q.shape[1] // PAIR
    for ref in (dka, dva, dkm, dvm):
        ref[...] = jnp.zeros(ref.shape, F32)

    @pl.loop(0, SEGS)
    def _(s):
        for pair in range(pairs):
            columns = pl.ds(pair * PAIR, PAIR)
            attend_back_pair(
                q, k, v, kmem, vmem, colbias, dmix, dq, dka, dva, dkm, dvm, s, columns, columns
            )

    for pair in range(pairs):
        columns = pl.ds(pair * PAIR, PAIR)
        dk[:, columns] = ((dka[:, columns] + spread(select[...], dkm[:, columns])) * HD ** (-0.5)).astype(BF)
        dv[:, columns] = (dva[:, columns] + spread(select[...], dvm[:, columns])).astype(BF)


def attention_call(kernel, outs, parent, slot_rows, arrays, scratch, name):
    rows, width = arrays[0].shape
    vm = pl.BlockSpec(memory_space=pltpu.VMEM)
    return pl.pallas_call(
        kernel,
        out_shape=[jax.ShapeDtypeStruct((rows, width), BF)] * outs,
        in_specs=[pl.BlockSpec(memory_space=pltpu.SMEM), vm] + [vm] * len(arrays),
        out_specs=[vm] * outs,
        scratch_shapes=[
            pltpu.VMEM((SEGS, WIN + MEMP), F32),
            pltpu.VMEM((MEMP, rows), BF),
            pltpu.VMEM((MEMP, width), BF),
            pltpu.VMEM((MEMP, width), BF),
        ]
        + scratch,
        compiler_params=pltpu.CompilerParams(vmem_limit_bytes=60 * 2**20),
        name=name,
    )(parent, slot_rows, *arrays)


def forward_attention(parent, slot_rows, q, k, v):
    return attention_call(forward_attention_kernel, 1, parent, slot_rows, (q, k, v), [], "attend")[0]


def backward_attention(parent, slot_rows, q, k, v, dmix):
    rows, width = q.shape
    scratch = [pltpu.VMEM((rows, width), F32)] * 2 + [pltpu.VMEM((MEMP, width), F32)] * 2
    return attention_call(
        backward_attention_kernel, 3, parent, slot_rows, (q, k, v, dmix), scratch, "attend_back"
    )


DOWN, UP, OUT, QKV, VEC = 0, 24, 48, 54, 72
COUNT = 73
CHUNK = 256
VEC_ROWS = 54


def backward_kernel(
    fast,
    parent,
    slot_rows,
    inverse,
    gain,
    vec_in,
    tokens_h,
    hidden_h,
    d_ffn_h,
    d_two_h,
    normed_h,
    acted_h,
    slope_own_h,
    slope_their_h,
    q_h,
    k_h,
    v_h,
    mixed_h,
    w_up_own,
    w_up_their,
    w_down_own,
    w_down_their,
    w_out_own,
    w_out_their,
    w_qkv_own,
    w_qkv_their,
    g_qkv,
    g_out,
    g_up,
    g_down,
    g_vec,
    g_tokens,
    grads,
    d_low,
    hidden,
    d_res,
    normed,
    acc_own,
    acc_their,
    a_buf,
    slope_buf,
    up_buf,
    down_buf,
    d_inner,
    sums,
    tokens,
    mixed,
    w_out,
    w_qkv,
    qkv,
    d_qkv,
    d_mixed,
    colbias,
    select,
    kmem,
    vmem,
    dkm,
    dvm,
    load_sem,
    chunk_sem,
    put_sem,
    *wires,
):
    rows, depth = tokens.shape
    width = mixed.shape[1]

    def fetch(index, source, target):
        return pltpu.make_async_copy(source, target, load_sem.at[index])

    load_d = fetch(0, d_ffn_h, d_low)
    load_hidden = fetch(1, hidden_h, hidden)
    load_two = fetch(2, d_two_h, d_res)
    load_normed = fetch(3, normed_h, normed)
    load_mixed = fetch(4, mixed_h.at[:, pl.ds(0, width)], mixed)
    load_out = [fetch(5 + i, w, w_out.at[i]) for i, w in enumerate((w_out_own, w_out_their))]
    load_w = [fetch(7 + i, w, w_qkv.at[i]) for i, w in enumerate((w_qkv_own, w_qkv_their))]
    load_tokens = fetch(9, tokens_h, tokens)
    load_qkv = [
        [fetch(10 + 3 * half + i, a.at[:, pl.ds(half * width, width)], qkv.at[i]) for i, a in enumerate((q_h, k_h, v_h))]
        for half in range(2)
    ]
    put_tokens = fetch(16, d_low, g_tokens)

    def load_acted(c):
        return pltpu.make_async_copy(acted_h.at[:, pl.ds(pl.multiple_of(c * BR, BR), BR)], a_buf.at[lax.rem(c, 2)], chunk_sem.at[0, lax.rem(c, 2)])

    def load_chunk(half, c):
        slot = lax.rem(c, 2)
        span = pl.ds(pl.multiple_of(c * CHUNK, CHUNK), CHUNK)
        slope_h, up_h, down_h = ((slope_own_h, w_up_own, w_down_own), (slope_their_h, w_up_their, w_down_their))[half]
        return (
            pltpu.make_async_copy(slope_h.at[:, span], slope_buf.at[slot], chunk_sem.at[1, slot]),
            pltpu.make_async_copy(up_h.at[:, span], up_buf.at[slot], chunk_sem.at[2, slot]),
            pltpu.make_async_copy(down_h.at[span, :], down_buf.at[slot], chunk_sem.at[3, slot]),
        )

    def start(copies):
        for copy in copies:
            copy.start()

    def wait(copies):
        for copy in copies:
            copy.wait()

    load_d.start()
    load_acted(0).start()
    start(load_chunk(0, 0))
    load_hidden.start()
    load_two.start()
    load_normed.start()
    load_mixed.start()
    start(load_out)
    start(load_w)
    load_tokens.start()
    start(load_qkv[0])

    def put(block, target):
        return pltpu.make_async_copy(grads.at[block], target, put_sem.at[lax.rem(block, 8)])

    def wait_put(block):
        put(block, g_vec).wait()

    def finish(block):
        @pl.when(block >= 8)
        def _():
            wait_put(block - 8)

        def at(row, column):
            return pl.ds(pl.multiple_of(row, BR), BR), pl.ds(pl.multiple_of(column, BC), BC)

        @pl.when(block < UP)
        def _():
            put(block, g_down.at[at(BR * (block // 6), BC * lax.rem(block, 6))]).start()

        @pl.when((block >= UP) & (block < OUT))
        def _():
            i = block - UP
            put(block, g_up.at[at(BR * lax.rem(i // 2, 2), CHUNK * (i // 4) + BC * lax.rem(i, 2))]).start()

        @pl.when((block >= OUT) & (block < QKV))
        def _():
            put(block, g_out.at[at(0, BC * (block - OUT))]).start()

        @pl.when((block >= QKV) & (block < VEC))
        def _():
            i = block - QKV
            put(block, g_qkv.at[at(BR * (i // 3), BC * lax.rem(i, 3))]).start()

        @pl.when(block == VEC)
        def _():
            put(block, g_vec).start()

    if fast:
        pos = Place()
        tick = make_tick(pos, grads, *wires, COUNT, finish)
        last = COUNT + 7 * SPREAD
    else:

        def tick(step):
            finish(step)

        last = COUNT
    done = [0]

    def ticks(index, each, trips):
        for i in range(each):
            tick(done[0] + index * each + i)
        return trips * each

    grads[VEC] = jnp.zeros((BR, BC), F32)
    grads[VEC, 36:54] = vec_in[...]
    acc_own[...] = jnp.zeros(acc_own.shape, F32)
    acc_their[...] = jnp.zeros(acc_their.shape, F32)
    sums[...] = jnp.zeros(sums.shape, F32)
    if fast:
        sum_barrier(pos)

    load_d.wait()

    @pl.loop(0, 4)
    def _(c):
        load_acted(c).wait()

        @pl.when(c < 3)
        def _():
            load_acted(c + 1).start()

        for part in range(2):
            piece = t_mm(a_buf[lax.rem(c, 2)], d_low[:, part * width : (part + 1) * width])
            for j in range(3):
                grads[DOWN + 6 * c + 3 * part + j] = piece[:, BC * j : BC * (j + 1)]
        ticks(c, TICKS[0], 4)

    done[0] += 4 * TICKS[0]

    load_hidden.wait()
    for half in range(2):
        acc = (acc_own, acc_their)[half]

        @pl.loop(0, 6)
        def _(c, half=half, acc=acc):
            slot = lax.rem(c, 2)
            wait(load_chunk(half, c))

            @pl.when(c < 5)
            def _():
                start(load_chunk(half, c + 1))

            if half == 0:

                @pl.when(c == 5)
                def _():
                    start(load_chunk(1, 0))

            d_inner[...] = (mm_t(d_low[...], down_buf[slot]) * slope_buf[slot].astype(F32)).astype(BF)
            if half == 0:
                piece = t_mm(hidden[...], d_inner[...])
                for r in range(2):
                    for j in range(2):
                        grads[UP + 4 * c + 2 * r + j] = piece[BR * r : BR * (r + 1), BC * j : BC * (j + 1)]
                total = jnp.sum(d_inner[...].astype(F32), axis=0, keepdims=True)
                for j in range(2):
                    grads[VEC, pl.ds(6 + 2 * c + j, 1), :] = total[:, BC * j : BC * (j + 1)]
            ticks(c, TICKS[1 + half], 6)
            for part in range(3):
                columns = slice(CHUNK * part, CHUNK * (part + 1))
                acc[:, columns] = acc[:, columns] + mm_t(d_inner[...], up_buf[slot, columns, :])

        done[0] += 6 * TICKS[1 + half]

    load_two.wait()
    load_normed.wait()
    tile = 32
    trips = rows // tile

    @pl.loop(0, trips)
    def _(i):
        span = pl.ds(pl.multiple_of(i * tile, tile), tile)
        total = d_res[span, :] + (acc_own[span, :] + acc_their[span, :])
        unit = normed[span, :]
        one = norm_back(total, unit, inverse[span, :], gain[...])
        d_res[span, :] = one
        low = one.astype(BF)
        d_low[span, :] = low
        for index, value in enumerate((low.astype(F32), total * unit, total)):
            sums[index] = sums[index] + value.reshape(tile // 8, 8, depth).sum(axis=0)

        @pl.when(lax.rem(i, TICK_TILES) == 0)
        def _():
            tick(done[0] + i // TICK_TILES)

    done[0] += -(-trips // TICK_TILES)
    for index in range(3):
        total = jnp.sum(sums[index], axis=0, keepdims=True)
        for j in range(6):
            grads[VEC, 18 + 6 * index + j : 19 + 6 * index + j, :] = total[:, BC * j : BC * (j + 1)]

    load_mixed.wait()
    wait(load_out)

    @pl.loop(0, 2)
    def _(half):
        d_mixed[half] = mm_t(d_low[...], w_out[half]).astype(BF)
        piece = t_mm(mixed[...], d_low[:, pl.ds(pl.multiple_of(half * width, BC), width)])
        for j in range(3):
            grads[OUT + 3 * half + j] = piece[:, BC * j : BC * (j + 1)]
        ticks(half, TICKS[3], 2)

    done[0] += 2 * TICKS[3]

    build_masks(parent, lax.axis_index("dp") * SEGS, colbias)
    build_select(slot_rows, select)
    wait(load_w)
    load_tokens.wait()
    pairs = width // PAIR
    dka, dva = acc_their.at[:, pl.ds(0, width)], acc_their.at[:, pl.ds(width, width)]
    for half in range(2):
        wait(load_qkv[half])
        q, k, v = (qkv.at[i] for i in range(3))
        kmem[...] = mm(select[...], k[...]).astype(BF)
        vmem[...] = mm(select[...], v[...]).astype(BF)
        acc_their[...] = jnp.zeros(acc_their.shape, F32)
        dkm[...] = jnp.zeros(dkm.shape, F32)
        dvm[...] = jnp.zeros(dvm.shape, F32)

        @pl.loop(0, SEGS)
        def _(s, half=half):
            for pair in range(pairs):
                columns = pl.ds(pair * PAIR, PAIR)
                attend_back_pair(
                    q, k, v, kmem, vmem, colbias, d_mixed.at[half], d_qkv.at[0], dka, dva, dkm, dvm, s, columns, columns
                )
                if pair < TICKS[4 + half]:
                    tick(done[0] + s * TICKS[4 + half] + pair)

        done[0] += SEGS * TICKS[4 + half]
        if half == 0:
            start(load_qkv[1])
        for pair in range(pairs):
            columns = pl.ds(pair * PAIR, PAIR)
            d_qkv[1, :, columns] = ((dka[:, columns] + spread(select[...], dkm[:, columns])) * HD ** (-0.5)).astype(BF)
            d_qkv[2, :, columns] = (dva[:, columns] + spread(select[...], dvm[:, columns])).astype(BF)
        if half == 0:

            @pl.loop(0, 3)
            def _(c):
                piece = t_mm(tokens[...], d_qkv[c])
                for r in range(2):
                    for j in range(3):
                        grads[QKV + 6 * c + 3 * r + j] = piece[BR * r : BR * (r + 1), BC * j : BC * (j + 1)]
                columns = pl.ds(pl.multiple_of(c * CHUNK, CHUNK), CHUNK)
                part = mm_t(d_qkv[0], w_qkv[half, pl.ds(pl.multiple_of(c * CHUNK, CHUNK), CHUNK), :])
                for i in (1, 2):
                    part = part + mm_t(d_qkv[i], w_qkv[half, pl.ds(pl.multiple_of(i * depth + c * CHUNK, CHUNK), CHUNK), :])
                acc_own[:, columns] = part
                ticks(c, TICKS[6], 3)

            done[0] += 3 * TICKS[6]
            for index, row in ((0, 0), (2, 3)):
                total = jnp.sum(d_qkv[index].astype(F32), axis=0, keepdims=True)
                for j in range(3):
                    grads[VEC, row + j : row + j + 1, :] = total[:, BC * j : BC * (j + 1)]
        else:

            @pl.loop(0, 3)
            def _(c):
                columns = pl.ds(pl.multiple_of(c * CHUNK, CHUNK), CHUNK)
                part = mm_t(d_qkv[0], w_qkv[half, pl.ds(pl.multiple_of(c * CHUNK, CHUNK), CHUNK), :])
                for i in (1, 2):
                    part = part + mm_t(d_qkv[i], w_qkv[half, pl.ds(pl.multiple_of(i * depth + c * CHUNK, CHUNK), CHUNK), :])
                d_low[:, columns] = ((acc_own[:, columns] + part) + d_res[:, columns]).astype(BF)
                ticks(c, TICKS[7], 3)

            done[0] += 3 * TICKS[7]
            put_tokens.start()
    assert done[0] <= COUNT

    @pl.loop(done[0], last)
    def _(step):
        tick(step)

    for block in range(COUNT - 8, COUNT):
        wait_put(block)
    put_tokens.wait()


TICKS = (1, 2, 1, 1, 2, 2, 2, 1)
TICK_TILES = 8


def backward(fast, parent, slot_rows, inverse, gain, vec_in, arrays):
    tokens, acted, mixed = arrays[0], arrays[5], arrays[11]
    rows, depth = tokens.shape
    units = acted.shape[1]
    width = mixed.shape[1] // 2
    vm = pl.BlockSpec(memory_space=pltpu.VMEM)
    hbm = pl.BlockSpec(memory_space=pl.ANY)
    sd = jax.ShapeDtypeStruct
    return pl.pallas_call(
        functools.partial(backward_kernel, fast),
        out_shape=[
            sd((3 * depth, width), F32),
            sd((width, depth), F32),
            sd((depth, units), F32),
            sd((units, depth), F32),
            sd((BR, BC), F32),
            sd((rows, depth), BF),
        ],
        in_specs=[pl.BlockSpec(memory_space=pltpu.SMEM), vm, vm, vm, vm] + [hbm] * len(arrays),
        out_specs=[hbm] * 6,
        scratch_shapes=[
            pltpu.VMEM((COUNT, BR, BC), F32),
            pltpu.VMEM((rows, depth), BF),
            pltpu.VMEM((rows, depth), BF),
            pltpu.VMEM((rows, depth), F32),
            pltpu.VMEM((rows, depth), F32),
            pltpu.VMEM((rows, depth), F32),
            pltpu.VMEM((rows, depth), F32),
            pltpu.VMEM((2, rows, BR), BF),
            pltpu.VMEM((2, rows, CHUNK), BF),
            pltpu.VMEM((2, depth, CHUNK), BF),
            pltpu.VMEM((2, CHUNK, depth), BF),
            pltpu.VMEM((rows, CHUNK), BF),
            pltpu.VMEM((3, 8, depth), F32),
            pltpu.VMEM((rows, depth), BF),
            pltpu.VMEM((rows, width), BF),
            pltpu.VMEM((2, width, depth), BF),
            pltpu.VMEM((2, 3 * depth, width), BF),
            pltpu.VMEM((3, rows, width), BF),
            pltpu.VMEM((3, rows, width), BF),
            pltpu.VMEM((2, rows, width), BF),
            pltpu.VMEM((SEGS, WIN + MEMP), F32),
            pltpu.VMEM((MEMP, rows), BF),
            pltpu.VMEM((MEMP, width), BF),
            pltpu.VMEM((MEMP, width), BF),
            pltpu.VMEM((MEMP, width), F32),
            pltpu.VMEM((MEMP, width), F32),
            pltpu.SemaphoreType.DMA((17,)),
            pltpu.SemaphoreType.DMA((4, 2)),
            pltpu.SemaphoreType.DMA((8,)),
        ]
        + (sum_scratch() if fast else []),
        compiler_params=pltpu.CompilerParams(
            collective_id=1 if fast else None, has_side_effects=fast, vmem_limit_bytes=67043328
        ),
        name="backward",
    )(parent, slot_rows, inverse, gain, vec_in, *arrays)


def halves_swap(own, small):
    unit = (lax.axis_index("dp") >= 0).astype(F32)

    def other(array):
        arrived = lax.ppermute(array.astype(F32), "tensor", [(0, 1), (1, 0)])
        return (arrived * unit).astype(array.dtype)

    return tuple(other(array) for array in own) + (other(small),)


def norm_stats(values):
    centered = values - jnp.mean(values, axis=-1, keepdims=True)
    inverse = lax.rsqrt(jnp.mean(centered * centered, axis=-1, keepdims=True) + EPSILON)
    return centered * inverse, inverse


def norm_back(grad, normed, inverse, gain):
    scaled = grad * gain
    return inverse * (
        scaled
        - jnp.mean(scaled, axis=-1, keepdims=True)
        - normed * jnp.mean(scaled * normed, axis=-1, keepdims=True)
    )


def gelu_parts(inner):
    phi = 0.5 * (1.0 + lax.erf(inner * (0.5**0.5)))
    density = jnp.exp(-0.5 * inner * inner) * (2.0 * jnp.pi) ** -0.5
    return (inner * phi).astype(BF), phi + inner * density


def split_blocks(array, rows, columns):
    height, width = array.shape
    return (
        array.reshape(height // rows, rows, width // columns, columns)
        .transpose(0, 2, 1, 3)
        .reshape(-1, rows, columns)
    )


def join_blocks(blocks, height, width):
    count, rows, columns = blocks.shape
    return (
        blocks.reshape(height // rows, width // columns, rows, columns)
        .transpose(0, 2, 1, 3)
        .reshape(height, width)
    )


def shards(
    fast,
    tokens,
    w_qkv,
    bias_qv,
    w_out,
    bias_out,
    gain_one,
    shift_one,
    w_up,
    bias_up,
    w_down,
    bias_down,
    gain_two,
    shift_two,
    grad_out,
    parent,
    mem_slots,
):
    depth, width = w_qkv.shape[1:]
    hidden_units = w_up.shape[1]
    own = (w_qkv.reshape(3 * depth, width), w_out, w_up, w_down)
    small = jnp.concatenate(
        [bias_qv, bias_up.reshape(-1, width), jnp.zeros((8 - 2 - hidden_units // width, width), F32)]
    )
    if fast:
        theirs = gather((*own, small))
    else:
        theirs = halves_swap(own, small)
    *theirs, small_theirs = theirs
    w_qkv_both = [own[0].reshape(w_qkv.shape), theirs[0].reshape(w_qkv.shape)]
    w_out_both, w_up_both, w_down_both = ([own[i], theirs[i]] for i in (1, 2, 3))
    bias_qv_both = [bias_qv, small_theirs[:2]]
    bias_up_both = [bias_up, small_theirs[2 : 2 + hidden_units // width].reshape(-1)]

    offsets = jnp.arange(SEGS, dtype=jnp.int32)[:, None] * SEG
    slot_rows = (mem_slots + offsets).reshape(-1, 1)
    slot_rows = jnp.concatenate([slot_rows, jnp.full((MEMP - slot_rows.shape[0], 1), -1, jnp.int32)])

    def project(index, bias):
        parts = []
        for half in range(2):
            part = mm(tokens, w_qkv_both[half][index])
            if bias is not None:
                part = part + bias_qv_both[half][bias]
            parts.append(part.astype(BF))
        return jnp.concatenate(parts, axis=1)

    queries, keys, values = project(0, 0), project(1, None), project(2, 1)
    mixed = forward_attention(parent, slot_rows, queries, keys, values)
    attended = mm(mixed[:, :width], w_out_both[0]) + mm(mixed[:, width:], w_out_both[1])
    resid_one = tokens.astype(F32) + (attended + bias_out)
    normed_one, inverse_one = norm_stats(resid_one)
    hidden = normed_one * gain_one + shift_one
    hidden_low = hidden.astype(BF)
    acted, slope, summed = [], [], []
    for half in range(2):
        inner = mm(hidden_low, w_up_both[half]) + bias_up_both[half]
        act, steep = gelu_parts(inner)
        acted.append(act)
        slope.append(steep)
        summed.append(mm(act, w_down_both[half]))
    resid_two = hidden + ((summed[0] + summed[1]) + bias_down)
    normed_two, inverse_two = norm_stats(resid_two)
    output = (normed_two * gain_two + shift_two).astype(BF)

    cotangent = grad_out.astype(F32)
    d_two = norm_back(cotangent, normed_two, inverse_two, gain_two)
    d_gain_two = jnp.sum(cotangent * normed_two, axis=0)
    d_shift_two = jnp.sum(cotangent, axis=0)
    d_ffn = d_two.astype(BF)
    d_bias_down = jnp.sum(d_ffn.astype(F32), axis=0)
    vec_in = jnp.concatenate([v.reshape(-1, BC) for v in (d_bias_down, d_gain_two, d_shift_two)])
    slope = [part.astype(BF) for part in slope]
    arrays = (tokens, hidden_low, d_ffn, d_two, normed_one, acted[0], *slope, queries, keys, values, mixed)
    weights = (*w_up_both, *w_down_both, *w_out_both, own[0], theirs[0])
    g_w_qkv, g_w_out, g_w_up, g_w_down, flat, grad_tokens = backward(
        fast, parent, slot_rows, inverse_one, gain_one.reshape(1, -1), vec_in, arrays + weights
    )
    if not fast:
        g_w_qkv, g_w_out, g_w_up, g_w_down, flat = lax.psum((g_w_qkv, g_w_out, g_w_up, g_w_down, flat), "dp")
    g_w_qkv = g_w_qkv.reshape(w_qkv.shape)
    sums, row = [], 0
    for size in (width, width, hidden_units) + (depth,) * 6:
        sums.append(flat[row : row + size // BC].reshape(-1))
        row += size // BC
    g_bias_q, g_bias_v, g_bias_up, g_bias_out, g_gain_one, g_shift_one, g_bias_down, g_gain_two, g_shift_two = sums
    return (
        output,
        grad_tokens,
        g_w_qkv,
        jnp.stack([g_bias_q, g_bias_v]),
        g_w_out,
        g_bias_out,
        g_gain_one,
        g_shift_one,
        g_w_up,
        g_bias_up,
        g_w_down,
        g_bias_down,
        g_gain_two,
        g_shift_two,
    )


def solution(mesh):
    fast = mesh.shape["dp"] == 16 and mesh.shape["tensor"] == 2
    rows, whole = P("dp", None), P()
    return jax.shard_map(
        functools.partial(shards, fast),
        mesh=mesh,
        in_specs=(
            rows,
            P(None, None, "tensor"),
            P(None, "tensor"),
            P("tensor", None),
            whole,
            whole,
            whole,
            P(None, "tensor"),
            P("tensor"),
            P("tensor", None),
            whole,
            whole,
            whole,
            rows,
            P("dp"),
            rows,
        ),
        out_specs=(
            rows,
            rows,
            P(None, None, "tensor"),
            P(None, "tensor"),
            P("tensor", None),
            whole,
            whole,
            whole,
            P(None, "tensor"),
            P("tensor"),
            P("tensor", None),
            whole,
            whole,
            whole,
        ),
        check_vma=False,
    )
```

```python
import functools


import jax
import jax.numpy as jnp
from jax import lax
from jax.experimental import pallas as pl
from jax.experimental.pallas import tpu as pltpu
from jax.sharding import PartitionSpec as P


MESH = pl.DeviceIdType.MESH
BR, BC = 384, 128
SPREAD = 2
SLOTS = 16


class Place:
    def __init__(self):
        me = lax.axis_index("dp")
        self.core = lax.rem(me, 2)
        self.x = lax.rem(me // 2, 2)
        self.z = me // 4
        self.sib = me + 1 - 2 * self.core
        self.xn = me + 2 - 4 * self.x
        self.zp = me + 4 - 8 * lax.rem(self.z, 2)
        self.zm = me + 4 * (3 - 2 * self.z)
        self.end = (self.z == 0) | (self.z == 3)
        self.mid = (self.z == 1) | (self.z == 2)


def sum_barrier(pos):
    barrier = pltpu.get_barrier_semaphore()

    def greet(dev):
        pl.semaphore_signal(barrier, inc=1, device_id={"dp": dev}, device_id_type=MESH)

    greet(pos.sib)
    greet(pos.xn)
    greet(pos.zp)

    @pl.when(pos.mid)
    def _():
        greet(pos.zm)

    pl.semaphore_wait(barrier, jnp.where(pos.mid, 4, 3))


def make_tick(pos, grads, from_core, from_one, from_two, from_three, sent, got, credit, count, finish):
    half = BR // 2
    quarter = BR // 4

    def copy(stage, block, source, target, device):
        slot = lax.rem(block, SLOTS)
        return pltpu.make_async_remote_copy(
            src_ref=source,
            dst_ref=target,
            send_sem=sent.at[stage, slot],
            recv_sem=got.at[stage, slot],
            device_id={"dp": device},
            device_id_type=MESH,
        )

    def rows(block, start, size):
        return grads.at[block, pl.ds(pl.multiple_of(start, quarter), size)]

    def add(block, start, size, landed):
        where = pl.ds(pl.multiple_of(start, quarter), size)
        grads[block, where] = grads[block, where] + landed[...]

    def free(index, device):
        pl.semaphore_signal(credit.at[index], inc=1, device_id={"dp": device}, device_id_type=MESH)

    def claim(index):
        pl.semaphore_wait(credit.at[index], 1)

    x_first = pos.core == 0
    z_first = pos.core == 1
    mine = pos.core * half
    xrow = pos.x * quarter
    xrow_other = (1 - pos.x) * quarter
    far = lax.rem(pos.z, 2) == 0
    keep = half + jnp.where(far, quarter, 0)
    give = half + jnp.where(far, 0, quarter)

    def core_out(block):
        return copy(0, block, rows(block, (1 - pos.core) * half, half), from_core.at[lax.rem(block, SLOTS)], pos.sib)

    def x_one(block):
        return copy(1, block, rows(block, xrow_other, quarter), from_one.at[lax.rem(block, SLOTS), pl.ds(0, quarter)], pos.xn)

    def z_one(block):
        return copy(1, block, rows(block, half, half), from_one.at[lax.rem(block, SLOTS)], pos.zp)

    def x_two(block):
        return copy(2, block, rows(block, xrow, quarter), from_two.at[lax.rem(block, SLOTS)], pos.zp)

    def z_two(block):
        return copy(2, block, rows(block, give, quarter), from_two.at[lax.rem(block, SLOTS)], pos.zm)

    def x_three(block):
        return copy(3, block, rows(block, xrow, quarter), from_three.at[lax.rem(block, SLOTS)], pos.zm)

    def z_three(block):
        return copy(3, block, rows(block, keep, quarter), from_three.at[lax.rem(block, SLOTS)], pos.xn)

    def x_four(block):
        return copy(4, block, rows(block, xrow, quarter), rows(block, xrow, quarter), pos.zp)

    def z_four(block):
        return copy(4, block, rows(block, keep, quarter), rows(block, keep, quarter), pos.zm)

    def z_four_in(block):
        return copy(4, block, rows(block, give, quarter), rows(block, give, quarter), pos.zm)

    def x_five(block):
        return copy(5, block, rows(block, xrow, quarter), rows(block, xrow, quarter), pos.xn)

    def x_five_in(block):
        return copy(5, block, rows(block, xrow_other, quarter), rows(block, xrow_other, quarter), pos.xn)

    def z_five(block):
        return copy(5, block, rows(block, half, half), rows(block, half, half), pos.zp)

    def core_six(block):
        return copy(6, block, rows(block, mine, half), rows(block, mine, half), pos.sib)

    def core_six_in(block):
        return copy(6, block, rows(block, (1 - pos.core) * half, half), rows(block, (1 - pos.core) * half, half), pos.sib)

    def stage_zero(block):
        core_out(block).start()

    def stage_one(block):
        core_out(block).wait()
        free(2, pos.sib)
        add(block, mine, half, from_core.at[lax.rem(block, SLOTS)])

        @pl.when(x_first)
        def _():
            x_one(block).start()

        @pl.when(z_first & pos.end)
        def _():
            z_one(block).start()

    def stage_two(block):
        @pl.when(x_first)
        def _():
            x_one(block).wait()
            free(1, pos.xn)
            add(block, xrow, quarter, from_one.at[lax.rem(block, SLOTS), pl.ds(0, quarter)])

            @pl.when(pos.end)
            def _():
                x_two(block).start()

        @pl.when(z_first & pos.end)
        def _():
            z_one(block).wait_send()
            free(1, pos.zp)

        @pl.when(z_first & pos.mid)
        def _():
            z_one(block).wait_recv()
            add(block, half, half, from_one.at[lax.rem(block, SLOTS)])
            z_two(block).start()

    def stage_three(block):
        @pl.when(x_first & pos.end)
        def _():
            x_two(block).wait_send()
            free(0, pos.zp)

        @pl.when(x_first & pos.mid)
        def _():
            x_two(block).wait_recv()
            add(block, xrow, quarter, from_two.at[lax.rem(block, SLOTS)])
            x_three(block).start()

        @pl.when(z_first & pos.mid)
        def _():
            z_two(block).wait()
            free(0, pos.zm)
            add(block, keep, quarter, from_two.at[lax.rem(block, SLOTS)])
            z_three(block).start()

    def stage_four(block):
        @pl.when(x_first & pos.mid)
        def _():
            x_three(block).wait()
            add(block, xrow, quarter, from_three.at[lax.rem(block, SLOTS)])
            claim(0)
            x_four(block).start()

        @pl.when(z_first & pos.mid)
        def _():
            z_three(block).wait()
            add(block, keep, quarter, from_three.at[lax.rem(block, SLOTS)])
            claim(0)
            z_four(block).start()

    def stage_five(block):
        @pl.when(x_first)
        def _():
            @pl.when(pos.end)
            def _():
                x_four(block).wait_recv()

            @pl.when(pos.mid)
            def _():
                x_four(block).wait_send()

            claim(1)
            x_five(block).start()

        @pl.when(z_first & pos.mid)
        def _():
            z_four(block).wait_send()
            z_four_in(block).wait_recv()
            claim(1)
            z_five(block).start()

    def stage_six(block):
        @pl.when(x_first)
        def _():
            x_five(block).wait_send()
            x_five_in(block).wait_recv()

        @pl.when(z_first & pos.end)
        def _():
            z_five(block).wait_recv()

        @pl.when(z_first & pos.mid)
        def _():
            z_five(block).wait_send()

        claim(2)
        core_six(block).start()

    def stage_seven(block):
        core_six(block).wait_send()
        core_six_in(block).wait_recv()
        finish(block)

    stages = (stage_zero, stage_one, stage_two, stage_three, stage_four, stage_five, stage_six, stage_seven)

    def tick(step):
        for index in reversed(range(8)):
            block = step - SPREAD * index

            @pl.when((block >= 0) & (block < count))
            def _(index=index, block=block):
                stages[index](block)

    return tick


def sum_scratch():
    return [
        pltpu.VMEM((SLOTS, BR // 2, BC), jnp.float32),
        pltpu.VMEM((SLOTS, BR // 2, BC), jnp.float32),
        pltpu.VMEM((SLOTS, BR // 4, BC), jnp.float32),
        pltpu.VMEM((SLOTS, BR // 4, BC), jnp.float32),
        pltpu.SemaphoreType.DMA((7, SLOTS)),
        pltpu.SemaphoreType.DMA((7, SLOTS)),
        pltpu.SemaphoreType.REGULAR((3,)),
    ]


CR, CC = 64, 384
CHUNKS = 24
RELAY = 1
BF = jnp.bfloat16


def gather_barrier(pos, other):
    barrier = pltpu.get_barrier_semaphore()
    for where in ({"tensor": other}, {"dp": pos.xn}, {"dp": pos.zp}, {"dp": pos.sib}):
        pl.semaphore_signal(barrier, inc=1, device_id=where, device_id_type=MESH)
    pl.semaphore_wait(barrier, 4)


def chunk_parts(piece, chunk, kind):
    if kind == 0:
        return [(piece * 384 + chunk * 64, 64, 0, 0)]
    if kind == 1:
        return [(piece * 64 + (chunk - 6) * 32, 32, 384 * q, 32 * q) for q in range(2)]
    if kind == 2:
        return [(piece * 128 + (chunk - 8) * 16, 16, 384 * q, 16 * q) for q in range(4)]
    return [(piece * 256 + (chunk - 16) * 32, 32, 384 * q, 32 * q) for q in range(2)]


BOUNDS = ((0, 6), (6, 8), (8, 16), (16, 24))
UNIT = (64, 32, 16, 32)


def make_gather(pos, own, theirs, staged, landed, sent, got):
    other = 1 - lax.axis_index("tensor")
    odd = lax.rem(pos.z, 2)
    ky = jnp.where(pos.x == 0, odd, 2)
    kx = jnp.where(pos.x == 0, 2, odd)
    kz = 1 - odd
    piece_y = 2 * ky + pos.core
    piece_x = 2 * kx + pos.core
    piece_z = 2 * kz + pos.core
    sib_y = 2 * ky + 1 - pos.core
    sib_x = 2 * kx + 1 - pos.core
    sib_z = 2 * kz + 1 - pos.core

    def copy(lane, chunk, source, piece, where):
        return pltpu.make_async_remote_copy(
            src_ref=source,
            dst_ref=landed.at[piece, chunk],
            send_sem=sent.at[lane, chunk],
            recv_sem=got.at[lane, chunk],
            device_id=where,
            device_id_type=MESH,
        )

    def over_y(chunk):
        return copy(0, chunk, staged.at[chunk], piece_y, {"tensor": other})

    def over_x(chunk, piece):
        return copy(1, chunk, landed.at[piece, chunk], piece, {"dp": pos.xn})

    def over_z(chunk, piece):
        return copy(2, chunk, landed.at[piece, chunk], piece, {"dp": pos.zp})

    def over_core(lane, chunk, piece):
        return copy(lane, chunk, landed.at[piece, chunk], piece, {"dp": pos.sib})

    def stage_own():
        for kind in range(4):
            lo, hi = BOUNDS[kind]

            @pl.loop(lo, hi)
            def _(chunk, kind=kind):
                for row, rows, column, at in chunk_parts(piece_y, chunk, kind):
                    staged[chunk, pl.ds(at, rows)] = own[kind][
                        pl.ds(pl.multiple_of(row, UNIT[kind]), rows), pl.ds(column, CC)
                    ].astype(jnp.float32)

    def send_own():
        @pl.loop(0, CHUNKS)
        def _(chunk):
            over_y(chunk).start()

    def unpack(chunk):
        for kind in range(4):
            lo, hi = BOUNDS[kind]

            @pl.when((chunk >= lo) & (chunk < hi))
            def _(kind=kind):
                @pl.loop(0, 6)
                def _(piece):
                    for row, rows, column, at in chunk_parts(piece, chunk, kind):
                        theirs[kind][pl.ds(pl.multiple_of(row, UNIT[kind]), rows), pl.ds(column, CC)] = landed[
                            piece, chunk, pl.ds(at, rows)
                        ].astype(BF)

    def guarded(chunk, body):
        @pl.when((chunk >= 0) & (chunk < CHUNKS))
        def _():
            body(chunk)

    def first(chunk):
        over_y(chunk).wait_recv()
        over_x(chunk, piece_y).start()

        @pl.when(pos.x == 0)
        def _():
            over_z(chunk, piece_y).start()

        over_core(3, chunk, piece_y).start()

    def second(chunk):
        over_x(chunk, piece_x).wait_recv()

        @pl.when(pos.x == 1)
        def _():
            over_z(chunk, piece_x).start()

        over_core(4, chunk, piece_x).start()

    def third(chunk):
        over_z(chunk, piece_z).wait_recv()
        over_core(5, chunk, piece_z).start()

    def fourth(chunk):
        over_core(3, chunk, sib_y).wait_recv()
        over_core(4, chunk, sib_x).wait_recv()
        over_core(5, chunk, sib_z).wait_recv()
        over_y(chunk).wait_send()
        over_x(chunk, piece_y).wait_send()
        over_z(chunk, piece_y).wait_send()
        over_core(3, chunk, piece_y).wait_send()
        over_core(4, chunk, piece_x).wait_send()
        over_core(5, chunk, piece_z).wait_send()
        unpack(chunk)

    def tick(step):
        guarded(step - 3 * RELAY, fourth)
        guarded(step - 2 * RELAY, third)
        guarded(step - RELAY, second)
        guarded(step, first)

    return stage_own, send_own, tick


GATHER_TICKS = CHUNKS + 3 * RELAY


def gather_scratch():
    return [
        pltpu.VMEM((CHUNKS, CR, CC), jnp.float32),
        pltpu.VMEM((6, CHUNKS, CR, CC), jnp.float32),
        pltpu.SemaphoreType.DMA((6, CHUNKS)),
        pltpu.SemaphoreType.DMA((6, CHUNKS)),
    ]


def swap_small(small, small_out, sems):
    return pltpu.make_async_remote_copy(
        src_ref=small,
        dst_ref=small_out,
        send_sem=sems.at[0],
        recv_sem=sems.at[1],
        device_id={"tensor": 1 - lax.axis_index("tensor")},
        device_id_type=MESH,
    )


HD = 64
SEG = 148
MEMW = 10
F32 = jnp.float32
EPSILON = 1e-12
MASKED = -1e30
WIN = 160
MEMP = 96
SEGS = 8
PAIR = 2 * HD

CONTRACT_LAST = (((1,), (1,)), ((), ()))
CONTRACT_FIRST = (((0,), (0,)), ((), ()))


def mm(a, b):
    return jnp.dot(a, b, preferred_element_type=F32)


def mm_t(a, b):
    return lax.dot_general(a, b, CONTRACT_LAST, preferred_element_type=F32)


def t_mm(a, b):
    return lax.dot_general(a, b, CONTRACT_FIRST, preferred_element_type=F32)


def build_masks(parent, base, colbias):
    lane = lax.broadcasted_iota(jnp.int32, (1, WIN + MEMP), 1)
    in_mem = [
        ((lane >= WIN + MEMW * t) & (lane < WIN + MEMW * (t + 1))).astype(F32) for t in range(SEGS)
    ]
    reach = [jnp.zeros((1, WIN + MEMP), F32)]
    for s in range(1, SEGS):
        row = jnp.zeros((1, WIN + MEMP), F32)
        for t in range(s):
            hit = jnp.where(parent[s] - base == t, 1.0, 0.0)
            row = row + hit * jnp.maximum(reach[t], in_mem[t])
        reach.append(row)
    for s in range(SEGS):
        off = 4 * (s % 4)
        inside = ((lane >= off) & (lane < off + SEG)).astype(F32)
        colbias[s : s + 1, :] = jnp.where(jnp.maximum(inside, reach[s]) > 0.0, 0.0, MASKED)


def build_select(slot_rows, select):
    place = lax.broadcasted_iota(jnp.int32, select.shape, 1)
    select[...] = (slot_rows[...] == place).astype(F32).astype(BF)


def window(s):
    return pl.multiple_of(144 * s + 16 * (s // 4), 16), 4 * lax.rem(s, 4)


def lane_halves():
    lane = lax.broadcasted_iota(jnp.int32, (1, PAIR), 1)
    left = (lane < HD).astype(F32)
    return left.astype(BF), (1.0 - left).astype(BF), lane < HD


def valid_rows(off):
    row = lax.broadcasted_iota(jnp.int32, (WIN, 1), 0)
    return row, (row >= off) & (row < off + SEG)


def softmax_parts(qs, kk, bias):
    scores = mm_t(qs, kk) * HD ** (-0.5) + bias
    top = jnp.max(scores, axis=-1, keepdims=True)
    raised = jnp.exp(scores - top)
    return raised, 1.0 / jnp.sum(raised, axis=-1, keepdims=True)


def attend_pair(q, k, v, kmem, vmem, colbias, mixed, s, columns):
    left, right, is_left = lane_halves()
    at, off = window(s)
    rows = pl.ds(at, WIN)
    qw = q[rows, columns]
    qs = jnp.concatenate([qw * left, qw * right], axis=0)
    kk = jnp.concatenate([k[rows, columns], kmem[:, columns]], axis=0)
    vv = jnp.concatenate([v[rows, columns], vmem[:, columns]], axis=0)
    raised, scale = softmax_parts(qs, kk, colbias[pl.ds(s, 1), :])
    both = mm((raised * scale).astype(BF), vv)
    out = jnp.where(is_left, both[:WIN], both[WIN:])
    row, valid = valid_rows(off)
    old = mixed[rows, columns].astype(F32)
    mixed[rows, columns] = jnp.where(row >= off, out, old).astype(BF)


def attend_back_pair(q, k, v, kmem, vmem, colbias, dmix, dq, dk, dv, dkmem, dvmem, s, columns, acc):
    left, right, is_left = lane_halves()
    at, off = window(s)
    rows = pl.ds(at, WIN)
    qw = q[rows, columns]
    qs = jnp.concatenate([qw * left, qw * right], axis=0)
    kk = jnp.concatenate([k[rows, columns], kmem[:, columns]], axis=0)
    vv = jnp.concatenate([v[rows, columns], vmem[:, columns]], axis=0)
    dw = dmix[rows, columns]
    ds_in = jnp.concatenate([dw * left, dw * right], axis=0)
    raised, scale = softmax_parts(qs, kk, colbias[pl.ds(s, 1), :])
    row, valid = valid_rows(off)
    keep = jnp.where(valid, 1.0, 0.0)
    chances = raised * (scale * jnp.concatenate([keep, keep], axis=0))
    dp = mm_t(ds_in, vv)
    inner = jnp.sum(chances * dp, axis=-1, keepdims=True)
    ds = (chances * (dp - inner)).astype(BF)
    pb = chances.astype(BF)
    dqs = mm(ds, kk)
    new = jnp.where(is_left, dqs[:WIN], dqs[WIN:]) * HD ** (-0.5)
    old = dq[rows, columns].astype(F32)
    dq[rows, columns] = jnp.where(row >= off, new, old).astype(BF)
    dks = t_mm(ds, qs)
    dvs = t_mm(pb, ds_in)
    dk[rows, acc] = dk[rows, acc] + dks[:WIN]
    dv[rows, acc] = dv[rows, acc] + dvs[:WIN]
    dkmem[:, acc] = dkmem[:, acc] + dks[WIN:]
    dvmem[:, acc] = dvmem[:, acc] + dvs[WIN:]


def spread(select, part):
    high = part.astype(BF)
    low = (part - high.astype(F32)).astype(BF)
    return t_mm(select, high) + t_mm(select, low)


def forward_attention_kernel(parent, slot_rows, q, k, v, mixed, colbias, select, kmem, vmem):
    base = lax.axis_index("dp") * SEGS
    build_masks(parent, base, colbias)
    build_select(slot_rows, select)
    kmem[...] = mm(select[...], k[...]).astype(BF)
    vmem[...] = mm(select[...], v[...]).astype(BF)
    pairs = q.shape[1] // PAIR

    @pl.loop(0, SEGS)
    def _(s):
        for pair in range(pairs):
            attend_pair(q, k, v, kmem, vmem, colbias, mixed, s, pl.ds(pair * PAIR, PAIR))


def backward_attention_kernel(
    parent, slot_rows, q, k, v, dmix, dq, dk, dv, colbias, select, kmem, vmem, dka, dva, dkm, dvm
):
    base = lax.axis_index("dp") * SEGS
    build_masks(parent, base, colbias)
    build_select(slot_rows, select)
    kmem[...] = mm(select[...], k[...]).astype(BF)
    vmem[...] = mm(select[...], v[...]).astype(BF)
    pairs = q.shape[1] // PAIR
    for ref in (dka, dva, dkm, dvm):
        ref[...] = jnp.zeros(ref.shape, F32)

    @pl.loop(0, SEGS)
    def _(s):
        for pair in range(pairs):
            columns = pl.ds(pair * PAIR, PAIR)
            attend_back_pair(
                q, k, v, kmem, vmem, colbias, dmix, dq, dka, dva, dkm, dvm, s, columns, columns
            )

    for pair in range(pairs):
        columns = pl.ds(pair * PAIR, PAIR)
        dk[:, columns] = ((dka[:, columns] + spread(select[...], dkm[:, columns])) * HD ** (-0.5)).astype(BF)
        dv[:, columns] = (dva[:, columns] + spread(select[...], dvm[:, columns])).astype(BF)


def attention_call(kernel, outs, parent, slot_rows, arrays, scratch, name):
    rows, width = arrays[0].shape
    vm = pl.BlockSpec(memory_space=pltpu.VMEM)
    return pl.pallas_call(
        kernel,
        out_shape=[jax.ShapeDtypeStruct((rows, width), BF)] * outs,
        in_specs=[pl.BlockSpec(memory_space=pltpu.SMEM), vm] + [vm] * len(arrays),
        out_specs=[vm] * outs,
        scratch_shapes=[
            pltpu.VMEM((SEGS, WIN + MEMP), F32),
            pltpu.VMEM((MEMP, rows), BF),
            pltpu.VMEM((MEMP, width), BF),
            pltpu.VMEM((MEMP, width), BF),
        ]
        + scratch,
        compiler_params=pltpu.CompilerParams(vmem_limit_bytes=60 * 2**20),
        name=name,
    )(parent, slot_rows, *arrays)


def forward_attention(parent, slot_rows, q, k, v):
    return attention_call(forward_attention_kernel, 1, parent, slot_rows, (q, k, v), [], "attend")[0]


def backward_attention(parent, slot_rows, q, k, v, dmix):
    rows, width = q.shape
    scratch = [pltpu.VMEM((rows, width), F32)] * 2 + [pltpu.VMEM((MEMP, width), F32)] * 2
    return attention_call(
        backward_attention_kernel, 3, parent, slot_rows, (q, k, v, dmix), scratch, "attend_back"
    )


def norm_stats(values):
    centered = values - jnp.mean(values, axis=-1, keepdims=True)
    inverse = lax.rsqrt(jnp.mean(centered * centered, axis=-1, keepdims=True) + EPSILON)
    return centered * inverse, inverse


def norm_back(grad, normed, inverse, gain):
    scaled = grad * gain
    return inverse * (
        scaled
        - jnp.mean(scaled, axis=-1, keepdims=True)
        - normed * jnp.mean(scaled * normed, axis=-1, keepdims=True)
    )


def gelu_parts(inner):
    phi = 0.5 + 0.5 * lax.erf(inner * (0.5**0.5))
    density = jnp.exp(-0.5 * inner * inner) * (2.0 * jnp.pi) ** -0.5
    return (inner * phi).astype(BF), (phi + inner * density).astype(BF)


TILE = 128


def row_tiles(rows, body):
    full = rows // TILE

    @pl.loop(0, full)
    def _(i):
        body(pl.ds(pl.multiple_of(i * TILE, TILE), TILE))

    if rows % TILE:
        body(pl.ds(full * TILE, rows % TILE))


def forward_kernel(
    fast,
    parent,
    slot_rows,
    small,
    rows_in,
    tokens_h,
    grad_h,
    own_qkv,
    own_out,
    own_up,
    own_down,
    *rest,
):
    count = 0 if fast else 5
    given, outs, rest = rest[:count], rest[count : count + 16], rest[count + 16 :]
    (
        output_h,
        their_qkv_h,
        their_out_h,
        their_up_h,
        their_down_h,
        qkv_h,
        mixed_h,
        normed_h,
        inverse,
        hidden_h,
        acted_h,
        slope_own_h,
        slope_their_h,
        d_two_h,
        d_ffn_h,
        vec,
    ) = outs
    (
        tokens,
        their_qkv,
        their_out,
        their_up,
        their_down,
        small_their,
        qkv,
        mixed,
        normed,
        hidden,
        acc_own,
        acc_their,
        acted,
        slopes,
        colbias,
        select,
        kmem,
        vmem,
        sums,
        io_sem,
        slope_sem,
        *wires,
    ) = rest
    rows, depth = tokens.shape
    width = mixed.shape[2]
    theirs = (their_qkv, their_out, their_up, their_down)
    own = (own_qkv, own_out, own_up, own_down)

    def move(index, source, target):
        return pltpu.make_async_copy(source, target, io_sem.at[index])

    load_tokens = move(0, tokens_h, tokens)
    load_grad = move(1, grad_h, tokens)
    put_qkv = move(2, qkv, qkv_h)
    put_mixed = move(3, mixed.at[0], mixed_h)
    put_normed = move(4, normed, normed_h)
    put_hidden = move(5, hidden, hidden_h)
    put_acted = move(6, acted, acted_h)
    put_two = move(7, acc_own, d_two_h)
    put_ffn = move(8, hidden, d_ffn_h)
    put_output = move(9, tokens, output_h)
    put_theirs = [
        move(10 + i, ref, target)
        for i, (ref, target) in enumerate(zip(theirs, (their_qkv_h, their_out_h, their_up_h, their_down_h)))
    ]
    load_tokens.start()
    done = [0]
    if fast:
        pos = Place()
        small_sem, *wires = wires
        stage_own, send_own, tick = make_gather(pos, own, theirs, *wires)
        stage_own()
        gather_barrier(pos, 1 - lax.axis_index("tensor"))
        swap = swap_small(small, small_their, small_sem)
        swap.start()
        send_own()
    else:
        copies = [move(10 + i, a, b) for i, (a, b) in enumerate(zip(given, theirs + (small_their,)))]
        for copy in copies:
            copy.start()
        for copy in copies:
            copy.wait()

        def tick(step):
            pass

    def ticks(index, each, trips):
        for i in range(each):
            tick(done[0] + index * each + i)

    def until(count):
        if done[0] < count:

            @pl.loop(done[0], count)
            def _(step):
                tick(step)

            done[0] = count

    build_masks(parent, lax.axis_index("dp") * SEGS, colbias)
    build_select(slot_rows, select)
    load_tokens.wait()
    pairs = width // PAIR
    for half in range(2):
        weights = (own_qkv, their_qkv)[half]
        table = (small, small_their)[half]
        if half == 1:
            until(BOUNDS[0][1] + 3 * RELAY)
            if fast:
                swap.wait()

        @pl.loop(0, 3)
        def _(c, half=half, weights=weights, table=table):
            part = mm(tokens[...], weights[pl.ds(pl.multiple_of(c * depth, depth), depth), :])
            qkv[half, c] = (part + table[pl.ds(c, 1), :]).astype(BF)
            ticks(c, GATHER[2 * half], 3)

        done[0] += 3 * GATHER[2 * half]
        q, k, v = (qkv.at[half, i] for i in range(3))
        kmem[...] = mm(select[...], k[...]).astype(BF)
        vmem[...] = mm(select[...], v[...]).astype(BF)

        @pl.loop(0, SEGS)
        def _(s, half=half, q=q, k=k, v=v):
            for pair in range(pairs):
                attend_pair(q, k, v, kmem, vmem, colbias, mixed.at[half], s, pl.ds(pair * PAIR, PAIR))
                if pair < GATHER[2 * half + 1]:
                    tick(done[0] + s * GATHER[2 * half + 1] + pair)

        done[0] += SEGS * GATHER[2 * half + 1]
    put_qkv.start()
    put_mixed.start()
    until(BOUNDS[1][1] + 3 * RELAY)

    @pl.loop(0, 3)
    def _(n):
        columns = pl.ds(pl.multiple_of(n * CHUNK, CHUNK), CHUNK)
        acc_own[:, columns] = mm(mixed[0], own_out[:, columns]) + mm(mixed[1], their_out[:, columns])
        ticks(n, GATHER[4], 3)

    done[0] += 3 * GATHER[4]

    def norm_one(span):
        resid = tokens[span, :].astype(F32) + (acc_own[span, :] + rows_in[0:1, :])
        unit, scale = norm_stats(resid)
        normed[span, :] = unit
        inverse[span, :] = scale
        hidden[span, :] = (unit * rows_in[1:2, :] + rows_in[2:3, :]).astype(BF)

    row_tiles(rows, norm_one)
    load_grad.start()
    put_normed.start()
    put_hidden.start()

    for half in range(2):
        up, down = ((own_up, own_down), (their_up, their_down))[half]
        table = (small, small_their)[half]
        slope_h = (slope_own_h, slope_their_h)[half]
        acc = (acc_own, acc_their)[half]

        def put_slope(c, slope_h=slope_h):
            span = pl.ds(pl.multiple_of(c * CHUNK, CHUNK), CHUNK)
            return pltpu.make_async_copy(slopes.at[lax.rem(c, 2)], slope_h.at[:, span], slope_sem.at[lax.rem(c, 2)])

        if half == 1:
            until(BOUNDS[2][1] + 3 * RELAY)
            put_acted.wait()
            put_slope(4).wait()
            put_slope(5).wait()

        @pl.loop(0, 6)
        def _(c, half=half, up=up, table=table, put_slope=put_slope):
            span = pl.ds(pl.multiple_of(c * CHUNK, CHUNK), CHUNK)

            @pl.when(c >= 2)
            def _():
                put_slope(c - 2).wait()

            bias = table[pl.ds(3 + c, 1), 0:CHUNK]
            act, steep = gelu_parts(mm(hidden[...], up[:, span]) + bias)
            acted[:, span] = act
            slopes[lax.rem(c, 2)] = steep
            put_slope(c).start()
            ticks(c, GATHER[5 + 2 * half], 6)

        done[0] += 6 * GATHER[5 + 2 * half]
        if half == 0:
            put_acted.start()
        else:
            until(BOUNDS[3][1] + 3 * RELAY)
            if fast:
                for copy in put_theirs:
                    copy.start()

        @pl.loop(0, 3)
        def _(n, half=half, down=down, acc=acc):
            columns = pl.ds(pl.multiple_of(n * CHUNK, CHUNK), CHUNK)
            acc[:, columns] = mm(acted[...], down[:, columns])
            ticks(n, GATHER[6 + 2 * half], 3)

        done[0] += 3 * GATHER[6 + 2 * half]
    put_slope(4).wait()
    put_slope(5).wait()

    load_grad.wait()
    put_hidden.wait()
    sums[...] = jnp.zeros(sums.shape, F32)

    def norm_two(span):
        first = normed[span, :] * rows_in[1:2, :] + rows_in[2:3, :]
        resid = first + ((acc_own[span, :] + acc_their[span, :]) + rows_in[3:4, :])
        unit, scale = norm_stats(resid)
        grad = tokens[span, :].astype(F32)
        tokens[span, :] = (unit * rows_in[4:5, :] + rows_in[5:6, :]).astype(BF)
        back = norm_back(grad, unit, scale, rows_in[4:5, :])
        acc_own[span, :] = back
        low = back.astype(BF)
        hidden[span, :] = low
        for index, value in enumerate((low.astype(F32), grad * unit, grad)):
            sums[index] = sums[index] + value.reshape(-1, 8, depth).sum(axis=0)

    row_tiles(rows, norm_two)
    put_two.start()
    put_ffn.start()
    put_output.start()
    for index in range(3):
        total = jnp.sum(sums[index], axis=0, keepdims=True)
        for j in range(6):
            vec[6 * index + j : 6 * index + j + 1, :] = total[:, BC * j : BC * (j + 1)]
    for copy in (put_qkv, put_mixed, put_normed, put_two, put_ffn, put_output):
        copy.wait()
    if fast:
        for copy in put_theirs:
            copy.wait()


GATHER = (0, 1, 1, 1, 0, 1, 0, 0, 0)


def forward(fast, parent, slot_rows, small, rows_in, tokens, grad_out, own, given):
    rows, depth = tokens.shape
    width = own[0].shape[1]
    units = own[2].shape[1]
    vm = pl.BlockSpec(memory_space=pltpu.VMEM)
    hbm = pl.BlockSpec(memory_space=pl.ANY)
    sd = jax.ShapeDtypeStruct
    out_shape = [
        sd((rows, depth), BF),
        *[sd(w.shape, BF) for w in own],
        sd((2, 3, rows, width), BF),
        sd((rows, width), BF),
        sd((rows, depth), F32),
        sd((rows, 1), F32),
        sd((rows, depth), BF),
        sd((rows, units), BF),
        sd((rows, units), BF),
        sd((rows, units), BF),
        sd((rows, depth), F32),
        sd((rows, depth), BF),
        sd((18, BC), F32),
    ]
    return pl.pallas_call(
        functools.partial(forward_kernel, fast),
        out_shape=out_shape,
        in_specs=[pl.BlockSpec(memory_space=pltpu.SMEM), vm, vm, vm, hbm, hbm] + [vm] * 4 + [hbm] * len(given),
        out_specs=[hbm] * 8 + [vm] + [hbm] * 6 + [vm],
        scratch_shapes=[
            pltpu.VMEM((rows, depth), BF),
            *[pltpu.VMEM(w.shape, BF) for w in own],
            pltpu.VMEM(small.shape, F32),
            pltpu.VMEM((2, 3, rows, width), BF),
            pltpu.VMEM((2, rows, width), BF),
            pltpu.VMEM((rows, depth), F32),
            pltpu.VMEM((rows, depth), BF),
            pltpu.VMEM((rows, depth), F32),
            pltpu.VMEM((rows, depth), F32),
            pltpu.VMEM((rows, units), BF),
            pltpu.VMEM((2, rows, CHUNK), BF),
            pltpu.VMEM((SEGS, WIN + MEMP), F32),
            pltpu.VMEM((MEMP, rows), BF),
            pltpu.VMEM((MEMP, width), BF),
            pltpu.VMEM((MEMP, width), BF),
            pltpu.VMEM((3, 8, depth), F32),
            pltpu.SemaphoreType.DMA((15,)),
            pltpu.SemaphoreType.DMA((2,)),
        ]
        + ([pltpu.SemaphoreType.DMA((2,))] + gather_scratch() if fast else []),
        compiler_params=pltpu.CompilerParams(
            collective_id=0 if fast else None, has_side_effects=fast, vmem_limit_bytes=67043328
        ),
        name="forward",
    )(parent, slot_rows, small, rows_in, tokens, grad_out, *own, *given)


DOWN, UP, OUT, QKV, VEC = 0, 24, 48, 54, 72
COUNT = 73
CHUNK = 256
VEC_ROWS = 54


def backward_kernel(
    fast,
    parent,
    slot_rows,
    inverse,
    gain,
    vec_in,
    tokens_h,
    hidden_h,
    d_ffn_h,
    d_two_h,
    normed_h,
    acted_h,
    slope_own_h,
    slope_their_h,
    qkv_h,
    mixed_h,
    w_up_own,
    w_up_their,
    w_down_own,
    w_down_their,
    w_out_own,
    w_out_their,
    w_qkv_own,
    w_qkv_their,
    g_qkv,
    g_out,
    g_up,
    g_down,
    g_vec,
    g_tokens,
    grads,
    d_low,
    hidden,
    d_res,
    normed,
    acc_own,
    acc_their,
    a_buf,
    slope_buf,
    up_buf,
    down_buf,
    d_inner,
    sums,
    tokens,
    mixed,
    w_out,
    w_qkv,
    qkv,
    d_qkv,
    d_mixed,
    colbias,
    select,
    kmem,
    vmem,
    dkm,
    dvm,
    load_sem,
    chunk_sem,
    put_sem,
    *wires,
):
    rows, depth = tokens.shape
    width = mixed.shape[1]

    def fetch(index, source, target):
        return pltpu.make_async_copy(source, target, load_sem.at[index])

    load_d = fetch(0, d_ffn_h, d_low)
    load_hidden = fetch(1, hidden_h, hidden)
    load_two = fetch(2, d_two_h, d_res)
    load_normed = fetch(3, normed_h, normed)
    load_mixed = fetch(4, mixed_h, mixed)
    load_out = [fetch(5 + i, w, w_out.at[i]) for i, w in enumerate((w_out_own, w_out_their))]
    load_w = [fetch(7 + i, w, w_qkv.at[i]) for i, w in enumerate((w_qkv_own, w_qkv_their))]
    load_tokens = fetch(9, tokens_h, tokens)
    load_qkv = [fetch(10 + half, qkv_h.at[half], qkv) for half in range(2)]
    put_tokens = fetch(12, d_low, g_tokens)

    def load_acted(c):
        return pltpu.make_async_copy(acted_h.at[:, pl.ds(pl.multiple_of(c * BR, BR), BR)], a_buf.at[lax.rem(c, 2)], chunk_sem.at[0, lax.rem(c, 2)])

    def load_chunk(half, c):
        slot = lax.rem(c, 2)
        span = pl.ds(pl.multiple_of(c * CHUNK, CHUNK), CHUNK)
        slope_h, up_h, down_h = ((slope_own_h, w_up_own, w_down_own), (slope_their_h, w_up_their, w_down_their))[half]
        return (
            pltpu.make_async_copy(slope_h.at[:, span], slope_buf.at[slot], chunk_sem.at[1, slot]),
            pltpu.make_async_copy(up_h.at[:, span], up_buf.at[slot], chunk_sem.at[2, slot]),
            pltpu.make_async_copy(down_h.at[span, :], down_buf.at[slot], chunk_sem.at[3, slot]),
        )

    def start(copies):
        for copy in copies:
            copy.start()

    def wait(copies):
        for copy in copies:
            copy.wait()

    load_d.start()
    load_acted(0).start()
    start(load_chunk(0, 0))
    load_hidden.start()
    load_two.start()
    load_normed.start()
    load_mixed.start()
    start(load_out)
    start(load_w)
    load_tokens.start()
    load_qkv[0].start()

    def put(block, target):
        return pltpu.make_async_copy(grads.at[block], target, put_sem.at[lax.rem(block, 8)])

    def wait_put(block):
        put(block, g_vec).wait()

    def finish(block):
        @pl.when(block >= 8)
        def _():
            wait_put(block - 8)

        def at(row, column):
            return pl.ds(pl.multiple_of(row, BR), BR), pl.ds(pl.multiple_of(column, BC), BC)

        @pl.when(block < UP)
        def _():
            put(block, g_down.at[at(BR * (block // 6), BC * lax.rem(block, 6))]).start()

        @pl.when((block >= UP) & (block < OUT))
        def _():
            i = block - UP
            put(block, g_up.at[at(BR * lax.rem(i // 2, 2), CHUNK * (i // 4) + BC * lax.rem(i, 2))]).start()

        @pl.when((block >= OUT) & (block < QKV))
        def _():
            put(block, g_out.at[at(0, BC * (block - OUT))]).start()

        @pl.when((block >= QKV) & (block < VEC))
        def _():
            i = block - QKV
            put(block, g_qkv.at[at(BR * (i // 3), BC * lax.rem(i, 3))]).start()

        @pl.when(block == VEC)
        def _():
            put(block, g_vec).start()

    if fast:
        pos = Place()
        tick = make_tick(pos, grads, *wires, COUNT, finish)
        last = COUNT + 7 * SPREAD
    else:

        def tick(step):
            finish(step)

        last = COUNT
    done = [0]

    def ticks(index, each, trips):
        for i in range(each):
            tick(done[0] + index * each + i)
        return trips * each

    grads[VEC] = jnp.zeros((BR, BC), F32)
    grads[VEC, 36:54] = vec_in[...]
    acc_own[...] = jnp.zeros(acc_own.shape, F32)
    acc_their[...] = jnp.zeros(acc_their.shape, F32)
    sums[...] = jnp.zeros(sums.shape, F32)
    if fast:
        sum_barrier(pos)

    load_d.wait()

    @pl.loop(0, 4)
    def _(c):
        load_acted(c).wait()

        @pl.when(c < 3)
        def _():
            load_acted(c + 1).start()

        for part in range(2):
            piece = t_mm(a_buf[lax.rem(c, 2)], d_low[:, part * width : (part + 1) * width])
            for j in range(3):
                grads[DOWN + 6 * c + 3 * part + j] = piece[:, BC * j : BC * (j + 1)]
        ticks(c, TICKS[0], 4)

    done[0] += 4 * TICKS[0]

    load_hidden.wait()
    for half in range(2):
        acc = (acc_own, acc_their)[half]

        @pl.loop(0, 6)
        def _(c, half=half, acc=acc):
            slot = lax.rem(c, 2)
            wait(load_chunk(half, c))

            @pl.when(c < 5)
            def _():
                start(load_chunk(half, c + 1))

            if half == 0:

                @pl.when(c == 5)
                def _():
                    start(load_chunk(1, 0))

            d_inner[...] = (mm_t(d_low[...], down_buf[slot]) * slope_buf[slot].astype(F32)).astype(BF)
            if half == 0:
                piece = t_mm(hidden[...], d_inner[...])
                for r in range(2):
                    for j in range(2):
                        grads[UP + 4 * c + 2 * r + j] = piece[BR * r : BR * (r + 1), BC * j : BC * (j + 1)]
                total = jnp.sum(d_inner[...].astype(F32), axis=0, keepdims=True)
                for j in range(2):
                    grads[VEC, pl.ds(6 + 2 * c + j, 1), :] = total[:, BC * j : BC * (j + 1)]
            ticks(c, TICKS[1 + half], 6)
            for part in range(3):
                columns = slice(CHUNK * part, CHUNK * (part + 1))
                acc[:, columns] = acc[:, columns] + mm_t(d_inner[...], up_buf[slot, columns, :])

        done[0] += 6 * TICKS[1 + half]

    load_two.wait()
    load_normed.wait()
    tile = 32
    trips = rows // tile

    @pl.loop(0, trips)
    def _(i):
        span = pl.ds(pl.multiple_of(i * tile, tile), tile)
        total = d_res[span, :] + (acc_own[span, :] + acc_their[span, :])
        unit = normed[span, :]
        one = norm_back(total, unit, inverse[span, :], gain[...])
        d_res[span, :] = one
        low = one.astype(BF)
        d_low[span, :] = low
        for index, value in enumerate((low.astype(F32), total * unit, total)):
            sums[index] = sums[index] + value.reshape(tile // 8, 8, depth).sum(axis=0)

        @pl.when(lax.rem(i, TICK_TILES) == 0)
        def _():
            tick(done[0] + i // TICK_TILES)

    done[0] += -(-trips // TICK_TILES)
    for index in range(3):
        total = jnp.sum(sums[index], axis=0, keepdims=True)
        for j in range(6):
            grads[VEC, 18 + 6 * index + j : 19 + 6 * index + j, :] = total[:, BC * j : BC * (j + 1)]

    load_mixed.wait()
    wait(load_out)

    @pl.loop(0, 2)
    def _(half):
        d_mixed[half] = mm_t(d_low[...], w_out[half]).astype(BF)
        piece = t_mm(mixed[...], d_low[:, pl.ds(pl.multiple_of(half * width, BC), width)])
        for j in range(3):
            grads[OUT + 3 * half + j] = piece[:, BC * j : BC * (j + 1)]
        ticks(half, TICKS[3], 2)

    done[0] += 2 * TICKS[3]

    build_masks(parent, lax.axis_index("dp") * SEGS, colbias)
    build_select(slot_rows, select)
    wait(load_w)
    load_tokens.wait()
    pairs = width // PAIR
    dka, dva = acc_their.at[:, pl.ds(0, width)], acc_their.at[:, pl.ds(width, width)]
    for half in range(2):
        load_qkv[half].wait()
        q, k, v = (qkv.at[i] for i in range(3))
        kmem[...] = mm(select[...], k[...]).astype(BF)
        vmem[...] = mm(select[...], v[...]).astype(BF)
        acc_their[...] = jnp.zeros(acc_their.shape, F32)
        dkm[...] = jnp.zeros(dkm.shape, F32)
        dvm[...] = jnp.zeros(dvm.shape, F32)

        @pl.loop(0, SEGS)
        def _(s, half=half):
            for pair in range(pairs):
                columns = pl.ds(pair * PAIR, PAIR)
                attend_back_pair(
                    q, k, v, kmem, vmem, colbias, d_mixed.at[half], d_qkv.at[0], dka, dva, dkm, dvm, s, columns, columns
                )
                if pair < TICKS[4 + half]:
                    tick(done[0] + s * TICKS[4 + half] + pair)

        done[0] += SEGS * TICKS[4 + half]
        if half == 0:
            load_qkv[1].start()
        for pair in range(pairs):
            columns = pl.ds(pair * PAIR, PAIR)
            d_qkv[1, :, columns] = ((dka[:, columns] + spread(select[...], dkm[:, columns])) * HD ** (-0.5)).astype(BF)
            d_qkv[2, :, columns] = (dva[:, columns] + spread(select[...], dvm[:, columns])).astype(BF)
        if half == 0:

            @pl.loop(0, 3)
            def _(c):
                piece = t_mm(tokens[...], d_qkv[c])
                for r in range(2):
                    for j in range(3):
                        grads[QKV + 6 * c + 3 * r + j] = piece[BR * r : BR * (r + 1), BC * j : BC * (j + 1)]
                columns = pl.ds(pl.multiple_of(c * CHUNK, CHUNK), CHUNK)
                part = mm_t(d_qkv[0], w_qkv[half, pl.ds(pl.multiple_of(c * CHUNK, CHUNK), CHUNK), :])
                for i in (1, 2):
                    part = part + mm_t(d_qkv[i], w_qkv[half, pl.ds(pl.multiple_of(i * depth + c * CHUNK, CHUNK), CHUNK), :])
                acc_own[:, columns] = part
                ticks(c, TICKS[6], 3)

            done[0] += 3 * TICKS[6]
            for index, row in ((0, 0), (2, 3)):
                total = jnp.sum(d_qkv[index].astype(F32), axis=0, keepdims=True)
                for j in range(3):
                    grads[VEC, row + j : row + j + 1, :] = total[:, BC * j : BC * (j + 1)]
        else:

            @pl.loop(0, 3)
            def _(c):
                columns = pl.ds(pl.multiple_of(c * CHUNK, CHUNK), CHUNK)
                part = mm_t(d_qkv[0], w_qkv[half, pl.ds(pl.multiple_of(c * CHUNK, CHUNK), CHUNK), :])
                for i in (1, 2):
                    part = part + mm_t(d_qkv[i], w_qkv[half, pl.ds(pl.multiple_of(i * depth + c * CHUNK, CHUNK), CHUNK), :])
                d_low[:, columns] = ((acc_own[:, columns] + part) + d_res[:, columns]).astype(BF)
                ticks(c, TICKS[7], 3)

            done[0] += 3 * TICKS[7]
            put_tokens.start()
    assert done[0] <= COUNT

    @pl.loop(done[0], last)
    def _(step):
        tick(step)

    for block in range(COUNT - 8, COUNT):
        wait_put(block)
    put_tokens.wait()


TICKS = (1, 2, 1, 1, 2, 2, 2, 1)
TICK_TILES = 8


def backward(fast, parent, slot_rows, inverse, gain, vec_in, arrays):
    tokens, acted, mixed = arrays[0], arrays[5], arrays[9]
    rows, depth = tokens.shape
    units = acted.shape[1]
    width = mixed.shape[1]
    vm = pl.BlockSpec(memory_space=pltpu.VMEM)
    hbm = pl.BlockSpec(memory_space=pl.ANY)
    sd = jax.ShapeDtypeStruct
    return pl.pallas_call(
        functools.partial(backward_kernel, fast),
        out_shape=[
            sd((3 * depth, width), F32),
            sd((width, depth), F32),
            sd((depth, units), F32),
            sd((units, depth), F32),
            sd((BR, BC), F32),
            sd((rows, depth), BF),
        ],
        in_specs=[pl.BlockSpec(memory_space=pltpu.SMEM), vm, vm, vm, vm] + [hbm] * len(arrays),
        out_specs=[hbm] * 6,
        scratch_shapes=[
            pltpu.VMEM((COUNT, BR, BC), F32),
            pltpu.VMEM((rows, depth), BF),
            pltpu.VMEM((rows, depth), BF),
            pltpu.VMEM((rows, depth), F32),
            pltpu.VMEM((rows, depth), F32),
            pltpu.VMEM((rows, depth), F32),
            pltpu.VMEM((rows, depth), F32),
            pltpu.VMEM((2, rows, BR), BF),
            pltpu.VMEM((2, rows, CHUNK), BF),
            pltpu.VMEM((2, depth, CHUNK), BF),
            pltpu.VMEM((2, CHUNK, depth), BF),
            pltpu.VMEM((rows, CHUNK), BF),
            pltpu.VMEM((3, 8, depth), F32),
            pltpu.VMEM((rows, depth), BF),
            pltpu.VMEM((rows, width), BF),
            pltpu.VMEM((2, width, depth), BF),
            pltpu.VMEM((2, 3 * depth, width), BF),
            pltpu.VMEM((3, rows, width), BF),
            pltpu.VMEM((3, rows, width), BF),
            pltpu.VMEM((2, rows, width), BF),
            pltpu.VMEM((SEGS, WIN + MEMP), F32),
            pltpu.VMEM((MEMP, rows), BF),
            pltpu.VMEM((MEMP, width), BF),
            pltpu.VMEM((MEMP, width), BF),
            pltpu.VMEM((MEMP, width), F32),
            pltpu.VMEM((MEMP, width), F32),
            pltpu.SemaphoreType.DMA((13,)),
            pltpu.SemaphoreType.DMA((4, 2)),
            pltpu.SemaphoreType.DMA((8,)),
        ]
        + (sum_scratch() if fast else []),
        compiler_params=pltpu.CompilerParams(
            collective_id=1 if fast else None, has_side_effects=fast, vmem_limit_bytes=67043328
        ),
        name="backward",
    )(parent, slot_rows, inverse, gain, vec_in, *arrays)


def halves_swap(own, small):
    unit = (lax.axis_index("dp") >= 0).astype(F32)

    def other(array):
        arrived = lax.ppermute(array.astype(F32), "tensor", [(0, 1), (1, 0)])
        return (arrived * unit).astype(array.dtype)

    return tuple(other(array) for array in own) + (other(small),)


def shards(
    fast,
    tokens,
    w_qkv,
    bias_qv,
    w_out,
    bias_out,
    gain_one,
    shift_one,
    w_up,
    bias_up,
    w_down,
    bias_down,
    gain_two,
    shift_two,
    grad_out,
    parent,
    mem_slots,
):
    depth, width = w_qkv.shape[1:]
    hidden_units = w_up.shape[1]
    own = (w_qkv.reshape(3 * depth, width), w_out, w_up, w_down)
    table = jnp.pad(bias_up.reshape(-1, CHUNK), ((0, 0), (0, width - CHUNK)))
    small = jnp.concatenate([bias_qv[:1], jnp.zeros((1, width), F32), bias_qv[1:], table])
    small = jnp.pad(small, ((0, 16 - small.shape[0]), (0, 0)))
    given = () if fast else halves_swap(own, small)
    slot_rows = mem_slots + jnp.arange(SEGS, dtype=jnp.int32)[:, None] * SEG
    slot_rows = jnp.pad(slot_rows.reshape(-1, 1), ((0, MEMP - MEMW * SEGS), (0, 0)), constant_values=-1)
    rows_in = jnp.stack(
        [bias_out, gain_one, shift_one, bias_down, gain_two, shift_two, jnp.zeros_like(gain_one), jnp.zeros_like(gain_one)]
    )
    (
        output,
        *theirs,
        qkv,
        mixed,
        normed,
        inverse,
        hidden_low,
        acted,
        slope_own,
        slope_their,
        d_two,
        d_ffn,
        vec,
    ) = forward(fast, parent, slot_rows, small, rows_in, tokens, grad_out, own, given)
    if not fast:
        theirs = given[:4]
    arrays = (tokens, hidden_low, d_ffn, d_two, normed, acted, slope_own, slope_their, qkv, mixed)
    weights = tuple(w[i] for i in (2, 3, 1, 0) for w in (own, theirs))
    g_w_qkv, g_w_out, g_w_up, g_w_down, flat, grad_tokens = backward(
        fast, parent, slot_rows, inverse, gain_one.reshape(1, -1), vec, arrays + weights
    )
    if not fast:
        g_w_qkv, g_w_out, g_w_up, g_w_down, flat = lax.psum((g_w_qkv, g_w_out, g_w_up, g_w_down, flat), "dp")
    g_w_qkv = g_w_qkv.reshape(w_qkv.shape)
    sums, row = [], 0
    for size in (width, width, hidden_units) + (depth,) * 6:
        sums.append(flat[row : row + size // BC].reshape(-1))
        row += size // BC
    g_bias_q, g_bias_v, g_bias_up, g_bias_out, g_gain_one, g_shift_one, g_bias_down, g_gain_two, g_shift_two = sums
    return (
        output,
        grad_tokens,
        g_w_qkv,
        jnp.stack([g_bias_q, g_bias_v]),
        g_w_out,
        g_bias_out,
        g_gain_one,
        g_shift_one,
        g_w_up,
        g_bias_up,
        g_w_down,
        g_bias_down,
        g_gain_two,
        g_shift_two,
    )


def solution(mesh):
    fast = mesh.shape["dp"] == 16 and mesh.shape["tensor"] == 2
    rows, whole = P("dp", None), P()
    return jax.shard_map(
        functools.partial(shards, fast),
        mesh=mesh,
        in_specs=(
            rows,
            P(None, None, "tensor"),
            P(None, "tensor"),
            P("tensor", None),
            whole,
            whole,
            whole,
            P(None, "tensor"),
            P("tensor"),
            P("tensor", None),
            whole,
            whole,
            whole,
            rows,
            P("dp"),
            rows,
        ),
        out_specs=(
            rows,
            rows,
            P(None, None, "tensor"),
            P(None, "tensor"),
            P("tensor", None),
            whole,
            whole,
            whole,
            P(None, "tensor"),
            P("tensor"),
            P("tensor", None),
            whole,
            whole,
            whole,
        ),
        check_vma=False,
    )
```

```python
import functools


import jax
import jax.numpy as jnp
from jax import lax
from jax.experimental import pallas as pl
from jax.experimental.pallas import tpu as pltpu
from jax.sharding import PartitionSpec as P


MESH = pl.DeviceIdType.MESH
BR, BC = 384, 128
SPREAD = 3
SLOTS = 16


class Place:
    def __init__(self):
        me = lax.axis_index("dp")
        self.core = lax.rem(me, 2)
        self.x = lax.rem(me // 2, 2)
        self.z = me // 4
        self.sib = me + 1 - 2 * self.core
        self.xn = me + 2 - 4 * self.x
        self.zp = me + 4 - 8 * lax.rem(self.z, 2)
        self.zm = me + 4 * (3 - 2 * self.z)
        self.end = (self.z == 0) | (self.z == 3)
        self.mid = (self.z == 1) | (self.z == 2)


def sum_barrier(pos):
    barrier = pltpu.get_barrier_semaphore()

    def greet(dev):
        pl.semaphore_signal(barrier, inc=1, device_id={"dp": dev}, device_id_type=MESH)

    greet(pos.sib)
    greet(pos.xn)
    greet(pos.zp)

    @pl.when(pos.mid)
    def _():
        greet(pos.zm)

    pl.semaphore_wait(barrier, jnp.where(pos.mid, 4, 3))


def make_tick(pos, grads, from_core, from_one, from_two, from_three, sent, got, credit, count, finish):
    half = BR // 2
    quarter = BR // 4

    def copy(stage, block, source, target, device):
        slot = lax.rem(block, SLOTS)
        return pltpu.make_async_remote_copy(
            src_ref=source,
            dst_ref=target,
            send_sem=sent.at[stage, slot],
            recv_sem=got.at[stage, slot],
            device_id={"dp": device},
            device_id_type=MESH,
        )

    def rows(block, start, size):
        return grads.at[block, pl.ds(pl.multiple_of(start, quarter), size)]

    def add(block, start, size, landed):
        where = pl.ds(pl.multiple_of(start, quarter), size)
        grads[block, where] = grads[block, where] + landed[...]

    def free(index, device):
        pl.semaphore_signal(credit.at[index], inc=1, device_id={"dp": device}, device_id_type=MESH)

    def claim(index):
        pl.semaphore_wait(credit.at[index], 1)

    x_first = pos.core == 0
    z_first = pos.core == 1
    mine = pos.core * half
    xrow = pos.x * quarter
    xrow_other = (1 - pos.x) * quarter
    far = lax.rem(pos.z, 2) == 0
    keep = half + jnp.where(far, quarter, 0)
    give = half + jnp.where(far, 0, quarter)

    def core_out(block):
        return copy(0, block, rows(block, (1 - pos.core) * half, half), from_core.at[lax.rem(block, SLOTS)], pos.sib)

    def x_one(block):
        return copy(1, block, rows(block, xrow_other, quarter), from_one.at[lax.rem(block, SLOTS), pl.ds(0, quarter)], pos.xn)

    def z_one(block):
        return copy(1, block, rows(block, half, half), from_one.at[lax.rem(block, SLOTS)], pos.zp)

    def x_two(block):
        return copy(2, block, rows(block, xrow, quarter), from_two.at[lax.rem(block, SLOTS)], pos.zp)

    def z_two(block):
        return copy(2, block, rows(block, give, quarter), from_two.at[lax.rem(block, SLOTS)], pos.zm)

    def x_three(block):
        return copy(3, block, rows(block, xrow, quarter), from_three.at[lax.rem(block, SLOTS)], pos.zm)

    def z_three(block):
        return copy(3, block, rows(block, keep, quarter), from_three.at[lax.rem(block, SLOTS)], pos.xn)

    def x_four(block):
        return copy(4, block, rows(block, xrow, quarter), rows(block, xrow, quarter), pos.zp)

    def z_four(block):
        return copy(4, block, rows(block, keep, quarter), rows(block, keep, quarter), pos.zm)

    def z_four_in(block):
        return copy(4, block, rows(block, give, quarter), rows(block, give, quarter), pos.zm)

    def x_five(block):
        return copy(5, block, rows(block, xrow, quarter), rows(block, xrow, quarter), pos.xn)

    def x_five_in(block):
        return copy(5, block, rows(block, xrow_other, quarter), rows(block, xrow_other, quarter), pos.xn)

    def z_five(block):
        return copy(5, block, rows(block, half, half), rows(block, half, half), pos.zp)

    def core_six(block):
        return copy(6, block, rows(block, mine, half), rows(block, mine, half), pos.sib)

    def core_six_in(block):
        return copy(6, block, rows(block, (1 - pos.core) * half, half), rows(block, (1 - pos.core) * half, half), pos.sib)

    def stage_zero(block):
        core_out(block).start()

    def stage_one(block):
        core_out(block).wait()
        free(2, pos.sib)
        add(block, mine, half, from_core.at[lax.rem(block, SLOTS)])

        @pl.when(x_first)
        def _():
            x_one(block).start()

        @pl.when(z_first & pos.end)
        def _():
            z_one(block).start()

    def stage_two(block):
        @pl.when(x_first)
        def _():
            x_one(block).wait()
            free(1, pos.xn)
            add(block, xrow, quarter, from_one.at[lax.rem(block, SLOTS), pl.ds(0, quarter)])

            @pl.when(pos.end)
            def _():
                x_two(block).start()

        @pl.when(z_first & pos.end)
        def _():
            z_one(block).wait_send()
            free(1, pos.zp)

        @pl.when(z_first & pos.mid)
        def _():
            z_one(block).wait_recv()
            add(block, half, half, from_one.at[lax.rem(block, SLOTS)])
            z_two(block).start()

    def stage_three(block):
        @pl.when(x_first & pos.end)
        def _():
            x_two(block).wait_send()
            free(0, pos.zp)

        @pl.when(x_first & pos.mid)
        def _():
            x_two(block).wait_recv()
            add(block, xrow, quarter, from_two.at[lax.rem(block, SLOTS)])
            x_three(block).start()

        @pl.when(z_first & pos.mid)
        def _():
            z_two(block).wait()
            free(0, pos.zm)
            add(block, keep, quarter, from_two.at[lax.rem(block, SLOTS)])
            z_three(block).start()

    def stage_four(block):
        @pl.when(x_first & pos.mid)
        def _():
            x_three(block).wait()
            add(block, xrow, quarter, from_three.at[lax.rem(block, SLOTS)])
            claim(0)
            x_four(block).start()

        @pl.when(z_first & pos.mid)
        def _():
            z_three(block).wait()
            add(block, keep, quarter, from_three.at[lax.rem(block, SLOTS)])
            claim(0)
            z_four(block).start()

    def stage_five(block):
        @pl.when(x_first)
        def _():
            @pl.when(pos.end)
            def _():
                x_four(block).wait_recv()

            @pl.when(pos.mid)
            def _():
                x_four(block).wait_send()

            claim(1)
            x_five(block).start()

        @pl.when(z_first & pos.mid)
        def _():
            z_four(block).wait_send()
            z_four_in(block).wait_recv()
            claim(1)
            z_five(block).start()

    def stage_six(block):
        @pl.when(x_first)
        def _():
            x_five(block).wait_send()
            x_five_in(block).wait_recv()

        @pl.when(z_first & pos.end)
        def _():
            z_five(block).wait_recv()

        @pl.when(z_first & pos.mid)
        def _():
            z_five(block).wait_send()

        claim(2)
        core_six(block).start()

    def stage_seven(block):
        core_six(block).wait_send()
        core_six_in(block).wait_recv()
        finish(block)

    stages = (stage_zero, stage_one, stage_two, stage_three, stage_four, stage_five, stage_six, stage_seven)

    def tick(step):
        for index in reversed(range(8)):
            block = step - SPREAD * index

            @pl.when((block >= 0) & (block < count))
            def _(index=index, block=block):
                stages[index](block)

    return tick


def sum_scratch():
    return [
        pltpu.VMEM((SLOTS, BR // 2, BC), jnp.float32),
        pltpu.VMEM((SLOTS, BR // 2, BC), jnp.float32),
        pltpu.VMEM((SLOTS, BR // 4, BC), jnp.float32),
        pltpu.VMEM((SLOTS, BR // 4, BC), jnp.float32),
        pltpu.SemaphoreType.DMA((7, SLOTS)),
        pltpu.SemaphoreType.DMA((7, SLOTS)),
        pltpu.SemaphoreType.REGULAR((3,)),
    ]


CR, CC = 64, 384
CHUNKS = 24
RELAY = 2
BF = jnp.bfloat16


def gather_barrier(pos, other):
    barrier = pltpu.get_barrier_semaphore()
    for where in ({"tensor": other}, {"dp": pos.xn}, {"dp": pos.zp}, {"dp": pos.sib}):
        pl.semaphore_signal(barrier, inc=1, device_id=where, device_id_type=MESH)
    pl.semaphore_wait(barrier, 4)


def chunk_parts(piece, chunk, kind):
    if kind == 0:
        return [(piece * 384 + chunk * 64, 64, 0, 0)]
    if kind == 1:
        return [(piece * 64 + (chunk - 6) * 32, 32, 384 * q, 32 * q) for q in range(2)]
    if kind == 2:
        return [(piece * 128 + (chunk - 8) * 16, 16, 384 * q, 16 * q) for q in range(4)]
    return [(piece * 256 + (chunk - 16) * 32, 32, 384 * q, 32 * q) for q in range(2)]


BOUNDS = ((0, 6), (6, 8), (8, 16), (16, 24))
UNIT = (64, 32, 16, 32)


def make_gather(pos, own, theirs, staged, landed, sent, got):
    other = 1 - lax.axis_index("tensor")
    odd = lax.rem(pos.z, 2)
    ky = jnp.where(pos.x == 0, odd, 2)
    kx = jnp.where(pos.x == 0, 2, odd)
    kz = 1 - odd
    piece_y = 2 * ky + pos.core
    piece_x = 2 * kx + pos.core
    piece_z = 2 * kz + pos.core
    sib_y = 2 * ky + 1 - pos.core
    sib_x = 2 * kx + 1 - pos.core
    sib_z = 2 * kz + 1 - pos.core

    def copy(lane, chunk, source, piece, where):
        return pltpu.make_async_remote_copy(
            src_ref=source,
            dst_ref=landed.at[piece, chunk],
            send_sem=sent.at[lane, chunk],
            recv_sem=got.at[lane, chunk],
            device_id=where,
            device_id_type=MESH,
        )

    def over_y(chunk):
        return copy(0, chunk, staged.at[chunk], piece_y, {"tensor": other})

    def over_x(chunk, piece):
        return copy(1, chunk, landed.at[piece, chunk], piece, {"dp": pos.xn})

    def over_z(chunk, piece):
        return copy(2, chunk, landed.at[piece, chunk], piece, {"dp": pos.zp})

    def over_core(lane, chunk, piece):
        return copy(lane, chunk, landed.at[piece, chunk], piece, {"dp": pos.sib})

    def stage_own():
        for kind in range(4):
            lo, hi = BOUNDS[kind]

            @pl.loop(lo, hi)
            def _(chunk, kind=kind):
                for row, rows, column, at in chunk_parts(piece_y, chunk, kind):
                    staged[chunk, pl.ds(at, rows)] = own[kind][
                        pl.ds(pl.multiple_of(row, UNIT[kind]), rows), pl.ds(column, CC)
                    ].astype(jnp.float32)

    def send_own():
        @pl.loop(0, CHUNKS)
        def _(chunk):
            over_y(chunk).start()

    def unpack(chunk):
        for kind in range(4):
            lo, hi = BOUNDS[kind]

            @pl.when((chunk >= lo) & (chunk < hi))
            def _(kind=kind):
                @pl.loop(0, 6)
                def _(piece):
                    for row, rows, column, at in chunk_parts(piece, chunk, kind):
                        theirs[kind][pl.ds(pl.multiple_of(row, UNIT[kind]), rows), pl.ds(column, CC)] = landed[
                            piece, chunk, pl.ds(at, rows)
                        ].astype(BF)

    def guarded(chunk, body):
        @pl.when((chunk >= 0) & (chunk < CHUNKS))
        def _():
            body(chunk)

    def first(chunk):
        over_y(chunk).wait_recv()
        over_x(chunk, piece_y).start()

        @pl.when(pos.x == 0)
        def _():
            over_z(chunk, piece_y).start()

        over_core(3, chunk, piece_y).start()

    def second(chunk):
        over_x(chunk, piece_x).wait_recv()

        @pl.when(pos.x == 1)
        def _():
            over_z(chunk, piece_x).start()

        over_core(4, chunk, piece_x).start()

    def third(chunk):
        over_z(chunk, piece_z).wait_recv()
        over_core(5, chunk, piece_z).start()

    def fourth(chunk):
        over_core(3, chunk, sib_y).wait_recv()
        over_core(4, chunk, sib_x).wait_recv()
        over_core(5, chunk, sib_z).wait_recv()
        over_y(chunk).wait_send()
        over_x(chunk, piece_y).wait_send()
        over_z(chunk, piece_y).wait_send()
        over_core(3, chunk, piece_y).wait_send()
        over_core(4, chunk, piece_x).wait_send()
        over_core(5, chunk, piece_z).wait_send()
        unpack(chunk)

    def tick(step):
        guarded(step - 3 * RELAY, fourth)
        guarded(step - 2 * RELAY, third)
        guarded(step - RELAY, second)
        guarded(step, first)

    return stage_own, send_own, tick


GATHER_TICKS = CHUNKS + 3 * RELAY


def gather_scratch():
    return [
        pltpu.VMEM((CHUNKS, CR, CC), jnp.float32),
        pltpu.VMEM((6, CHUNKS, CR, CC), jnp.float32),
        pltpu.SemaphoreType.DMA((6, CHUNKS)),
        pltpu.SemaphoreType.DMA((6, CHUNKS)),
    ]


def swap_small(small, small_out, sems):
    return pltpu.make_async_remote_copy(
        src_ref=small,
        dst_ref=small_out,
        send_sem=sems.at[0],
        recv_sem=sems.at[1],
        device_id={"tensor": 1 - lax.axis_index("tensor")},
        device_id_type=MESH,
    )


HD = 64
SEG = 148
MEMW = 10
F32 = jnp.float32
EPSILON = 1e-12
MASKED = -1e30
WIN = 160
MEMP = 96
SEGS = 8
PAIR = 2 * HD

CONTRACT_LAST = (((1,), (1,)), ((), ()))
CONTRACT_FIRST = (((0,), (0,)), ((), ()))


def mm(a, b):
    return jnp.dot(a, b, preferred_element_type=F32)


def mm_t(a, b):
    return lax.dot_general(a, b, CONTRACT_LAST, preferred_element_type=F32)


def t_mm(a, b):
    return lax.dot_general(a, b, CONTRACT_FIRST, preferred_element_type=F32)


def build_masks(parent, base, colbias):
    lane = lax.broadcasted_iota(jnp.int32, (1, WIN + MEMP), 1)
    in_mem = [
        ((lane >= WIN + MEMW * t) & (lane < WIN + MEMW * (t + 1))).astype(F32) for t in range(SEGS)
    ]
    reach = [jnp.zeros((1, WIN + MEMP), F32)]
    for s in range(1, SEGS):
        row = jnp.zeros((1, WIN + MEMP), F32)
        for t in range(s):
            hit = jnp.where(parent[s] - base == t, 1.0, 0.0)
            row = row + hit * jnp.maximum(reach[t], in_mem[t])
        reach.append(row)
    for s in range(SEGS):
        off = 4 * (s % 4)
        inside = ((lane >= off) & (lane < off + SEG)).astype(F32)
        colbias[s : s + 1, :] = jnp.where(jnp.maximum(inside, reach[s]) > 0.0, 0.0, MASKED)


def build_select(slot_rows, select):
    place = lax.broadcasted_iota(jnp.int32, select.shape, 1)
    select[...] = (slot_rows[...] == place).astype(F32).astype(BF)


def window(s):
    return pl.multiple_of(144 * s + 16 * (s // 4), 16), 4 * lax.rem(s, 4)


def lane_halves():
    lane = lax.broadcasted_iota(jnp.int32, (1, PAIR), 1)
    left = (lane < HD).astype(F32)
    return left.astype(BF), (1.0 - left).astype(BF), lane < HD


def valid_rows(off):
    row = lax.broadcasted_iota(jnp.int32, (WIN, 1), 0)
    return row, (row >= off) & (row < off + SEG)


def softmax_parts(qs, kk, bias):
    scores = mm_t(qs, kk) * HD ** (-0.5) + bias
    top = jnp.max(scores, axis=-1, keepdims=True)
    raised = jnp.exp(scores - top)
    return raised, 1.0 / jnp.sum(raised, axis=-1, keepdims=True)


def attend_pair(q, k, v, kmem, vmem, colbias, mixed, s, columns):
    left, right, is_left = lane_halves()
    at, off = window(s)
    rows = pl.ds(at, WIN)
    qw = q[rows, columns]
    qs = jnp.concatenate([qw * left, qw * right], axis=0)
    kk = jnp.concatenate([k[rows, columns], kmem[:, columns]], axis=0)
    vv = jnp.concatenate([v[rows, columns], vmem[:, columns]], axis=0)
    raised, scale = softmax_parts(qs, kk, colbias[pl.ds(s, 1), :])
    both = mm((raised * scale).astype(BF), vv)
    out = jnp.where(is_left, both[:WIN], both[WIN:])
    row, valid = valid_rows(off)
    old = mixed[rows, columns].astype(F32)
    mixed[rows, columns] = jnp.where(row >= off, out, old).astype(BF)


def attend_back_pair(q, k, v, kmem, vmem, colbias, dmix, dq, dk, dv, dkmem, dvmem, s, columns, acc):
    left, right, is_left = lane_halves()
    at, off = window(s)
    rows = pl.ds(at, WIN)
    qw = q[rows, columns]
    qs = jnp.concatenate([qw * left, qw * right], axis=0)
    kk = jnp.concatenate([k[rows, columns], kmem[:, columns]], axis=0)
    vv = jnp.concatenate([v[rows, columns], vmem[:, columns]], axis=0)
    dw = dmix[rows, columns]
    ds_in = jnp.concatenate([dw * left, dw * right], axis=0)
    raised, scale = softmax_parts(qs, kk, colbias[pl.ds(s, 1), :])
    row, valid = valid_rows(off)
    keep = jnp.where(valid, 1.0, 0.0)
    chances = raised * (scale * jnp.concatenate([keep, keep], axis=0))
    dp = mm_t(ds_in, vv)
    inner = jnp.sum(chances * dp, axis=-1, keepdims=True)
    ds = (chances * (dp - inner)).astype(BF)
    pb = chances.astype(BF)
    dqs = mm(ds, kk)
    new = jnp.where(is_left, dqs[:WIN], dqs[WIN:]) * HD ** (-0.5)
    old = dq[rows, columns].astype(F32)
    dq[rows, columns] = jnp.where(row >= off, new, old).astype(BF)
    dks = t_mm(ds, qs)
    dvs = t_mm(pb, ds_in)
    dk[rows, acc] = dk[rows, acc] + dks[:WIN]
    dv[rows, acc] = dv[rows, acc] + dvs[:WIN]
    dkmem[:, acc] = dkmem[:, acc] + dks[WIN:]
    dvmem[:, acc] = dvmem[:, acc] + dvs[WIN:]


def spread(select, part):
    high = part.astype(BF)
    low = (part - high.astype(F32)).astype(BF)
    return t_mm(select, high) + t_mm(select, low)


def forward_attention_kernel(parent, slot_rows, q, k, v, mixed, colbias, select, kmem, vmem):
    base = lax.axis_index("dp") * SEGS
    build_masks(parent, base, colbias)
    build_select(slot_rows, select)
    kmem[...] = mm(select[...], k[...]).astype(BF)
    vmem[...] = mm(select[...], v[...]).astype(BF)
    pairs = q.shape[1] // PAIR

    @pl.loop(0, SEGS)
    def _(s):
        for pair in range(pairs):
            attend_pair(q, k, v, kmem, vmem, colbias, mixed, s, pl.ds(pair * PAIR, PAIR))


def backward_attention_kernel(
    parent, slot_rows, q, k, v, dmix, dq, dk, dv, colbias, select, kmem, vmem, dka, dva, dkm, dvm
):
    base = lax.axis_index("dp") * SEGS
    build_masks(parent, base, colbias)
    build_select(slot_rows, select)
    kmem[...] = mm(select[...], k[...]).astype(BF)
    vmem[...] = mm(select[...], v[...]).astype(BF)
    pairs = q.shape[1] // PAIR
    for ref in (dka, dva, dkm, dvm):
        ref[...] = jnp.zeros(ref.shape, F32)

    @pl.loop(0, SEGS)
    def _(s):
        for pair in range(pairs):
            columns = pl.ds(pair * PAIR, PAIR)
            attend_back_pair(
                q, k, v, kmem, vmem, colbias, dmix, dq, dka, dva, dkm, dvm, s, columns, columns
            )

    for pair in range(pairs):
        columns = pl.ds(pair * PAIR, PAIR)
        dk[:, columns] = ((dka[:, columns] + spread(select[...], dkm[:, columns])) * HD ** (-0.5)).astype(BF)
        dv[:, columns] = (dva[:, columns] + spread(select[...], dvm[:, columns])).astype(BF)


def attention_call(kernel, outs, parent, slot_rows, arrays, scratch, name):
    rows, width = arrays[0].shape
    vm = pl.BlockSpec(memory_space=pltpu.VMEM)
    return pl.pallas_call(
        kernel,
        out_shape=[jax.ShapeDtypeStruct((rows, width), BF)] * outs,
        in_specs=[pl.BlockSpec(memory_space=pltpu.SMEM), vm] + [vm] * len(arrays),
        out_specs=[vm] * outs,
        scratch_shapes=[
            pltpu.VMEM((SEGS, WIN + MEMP), F32),
            pltpu.VMEM((MEMP, rows), BF),
            pltpu.VMEM((MEMP, width), BF),
            pltpu.VMEM((MEMP, width), BF),
        ]
        + scratch,
        compiler_params=pltpu.CompilerParams(vmem_limit_bytes=60 * 2**20),
        name=name,
    )(parent, slot_rows, *arrays)


def forward_attention(parent, slot_rows, q, k, v):
    return attention_call(forward_attention_kernel, 1, parent, slot_rows, (q, k, v), [], "attend")[0]


def backward_attention(parent, slot_rows, q, k, v, dmix):
    rows, width = q.shape
    scratch = [pltpu.VMEM((rows, width), F32)] * 2 + [pltpu.VMEM((MEMP, width), F32)] * 2
    return attention_call(
        backward_attention_kernel, 3, parent, slot_rows, (q, k, v, dmix), scratch, "attend_back"
    )


def norm_stats(values):
    centered = values - jnp.mean(values, axis=-1, keepdims=True)
    inverse = lax.rsqrt(jnp.mean(centered * centered, axis=-1, keepdims=True) + EPSILON)
    return centered * inverse, inverse


def norm_back(grad, normed, inverse, gain):
    scaled = grad * gain
    return inverse * (
        scaled
        - jnp.mean(scaled, axis=-1, keepdims=True)
        - normed * jnp.mean(scaled * normed, axis=-1, keepdims=True)
    )


def gelu_parts(inner):
    phi = 0.5 + 0.5 * lax.erf(inner * (0.5**0.5))
    density = jnp.exp(-0.5 * inner * inner) * (2.0 * jnp.pi) ** -0.5
    return (inner * phi).astype(BF), (phi + inner * density).astype(BF)


TILE = 128


def row_tiles(rows, body):
    full = rows // TILE

    @pl.loop(0, full)
    def _(i):
        body(pl.ds(pl.multiple_of(i * TILE, TILE), TILE))

    if rows % TILE:
        body(pl.ds(full * TILE, rows % TILE))


def forward_kernel(
    fast,
    parent,
    slot_rows,
    small,
    rows_in,
    tokens_h,
    grad_h,
    own_qkv,
    own_out,
    own_up,
    own_down,
    *rest,
):
    count = 0 if fast else 5
    given, outs, rest = rest[:count], rest[count : count + 16], rest[count + 16 :]
    (
        output_h,
        their_qkv_h,
        their_out_h,
        their_up_h,
        their_down_h,
        qkv_h,
        mixed_h,
        normed_h,
        inverse,
        hidden_h,
        acted_h,
        slope_own_h,
        slope_their_h,
        d_two_h,
        d_ffn_h,
        vec,
    ) = outs
    (
        tokens,
        their_qkv,
        their_out,
        their_up,
        their_down,
        small_their,
        qkv,
        mixed,
        normed,
        hidden,
        acc_own,
        acc_their,
        acted,
        slopes,
        colbias,
        select,
        kmem,
        vmem,
        sums,
        io_sem,
        slope_sem,
        *wires,
    ) = rest
    rows, depth = tokens.shape
    width = mixed.shape[2]
    theirs = (their_qkv, their_out, their_up, their_down)
    own = (own_qkv, own_out, own_up, own_down)

    def move(index, source, target):
        return pltpu.make_async_copy(source, target, io_sem.at[index])

    load_tokens = move(0, tokens_h, tokens)
    load_grad = move(1, grad_h, tokens)
    put_qkv = move(2, qkv, qkv_h)
    put_mixed = move(3, mixed.at[0], mixed_h)
    put_normed = move(4, normed, normed_h)
    put_hidden = move(5, hidden, hidden_h)
    put_acted = move(6, acted, acted_h)
    put_two = move(7, acc_own, d_two_h)
    put_ffn = move(8, hidden, d_ffn_h)
    put_output = move(9, tokens, output_h)
    put_theirs = [
        move(10 + i, ref, target)
        for i, (ref, target) in enumerate(zip(theirs, (their_qkv_h, their_out_h, their_up_h, their_down_h)))
    ]
    load_tokens.start()
    done = [0]
    if fast:
        pos = Place()
        small_sem, *wires = wires
        stage_own, send_own, tick = make_gather(pos, own, theirs, *wires)
        stage_own()
        gather_barrier(pos, 1 - lax.axis_index("tensor"))
        swap = swap_small(small, small_their, small_sem)
        swap.start()
        send_own()
    else:
        copies = [move(10 + i, a, b) for i, (a, b) in enumerate(zip(given, theirs + (small_their,)))]
        for copy in copies:
            copy.start()
        for copy in copies:
            copy.wait()

        def tick(step):
            pass

    def ticks(index, each, trips):
        for i in range(each):
            tick(done[0] + index * each + i)

    def until(count):
        if done[0] < count:

            @pl.loop(done[0], count)
            def _(step):
                tick(step)

            done[0] = count

    build_masks(parent, lax.axis_index("dp") * SEGS, colbias)
    build_select(slot_rows, select)
    load_tokens.wait()
    pairs = width // PAIR
    for half in range(2):
        weights = (own_qkv, their_qkv)[half]
        table = (small, small_their)[half]
        if half == 1:
            until(BOUNDS[0][1] + 3 * RELAY)
            if fast:
                swap.wait()

        @pl.loop(0, 3)
        def _(c, half=half, weights=weights, table=table):
            part = mm(tokens[...], weights[pl.ds(pl.multiple_of(c * depth, depth), depth), :])
            qkv[half, c] = (part + table[pl.ds(c, 1), :]).astype(BF)
            ticks(c, GATHER[2 * half], 3)

        done[0] += 3 * GATHER[2 * half]
        q, k, v = (qkv.at[half, i] for i in range(3))
        kmem[...] = mm(select[...], k[...]).astype(BF)
        vmem[...] = mm(select[...], v[...]).astype(BF)

        @pl.loop(0, SEGS)
        def _(s, half=half, q=q, k=k, v=v):
            for pair in range(pairs):
                attend_pair(q, k, v, kmem, vmem, colbias, mixed.at[half], s, pl.ds(pair * PAIR, PAIR))
                if pair < GATHER[2 * half + 1]:
                    tick(done[0] + s * GATHER[2 * half + 1] + pair)

        done[0] += SEGS * GATHER[2 * half + 1]
    put_qkv.start()
    put_mixed.start()
    until(BOUNDS[1][1] + 3 * RELAY)

    @pl.loop(0, 3)
    def _(n):
        columns = pl.ds(pl.multiple_of(n * CHUNK, CHUNK), CHUNK)
        acc_own[:, columns] = mm(mixed[0], own_out[:, columns]) + mm(mixed[1], their_out[:, columns])
        ticks(n, GATHER[4], 3)

    done[0] += 3 * GATHER[4]

    def norm_one(span):
        resid = tokens[span, :].astype(F32) + (acc_own[span, :] + rows_in[0:1, :])
        unit, scale = norm_stats(resid)
        normed[span, :] = unit
        inverse[span, :] = scale
        hidden[span, :] = (unit * rows_in[1:2, :] + rows_in[2:3, :]).astype(BF)

    row_tiles(rows, norm_one)
    load_grad.start()
    put_normed.start()
    put_hidden.start()

    for half in range(2):
        up, down = ((own_up, own_down), (their_up, their_down))[half]
        table = (small, small_their)[half]
        slope_h = (slope_own_h, slope_their_h)[half]
        acc = (acc_own, acc_their)[half]

        def put_slope(c, slope_h=slope_h):
            span = pl.ds(pl.multiple_of(c * CHUNK, CHUNK), CHUNK)
            return pltpu.make_async_copy(slopes.at[lax.rem(c, 2)], slope_h.at[:, span], slope_sem.at[lax.rem(c, 2)])

        if half == 1:
            until(BOUNDS[2][1] + 3 * RELAY)
            put_acted.wait()
            put_slope(4).wait()
            put_slope(5).wait()

        @pl.loop(0, 6)
        def _(c, half=half, up=up, table=table, put_slope=put_slope):
            span = pl.ds(pl.multiple_of(c * CHUNK, CHUNK), CHUNK)

            @pl.when(c >= 2)
            def _():
                put_slope(c - 2).wait()

            bias = table[pl.ds(3 + c, 1), 0:CHUNK]
            act, steep = gelu_parts(mm(hidden[...], up[:, span]) + bias)
            acted[:, span] = act
            slopes[lax.rem(c, 2)] = steep
            put_slope(c).start()
            ticks(c, GATHER[5 + 2 * half], 6)

        done[0] += 6 * GATHER[5 + 2 * half]
        if half == 0:
            put_acted.start()
        else:
            until(BOUNDS[3][1] + 3 * RELAY)
            if fast:
                for copy in put_theirs:
                    copy.start()

        @pl.loop(0, 3)
        def _(n, half=half, down=down, acc=acc):
            columns = pl.ds(pl.multiple_of(n * CHUNK, CHUNK), CHUNK)
            acc[:, columns] = mm(acted[...], down[:, columns])
            ticks(n, GATHER[6 + 2 * half], 3)

        done[0] += 3 * GATHER[6 + 2 * half]
    put_slope(4).wait()
    put_slope(5).wait()

    load_grad.wait()
    put_hidden.wait()
    sums[...] = jnp.zeros(sums.shape, F32)

    def norm_two(span):
        first = normed[span, :] * rows_in[1:2, :] + rows_in[2:3, :]
        resid = first + ((acc_own[span, :] + acc_their[span, :]) + rows_in[3:4, :])
        unit, scale = norm_stats(resid)
        grad = tokens[span, :].astype(F32)
        tokens[span, :] = (unit * rows_in[4:5, :] + rows_in[5:6, :]).astype(BF)
        back = norm_back(grad, unit, scale, rows_in[4:5, :])
        acc_own[span, :] = back
        low = back.astype(BF)
        hidden[span, :] = low
        for index, value in enumerate((low.astype(F32), grad * unit, grad)):
            sums[index] = sums[index] + value.reshape(-1, 8, depth).sum(axis=0)

    row_tiles(rows, norm_two)
    put_two.start()
    put_ffn.start()
    put_output.start()
    for index in range(3):
        total = jnp.sum(sums[index], axis=0, keepdims=True)
        for j in range(6):
            vec[6 * index + j : 6 * index + j + 1, :] = total[:, BC * j : BC * (j + 1)]
    for copy in (put_qkv, put_mixed, put_normed, put_two, put_ffn, put_output):
        copy.wait()
    if fast:
        for copy in put_theirs:
            copy.wait()


GATHER = (0, 1, 1, 1, 0, 1, 0, 0, 0)


def forward(fast, parent, slot_rows, small, rows_in, tokens, grad_out, own, given):
    rows, depth = tokens.shape
    width = own[0].shape[1]
    units = own[2].shape[1]
    vm = pl.BlockSpec(memory_space=pltpu.VMEM)
    hbm = pl.BlockSpec(memory_space=pl.ANY)
    sd = jax.ShapeDtypeStruct
    out_shape = [
        sd((rows, depth), BF),
        *[sd(w.shape, BF) for w in own],
        sd((2, 3, rows, width), BF),
        sd((rows, width), BF),
        sd((rows, depth), F32),
        sd((rows, 1), F32),
        sd((rows, depth), BF),
        sd((rows, units), BF),
        sd((rows, units), BF),
        sd((rows, units), BF),
        sd((rows, depth), F32),
        sd((rows, depth), BF),
        sd((18, BC), F32),
    ]
    return pl.pallas_call(
        functools.partial(forward_kernel, fast),
        out_shape=out_shape,
        in_specs=[pl.BlockSpec(memory_space=pltpu.SMEM), vm, vm, vm, hbm, hbm] + [vm] * 4 + [hbm] * len(given),
        out_specs=[hbm] * 8 + [vm] + [hbm] * 6 + [vm],
        scratch_shapes=[
            pltpu.VMEM((rows, depth), BF),
            *[pltpu.VMEM(w.shape, BF) for w in own],
            pltpu.VMEM(small.shape, F32),
            pltpu.VMEM((2, 3, rows, width), BF),
            pltpu.VMEM((2, rows, width), BF),
            pltpu.VMEM((rows, depth), F32),
            pltpu.VMEM((rows, depth), BF),
            pltpu.VMEM((rows, depth), F32),
            pltpu.VMEM((rows, depth), F32),
            pltpu.VMEM((rows, units), BF),
            pltpu.VMEM((2, rows, CHUNK), BF),
            pltpu.VMEM((SEGS, WIN + MEMP), F32),
            pltpu.VMEM((MEMP, rows), BF),
            pltpu.VMEM((MEMP, width), BF),
            pltpu.VMEM((MEMP, width), BF),
            pltpu.VMEM((3, 8, depth), F32),
            pltpu.SemaphoreType.DMA((15,)),
            pltpu.SemaphoreType.DMA((2,)),
        ]
        + ([pltpu.SemaphoreType.DMA((2,))] + gather_scratch() if fast else []),
        compiler_params=pltpu.CompilerParams(
            collective_id=0 if fast else None, has_side_effects=fast, vmem_limit_bytes=67043328
        ),
        name="forward",
    )(parent, slot_rows, small, rows_in, tokens, grad_out, *own, *given)


DOWN, UP, OUT, QKV, VEC = 0, 24, 48, 54, 72
COUNT = 73
CHUNK = 256
VEC_ROWS = 54


def backward_kernel(
    fast,
    parent,
    slot_rows,
    inverse,
    gain,
    vec_in,
    tokens_h,
    hidden_h,
    d_ffn_h,
    d_two_h,
    normed_h,
    acted_h,
    slope_own_h,
    slope_their_h,
    qkv_h,
    mixed_h,
    w_up_own,
    w_up_their,
    w_down_own,
    w_down_their,
    w_out_own,
    w_out_their,
    w_qkv_own,
    w_qkv_their,
    g_qkv,
    g_out,
    g_up,
    g_down,
    g_vec,
    g_tokens,
    grads,
    d_low,
    hidden,
    d_res,
    normed,
    acc_own,
    acc_their,
    a_buf,
    slope_buf,
    up_buf,
    down_buf,
    d_inner,
    sums,
    tokens,
    mixed,
    w_out,
    w_qkv,
    qkv,
    d_qkv,
    d_mixed,
    colbias,
    select,
    kmem,
    vmem,
    dkm,
    dvm,
    load_sem,
    chunk_sem,
    put_sem,
    *wires,
):
    rows, depth = tokens.shape
    width = mixed.shape[1]

    def fetch(index, source, target):
        return pltpu.make_async_copy(source, target, load_sem.at[index])

    load_d = fetch(0, d_ffn_h, d_low)
    load_hidden = fetch(1, hidden_h, hidden)
    load_two = fetch(2, d_two_h, d_res)
    load_normed = fetch(3, normed_h, normed)
    load_mixed = fetch(4, mixed_h, mixed)
    load_out = [fetch(5 + i, w, w_out.at[i]) for i, w in enumerate((w_out_own, w_out_their))]
    load_w = [fetch(7 + i, w, w_qkv.at[i]) for i, w in enumerate((w_qkv_own, w_qkv_their))]
    load_tokens = fetch(9, tokens_h, tokens)
    load_qkv = [fetch(10 + half, qkv_h.at[half], qkv) for half in range(2)]
    put_tokens = fetch(12, d_low, g_tokens)

    def load_acted(c):
        return pltpu.make_async_copy(acted_h.at[:, pl.ds(pl.multiple_of(c * BR, BR), BR)], a_buf.at[lax.rem(c, 2)], chunk_sem.at[0, lax.rem(c, 2)])

    def load_chunk(half, c):
        slot = lax.rem(c, 2)
        span = pl.ds(pl.multiple_of(c * CHUNK, CHUNK), CHUNK)
        slope_h, up_h, down_h = ((slope_own_h, w_up_own, w_down_own), (slope_their_h, w_up_their, w_down_their))[half]
        return (
            pltpu.make_async_copy(slope_h.at[:, span], slope_buf.at[slot], chunk_sem.at[1, slot]),
            pltpu.make_async_copy(up_h.at[:, span], up_buf.at[slot], chunk_sem.at[2, slot]),
            pltpu.make_async_copy(down_h.at[span, :], down_buf.at[slot], chunk_sem.at[3, slot]),
        )

    def start(copies):
        for copy in copies:
            copy.start()

    def wait(copies):
        for copy in copies:
            copy.wait()

    load_d.start()
    load_acted(0).start()
    start(load_chunk(0, 0))
    load_hidden.start()
    load_two.start()
    load_normed.start()
    load_mixed.start()
    start(load_out)
    start(load_w)
    load_tokens.start()
    load_qkv[0].start()

    def put(block, target):
        return pltpu.make_async_copy(grads.at[block], target, put_sem.at[lax.rem(block, 8)])

    def wait_put(block):
        put(block, g_vec).wait()

    def finish(block):
        @pl.when(block >= 8)
        def _():
            wait_put(block - 8)

        def at(row, column):
            return pl.ds(pl.multiple_of(row, BR), BR), pl.ds(pl.multiple_of(column, BC), BC)

        @pl.when(block < UP)
        def _():
            put(block, g_down.at[at(BR * (block // 6), BC * lax.rem(block, 6))]).start()

        @pl.when((block >= UP) & (block < OUT))
        def _():
            i = block - UP
            put(block, g_up.at[at(BR * lax.rem(i // 2, 2), CHUNK * (i // 4) + BC * lax.rem(i, 2))]).start()

        @pl.when((block >= OUT) & (block < QKV))
        def _():
            put(block, g_out.at[at(0, BC * (block - OUT))]).start()

        @pl.when((block >= QKV) & (block < VEC))
        def _():
            i = block - QKV
            put(block, g_qkv.at[at(BR * (i // 3), BC * lax.rem(i, 3))]).start()

        @pl.when(block == VEC)
        def _():
            put(block, g_vec).start()

    if fast:
        pos = Place()
        tick = make_tick(pos, grads, *wires, COUNT, finish)
        last = COUNT + 7 * SPREAD
    else:

        def tick(step):
            finish(step)

        last = COUNT
    done = [0]

    def ticks(index, each, trips):
        for i in range(each):
            tick(done[0] + index * each + i)
        return trips * each

    grads[VEC] = jnp.zeros((BR, BC), F32)
    grads[VEC, 36:54] = vec_in[...]
    acc_own[...] = jnp.zeros(acc_own.shape, F32)
    acc_their[...] = jnp.zeros(acc_their.shape, F32)
    sums[...] = jnp.zeros(sums.shape, F32)
    if fast:
        sum_barrier(pos)

    load_d.wait()

    @pl.loop(0, 4)
    def _(c):
        load_acted(c).wait()

        @pl.when(c < 3)
        def _():
            load_acted(c + 1).start()

        for part in range(2):
            piece = t_mm(a_buf[lax.rem(c, 2)], d_low[:, part * width : (part + 1) * width])
            for j in range(3):
                grads[DOWN + 6 * c + 3 * part + j] = piece[:, BC * j : BC * (j + 1)]
        ticks(c, TICKS[0], 4)

    done[0] += 4 * TICKS[0]

    load_hidden.wait()
    for half in range(2):
        acc = (acc_own, acc_their)[half]

        @pl.loop(0, 6)
        def _(c, half=half, acc=acc):
            slot = lax.rem(c, 2)
            wait(load_chunk(half, c))

            @pl.when(c < 5)
            def _():
                start(load_chunk(half, c + 1))

            if half == 0:

                @pl.when(c == 5)
                def _():
                    start(load_chunk(1, 0))

            d_inner[...] = (mm_t(d_low[...], down_buf[slot]) * slope_buf[slot].astype(F32)).astype(BF)
            if half == 0:
                piece = t_mm(hidden[...], d_inner[...])
                for r in range(2):
                    for j in range(2):
                        grads[UP + 4 * c + 2 * r + j] = piece[BR * r : BR * (r + 1), BC * j : BC * (j + 1)]
                total = jnp.sum(d_inner[...].astype(F32), axis=0, keepdims=True)
                for j in range(2):
                    grads[VEC, pl.ds(6 + 2 * c + j, 1), :] = total[:, BC * j : BC * (j + 1)]
            ticks(c, TICKS[1 + half], 6)
            for part in range(3):
                columns = slice(CHUNK * part, CHUNK * (part + 1))
                acc[:, columns] = acc[:, columns] + mm_t(d_inner[...], up_buf[slot, columns, :])

        done[0] += 6 * TICKS[1 + half]

    load_two.wait()
    load_normed.wait()
    tile = 32
    trips = rows // tile

    @pl.loop(0, trips)
    def _(i):
        span = pl.ds(pl.multiple_of(i * tile, tile), tile)
        total = d_res[span, :] + (acc_own[span, :] + acc_their[span, :])
        unit = normed[span, :]
        one = norm_back(total, unit, inverse[span, :], gain[...])
        d_res[span, :] = one
        low = one.astype(BF)
        d_low[span, :] = low
        for index, value in enumerate((low.astype(F32), total * unit, total)):
            sums[index] = sums[index] + value.reshape(tile // 8, 8, depth).sum(axis=0)

        @pl.when(lax.rem(i, TICK_TILES) == 0)
        def _():
            tick(done[0] + i // TICK_TILES)

    done[0] += -(-trips // TICK_TILES)
    for index in range(3):
        total = jnp.sum(sums[index], axis=0, keepdims=True)
        for j in range(6):
            grads[VEC, 18 + 6 * index + j : 19 + 6 * index + j, :] = total[:, BC * j : BC * (j + 1)]

    load_mixed.wait()
    wait(load_out)

    @pl.loop(0, 2)
    def _(half):
        d_mixed[half] = mm_t(d_low[...], w_out[half]).astype(BF)
        piece = t_mm(mixed[...], d_low[:, pl.ds(pl.multiple_of(half * width, BC), width)])
        for j in range(3):
            grads[OUT + 3 * half + j] = piece[:, BC * j : BC * (j + 1)]
        ticks(half, TICKS[3], 2)

    done[0] += 2 * TICKS[3]

    build_masks(parent, lax.axis_index("dp") * SEGS, colbias)
    build_select(slot_rows, select)
    wait(load_w)
    load_tokens.wait()
    pairs = width // PAIR
    dka, dva = acc_their.at[:, pl.ds(0, width)], acc_their.at[:, pl.ds(width, width)]
    for half in range(2):
        load_qkv[half].wait()
        q, k, v = (qkv.at[i] for i in range(3))
        kmem[...] = mm(select[...], k[...]).astype(BF)
        vmem[...] = mm(select[...], v[...]).astype(BF)
        acc_their[...] = jnp.zeros(acc_their.shape, F32)
        dkm[...] = jnp.zeros(dkm.shape, F32)
        dvm[...] = jnp.zeros(dvm.shape, F32)

        @pl.loop(0, SEGS)
        def _(s, half=half):
            for pair in range(pairs):
                columns = pl.ds(pair * PAIR, PAIR)
                attend_back_pair(
                    q, k, v, kmem, vmem, colbias, d_mixed.at[half], d_qkv.at[0], dka, dva, dkm, dvm, s, columns, columns
                )
                if pair < TICKS[4 + half]:
                    tick(done[0] + s * TICKS[4 + half] + pair)

        done[0] += SEGS * TICKS[4 + half]
        if half == 0:
            load_qkv[1].start()
        for pair in range(pairs):
            columns = pl.ds(pair * PAIR, PAIR)
            d_qkv[1, :, columns] = ((dka[:, columns] + spread(select[...], dkm[:, columns])) * HD ** (-0.5)).astype(BF)
            d_qkv[2, :, columns] = (dva[:, columns] + spread(select[...], dvm[:, columns])).astype(BF)
        if half == 0:

            @pl.loop(0, 3)
            def _(c):
                piece = t_mm(tokens[...], d_qkv[c])
                for r in range(2):
                    for j in range(3):
                        grads[QKV + 6 * c + 3 * r + j] = piece[BR * r : BR * (r + 1), BC * j : BC * (j + 1)]
                columns = pl.ds(pl.multiple_of(c * CHUNK, CHUNK), CHUNK)
                part = mm_t(d_qkv[0], w_qkv[half, pl.ds(pl.multiple_of(c * CHUNK, CHUNK), CHUNK), :])
                for i in (1, 2):
                    part = part + mm_t(d_qkv[i], w_qkv[half, pl.ds(pl.multiple_of(i * depth + c * CHUNK, CHUNK), CHUNK), :])
                acc_own[:, columns] = part
                ticks(c, TICKS[6], 3)

            done[0] += 3 * TICKS[6]
            for index, row in ((0, 0), (2, 3)):
                total = jnp.sum(d_qkv[index].astype(F32), axis=0, keepdims=True)
                for j in range(3):
                    grads[VEC, row + j : row + j + 1, :] = total[:, BC * j : BC * (j + 1)]
        else:

            @pl.loop(0, 3)
            def _(c):
                columns = pl.ds(pl.multiple_of(c * CHUNK, CHUNK), CHUNK)
                part = mm_t(d_qkv[0], w_qkv[half, pl.ds(pl.multiple_of(c * CHUNK, CHUNK), CHUNK), :])
                for i in (1, 2):
                    part = part + mm_t(d_qkv[i], w_qkv[half, pl.ds(pl.multiple_of(i * depth + c * CHUNK, CHUNK), CHUNK), :])
                d_low[:, columns] = ((acc_own[:, columns] + part) + d_res[:, columns]).astype(BF)
                ticks(c, TICKS[7], 3)

            done[0] += 3 * TICKS[7]
            put_tokens.start()
    assert done[0] <= COUNT

    @pl.loop(done[0], last)
    def _(step):
        tick(step)

    for block in range(COUNT - 8, COUNT):
        wait_put(block)
    put_tokens.wait()


TICKS = (1, 2, 1, 1, 2, 2, 2, 1)
TICK_TILES = 8


def backward(fast, parent, slot_rows, inverse, gain, vec_in, arrays):
    tokens, acted, mixed = arrays[0], arrays[5], arrays[9]
    rows, depth = tokens.shape
    units = acted.shape[1]
    width = mixed.shape[1]
    vm = pl.BlockSpec(memory_space=pltpu.VMEM)
    hbm = pl.BlockSpec(memory_space=pl.ANY)
    sd = jax.ShapeDtypeStruct
    return pl.pallas_call(
        functools.partial(backward_kernel, fast),
        out_shape=[
            sd((3 * depth, width), F32),
            sd((width, depth), F32),
            sd((depth, units), F32),
            sd((units, depth), F32),
            sd((BR, BC), F32),
            sd((rows, depth), BF),
        ],
        in_specs=[pl.BlockSpec(memory_space=pltpu.SMEM), vm, vm, vm, vm] + [hbm] * len(arrays),
        out_specs=[hbm] * 6,
        scratch_shapes=[
            pltpu.VMEM((COUNT, BR, BC), F32),
            pltpu.VMEM((rows, depth), BF),
            pltpu.VMEM((rows, depth), BF),
            pltpu.VMEM((rows, depth), F32),
            pltpu.VMEM((rows, depth), F32),
            pltpu.VMEM((rows, depth), F32),
            pltpu.VMEM((rows, depth), F32),
            pltpu.VMEM((2, rows, BR), BF),
            pltpu.VMEM((2, rows, CHUNK), BF),
            pltpu.VMEM((2, depth, CHUNK), BF),
            pltpu.VMEM((2, CHUNK, depth), BF),
            pltpu.VMEM((rows, CHUNK), BF),
            pltpu.VMEM((3, 8, depth), F32),
            pltpu.VMEM((rows, depth), BF),
            pltpu.VMEM((rows, width), BF),
            pltpu.VMEM((2, width, depth), BF),
            pltpu.VMEM((2, 3 * depth, width), BF),
            pltpu.VMEM((3, rows, width), BF),
            pltpu.VMEM((3, rows, width), BF),
            pltpu.VMEM((2, rows, width), BF),
            pltpu.VMEM((SEGS, WIN + MEMP), F32),
            pltpu.VMEM((MEMP, rows), BF),
            pltpu.VMEM((MEMP, width), BF),
            pltpu.VMEM((MEMP, width), BF),
            pltpu.VMEM((MEMP, width), F32),
            pltpu.VMEM((MEMP, width), F32),
            pltpu.SemaphoreType.DMA((13,)),
            pltpu.SemaphoreType.DMA((4, 2)),
            pltpu.SemaphoreType.DMA((8,)),
        ]
        + (sum_scratch() if fast else []),
        compiler_params=pltpu.CompilerParams(
            collective_id=1 if fast else None, has_side_effects=fast, vmem_limit_bytes=67043328
        ),
        name="backward",
    )(parent, slot_rows, inverse, gain, vec_in, *arrays)


def halves_swap(own, small):
    unit = (lax.axis_index("dp") >= 0).astype(F32)

    def other(array):
        arrived = lax.ppermute(array.astype(F32), "tensor", [(0, 1), (1, 0)])
        return (arrived * unit).astype(array.dtype)

    return tuple(other(array) for array in own) + (other(small),)


def shards(
    fast,
    tokens,
    w_qkv,
    bias_qv,
    w_out,
    bias_out,
    gain_one,
    shift_one,
    w_up,
    bias_up,
    w_down,
    bias_down,
    gain_two,
    shift_two,
    grad_out,
    parent,
    mem_slots,
):
    depth, width = w_qkv.shape[1:]
    hidden_units = w_up.shape[1]
    own = (w_qkv.reshape(3 * depth, width), w_out, w_up, w_down)
    table = jnp.pad(bias_up.reshape(-1, CHUNK), ((0, 0), (0, width - CHUNK)))
    small = jnp.concatenate([bias_qv[:1], jnp.zeros((1, width), F32), bias_qv[1:], table])
    small = jnp.pad(small, ((0, 16 - small.shape[0]), (0, 0)))
    given = () if fast else halves_swap(own, small)
    slot_rows = mem_slots + jnp.arange(SEGS, dtype=jnp.int32)[:, None] * SEG
    slot_rows = jnp.pad(slot_rows.reshape(-1, 1), ((0, MEMP - MEMW * SEGS), (0, 0)), constant_values=-1)
    rows_in = jnp.stack(
        [bias_out, gain_one, shift_one, bias_down, gain_two, shift_two, jnp.zeros_like(gain_one), jnp.zeros_like(gain_one)]
    )
    (
        output,
        *theirs,
        qkv,
        mixed,
        normed,
        inverse,
        hidden_low,
        acted,
        slope_own,
        slope_their,
        d_two,
        d_ffn,
        vec,
    ) = forward(fast, parent, slot_rows, small, rows_in, tokens, grad_out, own, given)
    if not fast:
        theirs = given[:4]
    arrays = (tokens, hidden_low, d_ffn, d_two, normed, acted, slope_own, slope_their, qkv, mixed)
    weights = tuple(w[i] for i in (2, 3, 1, 0) for w in (own, theirs))
    g_w_qkv, g_w_out, g_w_up, g_w_down, flat, grad_tokens = backward(
        fast, parent, slot_rows, inverse, gain_one.reshape(1, -1), vec, arrays + weights
    )
    if not fast:
        g_w_qkv, g_w_out, g_w_up, g_w_down, flat = lax.psum((g_w_qkv, g_w_out, g_w_up, g_w_down, flat), "dp")
    g_w_qkv = g_w_qkv.reshape(w_qkv.shape)
    sums, row = [], 0
    for size in (width, width, hidden_units) + (depth,) * 6:
        sums.append(flat[row : row + size // BC].reshape(-1))
        row += size // BC
    g_bias_q, g_bias_v, g_bias_up, g_bias_out, g_gain_one, g_shift_one, g_bias_down, g_gain_two, g_shift_two = sums
    return (
        output,
        grad_tokens,
        g_w_qkv,
        jnp.stack([g_bias_q, g_bias_v]),
        g_w_out,
        g_bias_out,
        g_gain_one,
        g_shift_one,
        g_w_up,
        g_bias_up,
        g_w_down,
        g_bias_down,
        g_gain_two,
        g_shift_two,
    )


def solution(mesh):
    fast = mesh.shape["dp"] == 16 and mesh.shape["tensor"] == 2
    rows, whole = P("dp", None), P()
    return jax.shard_map(
        functools.partial(shards, fast),
        mesh=mesh,
        in_specs=(
            rows,
            P(None, None, "tensor"),
            P(None, "tensor"),
            P("tensor", None),
            whole,
            whole,
            whole,
            P(None, "tensor"),
            P("tensor"),
            P("tensor", None),
            whole,
            whole,
            whole,
            rows,
            P("dp"),
            rows,
        ),
        out_specs=(
            rows,
            rows,
            P(None, None, "tensor"),
            P(None, "tensor"),
            P("tensor", None),
            whole,
            whole,
            whole,
            P(None, "tensor"),
            P("tensor"),
            P("tensor", None),
            whole,
            whole,
            whole,
        ),
        check_vma=False,
    )
```

```python
import functools


import jax
import jax.numpy as jnp
from jax import lax
from jax.experimental import pallas as pl
from jax.experimental.pallas import tpu as pltpu
from jax.sharding import PartitionSpec as P


MESH = pl.DeviceIdType.MESH
BR, BC = 384, 128
SPREAD = 3
SLOTS = 16


class Place:
    def __init__(self):
        me = lax.axis_index("dp")
        self.core = lax.rem(me, 2)
        self.x = lax.rem(me // 2, 2)
        self.z = me // 4
        self.sib = me + 1 - 2 * self.core
        self.xn = me + 2 - 4 * self.x
        self.zp = me + 4 - 8 * lax.rem(self.z, 2)
        self.zm = me + 4 * (3 - 2 * self.z)
        self.end = (self.z == 0) | (self.z == 3)
        self.mid = (self.z == 1) | (self.z == 2)


def sum_barrier(pos):
    barrier = pltpu.get_barrier_semaphore()

    def greet(dev):
        pl.semaphore_signal(barrier, inc=1, device_id={"dp": dev}, device_id_type=MESH)

    greet(pos.sib)
    greet(pos.xn)
    greet(pos.zp)

    @pl.when(pos.mid)
    def _():
        greet(pos.zm)

    pl.semaphore_wait(barrier, jnp.where(pos.mid, 4, 3))


def make_tick(pos, grads, from_core, from_one, from_two, from_three, sent, got, credit, count, finish):
    half = BR // 2
    quarter = BR // 4

    def copy(stage, block, source, target, device):
        slot = lax.rem(block, SLOTS)
        return pltpu.make_async_remote_copy(
            src_ref=source,
            dst_ref=target,
            send_sem=sent.at[stage, slot],
            recv_sem=got.at[stage, slot],
            device_id={"dp": device},
            device_id_type=MESH,
        )

    def rows(block, start, size):
        return grads.at[block, pl.ds(pl.multiple_of(start, quarter), size)]

    def add(block, start, size, landed):
        where = pl.ds(pl.multiple_of(start, quarter), size)
        grads[block, where] = grads[block, where] + landed[...]

    def free(index, device):
        pl.semaphore_signal(credit.at[index], inc=1, device_id={"dp": device}, device_id_type=MESH)

    def claim(index):
        pl.semaphore_wait(credit.at[index], 1)

    x_first = pos.core == 0
    z_first = pos.core == 1
    mine = pos.core * half
    xrow = pos.x * quarter
    xrow_other = (1 - pos.x) * quarter
    far = lax.rem(pos.z, 2) == 0
    keep = half + jnp.where(far, quarter, 0)
    give = half + jnp.where(far, 0, quarter)

    def core_out(block):
        return copy(0, block, rows(block, (1 - pos.core) * half, half), from_core.at[lax.rem(block, SLOTS)], pos.sib)

    def x_one(block):
        return copy(1, block, rows(block, xrow_other, quarter), from_one.at[lax.rem(block, SLOTS), pl.ds(0, quarter)], pos.xn)

    def z_one(block):
        return copy(1, block, rows(block, half, half), from_one.at[lax.rem(block, SLOTS)], pos.zp)

    def x_two(block):
        return copy(2, block, rows(block, xrow, quarter), from_two.at[lax.rem(block, SLOTS)], pos.zp)

    def z_two(block):
        return copy(2, block, rows(block, give, quarter), from_two.at[lax.rem(block, SLOTS)], pos.zm)

    def x_three(block):
        return copy(3, block, rows(block, xrow, quarter), from_three.at[lax.rem(block, SLOTS)], pos.zm)

    def z_three(block):
        return copy(3, block, rows(block, keep, quarter), from_three.at[lax.rem(block, SLOTS)], pos.xn)

    def x_four(block):
        return copy(4, block, rows(block, xrow, quarter), rows(block, xrow, quarter), pos.zp)

    def z_four(block):
        return copy(4, block, rows(block, keep, quarter), rows(block, keep, quarter), pos.zm)

    def z_four_in(block):
        return copy(4, block, rows(block, give, quarter), rows(block, give, quarter), pos.zm)

    def x_five(block):
        return copy(5, block, rows(block, xrow, quarter), rows(block, xrow, quarter), pos.xn)

    def x_five_in(block):
        return copy(5, block, rows(block, xrow_other, quarter), rows(block, xrow_other, quarter), pos.xn)

    def z_five(block):
        return copy(5, block, rows(block, half, half), rows(block, half, half), pos.zp)

    def core_six(block):
        return copy(6, block, rows(block, mine, half), rows(block, mine, half), pos.sib)

    def core_six_in(block):
        return copy(6, block, rows(block, (1 - pos.core) * half, half), rows(block, (1 - pos.core) * half, half), pos.sib)

    def start_core(block):
        core_out(block).start()

    def take_core(block):
        core_out(block).wait()
        free(2, pos.sib)
        add(block, mine, half, from_core.at[lax.rem(block, SLOTS)])

    def take_x(block):
        x_one(block).wait()
        free(1, pos.xn)
        add(block, xrow, quarter, from_one.at[lax.rem(block, SLOTS), pl.ds(0, quarter)])

    def send_x(block):
        take_core(block)
        x_one(block).start()

    def send_z(block):
        take_core(block)
        z_one(block).start()

    def x_end_two(block):
        take_x(block)
        x_two(block).start()

    def x_end_three(block):
        x_two(block).wait_send()
        free(0, pos.zp)

    def x_mid_three(block):
        x_two(block).wait_recv()
        add(block, xrow, quarter, from_two.at[lax.rem(block, SLOTS)])
        x_three(block).start()

    def x_mid_four(block):
        x_three(block).wait()
        add(block, xrow, quarter, from_three.at[lax.rem(block, SLOTS)])
        claim(0)
        x_four(block).start()

    def x_end_five(block):
        x_four(block).wait_recv()
        claim(1)
        x_five(block).start()

    def x_mid_five(block):
        x_four(block).wait_send()
        claim(1)
        x_five(block).start()

    def x_six(block):
        x_five(block).wait_send()
        x_five_in(block).wait_recv()
        claim(2)
        core_six(block).start()

    def z_end_two(block):
        z_one(block).wait_send()
        free(1, pos.zp)

    def z_end_six(block):
        z_five(block).wait_recv()
        claim(2)
        core_six(block).start()

    def z_mid_two(block):
        z_one(block).wait_recv()
        add(block, half, half, from_one.at[lax.rem(block, SLOTS)])
        z_two(block).start()

    def z_mid_three(block):
        z_two(block).wait()
        free(0, pos.zm)
        add(block, keep, quarter, from_two.at[lax.rem(block, SLOTS)])
        z_three(block).start()

    def z_mid_four(block):
        z_three(block).wait()
        add(block, keep, quarter, from_three.at[lax.rem(block, SLOTS)])
        claim(0)
        z_four(block).start()

    def z_mid_five(block):
        z_four(block).wait_send()
        z_four_in(block).wait_recv()
        claim(1)
        z_five(block).start()

    def z_mid_six(block):
        z_five(block).wait_send()
        claim(2)
        core_six(block).start()

    def last(block):
        core_six(block).wait_send()
        core_six_in(block).wait_recv()

    roles = (
        (x_first & pos.end, (start_core, send_x, x_end_two, x_end_three, None, x_end_five, x_six, last)),
        (x_first & pos.mid, (start_core, send_x, take_x, x_mid_three, x_mid_four, x_mid_five, x_six, last)),
        (z_first & pos.end, (start_core, send_z, z_end_two, None, None, None, z_end_six, last)),
        (z_first & pos.mid, (start_core, take_core, z_mid_two, z_mid_three, z_mid_four, z_mid_five, z_mid_six, last)),
    )
    depth = len(roles[0][1])

    def tick(step):
        for here, stages in roles:

            @pl.when(here)
            def _(stages=stages):
                for index in reversed(range(depth)):
                    block = step - SPREAD * index
                    if stages[index] is not None:

                        @pl.when((block >= 0) & (block < count))
                        def _(index=index, block=block, stages=stages):
                            stages[index](block)

        over = step - SPREAD * (depth - 1)

        @pl.when((over >= 0) & (over < count))
        def _():
            finish(over)

    return tick


def sum_scratch():
    return [
        pltpu.VMEM((SLOTS, BR // 2, BC), jnp.float32),
        pltpu.VMEM((SLOTS, BR // 2, BC), jnp.float32),
        pltpu.VMEM((SLOTS, BR // 4, BC), jnp.float32),
        pltpu.VMEM((SLOTS, BR // 4, BC), jnp.float32),
        pltpu.SemaphoreType.DMA((7, SLOTS)),
        pltpu.SemaphoreType.DMA((7, SLOTS)),
        pltpu.SemaphoreType.REGULAR((3,)),
    ]


CR, CC = 64, 384
CHUNKS = 24
RELAY = 2
BF = jnp.bfloat16


def gather_barrier(pos, other):
    barrier = pltpu.get_barrier_semaphore()
    for where in ({"tensor": other}, {"dp": pos.xn}, {"dp": pos.zp}, {"dp": pos.sib}):
        pl.semaphore_signal(barrier, inc=1, device_id=where, device_id_type=MESH)
    pl.semaphore_wait(barrier, 4)


def chunk_parts(piece, chunk, kind):
    if kind == 0:
        return [(piece * 384 + chunk * 64, 64, 0, 0)]
    if kind == 1:
        return [(piece * 64 + (chunk - 6) * 32, 32, 384 * q, 32 * q) for q in range(2)]
    if kind == 2:
        return [(piece * 128 + (chunk - 8) * 16, 16, 384 * q, 16 * q) for q in range(4)]
    return [(piece * 256 + (chunk - 16) * 32, 32, 384 * q, 32 * q) for q in range(2)]


BOUNDS = ((0, 6), (6, 8), (8, 16), (16, 24))
UNIT = (64, 32, 16, 32)


def make_gather(pos, own, theirs, staged, landed, sent, got):
    other = 1 - lax.axis_index("tensor")
    odd = lax.rem(pos.z, 2)
    ky = jnp.where(pos.x == 0, odd, 2)
    kx = jnp.where(pos.x == 0, 2, odd)
    kz = 1 - odd
    piece_y = 2 * ky + pos.core
    piece_x = 2 * kx + pos.core
    piece_z = 2 * kz + pos.core
    sib_y = 2 * ky + 1 - pos.core
    sib_x = 2 * kx + 1 - pos.core
    sib_z = 2 * kz + 1 - pos.core

    def copy(lane, chunk, source, piece, where):
        return pltpu.make_async_remote_copy(
            src_ref=source,
            dst_ref=landed.at[piece, chunk],
            send_sem=sent.at[lane, chunk],
            recv_sem=got.at[lane, chunk],
            device_id=where,
            device_id_type=MESH,
        )

    def over_y(chunk):
        return copy(0, chunk, staged.at[chunk], piece_y, {"tensor": other})

    def over_x(chunk, piece):
        return copy(1, chunk, landed.at[piece, chunk], piece, {"dp": pos.xn})

    def over_z(chunk, piece):
        return copy(2, chunk, landed.at[piece, chunk], piece, {"dp": pos.zp})

    def over_core(lane, chunk, piece):
        return copy(lane, chunk, landed.at[piece, chunk], piece, {"dp": pos.sib})

    def stage_own():
        for kind in range(4):
            lo, hi = BOUNDS[kind]

            @pl.loop(lo, hi)
            def _(chunk, kind=kind):
                for row, rows, column, at in chunk_parts(piece_y, chunk, kind):
                    staged[chunk, pl.ds(at, rows)] = own[kind][
                        pl.ds(pl.multiple_of(row, UNIT[kind]), rows), pl.ds(column, CC)
                    ].astype(jnp.float32)

    def send_own():
        @pl.loop(0, CHUNKS)
        def _(chunk):
            over_y(chunk).start()

    def unpack(chunk):
        for kind in range(4):
            lo, hi = BOUNDS[kind]

            @pl.when((chunk >= lo) & (chunk < hi))
            def _(kind=kind):
                @pl.loop(0, 6)
                def _(piece):
                    for row, rows, column, at in chunk_parts(piece, chunk, kind):
                        theirs[kind][pl.ds(pl.multiple_of(row, UNIT[kind]), rows), pl.ds(column, CC)] = landed[
                            piece, chunk, pl.ds(at, rows)
                        ].astype(BF)

    def guarded(chunk, body):
        @pl.when((chunk >= 0) & (chunk < CHUNKS))
        def _():
            body(chunk)

    def first(chunk):
        over_y(chunk).wait_recv()
        over_x(chunk, piece_y).start()

        @pl.when(pos.x == 0)
        def _():
            over_z(chunk, piece_y).start()

        over_core(3, chunk, piece_y).start()

    def second(chunk):
        over_x(chunk, piece_x).wait_recv()

        @pl.when(pos.x == 1)
        def _():
            over_z(chunk, piece_x).start()

        over_core(4, chunk, piece_x).start()

    def third(chunk):
        over_z(chunk, piece_z).wait_recv()
        over_core(5, chunk, piece_z).start()

    def fourth(chunk):
        over_core(3, chunk, sib_y).wait_recv()
        over_core(4, chunk, sib_x).wait_recv()
        over_core(5, chunk, sib_z).wait_recv()
        over_y(chunk).wait_send()
        over_x(chunk, piece_y).wait_send()
        over_z(chunk, piece_y).wait_send()
        over_core(3, chunk, piece_y).wait_send()
        over_core(4, chunk, piece_x).wait_send()
        over_core(5, chunk, piece_z).wait_send()
        unpack(chunk)

    def tick(step):
        guarded(step - 3 * RELAY, fourth)
        guarded(step - 2 * RELAY, third)
        guarded(step - RELAY, second)
        guarded(step, first)

    return stage_own, send_own, tick


GATHER_TICKS = CHUNKS + 3 * RELAY


def gather_scratch():
    return [
        pltpu.VMEM((CHUNKS, CR, CC), jnp.float32),
        pltpu.VMEM((6, CHUNKS, CR, CC), jnp.float32),
        pltpu.SemaphoreType.DMA((6, CHUNKS)),
        pltpu.SemaphoreType.DMA((6, CHUNKS)),
    ]


def swap_small(small, small_out, sems):
    return pltpu.make_async_remote_copy(
        src_ref=small,
        dst_ref=small_out,
        send_sem=sems.at[0],
        recv_sem=sems.at[1],
        device_id={"tensor": 1 - lax.axis_index("tensor")},
        device_id_type=MESH,
    )


HD = 64
SEG = 148
MEMW = 10
F32 = jnp.float32
EPSILON = 1e-12
MASKED = -1e30
WIN = 160
MEMP = 96
SEGS = 8
PAIR = 2 * HD

CONTRACT_LAST = (((1,), (1,)), ((), ()))
CONTRACT_FIRST = (((0,), (0,)), ((), ()))


def mm(a, b):
    return jnp.dot(a, b, preferred_element_type=F32)


def mm_t(a, b):
    return lax.dot_general(a, b, CONTRACT_LAST, preferred_element_type=F32)


def t_mm(a, b):
    return lax.dot_general(a, b, CONTRACT_FIRST, preferred_element_type=F32)


def build_masks(parent, base, colbias):
    lane = lax.broadcasted_iota(jnp.int32, (1, WIN + MEMP), 1)
    in_mem = [
        ((lane >= WIN + MEMW * t) & (lane < WIN + MEMW * (t + 1))).astype(F32) for t in range(SEGS)
    ]
    reach = [jnp.zeros((1, WIN + MEMP), F32)]
    for s in range(1, SEGS):
        row = jnp.zeros((1, WIN + MEMP), F32)
        for t in range(s):
            hit = jnp.where(parent[s] - base == t, 1.0, 0.0)
            row = row + hit * jnp.maximum(reach[t], in_mem[t])
        reach.append(row)
    for s in range(SEGS):
        off = 4 * (s % 4)
        inside = ((lane >= off) & (lane < off + SEG)).astype(F32)
        colbias[s : s + 1, :] = jnp.where(jnp.maximum(inside, reach[s]) > 0.0, 0.0, MASKED)


def build_select(slots, select):
    row = lax.broadcasted_iota(jnp.int32, (select.shape[0], 1), 0)
    where = jnp.full((select.shape[0], 1), -1, jnp.int32)
    for t in range(SEGS):
        for m in range(MEMW):
            where = jnp.where(row == MEMW * t + m, slots[t, m] + SEG * t, where)
    place = lax.broadcasted_iota(jnp.int32, select.shape, 1)
    select[...] = (where == place).astype(F32).astype(BF)


def window(s):
    return pl.multiple_of(144 * s + 16 * (s // 4), 16), 4 * lax.rem(s, 4)


def lane_halves():
    lane = lax.broadcasted_iota(jnp.int32, (1, PAIR), 1)
    left = (lane < HD).astype(F32)
    return left.astype(BF), (1.0 - left).astype(BF), lane < HD


def valid_rows(off):
    row = lax.broadcasted_iota(jnp.int32, (WIN, 1), 0)
    return row, (row >= off) & (row < off + SEG)


def softmax_parts(qs, kk, bias):
    scores = mm_t(qs, kk) * HD ** (-0.5) + bias
    top = jnp.max(scores, axis=-1, keepdims=True)
    raised = jnp.exp(scores - top)
    return raised, 1.0 / jnp.sum(raised, axis=-1, keepdims=True)


def attend_pair(q, k, v, kmem, vmem, colbias, mixed, probs, s, columns):
    left, right, is_left = lane_halves()
    at, off = window(s)
    rows = pl.ds(at, WIN)
    qw = q[rows, columns]
    qs = jnp.concatenate([qw * left, qw * right], axis=0)
    kk = jnp.concatenate([k[rows, columns], kmem[:, columns]], axis=0)
    vv = jnp.concatenate([v[rows, columns], vmem[:, columns]], axis=0)
    raised, scale = softmax_parts(qs, kk, colbias[pl.ds(s, 1), :])
    row, valid = valid_rows(off)
    keep = jnp.where(valid, 1.0, 0.0)
    chances = (raised * (scale * jnp.concatenate([keep, keep], axis=0))).astype(BF)
    probs[...] = chances
    both = mm(chances, vv)
    out = jnp.where(is_left, both[:WIN], both[WIN:])
    old = mixed[rows, columns].astype(F32)
    mixed[rows, columns] = jnp.where(row >= off, out, old).astype(BF)


def attend_back_pair(q, k, v, kmem, vmem, probs, dmix, dq, dk, dv, dkmem, dvmem, s, columns):
    left, right, is_left = lane_halves()
    at, off = window(s)
    rows = pl.ds(at, WIN)
    qw = q[rows, columns]
    qs = jnp.concatenate([qw * left, qw * right], axis=0)
    kk = jnp.concatenate([k[rows, columns], kmem[:, columns]], axis=0)
    vv = jnp.concatenate([v[rows, columns], vmem[:, columns]], axis=0)
    dw = dmix[rows, columns]
    ds_in = jnp.concatenate([dw * left, dw * right], axis=0)
    low = probs[...]
    chances = low.astype(F32)
    dp = mm_t(ds_in, vv)
    inner = jnp.sum(chances * dp, axis=-1, keepdims=True)
    ds = (chances * (dp - inner)).astype(BF)
    dqs = mm(ds, kk)
    row, valid = valid_rows(off)
    new = jnp.where(is_left, dqs[:WIN], dqs[WIN:]) * HD ** (-0.5)
    old = dq[rows, columns].astype(F32)
    dq[rows, columns] = jnp.where(row >= off, new, old).astype(BF)
    dks = t_mm(ds, qs)
    dvs = t_mm(low, ds_in)
    dk[rows, columns] = dk[rows, columns] + dks[:WIN]
    dv[rows, columns] = dv[rows, columns] + dvs[:WIN]
    dkmem[:, columns] = dkmem[:, columns] + dks[WIN:]
    dvmem[:, columns] = dvmem[:, columns] + dvs[WIN:]


def spread(select, part):
    high = part.astype(BF)
    low = (part - high.astype(F32)).astype(BF)
    return t_mm(select, high) + t_mm(select, low)


def norm_stats(values):
    centered = values - jnp.mean(values, axis=-1, keepdims=True)
    inverse = lax.rsqrt(jnp.mean(centered * centered, axis=-1, keepdims=True) + EPSILON)
    return centered * inverse, inverse


def norm_back(grad, normed, inverse, gain):
    scaled = grad * gain
    return inverse * (
        scaled
        - jnp.mean(scaled, axis=-1, keepdims=True)
        - normed * jnp.mean(scaled * normed, axis=-1, keepdims=True)
    )


def gelu_parts(inner):
    phi = 0.5 + 0.5 * lax.erf(inner * (0.5**0.5))
    density = jnp.exp(-0.5 * inner * inner) * (2.0 * jnp.pi) ** -0.5
    return (inner * phi).astype(BF), (phi + inner * density).astype(BF)


def flat_row(ref, start, size):
    return ref[pl.ds(start, size)].reshape(1, size)


TILE = 128


def row_tiles(rows, body):
    full = rows // TILE

    @pl.loop(0, full)
    def _(i):
        body(pl.ds(pl.multiple_of(i * TILE, TILE), TILE))

    if rows % TILE:
        body(pl.ds(full * TILE, rows % TILE))


def forward_kernel(
    fast,
    parent,
    slots,
    bias_qv,
    bias_out,
    gain_one,
    shift_one,
    bias_up,
    bias_down,
    gain_two,
    shift_two,
    tokens_h,
    grad_h,
    own_qkv,
    own_out,
    own_up,
    own_down,
    *rest,
):
    count = 0 if fast else 5
    given, outs, rest = rest[:count], rest[count : count + 18], rest[count + 18 :]
    (
        output_h,
        their_qkv_h,
        their_out_h,
        their_up_h,
        their_down_h,
        qkv_h,
        mixed_h,
        normed_h,
        inverse,
        hidden_h,
        acted_h,
        slope_own_h,
        slope_their_h,
        d_two_h,
        d_ffn_h,
        vec,
        probs_h,
        select,
    ) = outs
    (
        tokens,
        their_qkv,
        their_out,
        their_up,
        their_down,
        small,
        small_their,
        qkv,
        mixed,
        normed,
        hidden,
        acc_own,
        acc_their,
        acted,
        slopes,
        colbias,
        kmem,
        vmem,
        sums,
        probs,
        io_sem,
        slope_sem,
        probs_sem,
        *wires,
    ) = rest
    rows, depth = tokens.shape
    width = mixed.shape[2]
    units = acted.shape[1]
    theirs = (their_qkv, their_out, their_up, their_down)
    own = (own_qkv, own_out, own_up, own_down)

    def move(index, source, target):
        return pltpu.make_async_copy(source, target, io_sem.at[index])

    load_tokens = move(0, tokens_h, tokens)
    load_grad = move(1, grad_h, tokens)
    put_qkv = move(2, qkv, qkv_h)
    put_mixed = move(3, mixed.at[0], mixed_h)
    put_normed = move(4, normed, normed_h)
    put_hidden = move(5, hidden, hidden_h)
    put_acted = move(6, acted, acted_h)
    put_two = move(7, acc_own, d_two_h)
    put_ffn = move(8, hidden, d_ffn_h)
    put_output = move(9, tokens, output_h)
    put_theirs = [
        move(10 + i, ref, target)
        for i, (ref, target) in enumerate(zip(theirs, (their_qkv_h, their_out_h, their_up_h, their_down_h)))
    ]
    load_tokens.start()
    done = [0]
    small[...] = jnp.zeros(small.shape, F32)
    small[0:1, :] = bias_qv[0:1, :]
    small[2:3, :] = bias_qv[1:2, :]
    for c in range(units // CHUNK):
        small[3 + c : 4 + c, 0:CHUNK] = flat_row(bias_up, c * CHUNK, CHUNK)
    if fast:
        pos = Place()
        small_sem, *wires = wires
        stage_own, send_own, tick = make_gather(pos, own, theirs, *wires)
        stage_own()
        gather_barrier(pos, 1 - lax.axis_index("tensor"))
        swap = swap_small(small, small_their, small_sem)
        swap.start()
        send_own()
    else:
        copies = [move(10 + i, a, b) for i, (a, b) in enumerate(zip(given, theirs + (small_their,)))]
        for copy in copies:
            copy.start()
        for copy in copies:
            copy.wait()

        def tick(step):
            pass

    def ticks(index, each, trips):
        for i in range(each):
            tick(done[0] + index * each + i)

    def until(count):
        if done[0] < count:

            @pl.loop(done[0], count)
            def _(step):
                tick(step)

            done[0] = count

    build_masks(parent, lax.axis_index("dp") * SEGS, colbias)
    build_select(slots, select)
    load_tokens.wait()
    pairs = width // PAIR
    for half in range(2):
        weights = (own_qkv, their_qkv)[half]
        table = (small, small_their)[half]
        if half == 1:
            until(BOUNDS[0][1] + 3 * RELAY)
            if fast:
                swap.wait()

        @pl.loop(0, 3)
        def _(c, half=half, weights=weights, table=table):
            part = mm(tokens[...], weights[pl.ds(pl.multiple_of(c * depth, depth), depth), :])
            qkv[half, c] = (part + table[pl.ds(c, 1), :]).astype(BF)
            ticks(c, GATHER[2 * half], 3)

        done[0] += 3 * GATHER[2 * half]
        q, k, v = (qkv.at[half, i] for i in range(3))
        kmem[...] = mm(select[...], k[...]).astype(BF)
        vmem[...] = mm(select[...], v[...]).astype(BF)

        def put_probs(s, half=half):
            slot = lax.rem(s, 2)
            return pltpu.make_async_copy(probs.at[slot], probs_h.at[half, s], probs_sem.at[slot])

        @pl.loop(0, SEGS)
        def _(s, half=half, q=q, k=k, v=v, put_probs=put_probs):
            @pl.when(s >= 2)
            def _():
                put_probs(s - 2).wait()

            for pair in range(pairs):
                attend_pair(
                    q, k, v, kmem, vmem, colbias, mixed.at[half], probs.at[lax.rem(s, 2), pair], s, pl.ds(pair * PAIR, PAIR)
                )
                if pair < GATHER[2 * half + 1]:
                    tick(done[0] + s * GATHER[2 * half + 1] + pair)
            put_probs(s).start()

        done[0] += SEGS * GATHER[2 * half + 1]
        put_probs(SEGS - 2).wait()
        put_probs(SEGS - 1).wait()
    put_qkv.start()
    put_mixed.start()
    until(BOUNDS[1][1] + 3 * RELAY)

    @pl.loop(0, 3)
    def _(n):
        columns = pl.ds(pl.multiple_of(n * CHUNK, CHUNK), CHUNK)
        acc_own[:, columns] = mm(mixed[0], own_out[:, columns]) + mm(mixed[1], their_out[:, columns])
        ticks(n, GATHER[4], 3)

    done[0] += 3 * GATHER[4]

    def norm_one(span):
        resid = tokens[span, :].astype(F32) + (acc_own[span, :] + flat_row(bias_out, 0, depth))
        unit, scale = norm_stats(resid)
        normed[span, :] = unit
        inverse[span, :] = scale
        hidden[span, :] = (unit * flat_row(gain_one, 0, depth) + flat_row(shift_one, 0, depth)).astype(BF)

    row_tiles(rows, norm_one)
    load_grad.start()
    put_normed.start()
    put_hidden.start()

    for half in range(2):
        up, down = ((own_up, own_down), (their_up, their_down))[half]
        table = (small, small_their)[half]
        slope_h = (slope_own_h, slope_their_h)[half]
        acc = (acc_own, acc_their)[half]

        def put_slope(c, slope_h=slope_h):
            span = pl.ds(pl.multiple_of(c * CHUNK, CHUNK), CHUNK)
            return pltpu.make_async_copy(slopes.at[lax.rem(c, 2)], slope_h.at[:, span], slope_sem.at[lax.rem(c, 2)])

        if half == 1:
            until(BOUNDS[2][1] + 3 * RELAY)
            put_acted.wait()
            put_slope(4).wait()
            put_slope(5).wait()

        @pl.loop(0, 6)
        def _(c, half=half, up=up, table=table, put_slope=put_slope):
            span = pl.ds(pl.multiple_of(c * CHUNK, CHUNK), CHUNK)

            @pl.when(c >= 2)
            def _():
                put_slope(c - 2).wait()

            bias = table[pl.ds(3 + c, 1), 0:CHUNK]
            act, steep = gelu_parts(mm(hidden[...], up[:, span]) + bias)
            acted[:, span] = act
            slopes[lax.rem(c, 2)] = steep
            put_slope(c).start()
            ticks(c, GATHER[5 + 2 * half], 6)

        done[0] += 6 * GATHER[5 + 2 * half]
        if half == 0:
            put_acted.start()
        else:
            until(BOUNDS[3][1] + 3 * RELAY)
            if fast:
                for copy in put_theirs:
                    copy.start()

        @pl.loop(0, 3)
        def _(n, half=half, down=down, acc=acc):
            columns = pl.ds(pl.multiple_of(n * CHUNK, CHUNK), CHUNK)
            acc[:, columns] = mm(acted[...], down[:, columns])
            ticks(n, GATHER[6 + 2 * half], 3)

        done[0] += 3 * GATHER[6 + 2 * half]
    put_slope(4).wait()
    put_slope(5).wait()

    load_grad.wait()
    put_hidden.wait()
    sums[...] = jnp.zeros(sums.shape, F32)

    def norm_two(span):
        first = normed[span, :] * flat_row(gain_one, 0, depth) + flat_row(shift_one, 0, depth)
        resid = first + ((acc_own[span, :] + acc_their[span, :]) + flat_row(bias_down, 0, depth))
        unit, scale = norm_stats(resid)
        grad = tokens[span, :].astype(F32)
        tokens[span, :] = (unit * flat_row(gain_two, 0, depth) + flat_row(shift_two, 0, depth)).astype(BF)
        back = norm_back(grad, unit, scale, flat_row(gain_two, 0, depth))
        acc_own[span, :] = back
        low = back.astype(BF)
        hidden[span, :] = low
        for index, value in enumerate((low.astype(F32), grad * unit, grad)):
            sums[index] = sums[index] + value.reshape(-1, 8, depth).sum(axis=0)

    row_tiles(rows, norm_two)
    put_two.start()
    put_ffn.start()
    put_output.start()
    for index in range(3):
        total = jnp.sum(sums[index], axis=0, keepdims=True)
        for j in range(6):
            vec[6 * index + j : 6 * index + j + 1, :] = total[:, BC * j : BC * (j + 1)]
    for copy in (put_qkv, put_mixed, put_normed, put_two, put_ffn, put_output):
        copy.wait()
    if fast:
        for copy in put_theirs:
            copy.wait()


GATHER = (0, 1, 1, 1, 0, 1, 0, 0, 0)


def forward(fast, parent, slots, vectors, tokens, grad_out, own, given):
    rows, depth = tokens.shape
    width = own[0].shape[1]
    units = own[2].shape[1]
    vm = pl.BlockSpec(memory_space=pltpu.VMEM)
    hbm = pl.BlockSpec(memory_space=pl.ANY)
    sm = pl.BlockSpec(memory_space=pltpu.SMEM)
    sd = jax.ShapeDtypeStruct
    out_shape = [
        sd((rows, depth), BF),
        *[sd(w.shape, BF) for w in own],
        sd((2, 3, rows, width), BF),
        sd((rows, width), BF),
        sd((rows, depth), F32),
        sd((rows, 1), F32),
        sd((rows, depth), BF),
        sd((rows, units), BF),
        sd((rows, units), BF),
        sd((rows, units), BF),
        sd((rows, depth), F32),
        sd((rows, depth), BF),
        sd((18, BC), F32),
        sd((2, SEGS, width // PAIR, 2 * WIN, WIN + MEMP), BF),
        sd((MEMP, rows), BF),
    ]
    return pl.pallas_call(
        functools.partial(forward_kernel, fast),
        out_shape=out_shape,
        in_specs=[sm, sm] + [vm] * len(vectors) + [hbm, hbm] + [vm] * 4 + [hbm] * len(given),
        out_specs=[hbm] * 8 + [vm] + [hbm] * 6 + [vm, hbm, vm],
        scratch_shapes=[
            pltpu.VMEM((rows, depth), BF),
            *[pltpu.VMEM(w.shape, BF) for w in own],
            pltpu.VMEM((16, width), F32),
            pltpu.VMEM((16, width), F32),
            pltpu.VMEM((2, 3, rows, width), BF),
            pltpu.VMEM((2, rows, width), BF),
            pltpu.VMEM((rows, depth), F32),
            pltpu.VMEM((rows, depth), BF),
            pltpu.VMEM((rows, depth), F32),
            pltpu.VMEM((rows, depth), F32),
            pltpu.VMEM((rows, units), BF),
            pltpu.VMEM((2, rows, CHUNK), BF),
            pltpu.VMEM((SEGS, WIN + MEMP), F32),
            pltpu.VMEM((MEMP, width), BF),
            pltpu.VMEM((MEMP, width), BF),
            pltpu.VMEM((3, 8, depth), F32),
            pltpu.VMEM((2, width // PAIR, 2 * WIN, WIN + MEMP), BF),
            pltpu.SemaphoreType.DMA((15,)),
            pltpu.SemaphoreType.DMA((2,)),
            pltpu.SemaphoreType.DMA((2,)),
        ]
        + ([pltpu.SemaphoreType.DMA((2,))] + gather_scratch() if fast else []),
        compiler_params=pltpu.CompilerParams(
            collective_id=0 if fast else None, has_side_effects=fast, vmem_limit_bytes=67043328
        ),
        name="forward",
    )(parent, slots, *vectors, tokens, grad_out, *own, *given)


DOWN, UP, OUT, QKV, VEC = 0, 24, 48, 54, 72
COUNT = 73
CHUNK = 256
VEC_ROWS = 54


def backward_kernel(
    fast,
    select,
    inverse,
    gain,
    vec_in,
    tokens_h,
    hidden_h,
    d_ffn_h,
    d_two_h,
    normed_h,
    acted_h,
    slope_own_h,
    slope_their_h,
    qkv_h,
    mixed_h,
    probs_h,
    w_up_own,
    w_up_their,
    w_down_own,
    w_down_their,
    w_out_own,
    w_out_their,
    w_qkv_own,
    w_qkv_their,
    g_qkv,
    g_out,
    g_up,
    g_down,
    g_vec,
    g_tokens,
    grads,
    d_low,
    hidden,
    d_res,
    normed,
    acc_own,
    acc_their,
    a_buf,
    slope_buf,
    up_buf,
    down_buf,
    d_inner,
    sums,
    tokens,
    mixed,
    w_out,
    w_qkv,
    qkv,
    d_qkv,
    d_mixed,
    probs,
    kmem,
    vmem,
    dkm,
    dvm,
    load_sem,
    chunk_sem,
    put_sem,
    probs_sem,
    *wires,
):
    rows, depth = tokens.shape
    width = mixed.shape[1]

    def fetch(index, source, target):
        return pltpu.make_async_copy(source, target, load_sem.at[index])

    load_d = fetch(0, d_ffn_h, d_low)
    load_hidden = fetch(1, hidden_h, hidden)
    load_two = fetch(2, d_two_h, d_res)
    load_normed = fetch(3, normed_h, normed)
    load_mixed = fetch(4, mixed_h, mixed)
    load_out = [fetch(5 + i, w, w_out.at[i]) for i, w in enumerate((w_out_own, w_out_their))]
    load_w = [fetch(7 + i, w, w_qkv.at[i]) for i, w in enumerate((w_qkv_own, w_qkv_their))]
    load_tokens = fetch(9, tokens_h, tokens)
    load_qkv = [fetch(10 + half, qkv_h.at[half], qkv) for half in range(2)]
    put_tokens = fetch(12, d_low, g_tokens)

    def load_acted(c):
        return pltpu.make_async_copy(acted_h.at[:, pl.ds(pl.multiple_of(c * BR, BR), BR)], a_buf.at[lax.rem(c, 2)], chunk_sem.at[0, lax.rem(c, 2)])

    def load_chunk(half, c):
        slot = lax.rem(c, 2)
        span = pl.ds(pl.multiple_of(c * CHUNK, CHUNK), CHUNK)
        slope_h, up_h, down_h = ((slope_own_h, w_up_own, w_down_own), (slope_their_h, w_up_their, w_down_their))[half]
        return (
            pltpu.make_async_copy(slope_h.at[:, span], slope_buf.at[slot], chunk_sem.at[1, slot]),
            pltpu.make_async_copy(up_h.at[:, span], up_buf.at[slot], chunk_sem.at[2, slot]),
            pltpu.make_async_copy(down_h.at[span, :], down_buf.at[slot], chunk_sem.at[3, slot]),
        )

    def load_probs(half, s):
        slot = lax.rem(s, 2)
        return pltpu.make_async_copy(probs_h.at[half, s], probs.at[slot], probs_sem.at[slot])

    def start(copies):
        for copy in copies:
            copy.start()

    def wait(copies):
        for copy in copies:
            copy.wait()

    load_d.start()
    load_acted(0).start()
    start(load_chunk(0, 0))
    load_hidden.start()
    load_two.start()
    load_normed.start()
    load_mixed.start()
    start(load_out)
    start(load_w)
    load_tokens.start()
    load_qkv[0].start()
    load_probs(0, 0).start()

    def put(block, target):
        return pltpu.make_async_copy(grads.at[block], target, put_sem.at[lax.rem(block, 8)])

    def wait_put(block):
        put(block, g_vec).wait()

    def finish(block):
        @pl.when(block >= 8)
        def _():
            wait_put(block - 8)

        def at(row, column):
            return pl.ds(pl.multiple_of(row, BR), BR), pl.ds(pl.multiple_of(column, BC), BC)

        @pl.when(block < UP)
        def _():
            put(block, g_down.at[at(BR * (block // 6), BC * lax.rem(block, 6))]).start()

        @pl.when((block >= UP) & (block < OUT))
        def _():
            i = block - UP
            put(block, g_up.at[at(BR * lax.rem(i // 2, 2), CHUNK * (i // 4) + BC * lax.rem(i, 2))]).start()

        @pl.when((block >= OUT) & (block < QKV))
        def _():
            put(block, g_out.at[at(0, BC * (block - OUT))]).start()

        @pl.when((block >= QKV) & (block < VEC))
        def _():
            i = block - QKV
            put(block, g_qkv.at[at(BR * (i // 3), BC * lax.rem(i, 3))]).start()

        @pl.when(block == VEC)
        def _():
            put(block, g_vec).start()

    if fast:
        pos = Place()
        tick = make_tick(pos, grads, *wires, COUNT, finish)
        last = COUNT + 7 * SPREAD
    else:

        def tick(step):
            @pl.when(step < COUNT)
            def _():
                finish(step)

        last = COUNT
    done = [0]

    def ticks(index, each, trips):
        for i in range(each):
            tick(done[0] + index * each + i)
        return trips * each

    grads[VEC] = jnp.zeros((BR, BC), F32)
    grads[VEC, 36:54] = vec_in[...]
    acc_own[...] = jnp.zeros(acc_own.shape, F32)
    acc_their[...] = jnp.zeros(acc_their.shape, F32)
    sums[...] = jnp.zeros(sums.shape, F32)
    if fast:
        sum_barrier(pos)

    load_d.wait()

    @pl.loop(0, 4)
    def _(c):
        load_acted(c).wait()

        @pl.when(c < 3)
        def _():
            load_acted(c + 1).start()

        for part in range(2):
            piece = t_mm(a_buf[lax.rem(c, 2)], d_low[:, part * width : (part + 1) * width])
            for j in range(3):
                grads[DOWN + 6 * c + 3 * part + j] = piece[:, BC * j : BC * (j + 1)]
        ticks(c, TICKS[0], 4)

    done[0] += 4 * TICKS[0]

    load_hidden.wait()
    for half in range(2):
        acc = (acc_own, acc_their)[half]

        @pl.loop(0, 6)
        def _(c, half=half, acc=acc):
            slot = lax.rem(c, 2)
            wait(load_chunk(half, c))

            @pl.when(c < 5)
            def _():
                start(load_chunk(half, c + 1))

            if half == 0:

                @pl.when(c == 5)
                def _():
                    start(load_chunk(1, 0))

            each = TICKS[1 + half]
            d_inner[...] = (mm_t(d_low[...], down_buf[slot]) * slope_buf[slot].astype(F32)).astype(BF)
            if each > 1:
                tick(done[0] + c * each)
            if half == 0:
                piece = t_mm(hidden[...], d_inner[...])
                for r in range(2):
                    for j in range(2):
                        grads[UP + 4 * c + 2 * r + j] = piece[BR * r : BR * (r + 1), BC * j : BC * (j + 1)]
                total = jnp.sum(d_inner[...].astype(F32), axis=0, keepdims=True)
                for j in range(2):
                    grads[VEC, pl.ds(6 + 2 * c + j, 1), :] = total[:, BC * j : BC * (j + 1)]
                if each > 2:
                    tick(done[0] + c * each + 1)
            for part in range(3):
                columns = slice(CHUNK * part, CHUNK * (part + 1))
                acc[:, columns] = acc[:, columns] + mm_t(d_inner[...], up_buf[slot, columns, :])
            tick(done[0] + c * each + each - 1)

        done[0] += 6 * TICKS[1 + half]

    load_two.wait()
    load_normed.wait()
    tile = 32
    trips = rows // tile

    @pl.loop(0, trips)
    def _(i):
        span = pl.ds(pl.multiple_of(i * tile, tile), tile)
        total = d_res[span, :] + (acc_own[span, :] + acc_their[span, :])
        unit = normed[span, :]
        one = norm_back(total, unit, inverse[span, :], flat_row(gain, 0, depth))
        d_res[span, :] = one
        low = one.astype(BF)
        d_low[span, :] = low
        for index, value in enumerate((low.astype(F32), total * unit, total)):
            sums[index] = sums[index] + value.reshape(tile // 8, 8, depth).sum(axis=0)

        @pl.when(lax.rem(i, TICK_TILES) == 0)
        def _():
            tick(done[0] + i // TICK_TILES)

    done[0] += -(-trips // TICK_TILES)
    for index in range(3):
        total = jnp.sum(sums[index], axis=0, keepdims=True)
        for j in range(6):
            grads[VEC, 18 + 6 * index + j : 19 + 6 * index + j, :] = total[:, BC * j : BC * (j + 1)]

    load_mixed.wait()
    wait(load_out)

    @pl.loop(0, 2)
    def _(half):
        d_mixed[half] = mm_t(d_low[...], w_out[half]).astype(BF)
        piece = t_mm(mixed[...], d_low[:, pl.ds(pl.multiple_of(half * width, BC), width)])
        for j in range(3):
            grads[OUT + 3 * half + j] = piece[:, BC * j : BC * (j + 1)]
        ticks(half, TICKS[3], 2)

    done[0] += 2 * TICKS[3]

    wait(load_w)
    load_tokens.wait()
    pairs = width // PAIR
    dka, dva = acc_their.at[:, pl.ds(0, width)], acc_their.at[:, pl.ds(width, width)]
    for half in range(2):
        load_qkv[half].wait()
        q, k, v = (qkv.at[i] for i in range(3))
        kmem[...] = mm(select[...], k[...]).astype(BF)
        vmem[...] = mm(select[...], v[...]).astype(BF)
        acc_their[...] = jnp.zeros(acc_their.shape, F32)
        dkm[...] = jnp.zeros(dkm.shape, F32)
        dvm[...] = jnp.zeros(dvm.shape, F32)

        @pl.loop(0, SEGS * pairs)
        def _(spot, half=half):
            s, pair = spot // pairs, lax.rem(spot, pairs)

            @pl.when(pair == 0)
            def _():
                load_probs(half, s).wait()

                @pl.when(s < SEGS - 1)
                def _():
                    load_probs(half, s + 1).start()

                if half == 0:

                    @pl.when(s == SEGS - 1)
                    def _():
                        load_probs(1, 0).start()

            columns = pl.ds(pl.multiple_of(pair * PAIR, PAIR), PAIR)
            part = probs.at[lax.rem(s, 2), pair]
            attend_back_pair(q, k, v, kmem, vmem, part, d_mixed.at[half], d_qkv.at[0], dka, dva, dkm, dvm, s, columns)

            @pl.when(lax.rem(spot, TICKS[4 + half]) == 0)
            def _():
                tick(done[0] + spot // TICKS[4 + half])

        done[0] += -(-SEGS * pairs // TICKS[4 + half])
        if half == 0:
            assert done[0] <= QKV
        if half == 0:
            load_qkv[1].start()
        for pair in range(pairs):
            columns = pl.ds(pair * PAIR, PAIR)
            d_qkv[1, :, columns] = ((dka[:, columns] + spread(select[...], dkm[:, columns])) * HD ** (-0.5)).astype(BF)
            d_qkv[2, :, columns] = (dva[:, columns] + spread(select[...], dvm[:, columns])).astype(BF)
        if half == 0:

            @pl.loop(0, 3)
            def _(c):
                piece = t_mm(tokens[...], d_qkv[c])
                for r in range(2):
                    for j in range(3):
                        grads[QKV + 6 * c + 3 * r + j] = piece[BR * r : BR * (r + 1), BC * j : BC * (j + 1)]
                columns = pl.ds(pl.multiple_of(c * CHUNK, CHUNK), CHUNK)
                part = mm_t(d_qkv[0], w_qkv[half, pl.ds(pl.multiple_of(c * CHUNK, CHUNK), CHUNK), :])
                for i in (1, 2):
                    part = part + mm_t(d_qkv[i], w_qkv[half, pl.ds(pl.multiple_of(i * depth + c * CHUNK, CHUNK), CHUNK), :])
                acc_own[:, columns] = part
                ticks(c, TICKS[6], 3)

            done[0] += 3 * TICKS[6]
            for index, row in ((0, 0), (2, 3)):
                total = jnp.sum(d_qkv[index].astype(F32), axis=0, keepdims=True)
                for j in range(3):
                    grads[VEC, row + j : row + j + 1, :] = total[:, BC * j : BC * (j + 1)]
        else:

            @pl.loop(0, 3)
            def _(c):
                columns = pl.ds(pl.multiple_of(c * CHUNK, CHUNK), CHUNK)
                part = mm_t(d_qkv[0], w_qkv[half, pl.ds(pl.multiple_of(c * CHUNK, CHUNK), CHUNK), :])
                for i in (1, 2):
                    part = part + mm_t(d_qkv[i], w_qkv[half, pl.ds(pl.multiple_of(i * depth + c * CHUNK, CHUNK), CHUNK), :])
                d_low[:, columns] = ((acc_own[:, columns] + part) + d_res[:, columns]).astype(BF)
                ticks(c, TICKS[7], 3)

            done[0] += 3 * TICKS[7]
            put_tokens.start()
    @pl.loop(min(done[0], last), last)
    def _(step):
        tick(step)

    for block in range(COUNT - 8, COUNT):
        wait_put(block)
    put_tokens.wait()


TICKS = (1, 3, 2, 1, 2, 1, 3, 1)
TICK_TILES = 8


def backward(fast, select, inverse, gain, vec_in, arrays):
    tokens, acted, mixed = arrays[0], arrays[5], arrays[9]
    rows, depth = tokens.shape
    units = acted.shape[1]
    width = mixed.shape[1]
    vm = pl.BlockSpec(memory_space=pltpu.VMEM)
    hbm = pl.BlockSpec(memory_space=pl.ANY)
    sd = jax.ShapeDtypeStruct
    return pl.pallas_call(
        functools.partial(backward_kernel, fast),
        out_shape=[
            sd((3 * depth, width), F32),
            sd((width, depth), F32),
            sd((depth, units), F32),
            sd((units, depth), F32),
            sd((BR, BC), F32),
            sd((rows, depth), BF),
        ],
        in_specs=[vm, vm, vm, vm] + [hbm] * len(arrays),
        out_specs=[hbm] * 6,
        scratch_shapes=[
            pltpu.VMEM((COUNT, BR, BC), F32),
            pltpu.VMEM((rows, depth), BF),
            pltpu.VMEM((rows, depth), BF),
            pltpu.VMEM((rows, depth), F32),
            pltpu.VMEM((rows, depth), F32),
            pltpu.VMEM((rows, depth), F32),
            pltpu.VMEM((rows, depth), F32),
            pltpu.VMEM((2, rows, BR), BF),
            pltpu.VMEM((2, rows, CHUNK), BF),
            pltpu.VMEM((2, depth, CHUNK), BF),
            pltpu.VMEM((2, CHUNK, depth), BF),
            pltpu.VMEM((rows, CHUNK), BF),
            pltpu.VMEM((3, 8, depth), F32),
            pltpu.VMEM((rows, depth), BF),
            pltpu.VMEM((rows, width), BF),
            pltpu.VMEM((2, width, depth), BF),
            pltpu.VMEM((2, 3 * depth, width), BF),
            pltpu.VMEM((3, rows, width), BF),
            pltpu.VMEM((3, rows, width), BF),
            pltpu.VMEM((2, rows, width), BF),
            pltpu.VMEM((2, width // PAIR, 2 * WIN, WIN + MEMP), BF),
            pltpu.VMEM((MEMP, width), BF),
            pltpu.VMEM((MEMP, width), BF),
            pltpu.VMEM((MEMP, width), F32),
            pltpu.VMEM((MEMP, width), F32),
            pltpu.SemaphoreType.DMA((13,)),
            pltpu.SemaphoreType.DMA((4, 2)),
            pltpu.SemaphoreType.DMA((8,)),
            pltpu.SemaphoreType.DMA((2,)),
        ]
        + (sum_scratch() if fast else []),
        compiler_params=pltpu.CompilerParams(
            collective_id=1 if fast else None, has_side_effects=fast, vmem_limit_bytes=67043328
        ),
        name="backward",
    )(select, inverse, gain, vec_in, *arrays)


def halves_swap(own, small):
    unit = (lax.axis_index("dp") >= 0).astype(F32)

    def other(array):
        arrived = lax.ppermute(array.astype(F32), "tensor", [(0, 1), (1, 0)])
        return (arrived * unit).astype(array.dtype)

    return tuple(other(array) for array in own) + (other(small),)


def shards(
    fast,
    tokens,
    w_qkv,
    bias_qv,
    w_out,
    bias_out,
    gain_one,
    shift_one,
    w_up,
    bias_up,
    w_down,
    bias_down,
    gain_two,
    shift_two,
    grad_out,
    parent,
    mem_slots,
):
    depth, width = w_qkv.shape[1:]
    hidden_units = w_up.shape[1]
    own = (w_qkv.reshape(3 * depth, width), w_out, w_up, w_down)
    if fast:
        given = ()
    else:
        table = jnp.pad(bias_up.reshape(-1, CHUNK), ((0, 0), (0, width - CHUNK)))
        small = jnp.concatenate([bias_qv[:1], jnp.zeros((1, width), F32), bias_qv[1:], table])
        given = halves_swap(own, jnp.pad(small, ((0, 16 - small.shape[0]), (0, 0))))
    vectors = (bias_qv, bias_out, gain_one, shift_one, bias_up, bias_down, gain_two, shift_two)
    (
        output,
        *theirs,
        qkv,
        mixed,
        normed,
        inverse,
        hidden_low,
        acted,
        slope_own,
        slope_their,
        d_two,
        d_ffn,
        vec,
        probs,
        select,
    ) = forward(fast, parent, mem_slots, vectors, tokens, grad_out, own, given)
    if not fast:
        theirs = given[:4]
    arrays = (tokens, hidden_low, d_ffn, d_two, normed, acted, slope_own, slope_their, qkv, mixed, probs)
    weights = tuple(w[i] for i in (2, 3, 1, 0) for w in (own, theirs))
    g_w_qkv, g_w_out, g_w_up, g_w_down, flat, grad_tokens = backward(
        fast, select, inverse, gain_one, vec, arrays + weights
    )
    if not fast:
        g_w_qkv, g_w_out, g_w_up, g_w_down, flat = lax.psum((g_w_qkv, g_w_out, g_w_up, g_w_down, flat), "dp")
    g_w_qkv = g_w_qkv.reshape(w_qkv.shape)
    sums, row = [], 0
    for size in (width, width, hidden_units) + (depth,) * 6:
        sums.append(flat[row : row + size // BC].reshape(-1))
        row += size // BC
    g_bias_q, g_bias_v, g_bias_up, g_bias_out, g_gain_one, g_shift_one, g_bias_down, g_gain_two, g_shift_two = sums
    return (
        output,
        grad_tokens,
        g_w_qkv,
        jnp.stack([g_bias_q, g_bias_v]),
        g_w_out,
        g_bias_out,
        g_gain_one,
        g_shift_one,
        g_w_up,
        g_bias_up,
        g_w_down,
        g_bias_down,
        g_gain_two,
        g_shift_two,
    )


def solution(mesh):
    fast = mesh.shape["dp"] == 16 and mesh.shape["tensor"] == 2
    rows, whole = P("dp", None), P()
    return jax.shard_map(
        functools.partial(shards, fast),
        mesh=mesh,
        in_specs=(
            rows,
            P(None, None, "tensor"),
            P(None, "tensor"),
            P("tensor", None),
            whole,
            whole,
            whole,
            P(None, "tensor"),
            P("tensor"),
            P("tensor", None),
            whole,
            whole,
            whole,
            rows,
            P("dp"),
            rows,
        ),
        out_specs=(
            rows,
            rows,
            P(None, None, "tensor"),
            P(None, "tensor"),
            P("tensor", None),
            whole,
            whole,
            whole,
            P(None, "tensor"),
            P("tensor"),
            P("tensor", None),
            whole,
            whole,
            whole,
        ),
        check_vma=False,
    )
```

```python
import functools


import jax
import jax.numpy as jnp
from jax import lax
from jax.experimental import pallas as pl
from jax.experimental.pallas import tpu as pltpu
from jax.sharding import PartitionSpec as P


MESH = pl.DeviceIdType.MESH
BR, BC = 384, 128
SPREAD = 3
SLOTS = 16


class Place:
    def __init__(self):
        me = lax.axis_index("dp")
        self.core = lax.rem(me, 2)
        self.x = lax.rem(me // 2, 2)
        self.z = me // 4
        self.sib = me + 1 - 2 * self.core
        self.xn = me + 2 - 4 * self.x
        self.zp = me + 4 - 8 * lax.rem(self.z, 2)
        self.zm = me + 4 * (3 - 2 * self.z)
        self.end = (self.z == 0) | (self.z == 3)
        self.mid = (self.z == 1) | (self.z == 2)


def sum_greet(pos):
    barrier = pltpu.get_barrier_semaphore()

    def greet(dev):
        pl.semaphore_signal(barrier, inc=1, device_id={"dp": dev}, device_id_type=MESH)

    greet(pos.sib)
    greet(pos.xn)
    greet(pos.zp)

    @pl.when(pos.mid)
    def _():
        greet(pos.zm)


def sum_met(pos):
    pl.semaphore_wait(pltpu.get_barrier_semaphore(), jnp.where(pos.mid, 4, 3))


def make_tick(pos, grads, from_core, from_one, from_two, from_three, sent, got, credit, count, finish):
    half = BR // 2
    quarter = BR // 4

    def copy(stage, block, source, target, device):
        slot = lax.rem(block, SLOTS)
        return pltpu.make_async_remote_copy(
            src_ref=source,
            dst_ref=target,
            send_sem=sent.at[stage, slot],
            recv_sem=got.at[stage, slot],
            device_id={"dp": device},
            device_id_type=MESH,
        )

    def rows(block, start, size):
        return grads.at[block, pl.ds(pl.multiple_of(start, quarter), size)]

    def add(block, start, size, landed):
        where = pl.ds(pl.multiple_of(start, quarter), size)
        grads[block, where] = grads[block, where] + landed[...]

    def free(index, device):
        pl.semaphore_signal(credit.at[index], inc=1, device_id={"dp": device}, device_id_type=MESH)

    def claim(index):
        pl.semaphore_wait(credit.at[index], 1)

    x_first = pos.core == 0
    z_first = pos.core == 1
    mine = pos.core * half
    xrow = pos.x * quarter
    xrow_other = (1 - pos.x) * quarter
    far = lax.rem(pos.z, 2) == 0
    keep = half + jnp.where(far, quarter, 0)
    give = half + jnp.where(far, 0, quarter)

    def core_out(block):
        return copy(0, block, rows(block, (1 - pos.core) * half, half), from_core.at[lax.rem(block, SLOTS)], pos.sib)

    def x_one(block):
        return copy(1, block, rows(block, xrow_other, quarter), from_one.at[lax.rem(block, SLOTS), pl.ds(0, quarter)], pos.xn)

    def z_one(block):
        return copy(1, block, rows(block, half, half), from_one.at[lax.rem(block, SLOTS)], pos.zp)

    def x_two(block):
        return copy(2, block, rows(block, xrow, quarter), from_two.at[lax.rem(block, SLOTS)], pos.zp)

    def z_two(block):
        return copy(2, block, rows(block, give, quarter), from_two.at[lax.rem(block, SLOTS)], pos.zm)

    def x_three(block):
        return copy(3, block, rows(block, xrow, quarter), from_three.at[lax.rem(block, SLOTS)], pos.zm)

    def z_three(block):
        return copy(3, block, rows(block, keep, quarter), from_three.at[lax.rem(block, SLOTS)], pos.xn)

    def x_four(block):
        return copy(4, block, rows(block, xrow, quarter), rows(block, xrow, quarter), pos.zp)

    def z_four(block):
        return copy(4, block, rows(block, keep, quarter), rows(block, keep, quarter), pos.zm)

    def z_four_in(block):
        return copy(4, block, rows(block, give, quarter), rows(block, give, quarter), pos.zm)

    def x_five(block):
        return copy(5, block, rows(block, xrow, quarter), rows(block, xrow, quarter), pos.xn)

    def x_five_in(block):
        return copy(5, block, rows(block, xrow_other, quarter), rows(block, xrow_other, quarter), pos.xn)

    def z_five(block):
        return copy(5, block, rows(block, half, half), rows(block, half, half), pos.zp)

    def core_six(block):
        return copy(6, block, rows(block, mine, half), rows(block, mine, half), pos.sib)

    def core_six_in(block):
        return copy(6, block, rows(block, (1 - pos.core) * half, half), rows(block, (1 - pos.core) * half, half), pos.sib)

    def start_core(block):
        core_out(block).start()

    def take_core(block):
        core_out(block).wait()
        free(2, pos.sib)
        add(block, mine, half, from_core.at[lax.rem(block, SLOTS)])

    def take_x(block):
        x_one(block).wait()
        free(1, pos.xn)
        add(block, xrow, quarter, from_one.at[lax.rem(block, SLOTS), pl.ds(0, quarter)])

    def send_x(block):
        take_core(block)
        x_one(block).start()

    def send_z(block):
        take_core(block)
        z_one(block).start()

    def x_end_two(block):
        take_x(block)
        x_two(block).start()

    def x_end_three(block):
        x_two(block).wait_send()
        free(0, pos.zp)

    def x_mid_three(block):
        x_two(block).wait_recv()
        add(block, xrow, quarter, from_two.at[lax.rem(block, SLOTS)])
        x_three(block).start()

    def x_mid_four(block):
        x_three(block).wait()
        add(block, xrow, quarter, from_three.at[lax.rem(block, SLOTS)])
        claim(0)
        x_four(block).start()

    def x_end_five(block):
        x_four(block).wait_recv()
        claim(1)
        x_five(block).start()

    def x_mid_five(block):
        x_four(block).wait_send()
        claim(1)
        x_five(block).start()

    def x_six(block):
        x_five(block).wait_send()
        x_five_in(block).wait_recv()
        claim(2)
        core_six(block).start()

    def z_end_two(block):
        z_one(block).wait_send()
        free(1, pos.zp)

    def z_end_six(block):
        z_five(block).wait_recv()
        claim(2)
        core_six(block).start()

    def z_mid_two(block):
        z_one(block).wait_recv()
        add(block, half, half, from_one.at[lax.rem(block, SLOTS)])
        z_two(block).start()

    def z_mid_three(block):
        z_two(block).wait()
        free(0, pos.zm)
        add(block, keep, quarter, from_two.at[lax.rem(block, SLOTS)])
        z_three(block).start()

    def z_mid_four(block):
        z_three(block).wait()
        add(block, keep, quarter, from_three.at[lax.rem(block, SLOTS)])
        claim(0)
        z_four(block).start()

    def z_mid_five(block):
        z_four(block).wait_send()
        z_four_in(block).wait_recv()
        claim(1)
        z_five(block).start()

    def z_mid_six(block):
        z_five(block).wait_send()
        claim(2)
        core_six(block).start()

    def last(block):
        core_six(block).wait_send()
        core_six_in(block).wait_recv()

    roles = (
        (x_first & pos.end, (start_core, send_x, x_end_two, x_end_three, None, x_end_five, x_six, last)),
        (x_first & pos.mid, (start_core, send_x, take_x, x_mid_three, x_mid_four, x_mid_five, x_six, last)),
        (z_first & pos.end, (start_core, send_z, z_end_two, None, None, None, z_end_six, last)),
        (z_first & pos.mid, (start_core, take_core, z_mid_two, z_mid_three, z_mid_four, z_mid_five, z_mid_six, last)),
    )
    depth = len(roles[0][1])

    def tick(step):
        for here, stages in roles:

            @pl.when(here)
            def _(stages=stages):
                for index in reversed(range(depth)):
                    block = step - SPREAD * index
                    if stages[index] is not None:

                        @pl.when((block >= 0) & (block < count))
                        def _(index=index, block=block, stages=stages):
                            stages[index](block)

        over = step - SPREAD * (depth - 1)

        @pl.when((over >= 0) & (over < count))
        def _():
            finish(over)

    return tick


def sum_scratch():
    return [
        pltpu.VMEM((SLOTS, BR // 2, BC), jnp.float32),
        pltpu.VMEM((SLOTS, BR // 2, BC), jnp.float32),
        pltpu.VMEM((SLOTS, BR // 4, BC), jnp.float32),
        pltpu.VMEM((SLOTS, BR // 4, BC), jnp.float32),
        pltpu.SemaphoreType.DMA((7, SLOTS)),
        pltpu.SemaphoreType.DMA((7, SLOTS)),
        pltpu.SemaphoreType.REGULAR((3,)),
    ]


CR, CC = 64, 384
CHUNKS = 24
RELAY = 3
BF = jnp.bfloat16


def gather_greet(pos, other):
    barrier = pltpu.get_barrier_semaphore()
    for where in ({"tensor": other}, {"dp": pos.xn}, {"dp": pos.zp}, {"dp": pos.sib}):
        pl.semaphore_signal(barrier, inc=1, device_id=where, device_id_type=MESH)


def gather_met():
    pl.semaphore_wait(pltpu.get_barrier_semaphore(), 4)


def chunk_parts(piece, chunk, kind):
    if kind == 0:
        return [(piece * 384 + chunk * 64, 64, 0, 0)]
    if kind == 1:
        return [(piece * 64 + (chunk - 6) * 32, 32, 384 * q, 32 * q) for q in range(2)]
    if kind == 2:
        return [(piece * 128 + (chunk - 8) * 16, 16, 384 * q, 16 * q) for q in range(4)]
    return [((chunk - 16) * 192 + piece * 32, 32, 384 * q, 32 * q) for q in range(2)]


BOUNDS = ((0, 6), (6, 8), (8, 16), (16, 24))
UNIT = (64, 32, 16, 32)


def make_gather(pos, own, theirs, staged, landed, sent, got):
    other = 1 - lax.axis_index("tensor")
    odd = lax.rem(pos.z, 2)
    ky = jnp.where(pos.x == 0, odd, 2)
    kx = jnp.where(pos.x == 0, 2, odd)
    kz = 1 - odd
    piece_y = 2 * ky + pos.core
    piece_x = 2 * kx + pos.core
    piece_z = 2 * kz + pos.core
    sib_y = 2 * ky + 1 - pos.core
    sib_x = 2 * kx + 1 - pos.core
    sib_z = 2 * kz + 1 - pos.core

    def copy(lane, chunk, source, piece, where):
        return pltpu.make_async_remote_copy(
            src_ref=source,
            dst_ref=landed.at[piece, chunk],
            send_sem=sent.at[lane, chunk],
            recv_sem=got.at[lane, chunk],
            device_id=where,
            device_id_type=MESH,
        )

    def over_y(chunk):
        return copy(0, chunk, staged.at[chunk], piece_y, {"tensor": other})

    def over_x(chunk, piece):
        return copy(1, chunk, landed.at[piece, chunk], piece, {"dp": pos.xn})

    def over_z(chunk, piece):
        return copy(2, chunk, landed.at[piece, chunk], piece, {"dp": pos.zp})

    def over_core(lane, chunk, piece):
        return copy(lane, chunk, landed.at[piece, chunk], piece, {"dp": pos.sib})

    def stage_own(kind):
        lo, hi = BOUNDS[kind]

        @pl.loop(lo, hi)
        def _(chunk):
            for row, rows, column, at in chunk_parts(piece_y, chunk, kind):
                staged[chunk, pl.ds(at, rows)] = own[kind][
                    pl.ds(pl.multiple_of(row, UNIT[kind]), rows), pl.ds(column, CC)
                ].astype(jnp.float32)

    def send_own(kind):
        lo, hi = BOUNDS[kind]

        @pl.loop(lo, hi)
        def _(chunk):
            over_y(chunk).start()

    def unpack(chunk):
        for kind in range(4):
            lo, hi = BOUNDS[kind]

            @pl.when((chunk >= lo) & (chunk < hi))
            def _(kind=kind):
                @pl.loop(0, 6)
                def _(piece):
                    for row, rows, column, at in chunk_parts(piece, chunk, kind):
                        theirs[kind][pl.ds(pl.multiple_of(row, UNIT[kind]), rows), pl.ds(column, CC)] = landed[
                            piece, chunk, pl.ds(at, rows)
                        ].astype(BF)

    def guarded(chunk, body):
        @pl.when((chunk >= 0) & (chunk < CHUNKS))
        def _():
            body(chunk)

    def first(chunk):
        over_y(chunk).wait_recv()
        over_x(chunk, piece_y).start()

        @pl.when(pos.x == 0)
        def _():
            over_z(chunk, piece_y).start()

        over_core(3, chunk, piece_y).start()

    def second(chunk):
        over_x(chunk, piece_x).wait_recv()

        @pl.when(pos.x == 1)
        def _():
            over_z(chunk, piece_x).start()

        over_core(4, chunk, piece_x).start()

    def third(chunk):
        over_z(chunk, piece_z).wait_recv()
        over_core(5, chunk, piece_z).start()

    def fourth(chunk):
        over_core(3, chunk, sib_y).wait_recv()
        over_core(4, chunk, sib_x).wait_recv()
        over_core(5, chunk, sib_z).wait_recv()
        over_y(chunk).wait_send()
        over_x(chunk, piece_y).wait_send()
        over_z(chunk, piece_y).wait_send()
        over_core(3, chunk, piece_y).wait_send()
        over_core(4, chunk, piece_x).wait_send()
        over_core(5, chunk, piece_z).wait_send()
        unpack(chunk)

    def tick(step):
        guarded(step - 3 * RELAY, fourth)
        guarded(step - 2 * RELAY, third)
        guarded(step - RELAY, second)
        guarded(step, first)

    return stage_own, send_own, tick


GATHER_TICKS = CHUNKS + 3 * RELAY


def gather_scratch():
    return [
        pltpu.VMEM((CHUNKS, CR, CC), jnp.float32),
        pltpu.VMEM((6, CHUNKS, CR, CC), jnp.float32),
        pltpu.SemaphoreType.DMA((6, CHUNKS)),
        pltpu.SemaphoreType.DMA((6, CHUNKS)),
    ]


def swap_small(small, small_out, sems):
    return pltpu.make_async_remote_copy(
        src_ref=small,
        dst_ref=small_out,
        send_sem=sems.at[0],
        recv_sem=sems.at[1],
        device_id={"tensor": 1 - lax.axis_index("tensor")},
        device_id_type=MESH,
    )


HD = 64
SEG = 148
MEMW = 10
F32 = jnp.float32
EPSILON = 1e-12
MASKED = -1e30
WIN = 160
MEMP = 96
SEGS = 8
PAIR = 2 * HD

CONTRACT_LAST = (((1,), (1,)), ((), ()))
CONTRACT_FIRST = (((0,), (0,)), ((), ()))


def mm(a, b):
    return jnp.dot(a, b, preferred_element_type=F32)


def mm_t(a, b):
    return lax.dot_general(a, b, CONTRACT_LAST, preferred_element_type=F32)


def t_mm(a, b):
    return lax.dot_general(a, b, CONTRACT_FIRST, preferred_element_type=F32)


def build_masks(parent, base, colbias):
    lane = lax.broadcasted_iota(jnp.int32, (1, WIN + MEMP), 1)
    in_mem = [
        ((lane >= WIN + MEMW * t) & (lane < WIN + MEMW * (t + 1))).astype(F32) for t in range(SEGS)
    ]
    reach = [jnp.zeros((1, WIN + MEMP), F32)]
    for s in range(1, SEGS):
        row = jnp.zeros((1, WIN + MEMP), F32)
        for t in range(s):
            hit = jnp.where(parent[s] - base == t, 1.0, 0.0)
            row = row + hit * jnp.maximum(reach[t], in_mem[t])
        reach.append(row)
    for s in range(SEGS):
        off = 4 * (s % 4)
        inside = ((lane >= off) & (lane < off + SEG)).astype(F32)
        colbias[s : s + 1, :] = jnp.where(jnp.maximum(inside, reach[s]) > 0.0, 0.0, MASKED)


def build_select(slots, select):
    row = lax.broadcasted_iota(jnp.int32, (select.shape[0], 1), 0)
    where = jnp.full((select.shape[0], 1), -1, jnp.int32)
    for t in range(SEGS):
        for m in range(MEMW):
            where = jnp.where(row == MEMW * t + m, slots[t, m] + SEG * t, where)
    place = lax.broadcasted_iota(jnp.int32, select.shape, 1)
    select[...] = (where == place).astype(F32).astype(BF)


def window(s):
    return pl.multiple_of(144 * s + 16 * (s // 4), 16), 4 * lax.rem(s, 4)


def lane_halves():
    lane = lax.broadcasted_iota(jnp.int32, (1, PAIR), 1)
    left = (lane < HD).astype(F32)
    return left.astype(BF), (1.0 - left).astype(BF), lane < HD


def valid_rows(off):
    row = lax.broadcasted_iota(jnp.int32, (WIN, 1), 0)
    return row, (row >= off) & (row < off + SEG)


def softmax_parts(qs, kk, bias):
    scores = mm_t(qs, kk) * HD ** (-0.5) + bias
    top = jnp.max(scores, axis=-1, keepdims=True)
    raised = jnp.exp(scores - top)
    return raised, 1.0 / jnp.sum(raised, axis=-1, keepdims=True)


def attend_pair(q, k, v, kmem, vmem, colbias, mixed, probs, s, columns):
    left, right, is_left = lane_halves()
    at, off = window(s)
    rows = pl.ds(at, WIN)
    qw = q[rows, columns]
    qs = jnp.concatenate([qw * left, qw * right], axis=0)
    kk = jnp.concatenate([k[rows, columns], kmem[:, columns]], axis=0)
    vv = jnp.concatenate([v[rows, columns], vmem[:, columns]], axis=0)
    raised, scale = softmax_parts(qs, kk, colbias[pl.ds(s, 1), :])
    row, valid = valid_rows(off)
    keep = jnp.where(valid, 1.0, 0.0)
    chances = (raised * (scale * jnp.concatenate([keep, keep], axis=0))).astype(BF)
    probs[...] = chances
    both = mm(chances, vv)
    out = jnp.where(is_left, both[:WIN], both[WIN:])
    old = mixed[rows, columns].astype(F32)
    mixed[rows, columns] = jnp.where(row >= off, out, old).astype(BF)


def attend_back_pair(q, k, v, kmem, vmem, probs, dmix, dq, dk, dv, dkmem, dvmem, s, columns):
    left, right, is_left = lane_halves()
    at, off = window(s)
    rows = pl.ds(at, WIN)
    qw = q[rows, columns]
    qs = jnp.concatenate([qw * left, qw * right], axis=0)
    kk = jnp.concatenate([k[rows, columns], kmem[:, columns]], axis=0)
    vv = jnp.concatenate([v[rows, columns], vmem[:, columns]], axis=0)
    dw = dmix[rows, columns]
    ds_in = jnp.concatenate([dw * left, dw * right], axis=0)
    low = probs[...]
    chances = low.astype(F32)
    dp = mm_t(ds_in, vv)
    inner = jnp.sum(chances * dp, axis=-1, keepdims=True)
    ds = (chances * (dp - inner)).astype(BF)
    dqs = mm(ds, kk)
    row, valid = valid_rows(off)
    new = jnp.where(is_left, dqs[:WIN], dqs[WIN:]) * HD ** (-0.5)
    old = dq[rows, columns].astype(F32)
    dq[rows, columns] = jnp.where(row >= off, new, old).astype(BF)
    dks = t_mm(ds, qs)
    dvs = t_mm(low, ds_in)
    dk[rows, columns] = dk[rows, columns] + dks[:WIN]
    dv[rows, columns] = dv[rows, columns] + dvs[:WIN]
    dkmem[:, columns] = dkmem[:, columns] + dks[WIN:]
    dvmem[:, columns] = dvmem[:, columns] + dvs[WIN:]


def spread(select, part):
    high = part.astype(BF)
    low = (part - high.astype(F32)).astype(BF)
    return t_mm(select, high) + t_mm(select, low)


def norm_stats(values):
    centered = values - jnp.mean(values, axis=-1, keepdims=True)
    inverse = lax.rsqrt(jnp.mean(centered * centered, axis=-1, keepdims=True) + EPSILON)
    return centered * inverse, inverse


def norm_back(grad, normed, inverse, gain):
    scaled = grad * gain
    return inverse * (
        scaled
        - jnp.mean(scaled, axis=-1, keepdims=True)
        - normed * jnp.mean(scaled * normed, axis=-1, keepdims=True)
    )


def gelu_parts(inner):
    phi = 0.5 + 0.5 * lax.erf(inner * (0.5**0.5))
    density = jnp.exp(-0.5 * inner * inner) * (2.0 * jnp.pi) ** -0.5
    return (inner * phi).astype(BF), (phi + inner * density).astype(BF)


def flat_row(ref, start, size):
    return ref[pl.ds(start, size)].reshape(1, size)


TILE = 128


SPLIT = 6 * TILE


def row_tiles(first, last, body):
    full = (last - first) // TILE

    @pl.loop(0, full)
    def _(i):
        body(pl.ds(pl.multiple_of(first + i * TILE, TILE), TILE))

    if (last - first) % TILE:
        body(pl.ds(first + full * TILE, (last - first) % TILE))


def forward_kernel(
    fast,
    parent,
    slots,
    bias_qv,
    bias_out,
    gain_one,
    shift_one,
    bias_up,
    bias_down,
    gain_two,
    shift_two,
    tokens_h,
    grad_h,
    qkv_in,
    out_in,
    up_in,
    down_in,
    *rest,
):
    count = 0 if fast else 5
    given, outs, rest = rest[:count], rest[count : count + 18], rest[count + 18 :]
    (
        output_h,
        their_qkv_h,
        their_out_h,
        their_up_h,
        their_down_h,
        qkv_h,
        mixed_h,
        normed_h,
        inverse,
        hidden_h,
        acted_h,
        slope_own_h,
        slope_their_h,
        d_two_h,
        d_ffn_h,
        vec,
        probs_h,
        select,
    ) = outs
    (
        tokens,
        own_qkv,
        own_out,
        own_up,
        own_down,
        their_qkv,
        their_out,
        their_up,
        their_down,
        small,
        small_their,
        qkv,
        mixed,
        normed,
        hidden,
        acc_own,
        acc_their,
        acted,
        slopes,
        colbias,
        kmem,
        vmem,
        sums,
        probs,
        io_sem,
        slope_sem,
        probs_sem,
        *wires,
    ) = rest
    rows, depth = tokens.shape
    width = mixed.shape[2]
    units = acted.shape[1]
    theirs = (their_qkv, their_out, their_up, their_down)
    own = (own_qkv, own_out, own_up, own_down)

    def move(index, source, target):
        return pltpu.make_async_copy(source, target, io_sem.at[index])

    load_tokens = move(0, tokens_h, tokens)
    load_grad = move(1, grad_h, tokens)
    put_qkv = move(2, qkv, qkv_h)
    put_mixed = move(3, mixed.at[0], mixed_h)
    put_normed = move(4, normed, normed_h)
    put_hidden = move(5, hidden, hidden_h)
    put_acted = move(6, acted, acted_h)
    late = ((acc_own, d_two_h), (hidden, d_ffn_h), (tokens, output_h))
    put_late = [
        [move(7 + 3 * part + i, ref.at[rows_of], target.at[rows_of]) for i, (ref, target) in enumerate(late)]
        for part, rows_of in enumerate((pl.ds(0, SPLIT), pl.ds(SPLIT, rows - SPLIT)))
    ]
    put_theirs = [
        move(13 + i, ref, target)
        for i, (ref, target) in enumerate(zip(theirs, (their_qkv_h, their_out_h, their_up_h, their_down_h)))
    ]
    load_own = [move(17 + i, a, b) for i, (a, b) in enumerate(zip((qkv_in, out_in, up_in, down_in), own))]
    if fast:
        pos = Place()
        gather_greet(pos, 1 - lax.axis_index("tensor"))
    load_own[0].start()
    load_tokens.start()
    for copy in load_own[1:]:
        copy.start()
    done = [0]
    small[...] = jnp.zeros(small.shape, F32)
    small[0:1, :] = bias_qv[0:1, :]
    small[2:3, :] = bias_qv[1:2, :]
    for c in range(units // CHUNK):
        small[3 + c : 4 + c, 0:CHUNK] = flat_row(bias_up, c * CHUNK, CHUNK)
    if fast:
        small_sem, *wires = wires
        stage_own, send_own, tick = make_gather(pos, own, theirs, *wires)
        load_own[0].wait()
        stage_own(0)
        gather_met()
        send_own(0)
        swap = swap_small(small, small_their, small_sem)
        swap.start()
        for kind in range(1, 4):
            load_own[kind].wait()
            stage_own(kind)
            send_own(kind)
    else:
        for copy in load_own:
            copy.wait()
        copies = [move(13 + i, a, b) for i, (a, b) in enumerate(zip(given, theirs + (small_their,)))]
        for copy in copies:
            copy.start()
        for copy in copies:
            copy.wait()

        def tick(step):
            pass

    def ticks(index, each, trips):
        for i in range(each):
            tick(done[0] + index * each + i)

    def tick_every(index, every, trips):
        @pl.when(lax.rem(index, every) == 0)
        def _():
            tick(done[0] + index // every)

        return -(-trips // every)

    def until(count):
        if done[0] < count:

            @pl.loop(done[0], count)
            def _(step):
                tick(step)

            done[0] = count

    build_masks(parent, lax.axis_index("dp") * SEGS, colbias)
    build_select(slots, select)
    load_tokens.wait()
    pairs = width // PAIR
    for half in range(2):
        weights = (own_qkv, their_qkv)[half]
        table = (small, small_their)[half]
        if half == 1:
            until(BOUNDS[0][1] + 3 * RELAY)
            if fast:
                swap.wait()

        @pl.loop(0, 3)
        def _(c, half=half, weights=weights, table=table):
            part = mm(tokens[...], weights[pl.ds(pl.multiple_of(c * depth, depth), depth), :])
            qkv[half, c] = (part + table[pl.ds(c, 1), :]).astype(BF)

        q, k, v = (qkv.at[half, i] for i in range(3))
        kmem[...] = mm(select[...], k[...]).astype(BF)
        vmem[...] = mm(select[...], v[...]).astype(BF)

        def put_probs(s, half=half):
            slot = lax.rem(s, 2)
            return pltpu.make_async_copy(probs.at[slot], probs_h.at[half, s], probs_sem.at[slot])

        @pl.loop(0, SEGS)
        def _(s, half=half, q=q, k=k, v=v, put_probs=put_probs):
            @pl.when(s >= 2)
            def _():
                put_probs(s - 2).wait()

            for pair in range(pairs):
                attend_pair(
                    q, k, v, kmem, vmem, colbias, mixed.at[half], probs.at[lax.rem(s, 2), pair], s, pl.ds(pair * PAIR, PAIR)
                )
                if pair == 0 and half == 0:
                    tick(done[0] + s)
                if pair == 2 and half == 1:
                    tick_every(s, GATHER[0], SEGS)
            put_probs(s).start()

        done[0] += SEGS if half == 0 else -(-SEGS // GATHER[0])
        put_probs(SEGS - 2).wait()
        put_probs(SEGS - 1).wait()

        if half == 1:
            until(BOUNDS[1][1] + 3 * RELAY)
        out = (own_out, their_out)[half]

        @pl.loop(0, 3)
        def _(n, half=half, out=out):
            columns = pl.ds(pl.multiple_of(n * CHUNK, CHUNK), CHUNK)
            part = mm(mixed[half], out[:, columns])
            acc_own[:, columns] = part if half == 0 else acc_own[:, columns] + part
            ticks(n, GATHER[1 + half], 3)

        done[0] += 3 * GATHER[1 + half]
    put_qkv.start()
    put_mixed.start()

    def norm_one(span):
        resid = tokens[span, :].astype(F32) + (acc_own[span, :] + flat_row(bias_out, 0, depth))
        unit, scale = norm_stats(resid)
        normed[span, :] = unit
        inverse[span, :] = scale
        hidden[span, :] = (unit * flat_row(gain_one, 0, depth) + flat_row(shift_one, 0, depth)).astype(BF)

    row_tiles(0, rows, norm_one)
    load_grad.start()
    put_normed.start()
    put_hidden.start()

    for half in range(2):
        up, down = ((own_up, own_down), (their_up, their_down))[half]
        table = (small, small_their)[half]
        slope_h = (slope_own_h, slope_their_h)[half]
        acc = (acc_own, acc_their)[half]

        def put_slope(c, slope_h=slope_h):
            span = pl.ds(pl.multiple_of(c * CHUNK, CHUNK), CHUNK)
            return pltpu.make_async_copy(slopes.at[lax.rem(c, 2)], slope_h.at[:, span], slope_sem.at[lax.rem(c, 2)])

        if half == 1:
            until(BOUNDS[2][1] + 3 * RELAY)
            put_acted.wait()
            put_slope(4).wait()
            put_slope(5).wait()

        @pl.loop(0, 6)
        def _(c, half=half, up=up, table=table, put_slope=put_slope):
            span = pl.ds(pl.multiple_of(c * CHUNK, CHUNK), CHUNK)

            @pl.when(c >= 2)
            def _():
                put_slope(c - 2).wait()

            bias = table[pl.ds(3 + c, 1), 0:CHUNK]
            act, steep = gelu_parts(mm(hidden[...], up[:, span]) + bias)
            acted[:, span] = act
            slopes[lax.rem(c, 2)] = steep
            put_slope(c).start()
            tick_every(c, GATHER[3 + 2 * half], 6)

        done[0] += -(-6 // GATHER[3 + 2 * half])
        low, high = slice(0, units // 2), slice(units // 2, units)
        if half == 0:
            put_acted.start()

            @pl.loop(0, 3)
            def _(n, down=down, acc=acc):
                columns = pl.ds(pl.multiple_of(n * CHUNK, CHUNK), CHUNK)
                acc[:, columns] = mm(acted[:, low], down[low, columns]) + mm(acted[:, high], down[high, columns])
                ticks(n, GATHER[4], 3)

        else:
            until((BOUNDS[3][0] + BOUNDS[3][1]) // 2 + 3 * RELAY)

            @pl.loop(0, 3)
            def _(n, down=down, acc=acc):
                columns = pl.ds(pl.multiple_of(n * CHUNK, CHUNK), CHUNK)
                acc[:, columns] = mm(acted[:, low], down[low, columns])
                ticks(n, 1, 3)

            done[0] += 3
            until(BOUNDS[3][1] + 3 * RELAY)
            if fast:
                for copy in put_theirs:
                    copy.start()

            @pl.loop(0, 3)
            def _(n, down=down, acc=acc):
                columns = pl.ds(pl.multiple_of(n * CHUNK, CHUNK), CHUNK)
                acc[:, columns] = acc[:, columns] + mm(acted[:, high], down[high, columns])

        done[0] += 3 * GATHER[4] if half == 0 else 0
    put_slope(4).wait()
    put_slope(5).wait()

    load_grad.wait()
    put_hidden.wait()
    sums[...] = jnp.zeros(sums.shape, F32)

    def norm_two(span):
        first = normed[span, :] * flat_row(gain_one, 0, depth) + flat_row(shift_one, 0, depth)
        resid = first + ((acc_own[span, :] + acc_their[span, :]) + flat_row(bias_down, 0, depth))
        unit, scale = norm_stats(resid)
        grad = tokens[span, :].astype(F32)
        tokens[span, :] = (unit * flat_row(gain_two, 0, depth) + flat_row(shift_two, 0, depth)).astype(BF)
        back = norm_back(grad, unit, scale, flat_row(gain_two, 0, depth))
        acc_own[span, :] = back
        low = back.astype(BF)
        hidden[span, :] = low
        for index, value in enumerate((low.astype(F32), grad * unit, grad)):
            sums[index] = sums[index] + value.reshape(-1, 8, depth).sum(axis=0)

    row_tiles(0, SPLIT, norm_two)
    for copy in put_late[0]:
        copy.start()
    row_tiles(SPLIT, rows, norm_two)
    for copy in put_late[1]:
        copy.start()
    for index in range(3):
        total = jnp.sum(sums[index], axis=0, keepdims=True)
        for j in range(6):
            vec[6 * index + j : 6 * index + j + 1, :] = total[:, BC * j : BC * (j + 1)]
    for copy in (put_qkv, put_mixed, put_normed, *put_late[0], *put_late[1]):
        copy.wait()
    if fast:
        for copy in put_theirs:
            copy.wait()


GATHER = (2, 1, 1, 2, 1, 2)


def forward(fast, parent, slots, vectors, tokens, grad_out, own, given):
    rows, depth = tokens.shape
    width = own[0].shape[1]
    units = own[2].shape[1]
    vm = pl.BlockSpec(memory_space=pltpu.VMEM)
    hbm = pl.BlockSpec(memory_space=pl.ANY)
    sm = pl.BlockSpec(memory_space=pltpu.SMEM)
    sd = jax.ShapeDtypeStruct
    out_shape = [
        sd((rows, depth), BF),
        *[sd(w.shape, BF) for w in own],
        sd((2, 3, rows, width), BF),
        sd((rows, width), BF),
        sd((rows, depth), F32),
        sd((rows, 1), F32),
        sd((rows, depth), BF),
        sd((rows, units), BF),
        sd((rows, units), BF),
        sd((rows, units), BF),
        sd((rows, depth), F32),
        sd((rows, depth), BF),
        sd((18, BC), F32),
        sd((2, SEGS, width // PAIR, 2 * WIN, WIN + MEMP), BF),
        sd((MEMP, rows), BF),
    ]
    return pl.pallas_call(
        functools.partial(forward_kernel, fast),
        out_shape=out_shape,
        in_specs=[sm, sm] + [vm] * len(vectors) + [hbm, hbm] + [hbm] * (4 + len(given)),
        out_specs=[hbm] * 8 + [vm] + [hbm] * 6 + [vm, hbm, vm],
        scratch_shapes=[
            pltpu.VMEM((rows, depth), BF),
            *[pltpu.VMEM(w.shape, BF) for w in own],
            *[pltpu.VMEM(w.shape, BF) for w in own],
            pltpu.VMEM((16, width), F32),
            pltpu.VMEM((16, width), F32),
            pltpu.VMEM((2, 3, rows, width), BF),
            pltpu.VMEM((2, rows, width), BF),
            pltpu.VMEM((rows, depth), F32),
            pltpu.VMEM((rows, depth), BF),
            pltpu.VMEM((rows, depth), F32),
            pltpu.VMEM((rows, depth), F32),
            pltpu.VMEM((rows, units), BF),
            pltpu.VMEM((2, rows, CHUNK), BF),
            pltpu.VMEM((SEGS, WIN + MEMP), F32),
            pltpu.VMEM((MEMP, width), BF),
            pltpu.VMEM((MEMP, width), BF),
            pltpu.VMEM((3, 8, depth), F32),
            pltpu.VMEM((2, width // PAIR, 2 * WIN, WIN + MEMP), BF),
            pltpu.SemaphoreType.DMA((21,)),
            pltpu.SemaphoreType.DMA((2,)),
            pltpu.SemaphoreType.DMA((2,)),
        ]
        + ([pltpu.SemaphoreType.DMA((2,))] + gather_scratch() if fast else []),
        compiler_params=pltpu.CompilerParams(
            collective_id=0 if fast else None, has_side_effects=fast, vmem_limit_bytes=67043328
        ),
        name="forward",
    )(parent, slots, *vectors, tokens, grad_out, *own, *given)


DOWN, UP, OUT, QKV, VEC = 0, 24, 48, 54, 72
COUNT = 73
CHUNK = 256
VEC_ROWS = 54


def backward_kernel(
    fast,
    select,
    inverse,
    gain,
    vec_in,
    tokens_h,
    hidden_h,
    d_ffn_h,
    d_two_h,
    normed_h,
    acted_h,
    slope_own_h,
    slope_their_h,
    qkv_h,
    mixed_h,
    probs_h,
    w_up_own,
    w_up_their,
    w_down_own,
    w_down_their,
    w_out_own,
    w_out_their,
    w_qkv_own,
    w_qkv_their,
    g_qkv,
    g_out,
    g_up,
    g_down,
    g_vec,
    g_tokens,
    grads,
    d_low,
    hidden,
    d_res,
    normed,
    acc_own,
    acc_their,
    a_buf,
    slope_buf,
    up_buf,
    down_buf,
    d_inner,
    sums,
    tokens,
    mixed,
    w_out,
    w_qkv,
    qkv,
    d_qkv,
    d_mixed,
    probs,
    kmem,
    vmem,
    dkm,
    dvm,
    load_sem,
    chunk_sem,
    put_sem,
    probs_sem,
    *wires,
):
    rows, depth = tokens.shape
    width = mixed.shape[1]

    def fetch(index, source, target):
        return pltpu.make_async_copy(source, target, load_sem.at[index])

    load_d = fetch(0, d_ffn_h, d_low)
    load_hidden = fetch(1, hidden_h, hidden)
    load_two = fetch(2, d_two_h, d_res)
    load_normed = fetch(3, normed_h, normed)
    load_mixed = fetch(4, mixed_h, mixed)
    load_out = [fetch(5 + i, w, w_out.at[i]) for i, w in enumerate((w_out_own, w_out_their))]
    load_w = [fetch(7 + i, w, w_qkv.at[i]) for i, w in enumerate((w_qkv_own, w_qkv_their))]
    load_tokens = fetch(9, tokens_h, tokens)
    load_qkv = [fetch(10 + half, qkv_h.at[half], qkv) for half in range(2)]
    put_tokens = fetch(12, d_low, g_tokens)

    def load_acted(c):
        return pltpu.make_async_copy(acted_h.at[:, pl.ds(pl.multiple_of(c * BR, BR), BR)], a_buf.at[lax.rem(c, 2)], chunk_sem.at[0, lax.rem(c, 2)])

    def load_chunk(half, c):
        slot = lax.rem(c, 2)
        span = pl.ds(pl.multiple_of(c * CHUNK, CHUNK), CHUNK)
        slope_h, up_h, down_h = ((slope_own_h, w_up_own, w_down_own), (slope_their_h, w_up_their, w_down_their))[half]
        return (
            pltpu.make_async_copy(slope_h.at[:, span], slope_buf.at[slot], chunk_sem.at[1, slot]),
            pltpu.make_async_copy(up_h.at[:, span], up_buf.at[slot], chunk_sem.at[2, slot]),
            pltpu.make_async_copy(down_h.at[span, :], down_buf.at[slot], chunk_sem.at[3, slot]),
        )

    def load_probs(half, s):
        slot = lax.rem(s, 2)
        return pltpu.make_async_copy(probs_h.at[half, s], probs.at[slot], probs_sem.at[slot])

    def start(copies):
        for copy in copies:
            copy.start()

    def wait(copies):
        for copy in copies:
            copy.wait()

    if fast:
        pos = Place()
        sum_greet(pos)
    load_d.start()
    load_acted(0).start()
    start(load_chunk(0, 0))
    load_hidden.start()
    load_two.start()
    load_normed.start()
    load_mixed.start()
    start(load_out)
    start(load_w)
    load_tokens.start()
    load_qkv[0].start()
    load_probs(0, 0).start()

    def put(block, target):
        return pltpu.make_async_copy(grads.at[block], target, put_sem.at[lax.rem(block, 8)])

    def wait_put(block):
        put(block, g_vec).wait()

    def finish(block):
        @pl.when(block >= 8)
        def _():
            wait_put(block - 8)

        def at(row, column):
            return pl.ds(pl.multiple_of(row, BR), BR), pl.ds(pl.multiple_of(column, BC), BC)

        @pl.when(block < UP)
        def _():
            put(block, g_down.at[at(BR * (block // 6), BC * lax.rem(block, 6))]).start()

        @pl.when((block >= UP) & (block < OUT))
        def _():
            i = block - UP
            put(block, g_up.at[at(BR * lax.rem(i // 2, 2), CHUNK * (i // 4) + BC * lax.rem(i, 2))]).start()

        @pl.when((block >= OUT) & (block < QKV))
        def _():
            put(block, g_out.at[at(0, BC * (block - OUT))]).start()

        @pl.when((block >= QKV) & (block < VEC))
        def _():
            i = block - QKV
            put(block, g_qkv.at[at(BR * (i // 3), BC * lax.rem(i, 3))]).start()

        @pl.when(block == VEC)
        def _():
            put(block, g_vec).start()

    if fast:
        tick = make_tick(pos, grads, *wires, COUNT, finish)
        last = COUNT + 7 * SPREAD
    else:

        def tick(step):
            @pl.when(step < COUNT)
            def _():
                finish(step)

        last = COUNT
    done = [0]

    def ticks(index, each, trips):
        for i in range(each):
            tick(done[0] + index * each + i)
        return trips * each

    grads[VEC] = jnp.zeros((BR, BC), F32)
    grads[VEC, 36:54] = vec_in[...]
    acc_own[...] = jnp.zeros(acc_own.shape, F32)
    acc_their[...] = jnp.zeros(acc_their.shape, F32)
    sums[...] = jnp.zeros(sums.shape, F32)
    if fast:
        sum_met(pos)

    load_d.wait()

    @pl.loop(0, 4)
    def _(c):
        load_acted(c).wait()

        @pl.when(c < 3)
        def _():
            load_acted(c + 1).start()

        for part in range(2):
            piece = t_mm(a_buf[lax.rem(c, 2)], d_low[:, part * width : (part + 1) * width])
            for j in range(3):
                grads[DOWN + 6 * c + 3 * part + j] = piece[:, BC * j : BC * (j + 1)]
        ticks(c, TICKS[0], 4)

    done[0] += 4 * TICKS[0]

    load_hidden.wait()
    for half in range(2):
        acc = (acc_own, acc_their)[half]

        @pl.loop(0, 6)
        def _(c, half=half, acc=acc):
            slot = lax.rem(c, 2)
            wait(load_chunk(half, c))

            @pl.when(c < 5)
            def _():
                start(load_chunk(half, c + 1))

            if half == 0:

                @pl.when(c == 5)
                def _():
                    start(load_chunk(1, 0))

            each = TICKS[1 + half]
            d_inner[...] = (mm_t(d_low[...], down_buf[slot]) * slope_buf[slot].astype(F32)).astype(BF)
            if each > 1:
                tick(done[0] + c * each)
            if half == 0:
                piece = t_mm(hidden[...], d_inner[...])
                for r in range(2):
                    for j in range(2):
                        grads[UP + 4 * c + 2 * r + j] = piece[BR * r : BR * (r + 1), BC * j : BC * (j + 1)]
                total = jnp.sum(d_inner[...].astype(F32), axis=0, keepdims=True)
                for j in range(2):
                    grads[VEC, pl.ds(6 + 2 * c + j, 1), :] = total[:, BC * j : BC * (j + 1)]
                if each > 2:
                    tick(done[0] + c * each + 1)
            for part in range(3):
                columns = slice(CHUNK * part, CHUNK * (part + 1))
                acc[:, columns] = acc[:, columns] + mm_t(d_inner[...], up_buf[slot, columns, :])
            tick(done[0] + c * each + each - 1)

        done[0] += 6 * TICKS[1 + half]

    load_two.wait()
    load_normed.wait()
    tile = 32
    trips = rows // tile

    @pl.loop(0, trips)
    def _(i):
        span = pl.ds(pl.multiple_of(i * tile, tile), tile)
        total = d_res[span, :] + (acc_own[span, :] + acc_their[span, :])
        unit = normed[span, :]
        one = norm_back(total, unit, inverse[span, :], flat_row(gain, 0, depth))
        d_res[span, :] = one
        low = one.astype(BF)
        d_low[span, :] = low
        for index, value in enumerate((low.astype(F32), total * unit, total)):
            sums[index] = sums[index] + value.reshape(tile // 8, 8, depth).sum(axis=0)

        @pl.when(lax.rem(i, TICK_TILES) == 0)
        def _():
            tick(done[0] + i // TICK_TILES)

    done[0] += -(-trips // TICK_TILES)
    for index in range(3):
        total = jnp.sum(sums[index], axis=0, keepdims=True)
        for j in range(6):
            grads[VEC, 18 + 6 * index + j : 19 + 6 * index + j, :] = total[:, BC * j : BC * (j + 1)]

    load_mixed.wait()
    wait(load_out)

    @pl.loop(0, 2)
    def _(half):
        d_mixed[half] = mm_t(d_low[...], w_out[half]).astype(BF)
        piece = t_mm(mixed[...], d_low[:, pl.ds(pl.multiple_of(half * width, BC), width)])
        for j in range(3):
            grads[OUT + 3 * half + j] = piece[:, BC * j : BC * (j + 1)]
        ticks(half, TICKS[3], 2)

    done[0] += 2 * TICKS[3]

    wait(load_w)
    load_tokens.wait()
    pairs = width // PAIR
    dka, dva = acc_their.at[:, pl.ds(0, width)], acc_their.at[:, pl.ds(width, width)]
    for half in range(2):
        load_qkv[half].wait()
        q, k, v = (qkv.at[i] for i in range(3))
        kmem[...] = mm(select[...], k[...]).astype(BF)
        vmem[...] = mm(select[...], v[...]).astype(BF)
        acc_their[...] = jnp.zeros(acc_their.shape, F32)
        dkm[...] = jnp.zeros(dkm.shape, F32)
        dvm[...] = jnp.zeros(dvm.shape, F32)

        @pl.loop(0, SEGS * pairs)
        def _(spot, half=half):
            s, pair = spot // pairs, lax.rem(spot, pairs)

            @pl.when(pair == 0)
            def _():
                load_probs(half, s).wait()

                @pl.when(s < SEGS - 1)
                def _():
                    load_probs(half, s + 1).start()

                if half == 0:

                    @pl.when(s == SEGS - 1)
                    def _():
                        load_probs(1, 0).start()

            columns = pl.ds(pl.multiple_of(pair * PAIR, PAIR), PAIR)
            part = probs.at[lax.rem(s, 2), pair]
            attend_back_pair(q, k, v, kmem, vmem, part, d_mixed.at[half], d_qkv.at[0], dka, dva, dkm, dvm, s, columns)

            @pl.when(lax.rem(spot, TICKS[4 + half]) == 0)
            def _():
                tick(done[0] + spot // TICKS[4 + half])

        done[0] += -(-SEGS * pairs // TICKS[4 + half])
        if half == 0:
            assert done[0] <= QKV
        if half == 0:
            load_qkv[1].start()
        for pair in range(pairs):
            columns = pl.ds(pair * PAIR, PAIR)
            d_qkv[1, :, columns] = ((dka[:, columns] + spread(select[...], dkm[:, columns])) * HD ** (-0.5)).astype(BF)
            d_qkv[2, :, columns] = (dva[:, columns] + spread(select[...], dvm[:, columns])).astype(BF)
        if half == 0:

            @pl.loop(0, 3)
            def _(c):
                piece = t_mm(tokens[...], d_qkv[c])
                for r in range(2):
                    for j in range(3):
                        grads[QKV + 6 * c + 3 * r + j] = piece[BR * r : BR * (r + 1), BC * j : BC * (j + 1)]
                columns = pl.ds(pl.multiple_of(c * CHUNK, CHUNK), CHUNK)
                part = mm_t(d_qkv[0], w_qkv[half, pl.ds(pl.multiple_of(c * CHUNK, CHUNK), CHUNK), :])
                for i in (1, 2):
                    part = part + mm_t(d_qkv[i], w_qkv[half, pl.ds(pl.multiple_of(i * depth + c * CHUNK, CHUNK), CHUNK), :])
                acc_own[:, columns] = part
                ticks(c, TICKS[6], 3)

            done[0] += 3 * TICKS[6]
            for index, row in ((0, 0), (2, 3)):
                total = jnp.sum(d_qkv[index].astype(F32), axis=0, keepdims=True)
                for j in range(3):
                    grads[VEC, row + j : row + j + 1, :] = total[:, BC * j : BC * (j + 1)]
        else:

            @pl.loop(0, 3)
            def _(c):
                columns = pl.ds(pl.multiple_of(c * CHUNK, CHUNK), CHUNK)
                part = mm_t(d_qkv[0], w_qkv[half, pl.ds(pl.multiple_of(c * CHUNK, CHUNK), CHUNK), :])
                for i in (1, 2):
                    part = part + mm_t(d_qkv[i], w_qkv[half, pl.ds(pl.multiple_of(i * depth + c * CHUNK, CHUNK), CHUNK), :])
                d_low[:, columns] = ((acc_own[:, columns] + part) + d_res[:, columns]).astype(BF)
                ticks(c, TICKS[7], 3)

            done[0] += 3 * TICKS[7]
            put_tokens.start()
    @pl.loop(min(done[0], last), last)
    def _(step):
        tick(step)

    for block in range(COUNT - 8, COUNT):
        wait_put(block)
    put_tokens.wait()


TICKS = (1, 3, 2, 1, 2, 1, 3, 1)
TICK_TILES = 8


def backward(fast, select, inverse, gain, vec_in, arrays):
    tokens, acted, mixed = arrays[0], arrays[5], arrays[9]
    rows, depth = tokens.shape
    units = acted.shape[1]
    width = mixed.shape[1]
    vm = pl.BlockSpec(memory_space=pltpu.VMEM)
    hbm = pl.BlockSpec(memory_space=pl.ANY)
    sd = jax.ShapeDtypeStruct
    return pl.pallas_call(
        functools.partial(backward_kernel, fast),
        out_shape=[
            sd((3 * depth, width), F32),
            sd((width, depth), F32),
            sd((depth, units), F32),
            sd((units, depth), F32),
            sd((BR, BC), F32),
            sd((rows, depth), BF),
        ],
        in_specs=[vm, vm, vm, vm] + [hbm] * len(arrays),
        out_specs=[hbm] * 6,
        scratch_shapes=[
            pltpu.VMEM((COUNT, BR, BC), F32),
            pltpu.VMEM((rows, depth), BF),
            pltpu.VMEM((rows, depth), BF),
            pltpu.VMEM((rows, depth), F32),
            pltpu.VMEM((rows, depth), F32),
            pltpu.VMEM((rows, depth), F32),
            pltpu.VMEM((rows, depth), F32),
            pltpu.VMEM((2, rows, BR), BF),
            pltpu.VMEM((2, rows, CHUNK), BF),
            pltpu.VMEM((2, depth, CHUNK), BF),
            pltpu.VMEM((2, CHUNK, depth), BF),
            pltpu.VMEM((rows, CHUNK), BF),
            pltpu.VMEM((3, 8, depth), F32),
            pltpu.VMEM((rows, depth), BF),
            pltpu.VMEM((rows, width), BF),
            pltpu.VMEM((2, width, depth), BF),
            pltpu.VMEM((2, 3 * depth, width), BF),
            pltpu.VMEM((3, rows, width), BF),
            pltpu.VMEM((3, rows, width), BF),
            pltpu.VMEM((2, rows, width), BF),
            pltpu.VMEM((2, width // PAIR, 2 * WIN, WIN + MEMP), BF),
            pltpu.VMEM((MEMP, width), BF),
            pltpu.VMEM((MEMP, width), BF),
            pltpu.VMEM((MEMP, width), F32),
            pltpu.VMEM((MEMP, width), F32),
            pltpu.SemaphoreType.DMA((13,)),
            pltpu.SemaphoreType.DMA((4, 2)),
            pltpu.SemaphoreType.DMA((8,)),
            pltpu.SemaphoreType.DMA((2,)),
        ]
        + (sum_scratch() if fast else []),
        compiler_params=pltpu.CompilerParams(
            collective_id=1 if fast else None, has_side_effects=fast, vmem_limit_bytes=67043328
        ),
        name="backward",
    )(select, inverse, gain, vec_in, *arrays)


def results_kernel(count, vec, *refs):
    sources, rest = refs[:count], refs[count:]
    targets, rest = rest[:count], rest[count:]
    vectors, rest = rest[:8], rest[8:]
    buffers, (in_sem, out_sem) = rest[:count], rest[count:]
    pieces = []
    for i, source in enumerate(sources):
        rows = source.shape[0]
        parts = max(1, rows * source.shape[1] * source.dtype.itemsize // 2**20)
        while rows % parts or (rows // parts) % 16:
            parts -= 1
        size = rows // parts
        for part in range(parts):
            at = pl.ds(part * size, size)
            pieces.append((source.at[at], buffers[i].at[at], targets[i].at[at]))
    loads = [pltpu.make_async_copy(a, b, in_sem.at[i]) for i, (a, b, c) in enumerate(pieces)]
    stores = [pltpu.make_async_copy(b, c, out_sem.at[i]) for i, (a, b, c) in enumerate(pieces)]
    for load in loads:
        load.start()
    bias_qv, *flat = vectors
    for j in range(6):
        bias_qv[j // 3 : j // 3 + 1, BC * (j % 3) : BC * (j % 3 + 1)] = vec[j : j + 1, :]
    row = 6
    for ref in flat:
        for j in range(ref.shape[0] // BC):
            ref[pl.ds(BC * j, BC)] = vec[row, :]
            row += 1
    for load, store in zip(loads, stores):
        load.wait()
        store.start()
    for store in stores:
        store.wait()


def results(vec, large, width, units, depth):
    vm = pl.BlockSpec(memory_space=pltpu.VMEM)
    hbm = pl.BlockSpec(memory_space=pl.ANY)
    sd = jax.ShapeDtypeStruct
    small = [sd((2, width), F32), sd((units,), F32)] + [sd((depth,), F32)] * 6
    count = len(large)
    return pl.pallas_call(
        functools.partial(results_kernel, count),
        out_shape=[sd(a.shape, a.dtype) for a in large] + small,
        in_specs=[vm] + [hbm] * count,
        out_specs=[hbm] * count + [vm] * len(small),
        scratch_shapes=[pltpu.VMEM(a.shape, a.dtype) for a in large] + [pltpu.SemaphoreType.DMA((32,))] * 2,
        compiler_params=pltpu.CompilerParams(vmem_limit_bytes=60 * 2**20),
        name="results",
    )(vec, *large)


def halves_swap(own, small):
    unit = (lax.axis_index("dp") >= 0).astype(F32)

    def other(array):
        arrived = lax.ppermute(array.astype(F32), "tensor", [(0, 1), (1, 0)])
        return (arrived * unit).astype(array.dtype)

    return tuple(other(array) for array in own) + (other(small),)


def shards(
    fast,
    tokens,
    w_qkv,
    bias_qv,
    w_out,
    bias_out,
    gain_one,
    shift_one,
    w_up,
    bias_up,
    w_down,
    bias_down,
    gain_two,
    shift_two,
    grad_out,
    parent,
    mem_slots,
):
    depth, width = w_qkv.shape[1:]
    hidden_units = w_up.shape[1]
    own = (w_qkv.reshape(3 * depth, width), w_out, w_up, w_down)
    if fast:
        given = ()
    else:
        table = jnp.pad(bias_up.reshape(-1, CHUNK), ((0, 0), (0, width - CHUNK)))
        small = jnp.concatenate([bias_qv[:1], jnp.zeros((1, width), F32), bias_qv[1:], table])
        given = halves_swap(own, jnp.pad(small, ((0, 16 - small.shape[0]), (0, 0))))
    vectors = (bias_qv, bias_out, gain_one, shift_one, bias_up, bias_down, gain_two, shift_two)
    (
        output,
        *theirs,
        qkv,
        mixed,
        normed,
        inverse,
        hidden_low,
        acted,
        slope_own,
        slope_their,
        d_two,
        d_ffn,
        vec,
        probs,
        select,
    ) = forward(fast, parent, mem_slots, vectors, tokens, grad_out, own, given)
    if not fast:
        theirs = given[:4]
    arrays = (tokens, hidden_low, d_ffn, d_two, normed, acted, slope_own, slope_their, qkv, mixed, probs)
    weights = tuple(w[i] for i in (2, 3, 1, 0) for w in (own, theirs))
    g_w_qkv, g_w_out, g_w_up, g_w_down, flat, grad_tokens = backward(
        fast, select, inverse, gain_one, vec, arrays + weights
    )
    if not fast:
        g_w_qkv, g_w_out, g_w_up, g_w_down, flat = lax.psum((g_w_qkv, g_w_out, g_w_up, g_w_down, flat), "dp")
    (
        g_w_qkv,
        g_w_out,
        g_w_up,
        g_w_down,
        grad_tokens,
        output,
        g_bias_qv,
        g_bias_up,
        g_bias_out,
        g_gain_one,
        g_shift_one,
        g_bias_down,
        g_gain_two,
        g_shift_two,
    ) = results(flat, (g_w_qkv, g_w_out, g_w_up, g_w_down, grad_tokens, output), width, hidden_units, depth)
    return (
        output,
        grad_tokens,
        g_w_qkv.reshape(w_qkv.shape),
        g_bias_qv,
        g_w_out,
        g_bias_out,
        g_gain_one,
        g_shift_one,
        g_w_up,
        g_bias_up,
        g_w_down,
        g_bias_down,
        g_gain_two,
        g_shift_two,
    )


def solution(mesh):
    fast = mesh.shape["dp"] == 16 and mesh.shape["tensor"] == 2
    rows, whole = P("dp", None), P()
    return jax.shard_map(
        functools.partial(shards, fast),
        mesh=mesh,
        in_specs=(
            rows,
            P(None, None, "tensor"),
            P(None, "tensor"),
            P("tensor", None),
            whole,
            whole,
            whole,
            P(None, "tensor"),
            P("tensor"),
            P("tensor", None),
            whole,
            whole,
            whole,
            rows,
            P("dp"),
            rows,
        ),
        out_specs=(
            rows,
            rows,
            P(None, None, "tensor"),
            P(None, "tensor"),
            P("tensor", None),
            whole,
            whole,
            whole,
            P(None, "tensor"),
            P("tensor"),
            P("tensor", None),
            whole,
            whole,
            whole,
        ),
        check_vma=False,
    )
```

```python
import functools


import jax
import jax.numpy as jnp
from jax import lax
from jax.experimental import pallas as pl
from jax.experimental.pallas import tpu as pltpu
from jax.sharding import PartitionSpec as P


MESH = pl.DeviceIdType.MESH
BR, BC = 384, 128
SPREAD = 3
SLOTS = 16


class Place:
    def __init__(self):
        me = lax.axis_index("dp")
        self.core = lax.rem(me, 2)
        self.x = lax.rem(me // 2, 2)
        self.z = me // 4
        self.sib = me + 1 - 2 * self.core
        self.xn = me + 2 - 4 * self.x
        self.zp = me + 4 - 8 * lax.rem(self.z, 2)
        self.zm = me + 4 * (3 - 2 * self.z)
        self.end = (self.z == 0) | (self.z == 3)
        self.mid = (self.z == 1) | (self.z == 2)


def sum_greet(pos):
    barrier = pltpu.get_barrier_semaphore()

    def greet(dev):
        pl.semaphore_signal(barrier, inc=1, device_id={"dp": dev}, device_id_type=MESH)

    greet(pos.sib)
    greet(pos.xn)
    greet(pos.zp)

    @pl.when(pos.mid)
    def _():
        greet(pos.zm)


def sum_met(pos):
    pl.semaphore_wait(pltpu.get_barrier_semaphore(), jnp.where(pos.mid, 4, 3))


def make_tick(pos, grads, from_core, from_one, from_two, from_three, sent, got, credit, count, finish):
    half = BR // 2
    quarter = BR // 4

    def copy(stage, block, source, target, device):
        slot = lax.rem(block, SLOTS)
        return pltpu.make_async_remote_copy(
            src_ref=source,
            dst_ref=target,
            send_sem=sent.at[stage, slot],
            recv_sem=got.at[stage, slot],
            device_id={"dp": device},
            device_id_type=MESH,
        )

    def rows(block, start, size):
        return grads.at[block, pl.ds(pl.multiple_of(start, quarter), size)]

    def add(block, start, size, landed):
        where = pl.ds(pl.multiple_of(start, quarter), size)
        grads[block, where] = grads[block, where] + landed[...]

    def free(index, device):
        pl.semaphore_signal(credit.at[index], inc=1, device_id={"dp": device}, device_id_type=MESH)

    def claim(index):
        pl.semaphore_wait(credit.at[index], 1)

    x_first = pos.core == 0
    z_first = pos.core == 1
    mine = pos.core * half
    xrow = pos.x * quarter
    xrow_other = (1 - pos.x) * quarter
    far = lax.rem(pos.z, 2) == 0
    keep = half + jnp.where(far, quarter, 0)
    give = half + jnp.where(far, 0, quarter)

    def core_out(block):
        return copy(0, block, rows(block, (1 - pos.core) * half, half), from_core.at[lax.rem(block, SLOTS)], pos.sib)

    def x_one(block):
        return copy(1, block, rows(block, xrow_other, quarter), from_one.at[lax.rem(block, SLOTS), pl.ds(0, quarter)], pos.xn)

    def z_one(block):
        return copy(1, block, rows(block, half, half), from_one.at[lax.rem(block, SLOTS)], pos.zp)

    def x_two(block):
        return copy(2, block, rows(block, xrow, quarter), from_two.at[lax.rem(block, SLOTS)], pos.zp)

    def z_two(block):
        return copy(2, block, rows(block, give, quarter), from_two.at[lax.rem(block, SLOTS)], pos.zm)

    def x_three(block):
        return copy(3, block, rows(block, xrow, quarter), from_three.at[lax.rem(block, SLOTS)], pos.zm)

    def z_three(block):
        return copy(3, block, rows(block, keep, quarter), from_three.at[lax.rem(block, SLOTS)], pos.xn)

    def x_four(block):
        return copy(4, block, rows(block, xrow, quarter), rows(block, xrow, quarter), pos.zp)

    def z_four(block):
        return copy(4, block, rows(block, keep, quarter), rows(block, keep, quarter), pos.zm)

    def z_four_in(block):
        return copy(4, block, rows(block, give, quarter), rows(block, give, quarter), pos.zm)

    def x_five(block):
        return copy(5, block, rows(block, xrow, quarter), rows(block, xrow, quarter), pos.xn)

    def x_five_in(block):
        return copy(5, block, rows(block, xrow_other, quarter), rows(block, xrow_other, quarter), pos.xn)

    def z_five(block):
        return copy(5, block, rows(block, half, half), rows(block, half, half), pos.zp)

    def core_six(block):
        return copy(6, block, rows(block, mine, half), rows(block, mine, half), pos.sib)

    def core_six_in(block):
        return copy(6, block, rows(block, (1 - pos.core) * half, half), rows(block, (1 - pos.core) * half, half), pos.sib)

    def start_core(block):
        core_out(block).start()

    def take_core(block):
        core_out(block).wait()
        free(2, pos.sib)
        add(block, mine, half, from_core.at[lax.rem(block, SLOTS)])

    def take_x(block):
        x_one(block).wait()
        free(1, pos.xn)
        add(block, xrow, quarter, from_one.at[lax.rem(block, SLOTS), pl.ds(0, quarter)])

    def send_x(block):
        take_core(block)
        x_one(block).start()

    def send_z(block):
        take_core(block)
        z_one(block).start()

    def x_end_two(block):
        take_x(block)
        x_two(block).start()

    def x_end_three(block):
        x_two(block).wait_send()
        free(0, pos.zp)

    def x_mid_three(block):
        x_two(block).wait_recv()
        add(block, xrow, quarter, from_two.at[lax.rem(block, SLOTS)])
        x_three(block).start()

    def x_mid_four(block):
        x_three(block).wait()
        add(block, xrow, quarter, from_three.at[lax.rem(block, SLOTS)])
        claim(0)
        x_four(block).start()

    def x_end_five(block):
        x_four(block).wait_recv()
        claim(1)
        x_five(block).start()

    def x_mid_five(block):
        x_four(block).wait_send()
        claim(1)
        x_five(block).start()

    def x_six(block):
        x_five(block).wait_send()
        x_five_in(block).wait_recv()
        claim(2)
        core_six(block).start()

    def z_end_two(block):
        z_one(block).wait_send()
        free(1, pos.zp)

    def z_end_six(block):
        z_five(block).wait_recv()
        claim(2)
        core_six(block).start()

    def z_mid_two(block):
        z_one(block).wait_recv()
        add(block, half, half, from_one.at[lax.rem(block, SLOTS)])
        z_two(block).start()

    def z_mid_three(block):
        z_two(block).wait()
        free(0, pos.zm)
        add(block, keep, quarter, from_two.at[lax.rem(block, SLOTS)])
        z_three(block).start()

    def z_mid_four(block):
        z_three(block).wait()
        add(block, keep, quarter, from_three.at[lax.rem(block, SLOTS)])
        claim(0)
        z_four(block).start()

    def z_mid_five(block):
        z_four(block).wait_send()
        z_four_in(block).wait_recv()
        claim(1)
        z_five(block).start()

    def z_mid_six(block):
        z_five(block).wait_send()
        claim(2)
        core_six(block).start()

    def last(block):
        core_six(block).wait_send()
        core_six_in(block).wait_recv()

    roles = (
        (x_first & pos.end, (start_core, send_x, x_end_two, x_end_three, None, x_end_five, x_six, last)),
        (x_first & pos.mid, (start_core, send_x, take_x, x_mid_three, x_mid_four, x_mid_five, x_six, last)),
        (z_first & pos.end, (start_core, send_z, z_end_two, None, None, None, z_end_six, last)),
        (z_first & pos.mid, (start_core, take_core, z_mid_two, z_mid_three, z_mid_four, z_mid_five, z_mid_six, last)),
    )
    depth = len(roles[0][1])

    def tick(step):
        for here, stages in roles:

            @pl.when(here)
            def _(stages=stages):
                for index in reversed(range(depth)):
                    block = step - SPREAD * index
                    if stages[index] is not None:

                        @pl.when((block >= 0) & (block < count))
                        def _(index=index, block=block, stages=stages):
                            stages[index](block)

        over = step - SPREAD * (depth - 1)

        @pl.when((over >= 0) & (over < count))
        def _():
            finish(over)

    return tick


def sum_scratch():
    return [
        pltpu.VMEM((SLOTS, BR // 2, BC), jnp.float32),
        pltpu.VMEM((SLOTS, BR // 2, BC), jnp.float32),
        pltpu.VMEM((SLOTS, BR // 4, BC), jnp.float32),
        pltpu.VMEM((SLOTS, BR // 4, BC), jnp.float32),
        pltpu.SemaphoreType.DMA((7, SLOTS)),
        pltpu.SemaphoreType.DMA((7, SLOTS)),
        pltpu.SemaphoreType.REGULAR((3,)),
    ]


CR, CC = 64, 384
CHUNKS = 24
RELAY = 3
BF = jnp.bfloat16


def gather_greet(pos, other):
    barrier = pltpu.get_barrier_semaphore()
    for where in ({"tensor": other}, {"dp": pos.xn}, {"dp": pos.zp}, {"dp": pos.sib}):
        pl.semaphore_signal(barrier, inc=1, device_id=where, device_id_type=MESH)


def gather_met():
    pl.semaphore_wait(pltpu.get_barrier_semaphore(), 4)


def chunk_parts(piece, chunk, kind):
    if kind == 0:
        return [(piece * 384 + chunk * 64, 64, 0, 0)]
    if kind == 1:
        return [(piece * 64 + (chunk - 6) * 32, 32, 384 * q, 32 * q) for q in range(2)]
    if kind == 2:
        return [(piece * 128 + (chunk - 8) * 16, 16, 384 * q, 16 * q) for q in range(4)]
    return [((chunk - 16) * 192 + piece * 32, 32, 384 * q, 32 * q) for q in range(2)]


BOUNDS = ((0, 6), (6, 8), (8, 16), (16, 24))
UNIT = (64, 32, 16, 32)


def make_gather(pos, own, theirs, staged, landed, sent, got):
    other = 1 - lax.axis_index("tensor")
    odd = lax.rem(pos.z, 2)
    ky = jnp.where(pos.x == 0, odd, 2)
    kx = jnp.where(pos.x == 0, 2, odd)
    kz = 1 - odd
    piece_y = 2 * ky + pos.core
    piece_x = 2 * kx + pos.core
    piece_z = 2 * kz + pos.core
    sib_y = 2 * ky + 1 - pos.core
    sib_x = 2 * kx + 1 - pos.core
    sib_z = 2 * kz + 1 - pos.core

    def copy(lane, chunk, source, piece, where):
        return pltpu.make_async_remote_copy(
            src_ref=source,
            dst_ref=landed.at[piece, chunk],
            send_sem=sent.at[lane, chunk],
            recv_sem=got.at[lane, chunk],
            device_id=where,
            device_id_type=MESH,
        )

    def over_y(chunk):
        return copy(0, chunk, staged.at[chunk], piece_y, {"tensor": other})

    def over_x(chunk, piece):
        return copy(1, chunk, landed.at[piece, chunk], piece, {"dp": pos.xn})

    def over_z(chunk, piece):
        return copy(2, chunk, landed.at[piece, chunk], piece, {"dp": pos.zp})

    def over_core(lane, chunk, piece):
        return copy(lane, chunk, landed.at[piece, chunk], piece, {"dp": pos.sib})

    def stage_own(kind):
        lo, hi = BOUNDS[kind]

        @pl.loop(lo, hi)
        def _(chunk):
            for row, rows, column, at in chunk_parts(piece_y, chunk, kind):
                staged[chunk, pl.ds(at, rows)] = own[kind][
                    pl.ds(pl.multiple_of(row, UNIT[kind]), rows), pl.ds(column, CC)
                ].astype(jnp.float32)

    def send_own(kind):
        lo, hi = BOUNDS[kind]

        @pl.loop(lo, hi)
        def _(chunk):
            over_y(chunk).start()

    def unpack(chunk):
        for kind in range(4):
            lo, hi = BOUNDS[kind]

            @pl.when((chunk >= lo) & (chunk < hi))
            def _(kind=kind):
                @pl.loop(0, 6)
                def _(piece):
                    for row, rows, column, at in chunk_parts(piece, chunk, kind):
                        theirs[kind][pl.ds(pl.multiple_of(row, UNIT[kind]), rows), pl.ds(column, CC)] = landed[
                            piece, chunk, pl.ds(at, rows)
                        ].astype(BF)

    def guarded(chunk, body):
        @pl.when((chunk >= 0) & (chunk < CHUNKS))
        def _():
            body(chunk)

    def first(chunk):
        over_y(chunk).wait_recv()
        over_x(chunk, piece_y).start()

        @pl.when(pos.x == 0)
        def _():
            over_z(chunk, piece_y).start()

        over_core(3, chunk, piece_y).start()

    def second(chunk):
        over_x(chunk, piece_x).wait_recv()

        @pl.when(pos.x == 1)
        def _():
            over_z(chunk, piece_x).start()

        over_core(4, chunk, piece_x).start()

    def third(chunk):
        over_z(chunk, piece_z).wait_recv()
        over_core(5, chunk, piece_z).start()

    def fourth(chunk):
        over_core(3, chunk, sib_y).wait_recv()
        over_core(4, chunk, sib_x).wait_recv()
        over_core(5, chunk, sib_z).wait_recv()
        over_y(chunk).wait_send()
        over_x(chunk, piece_y).wait_send()
        over_z(chunk, piece_y).wait_send()
        over_core(3, chunk, piece_y).wait_send()
        over_core(4, chunk, piece_x).wait_send()
        over_core(5, chunk, piece_z).wait_send()
        unpack(chunk)

    def tick(step):
        guarded(step - 3 * RELAY, fourth)
        guarded(step - 2 * RELAY, third)
        guarded(step - RELAY, second)
        guarded(step, first)

    return stage_own, send_own, tick


GATHER_TICKS = CHUNKS + 3 * RELAY


def gather_scratch():
    return [
        pltpu.VMEM((CHUNKS, CR, CC), jnp.float32),
        pltpu.VMEM((6, CHUNKS, CR, CC), jnp.float32),
        pltpu.SemaphoreType.DMA((6, CHUNKS)),
        pltpu.SemaphoreType.DMA((6, CHUNKS)),
    ]


def swap_small(small, small_out, sems):
    return pltpu.make_async_remote_copy(
        src_ref=small,
        dst_ref=small_out,
        send_sem=sems.at[0],
        recv_sem=sems.at[1],
        device_id={"tensor": 1 - lax.axis_index("tensor")},
        device_id_type=MESH,
    )


HD = 64
SEG = 148
MEMW = 10
F32 = jnp.float32
EPSILON = 1e-12
MASKED = -1e30
WIN = 160
MEMP = 96
SEGS = 8
PAIR = 2 * HD

CONTRACT_LAST = (((1,), (1,)), ((), ()))
CONTRACT_FIRST = (((0,), (0,)), ((), ()))


def mm(a, b):
    return jnp.dot(a, b, preferred_element_type=F32)


def mm_t(a, b):
    return lax.dot_general(a, b, CONTRACT_LAST, preferred_element_type=F32)


def t_mm(a, b):
    return lax.dot_general(a, b, CONTRACT_FIRST, preferred_element_type=F32)


def build_masks(parent, base, colbias):
    lane = lax.broadcasted_iota(jnp.int32, (1, WIN + MEMP), 1)
    in_mem = [
        ((lane >= WIN + MEMW * t) & (lane < WIN + MEMW * (t + 1))).astype(F32) for t in range(SEGS)
    ]
    reach = [jnp.zeros((1, WIN + MEMP), F32)]
    for s in range(1, SEGS):
        row = jnp.zeros((1, WIN + MEMP), F32)
        for t in range(s):
            hit = jnp.where(parent[s] - base == t, 1.0, 0.0)
            row = row + hit * jnp.maximum(reach[t], in_mem[t])
        reach.append(row)
    for s in range(SEGS):
        off = 4 * (s % 4)
        inside = ((lane >= off) & (lane < off + SEG)).astype(F32)
        colbias[s : s + 1, :] = jnp.where(jnp.maximum(inside, reach[s]) > 0.0, 0.0, MASKED)


def build_select(slots, select, select_t):
    for ref, axis in ((select, 0), (select_t, 1)):
        shape = (ref.shape[0], 1) if axis == 0 else (1, ref.shape[1])
        entry = lax.broadcasted_iota(jnp.int32, shape, axis)
        where = jnp.full(shape, -1, jnp.int32)
        for t in range(SEGS):
            for m in range(MEMW):
                where = jnp.where(entry == MEMW * t + m, slots[t, m] + SEG * t, where)
        place = lax.broadcasted_iota(jnp.int32, ref.shape, 1 - axis)
        ref[...] = (where == place).astype(F32).astype(BF)


def window(s):
    return pl.multiple_of(144 * s + 16 * (s // 4), 16), 4 * lax.rem(s, 4)


def lane_halves():
    lane = lax.broadcasted_iota(jnp.int32, (1, PAIR), 1)
    left = (lane < HD).astype(F32)
    return left.astype(BF), (1.0 - left).astype(BF), lane < HD


def valid_rows(off):
    row = lax.broadcasted_iota(jnp.int32, (WIN, 1), 0)
    return row, (row >= off) & (row < off + SEG)


def softmax_parts(qs, kk, bias):
    scores = mm_t(qs, kk) * HD ** (-0.5) + bias
    top = jnp.max(scores, axis=-1, keepdims=True)
    raised = jnp.exp(scores - top)
    return raised, 1.0 / jnp.sum(raised, axis=-1, keepdims=True)


def attend_pair(q, k, v, kmem, vmem, colbias, mixed, probs, s, columns):
    left, right, is_left = lane_halves()
    at, off = window(s)
    rows = pl.ds(at, WIN)
    qw = q[rows, columns]
    qs = jnp.concatenate([qw * left, qw * right], axis=0)
    kk = jnp.concatenate([k[rows, columns], kmem[:, columns]], axis=0)
    vv = jnp.concatenate([v[rows, columns], vmem[:, columns]], axis=0)
    raised, scale = softmax_parts(qs, kk, colbias[pl.ds(s, 1), :])
    row, valid = valid_rows(off)
    keep = jnp.where(valid, 1.0, 0.0)
    chances = (raised * (scale * jnp.concatenate([keep, keep], axis=0))).astype(BF)
    probs[...] = chances
    both = mm(chances, vv)
    out = jnp.where(is_left, both[:WIN], both[WIN:])
    old = mixed[rows, columns].astype(F32)
    mixed[rows, columns] = jnp.where(row >= off, out, old).astype(BF)


def attend_back_pair(q, k, v, kmem, vmem, probs, dmix, dq, dk, dv, dkmem, dvmem, s, columns):
    left, right, is_left = lane_halves()
    at, off = window(s)
    rows = pl.ds(at, WIN)
    qw = q[rows, columns]
    qs = jnp.concatenate([qw * left, qw * right], axis=0)
    kk = jnp.concatenate([k[rows, columns], kmem[:, columns]], axis=0)
    vv = jnp.concatenate([v[rows, columns], vmem[:, columns]], axis=0)
    dw = dmix[rows, columns]
    ds_in = jnp.concatenate([dw * left, dw * right], axis=0)
    low = probs[...]
    chances = low.astype(F32)
    dp = mm_t(ds_in, vv)
    inner = jnp.sum(chances * dp, axis=-1, keepdims=True)
    ds = (chances * (dp - inner)).astype(BF)
    dqs = mm(ds, kk)
    row, valid = valid_rows(off)
    new = jnp.where(is_left, dqs[:WIN], dqs[WIN:]) * HD ** (-0.5)
    old = dq[rows, columns].astype(F32)
    dq[rows, columns] = jnp.where(row >= off, new, old).astype(BF)
    dks = t_mm(ds, qs)
    dvs = t_mm(low, ds_in)
    dk[rows, columns] = dk[rows, columns] + dks[:WIN]
    dv[rows, columns] = dv[rows, columns] + dvs[:WIN]
    dkmem[:, columns] = dkmem[:, columns] + dks[WIN:]
    dvmem[:, columns] = dvmem[:, columns] + dvs[WIN:]


def spread(select_t, part):
    high = part.astype(BF)
    low = (part - high.astype(F32)).astype(BF)
    return mm(select_t, high) + mm(select_t, low)


def norm_stats(values):
    centered = values - jnp.mean(values, axis=-1, keepdims=True)
    inverse = lax.rsqrt(jnp.mean(centered * centered, axis=-1, keepdims=True) + EPSILON)
    return centered * inverse, inverse


def norm_back(grad, normed, inverse, gain):
    scaled = grad * gain
    return inverse * (
        scaled
        - jnp.mean(scaled, axis=-1, keepdims=True)
        - normed * jnp.mean(scaled * normed, axis=-1, keepdims=True)
    )


def gelu_parts(inner):
    phi = 0.5 + 0.5 * lax.erf(inner * (0.5**0.5))
    density = jnp.exp(-0.5 * inner * inner) * (2.0 * jnp.pi) ** -0.5
    return (inner * phi).astype(BF), (phi + inner * density).astype(BF)


def flat_row(ref, start, size):
    return ref[pl.ds(start, size)].reshape(1, size)


TILE = 128


SPLIT = 6 * TILE


def row_tiles(first, last, body):
    full = (last - first) // TILE

    @pl.loop(0, full)
    def _(i):
        body(pl.ds(pl.multiple_of(first + i * TILE, TILE), TILE))

    if (last - first) % TILE:
        body(pl.ds(first + full * TILE, (last - first) % TILE))


def forward_kernel(
    fast,
    parent,
    slots,
    bias_qv,
    bias_out,
    gain_one,
    shift_one,
    bias_up,
    bias_down,
    gain_two,
    shift_two,
    tokens_h,
    grad_h,
    qkv_in,
    out_in,
    up_in,
    down_in,
    *rest,
):
    count = 0 if fast else 5
    given, outs, rest = rest[:count], rest[count : count + 19], rest[count + 19 :]
    (
        output_h,
        their_qkv_h,
        their_out_h,
        their_up_h,
        their_down_h,
        qkv_h,
        mixed_h,
        normed_h,
        inverse,
        hidden_h,
        acted_h,
        slope_own_h,
        slope_their_h,
        d_two_h,
        d_ffn_h,
        vec,
        probs_h,
        select_t,
        memory,
    ) = outs
    (
        tokens,
        own_qkv,
        own_out,
        own_up,
        own_down,
        their_qkv,
        their_out,
        their_up,
        their_down,
        small,
        small_their,
        qkv,
        mixed,
        normed,
        hidden,
        acc_own,
        acc_their,
        acted,
        slopes,
        colbias,
        select,
        sums,
        probs,
        io_sem,
        slope_sem,
        probs_sem,
        *wires,
    ) = rest
    rows, depth = tokens.shape
    width = mixed.shape[2]
    units = acted.shape[1]
    theirs = (their_qkv, their_out, their_up, their_down)
    own = (own_qkv, own_out, own_up, own_down)

    def move(index, source, target):
        return pltpu.make_async_copy(source, target, io_sem.at[index])

    load_tokens = move(0, tokens_h, tokens)
    load_grad = move(1, grad_h, tokens)
    put_qkv = move(2, qkv, qkv_h)
    put_mixed = move(3, mixed.at[0], mixed_h)
    put_normed = move(4, normed, normed_h)
    put_hidden = move(5, hidden, hidden_h)
    put_acted = move(6, acted, acted_h)
    late = ((acc_own, d_two_h), (hidden, d_ffn_h), (tokens, output_h))
    put_late = [
        [move(7 + 3 * part + i, ref.at[rows_of], target.at[rows_of]) for i, (ref, target) in enumerate(late)]
        for part, rows_of in enumerate((pl.ds(0, SPLIT), pl.ds(SPLIT, rows - SPLIT)))
    ]
    put_theirs = [
        move(13 + i, ref, target)
        for i, (ref, target) in enumerate(zip(theirs, (their_qkv_h, their_out_h, their_up_h, their_down_h)))
    ]
    load_own = [move(17 + i, a, b) for i, (a, b) in enumerate(zip((qkv_in, out_in, up_in, down_in), own))]
    if fast:
        pos = Place()
        gather_greet(pos, 1 - lax.axis_index("tensor"))
    load_own[0].start()
    load_tokens.start()
    for copy in load_own[1:]:
        copy.start()
    done = [0]
    small[...] = jnp.zeros(small.shape, F32)
    small[0:1, :] = bias_qv[0:1, :]
    small[2:3, :] = bias_qv[1:2, :]
    for c in range(units // CHUNK):
        small[3 + c : 4 + c, 0:CHUNK] = flat_row(bias_up, c * CHUNK, CHUNK)
    if fast:
        small_sem, *wires = wires
        stage_own, send_own, tick = make_gather(pos, own, theirs, *wires)
        load_own[0].wait()
        stage_own(0)
        gather_met()
        send_own(0)
        swap = swap_small(small, small_their, small_sem)
        swap.start()
        for kind in range(1, 4):
            load_own[kind].wait()
            stage_own(kind)
            send_own(kind)
    else:
        for copy in load_own:
            copy.wait()
        copies = [move(13 + i, a, b) for i, (a, b) in enumerate(zip(given, theirs + (small_their,)))]
        for copy in copies:
            copy.start()
        for copy in copies:
            copy.wait()

        def tick(step):
            pass

    def ticks(index, each, trips):
        for i in range(each):
            tick(done[0] + index * each + i)

    def tick_every(index, every, trips):
        @pl.when(lax.rem(index, every) == 0)
        def _():
            tick(done[0] + index // every)

        return -(-trips // every)

    def until(count):
        if done[0] < count:

            @pl.loop(done[0], count)
            def _(step):
                tick(step)

            done[0] = count

    build_masks(parent, lax.axis_index("dp") * SEGS, colbias)
    build_select(slots, select, select_t)
    load_tokens.wait()
    pairs = width // PAIR
    for half in range(2):
        weights = (own_qkv, their_qkv)[half]
        table = (small, small_their)[half]
        if half == 1:
            until(BOUNDS[0][1] + 3 * RELAY)
            if fast:
                swap.wait()

        @pl.loop(0, 3)
        def _(c, half=half, weights=weights, table=table):
            part = mm(tokens[...], weights[pl.ds(pl.multiple_of(c * depth, depth), depth), :])
            qkv[half, c] = (part + table[pl.ds(c, 1), :]).astype(BF)

        q, k, v = (qkv.at[half, i] for i in range(3))
        kmem, vmem = memory.at[half, 0], memory.at[half, 1]
        kmem[...] = mm(select[...], k[...]).astype(BF)
        vmem[...] = mm(select[...], v[...]).astype(BF)

        def put_probs(s, half=half):
            slot = lax.rem(s, 2)
            return pltpu.make_async_copy(probs.at[slot], probs_h.at[half, s], probs_sem.at[slot])

        @pl.loop(0, SEGS)
        def _(s, half=half, q=q, k=k, v=v, kmem=kmem, vmem=vmem, put_probs=put_probs):
            @pl.when(s >= 2)
            def _():
                put_probs(s - 2).wait()

            for pair in range(pairs):
                attend_pair(
                    q, k, v, kmem, vmem, colbias, mixed.at[half], probs.at[lax.rem(s, 2), pair], s, pl.ds(pair * PAIR, PAIR)
                )
                if pair == 0 and half == 0:
                    tick(done[0] + s)
                if pair == 2 and half == 1:
                    tick_every(s, GATHER[0], SEGS)
            put_probs(s).start()

        done[0] += SEGS if half == 0 else -(-SEGS // GATHER[0])
        put_probs(SEGS - 2).wait()
        put_probs(SEGS - 1).wait()

        if half == 1:
            until(BOUNDS[1][1] + 3 * RELAY)
        out = (own_out, their_out)[half]

        @pl.loop(0, 3)
        def _(n, half=half, out=out):
            columns = pl.ds(pl.multiple_of(n * CHUNK, CHUNK), CHUNK)
            part = mm(mixed[half], out[:, columns])
            acc_own[:, columns] = part if half == 0 else acc_own[:, columns] + part
            ticks(n, GATHER[1 + half], 3)

        done[0] += 3 * GATHER[1 + half]
    put_qkv.start()
    put_mixed.start()

    def norm_one(span):
        resid = tokens[span, :].astype(F32) + (acc_own[span, :] + flat_row(bias_out, 0, depth))
        unit, scale = norm_stats(resid)
        normed[span, :] = unit
        inverse[span, :] = scale
        hidden[span, :] = (unit * flat_row(gain_one, 0, depth) + flat_row(shift_one, 0, depth)).astype(BF)

    row_tiles(0, rows, norm_one)
    load_grad.start()
    put_normed.start()
    put_hidden.start()

    for half in range(2):
        up, down = ((own_up, own_down), (their_up, their_down))[half]
        table = (small, small_their)[half]
        slope_h = (slope_own_h, slope_their_h)[half]
        acc = (acc_own, acc_their)[half]

        def put_slope(c, slope_h=slope_h):
            span = pl.ds(pl.multiple_of(c * CHUNK, CHUNK), CHUNK)
            return pltpu.make_async_copy(slopes.at[lax.rem(c, 2)], slope_h.at[:, span], slope_sem.at[lax.rem(c, 2)])

        if half == 1:
            until(BOUNDS[2][1] + 3 * RELAY)
            put_acted.wait()
            put_slope(4).wait()
            put_slope(5).wait()

        @pl.loop(0, 6)
        def _(c, half=half, up=up, table=table, put_slope=put_slope):
            span = pl.ds(pl.multiple_of(c * CHUNK, CHUNK), CHUNK)

            @pl.when(c >= 2)
            def _():
                put_slope(c - 2).wait()

            bias = table[pl.ds(3 + c, 1), 0:CHUNK]
            act, steep = gelu_parts(mm(hidden[...], up[:, span]) + bias)
            acted[:, span] = act
            slopes[lax.rem(c, 2)] = steep
            put_slope(c).start()
            tick_every(c, GATHER[3 + 2 * half], 6)

        done[0] += -(-6 // GATHER[3 + 2 * half])
        low, high = slice(0, units // 2), slice(units // 2, units)
        if half == 0:
            put_acted.start()

            @pl.loop(0, 3)
            def _(n, down=down, acc=acc):
                columns = pl.ds(pl.multiple_of(n * CHUNK, CHUNK), CHUNK)
                acc[:, columns] = mm(acted[:, low], down[low, columns]) + mm(acted[:, high], down[high, columns])
                ticks(n, GATHER[4], 3)

        else:
            until((BOUNDS[3][0] + BOUNDS[3][1]) // 2 + 3 * RELAY)

            @pl.loop(0, 3)
            def _(n, down=down, acc=acc):
                columns = pl.ds(pl.multiple_of(n * CHUNK, CHUNK), CHUNK)
                acc[:, columns] = mm(acted[:, low], down[low, columns])
                ticks(n, 1, 3)

            done[0] += 3
            until(BOUNDS[3][1] + 3 * RELAY)
            if fast:
                for copy in put_theirs:
                    copy.start()

            @pl.loop(0, 3)
            def _(n, down=down, acc=acc):
                columns = pl.ds(pl.multiple_of(n * CHUNK, CHUNK), CHUNK)
                acc[:, columns] = acc[:, columns] + mm(acted[:, high], down[high, columns])

        done[0] += 3 * GATHER[4] if half == 0 else 0
    put_slope(4).wait()
    put_slope(5).wait()

    load_grad.wait()
    put_hidden.wait()
    sums[...] = jnp.zeros(sums.shape, F32)

    def norm_two(span):
        first = normed[span, :] * flat_row(gain_one, 0, depth) + flat_row(shift_one, 0, depth)
        resid = first + ((acc_own[span, :] + acc_their[span, :]) + flat_row(bias_down, 0, depth))
        unit, scale = norm_stats(resid)
        grad = tokens[span, :].astype(F32)
        tokens[span, :] = (unit * flat_row(gain_two, 0, depth) + flat_row(shift_two, 0, depth)).astype(BF)
        back = norm_back(grad, unit, scale, flat_row(gain_two, 0, depth))
        acc_own[span, :] = back
        low = back.astype(BF)
        hidden[span, :] = low
        for index, value in enumerate((low.astype(F32), grad * unit, grad)):
            sums[index] = sums[index] + value.reshape(-1, 8, depth).sum(axis=0)

    row_tiles(0, SPLIT, norm_two)
    for copy in put_late[0]:
        copy.start()
    row_tiles(SPLIT, rows, norm_two)
    for copy in put_late[1]:
        copy.start()
    for index in range(3):
        total = jnp.sum(sums[index], axis=0, keepdims=True)
        for j in range(6):
            vec[6 * index + j : 6 * index + j + 1, :] = total[:, BC * j : BC * (j + 1)]
    for copy in (put_qkv, put_mixed, put_normed, *put_late[0], *put_late[1]):
        copy.wait()
    if fast:
        for copy in put_theirs:
            copy.wait()


GATHER = (2, 1, 1, 2, 1, 2)


def forward(fast, parent, slots, vectors, tokens, grad_out, own, given):
    rows, depth = tokens.shape
    width = own[0].shape[1]
    units = own[2].shape[1]
    vm = pl.BlockSpec(memory_space=pltpu.VMEM)
    hbm = pl.BlockSpec(memory_space=pl.ANY)
    sm = pl.BlockSpec(memory_space=pltpu.SMEM)
    sd = jax.ShapeDtypeStruct
    out_shape = [
        sd((rows, depth), BF),
        *[sd(w.shape, BF) for w in own],
        sd((2, 3, rows, width), BF),
        sd((rows, width), BF),
        sd((rows, depth), F32),
        sd((rows, 1), F32),
        sd((rows, depth), BF),
        sd((rows, units), BF),
        sd((rows, units), BF),
        sd((rows, units), BF),
        sd((rows, depth), F32),
        sd((rows, depth), BF),
        sd((18, BC), F32),
        sd((2, SEGS, width // PAIR, 2 * WIN, WIN + MEMP), BF),
        sd((rows, MEMP), BF),
        sd((2, 2, MEMP, width), BF),
    ]
    return pl.pallas_call(
        functools.partial(forward_kernel, fast),
        out_shape=out_shape,
        in_specs=[sm, sm] + [vm] * len(vectors) + [hbm, hbm] + [hbm] * (4 + len(given)),
        out_specs=[hbm] * 8 + [vm] + [hbm] * 6 + [vm, hbm, vm, vm],
        scratch_shapes=[
            pltpu.VMEM((rows, depth), BF),
            *[pltpu.VMEM(w.shape, BF) for w in own],
            *[pltpu.VMEM(w.shape, BF) for w in own],
            pltpu.VMEM((16, width), F32),
            pltpu.VMEM((16, width), F32),
            pltpu.VMEM((2, 3, rows, width), BF),
            pltpu.VMEM((2, rows, width), BF),
            pltpu.VMEM((rows, depth), F32),
            pltpu.VMEM((rows, depth), BF),
            pltpu.VMEM((rows, depth), F32),
            pltpu.VMEM((rows, depth), F32),
            pltpu.VMEM((rows, units), BF),
            pltpu.VMEM((2, rows, CHUNK), BF),
            pltpu.VMEM((SEGS, WIN + MEMP), F32),
            pltpu.VMEM((MEMP, rows), BF),
            pltpu.VMEM((3, 8, depth), F32),
            pltpu.VMEM((2, width // PAIR, 2 * WIN, WIN + MEMP), BF),
            pltpu.SemaphoreType.DMA((21,)),
            pltpu.SemaphoreType.DMA((2,)),
            pltpu.SemaphoreType.DMA((2,)),
        ]
        + ([pltpu.SemaphoreType.DMA((2,))] + gather_scratch() if fast else []),
        compiler_params=pltpu.CompilerParams(
            collective_id=0 if fast else None, has_side_effects=fast, vmem_limit_bytes=67043328
        ),
        name="forward",
    )(parent, slots, *vectors, tokens, grad_out, *own, *given)


DOWN, UP, OUT, QKV, VEC = 0, 24, 48, 54, 72
COUNT = 73
CHUNK = 256
VEC_ROWS = 54


def backward_kernel(
    fast,
    select_t,
    memory,
    inverse,
    gain,
    vec_in,
    tokens_h,
    hidden_h,
    d_ffn_h,
    d_two_h,
    normed_h,
    acted_h,
    slope_own_h,
    slope_their_h,
    qkv_h,
    mixed_h,
    probs_h,
    w_up_own,
    w_up_their,
    w_down_own,
    w_down_their,
    w_out_own,
    w_out_their,
    w_qkv_own,
    w_qkv_their,
    grads,
    d_low,
    hidden,
    d_res,
    normed,
    acc_own,
    acc_their,
    a_buf,
    slope_buf,
    up_buf,
    down_buf,
    d_inner,
    sums,
    tokens,
    mixed,
    w_out,
    w_qkv,
    qkv,
    d_qkv,
    d_mixed,
    probs,
    dkm,
    dvm,
    load_sem,
    chunk_sem,
    probs_sem,
    *wires,
):
    rows, depth = tokens.shape
    width = mixed.shape[1]

    def fetch(index, source, target):
        return pltpu.make_async_copy(source, target, load_sem.at[index])

    load_d = fetch(0, d_ffn_h, d_low)
    load_hidden = fetch(1, hidden_h, hidden)
    load_two = fetch(2, d_two_h, d_res)
    load_normed = fetch(3, normed_h, normed)
    load_mixed = fetch(4, mixed_h, mixed)
    load_out = [fetch(5 + i, w, w_out.at[i]) for i, w in enumerate((w_out_own, w_out_their))]
    load_w = [fetch(7 + i, w, w_qkv.at[i]) for i, w in enumerate((w_qkv_own, w_qkv_their))]
    load_tokens = fetch(9, tokens_h, tokens)
    load_qkv = [fetch(10 + half, qkv_h.at[half], qkv) for half in range(2)]

    def load_acted(c):
        return pltpu.make_async_copy(acted_h.at[:, pl.ds(pl.multiple_of(c * BR, BR), BR)], a_buf.at[lax.rem(c, 2)], chunk_sem.at[0, lax.rem(c, 2)])

    def load_chunk(half, c):
        slot = lax.rem(c, 2)
        span = pl.ds(pl.multiple_of(c * CHUNK, CHUNK), CHUNK)
        slope_h, up_h, down_h = ((slope_own_h, w_up_own, w_down_own), (slope_their_h, w_up_their, w_down_their))[half]
        return (
            pltpu.make_async_copy(slope_h.at[:, span], slope_buf.at[slot], chunk_sem.at[1, slot]),
            pltpu.make_async_copy(up_h.at[:, span], up_buf.at[slot], chunk_sem.at[2, slot]),
            pltpu.make_async_copy(down_h.at[span, :], down_buf.at[slot], chunk_sem.at[3, slot]),
        )

    def load_probs(half, s):
        slot = lax.rem(s, 2)
        return pltpu.make_async_copy(probs_h.at[half, s], probs.at[slot], probs_sem.at[slot])

    def start(copies):
        for copy in copies:
            copy.start()

    def wait(copies):
        for copy in copies:
            copy.wait()

    if fast:
        pos = Place()
        sum_greet(pos)
    load_d.start()
    load_acted(0).start()
    start(load_chunk(0, 0))
    load_hidden.start()
    load_two.start()
    load_normed.start()
    load_mixed.start()
    start(load_out)
    start(load_w)
    load_tokens.start()
    load_qkv[0].start()
    load_probs(0, 0).start()

    def finish(block):
        pass

    if fast:
        tick = make_tick(pos, grads, *wires, COUNT, finish)
        last = COUNT + 7 * SPREAD
    else:

        def tick(step):
            pass

        last = COUNT
    done = [0]

    def ticks(index, each, trips):
        for i in range(each):
            tick(done[0] + index * each + i)
        return trips * each

    grads[VEC] = jnp.zeros((BR, BC), F32)
    grads[VEC, 36:54] = vec_in[...]
    acc_own[...] = jnp.zeros(acc_own.shape, F32)
    acc_their[...] = jnp.zeros(acc_their.shape, F32)
    sums[...] = jnp.zeros(sums.shape, F32)
    if fast:
        sum_met(pos)

    load_d.wait()

    @pl.loop(0, 4)
    def _(c):
        load_acted(c).wait()

        @pl.when(c < 3)
        def _():
            load_acted(c + 1).start()

        for part in range(2):
            piece = t_mm(a_buf[lax.rem(c, 2)], d_low[:, part * width : (part + 1) * width])
            for j in range(3):
                grads[DOWN + 6 * c + 3 * part + j] = piece[:, BC * j : BC * (j + 1)]
        ticks(c, TICKS[0], 4)

    done[0] += 4 * TICKS[0]

    load_hidden.wait()
    for half in range(2):
        acc = (acc_own, acc_their)[half]

        @pl.loop(0, 6)
        def _(c, half=half, acc=acc):
            slot = lax.rem(c, 2)
            wait(load_chunk(half, c))

            @pl.when(c < 5)
            def _():
                start(load_chunk(half, c + 1))

            if half == 0:

                @pl.when(c == 5)
                def _():
                    start(load_chunk(1, 0))

            each = TICKS[1 + half]
            d_inner[...] = (mm_t(d_low[...], down_buf[slot]) * slope_buf[slot].astype(F32)).astype(BF)
            if each > 1:
                tick(done[0] + c * each)
            if half == 0:
                piece = t_mm(hidden[...], d_inner[...])
                for r in range(2):
                    for j in range(2):
                        grads[UP + 4 * c + 2 * r + j] = piece[BR * r : BR * (r + 1), BC * j : BC * (j + 1)]
                total = jnp.sum(d_inner[...].astype(F32), axis=0, keepdims=True)
                for j in range(2):
                    grads[VEC, pl.ds(6 + 2 * c + j, 1), :] = total[:, BC * j : BC * (j + 1)]
                if each > 2:
                    tick(done[0] + c * each + 1)
            for part in range(3):
                columns = slice(CHUNK * part, CHUNK * (part + 1))
                acc[:, columns] = acc[:, columns] + mm_t(d_inner[...], up_buf[slot, columns, :])
            tick(done[0] + c * each + each - 1)

        done[0] += 6 * TICKS[1 + half]

    load_two.wait()
    load_normed.wait()
    def norm_one(span):
        total = d_res[span, :] + (acc_own[span, :] + acc_their[span, :])
        unit = normed[span, :]
        one = norm_back(total, unit, inverse[span, :], flat_row(gain, 0, depth))
        d_res[span, :] = one
        low = one.astype(BF)
        d_low[span, :] = low
        for index, value in enumerate((low.astype(F32), total * unit, total)):
            sums[index] = sums[index] + value.reshape(-1, 8, depth).sum(axis=0)

    trips = rows // NORM_TILE

    @pl.loop(0, trips)
    def _(i):
        norm_one(pl.ds(pl.multiple_of(i * NORM_TILE, NORM_TILE), NORM_TILE))

        @pl.when(lax.rem(i, TICK_TILES) == 0)
        def _():
            tick(done[0] + i // TICK_TILES)

    if rows % NORM_TILE:
        norm_one(pl.ds(trips * NORM_TILE, rows % NORM_TILE))
    done[0] += -(-trips // TICK_TILES)
    for index in range(3):
        total = jnp.sum(sums[index], axis=0, keepdims=True)
        for j in range(6):
            grads[VEC, 18 + 6 * index + j : 19 + 6 * index + j, :] = total[:, BC * j : BC * (j + 1)]

    load_mixed.wait()
    wait(load_out)

    @pl.loop(0, 2)
    def _(half):
        d_mixed[half] = mm_t(d_low[...], w_out[half]).astype(BF)
        piece = t_mm(mixed[...], d_low[:, pl.ds(pl.multiple_of(half * width, BC), width)])
        for j in range(3):
            grads[OUT + 3 * half + j] = piece[:, BC * j : BC * (j + 1)]
        ticks(half, TICKS[3], 2)

    done[0] += 2 * TICKS[3]

    wait(load_w)
    load_tokens.wait()
    pairs = width // PAIR
    dka, dva = acc_their.at[:, pl.ds(0, width)], acc_their.at[:, pl.ds(width, width)]
    for half in range(2):
        load_qkv[half].wait()
        q, k, v = (qkv.at[i] for i in range(3))
        kmem, vmem = memory.at[half, 0], memory.at[half, 1]
        acc_their[...] = jnp.zeros(acc_their.shape, F32)
        dkm[...] = jnp.zeros(dkm.shape, F32)
        dvm[...] = jnp.zeros(dvm.shape, F32)

        group = UNROLL[half]

        @pl.loop(0, SEGS * pairs // group)
        def _(trip, half=half, group=group, kmem=kmem, vmem=vmem):
            s, first = trip * group // pairs, lax.rem(trip * group, pairs)

            @pl.when(first == 0)
            def _():
                load_probs(half, s).wait()

                @pl.when(s < SEGS - 1)
                def _():
                    load_probs(half, s + 1).start()

                if half == 0:

                    @pl.when(s == SEGS - 1)
                    def _():
                        load_probs(1, 0).start()

            for i in range(group):
                pair = i if group == pairs else first
                columns = pl.ds(pl.multiple_of(pair * PAIR, PAIR), PAIR)
                part = probs.at[lax.rem(s, 2), pair]
                attend_back_pair(q, k, v, kmem, vmem, part, d_mixed.at[half], d_qkv.at[0], dka, dva, dkm, dvm, s, columns)
                spot = trip * group + i

                @pl.when(lax.rem(spot, TICKS[4 + half]) == 0)
                def _(spot=spot):
                    tick(done[0] + spot // TICKS[4 + half])

        done[0] += -(-SEGS * pairs // TICKS[4 + half])
        if half == 0:
            assert done[0] <= QKV
        if half == 0:
            load_qkv[1].start()
        d_qkv[1] = ((dka[...] + spread(select_t[...], dkm[...])) * HD ** (-0.5)).astype(BF)
        d_qkv[2] = (dva[...] + spread(select_t[...], dvm[...])).astype(BF)
        if half == 0:

            @pl.loop(0, 3)
            def _(c):
                piece = t_mm(tokens[...], d_qkv[c])
                for r in range(2):
                    for j in range(3):
                        grads[QKV + 6 * c + 3 * r + j] = piece[BR * r : BR * (r + 1), BC * j : BC * (j + 1)]
                columns = pl.ds(pl.multiple_of(c * CHUNK, CHUNK), CHUNK)
                part = mm_t(d_qkv[0], w_qkv[half, pl.ds(pl.multiple_of(c * CHUNK, CHUNK), CHUNK), :])
                for i in (1, 2):
                    part = part + mm_t(d_qkv[i], w_qkv[half, pl.ds(pl.multiple_of(i * depth + c * CHUNK, CHUNK), CHUNK), :])
                acc_own[:, columns] = part
                ticks(c, TICKS[6], 3)

            done[0] += 3 * TICKS[6]
            for index, row in ((0, 0), (2, 3)):
                total = jnp.sum(d_qkv[index].astype(F32), axis=0, keepdims=True)
                for j in range(3):
                    grads[VEC, row + j : row + j + 1, :] = total[:, BC * j : BC * (j + 1)]
        else:

            @pl.loop(0, 3)
            def _(c):
                columns = pl.ds(pl.multiple_of(c * CHUNK, CHUNK), CHUNK)
                part = mm_t(d_qkv[0], w_qkv[half, pl.ds(pl.multiple_of(c * CHUNK, CHUNK), CHUNK), :])
                for i in (1, 2):
                    part = part + mm_t(d_qkv[i], w_qkv[half, pl.ds(pl.multiple_of(i * depth + c * CHUNK, CHUNK), CHUNK), :])
                d_low[:, columns] = ((acc_own[:, columns] + part) + d_res[:, columns]).astype(BF)
                ticks(c, TICKS[7], 3)

            done[0] += 3 * TICKS[7]
    @pl.loop(min(done[0], last), last)
    def _(step):
        tick(step)


TICKS = (1, 3, 2, 1, 2, 1, 3, 1)
TICK_TILES = 2
NORM_TILE = 128
UNROLL = (3, 1)


def backward(fast, select_t, memory, inverse, gain, vec_in, arrays):
    tokens, acted, mixed = arrays[0], arrays[5], arrays[9]
    rows, depth = tokens.shape
    units = acted.shape[1]
    width = mixed.shape[1]
    vm = pl.BlockSpec(memory_space=pltpu.VMEM)
    hbm = pl.BlockSpec(memory_space=pl.ANY)
    kept = pltpu.VMEM if fast else jax.ShapeDtypeStruct
    return pl.pallas_call(
        functools.partial(backward_kernel, fast),
        out_shape=[kept((COUNT, BR, BC), F32), kept((rows, depth), BF)],
        in_specs=[vm, vm, vm, vm, vm] + [hbm] * len(arrays),
        out_specs=[vm, vm],
        scratch_shapes=[
            pltpu.VMEM((rows, depth), BF),
            pltpu.VMEM((rows, depth), F32),
            pltpu.VMEM((rows, depth), F32),
            pltpu.VMEM((rows, depth), F32),
            pltpu.VMEM((rows, depth), F32),
            pltpu.VMEM((2, rows, BR), BF),
            pltpu.VMEM((2, rows, CHUNK), BF),
            pltpu.VMEM((2, depth, CHUNK), BF),
            pltpu.VMEM((2, CHUNK, depth), BF),
            pltpu.VMEM((rows, CHUNK), BF),
            pltpu.VMEM((3, 8, depth), F32),
            pltpu.VMEM((rows, depth), BF),
            pltpu.VMEM((rows, width), BF),
            pltpu.VMEM((2, width, depth), BF),
            pltpu.VMEM((2, 3 * depth, width), BF),
            pltpu.VMEM((3, rows, width), BF),
            pltpu.VMEM((3, rows, width), BF),
            pltpu.VMEM((2, rows, width), BF),
            pltpu.VMEM((2, width // PAIR, 2 * WIN, WIN + MEMP), BF),
            pltpu.VMEM((MEMP, width), F32),
            pltpu.VMEM((MEMP, width), F32),
            pltpu.SemaphoreType.DMA((12,)),
            pltpu.SemaphoreType.DMA((4, 2)),
            pltpu.SemaphoreType.DMA((2,)),
        ]
        + (sum_scratch() if fast else []),
        compiler_params=pltpu.CompilerParams(
            collective_id=1 if fast else None, has_side_effects=fast, vmem_limit_bytes=47 * 2**20 if fast else 67043328
        ),
        name="backward",
    )(select_t, memory, inverse, gain, vec_in, *arrays)


def results_kernel(blocks, grad_tokens, output, g_qkv, g_out, g_up, g_down, tokens_h, output_out, *rest):
    vectors, (sems, out_sem) = rest[:8], rest[8:]
    places = [(g_down, BR * (i // 6), BC * (i % 6)) for i in range(24)]
    places += [(g_up, BR * (i // 2 % 2), CHUNK * (i // 4) + BC * (i % 2)) for i in range(24)]
    places += [(g_out, 0, BC * i) for i in range(6)]
    places += [(g_qkv, BR * (i // 3), BC * (i % 3)) for i in range(18)]
    copies = [
        pltpu.make_async_copy(blocks.at[i], target.at[pl.ds(row, BR), pl.ds(column, BC)], sems.at[i])
        for i, (target, row, column) in enumerate(places)
    ]
    copies.append(pltpu.make_async_copy(grad_tokens, tokens_h, out_sem.at[0]))
    copies.append(pltpu.make_async_copy(output, output_out, out_sem.at[1]))
    for copy in copies:
        copy.start()
    bias_qv, *flat = vectors
    for j in range(6):
        bias_qv[j // 3 : j // 3 + 1, BC * (j % 3) : BC * (j % 3 + 1)] = blocks[VEC, j : j + 1, :]
    row = 6
    for ref in flat:
        for j in range(ref.shape[0] // BC):
            ref[pl.ds(BC * j, BC)] = blocks[VEC, row, :]
            row += 1
    for copy in copies:
        copy.wait()


def results(fast, blocks, grad_tokens, output, width, units):
    vm = pl.BlockSpec(memory_space=pltpu.VMEM)
    hbm = pl.BlockSpec(memory_space=pl.ANY)
    sd = jax.ShapeDtypeStruct
    rows, depth = output.shape
    if fast:
        blocks, grad_tokens, output = (
            pltpu.with_memory_space_constraint(a, pltpu.VMEM) for a in (blocks, grad_tokens, output)
        )
    large = [sd((3 * depth, width), F32), sd((width, depth), F32), sd((depth, units), F32), sd((units, depth), F32)]
    large += [sd((rows, depth), BF)] * 2
    small = [sd((2, width), F32), sd((units,), F32)] + [sd((depth,), F32)] * 6
    return pl.pallas_call(
        results_kernel,
        out_shape=large + small,
        in_specs=[vm, vm, vm],
        out_specs=[hbm] * 6 + [vm] * len(small),
        scratch_shapes=[
            pltpu.SemaphoreType.DMA((VEC,)),
            pltpu.SemaphoreType.DMA((2,)),
        ],
        compiler_params=pltpu.CompilerParams(vmem_limit_bytes=(8 if fast else 40) * 2**20),
        name="results",
    )(blocks, grad_tokens, output)


def halves_swap(own, small):
    unit = (lax.axis_index("dp") >= 0).astype(F32)

    def other(array):
        arrived = lax.ppermute(array.astype(F32), "tensor", [(0, 1), (1, 0)])
        return (arrived * unit).astype(array.dtype)

    return tuple(other(array) for array in own) + (other(small),)


def shards(
    fast,
    tokens,
    w_qkv,
    bias_qv,
    w_out,
    bias_out,
    gain_one,
    shift_one,
    w_up,
    bias_up,
    w_down,
    bias_down,
    gain_two,
    shift_two,
    grad_out,
    parent,
    mem_slots,
):
    depth, width = w_qkv.shape[1:]
    hidden_units = w_up.shape[1]
    own = (w_qkv.reshape(3 * depth, width), w_out, w_up, w_down)
    if fast:
        given = ()
    else:
        table = jnp.pad(bias_up.reshape(-1, CHUNK), ((0, 0), (0, width - CHUNK)))
        small = jnp.concatenate([bias_qv[:1], jnp.zeros((1, width), F32), bias_qv[1:], table])
        given = halves_swap(own, jnp.pad(small, ((0, 16 - small.shape[0]), (0, 0))))
    vectors = (bias_qv, bias_out, gain_one, shift_one, bias_up, bias_down, gain_two, shift_two)
    (
        output,
        *theirs,
        qkv,
        mixed,
        normed,
        inverse,
        hidden_low,
        acted,
        slope_own,
        slope_their,
        d_two,
        d_ffn,
        vec,
        probs,
        select_t,
        memory,
    ) = forward(fast, parent, mem_slots, vectors, tokens, grad_out, own, given)
    if not fast:
        theirs = given[:4]
    arrays = (tokens, hidden_low, d_ffn, d_two, normed, acted, slope_own, slope_their, qkv, mixed, probs)
    weights = tuple(w[i] for i in (2, 3, 1, 0) for w in (own, theirs))
    blocks, grad_tokens = backward(fast, select_t, memory, inverse, gain_one, vec, arrays + weights)
    if not fast:
        blocks = lax.psum(blocks, "dp")
    (
        g_w_qkv,
        g_w_out,
        g_w_up,
        g_w_down,
        grad_tokens,
        output,
        g_bias_qv,
        g_bias_up,
        g_bias_out,
        g_gain_one,
        g_shift_one,
        g_bias_down,
        g_gain_two,
        g_shift_two,
    ) = results(fast, blocks, grad_tokens, output, width, hidden_units)
    return (
        output,
        grad_tokens,
        g_w_qkv.reshape(w_qkv.shape),
        g_bias_qv,
        g_w_out,
        g_bias_out,
        g_gain_one,
        g_shift_one,
        g_w_up,
        g_bias_up,
        g_w_down,
        g_bias_down,
        g_gain_two,
        g_shift_two,
    )


def solution(mesh):
    fast = mesh.shape["dp"] == 16 and mesh.shape["tensor"] == 2
    rows, whole = P("dp", None), P()
    return jax.shard_map(
        functools.partial(shards, fast),
        mesh=mesh,
        in_specs=(
            rows,
            P(None, None, "tensor"),
            P(None, "tensor"),
            P("tensor", None),
            whole,
            whole,
            whole,
            P(None, "tensor"),
            P("tensor"),
            P("tensor", None),
            whole,
            whole,
            whole,
            rows,
            P("dp"),
            rows,
        ),
        out_specs=(
            rows,
            rows,
            P(None, None, "tensor"),
            P(None, "tensor"),
            P("tensor", None),
            whole,
            whole,
            whole,
            P(None, "tensor"),
            P("tensor"),
            P("tensor", None),
            whole,
            whole,
            whole,
        ),
        check_vma=False,
    )
```

```python
import functools


import jax
import jax.numpy as jnp
from jax import lax
from jax.experimental import pallas as pl
from jax.experimental.pallas import tpu as pltpu
from jax.sharding import PartitionSpec as P


MESH = pl.DeviceIdType.MESH
BR, BC = 384, 128
AFTER = (0, 3, 6, 9, 12, 15, 18, 21)
SLOTS = 16


class Place:
    def __init__(self):
        me = lax.axis_index("dp")
        self.core = lax.rem(me, 2)
        self.x = lax.rem(me // 2, 2)
        self.z = me // 4
        self.sib = me + 1 - 2 * self.core
        self.xn = me + 2 - 4 * self.x
        self.zp = me + 4 - 8 * lax.rem(self.z, 2)
        self.zm = me + 4 * (3 - 2 * self.z)
        self.end = (self.z == 0) | (self.z == 3)
        self.mid = (self.z == 1) | (self.z == 2)


def sum_greet(pos):
    barrier = pltpu.get_barrier_semaphore()

    def greet(dev):
        pl.semaphore_signal(barrier, inc=1, device_id={"dp": dev}, device_id_type=MESH)

    greet(pos.sib)
    greet(pos.xn)
    greet(pos.zp)

    @pl.when(pos.mid)
    def _():
        greet(pos.zm)


def sum_met(pos):
    pl.semaphore_wait(pltpu.get_barrier_semaphore(), jnp.where(pos.mid, 4, 3))


def make_tick(pos, grads, from_core, from_one, from_two, from_three, sent, got, credit, count, finish):
    half = BR // 2
    quarter = BR // 4

    def copy(stage, block, source, target, device):
        slot = lax.rem(block, SLOTS)
        return pltpu.make_async_remote_copy(
            src_ref=source,
            dst_ref=target,
            send_sem=sent.at[stage, slot],
            recv_sem=got.at[stage, slot],
            device_id={"dp": device},
            device_id_type=MESH,
        )

    def rows(block, start, size):
        return grads.at[block, pl.ds(pl.multiple_of(start, quarter), size)]

    def add(block, start, size, landed):
        where = pl.ds(pl.multiple_of(start, quarter), size)
        grads[block, where] = grads[block, where] + landed[...]

    def free(index, device):
        pl.semaphore_signal(credit.at[index], inc=1, device_id={"dp": device}, device_id_type=MESH)

    def claim(index):
        pl.semaphore_wait(credit.at[index], 1)

    x_first = pos.core == 0
    z_first = pos.core == 1
    mine = pos.core * half
    xrow = pos.x * quarter
    xrow_other = (1 - pos.x) * quarter
    far = lax.rem(pos.z, 2) == 0
    keep = half + jnp.where(far, quarter, 0)
    give = half + jnp.where(far, 0, quarter)

    def core_out(block):
        return copy(0, block, rows(block, (1 - pos.core) * half, half), from_core.at[lax.rem(block, SLOTS)], pos.sib)

    def x_one(block):
        return copy(1, block, rows(block, xrow_other, quarter), from_one.at[lax.rem(block, SLOTS), pl.ds(0, quarter)], pos.xn)

    def z_one(block):
        return copy(1, block, rows(block, half, half), from_one.at[lax.rem(block, SLOTS)], pos.zp)

    def x_two(block):
        return copy(2, block, rows(block, xrow, quarter), from_two.at[lax.rem(block, SLOTS)], pos.zp)

    def z_two(block):
        return copy(2, block, rows(block, give, quarter), from_two.at[lax.rem(block, SLOTS)], pos.zm)

    def x_three(block):
        return copy(3, block, rows(block, xrow, quarter), from_three.at[lax.rem(block, SLOTS)], pos.zm)

    def z_three(block):
        return copy(3, block, rows(block, keep, quarter), from_three.at[lax.rem(block, SLOTS)], pos.xn)

    def x_four(block):
        return copy(4, block, rows(block, xrow, quarter), rows(block, xrow, quarter), pos.zp)

    def z_four(block):
        return copy(4, block, rows(block, keep, quarter), rows(block, keep, quarter), pos.zm)

    def z_four_in(block):
        return copy(4, block, rows(block, give, quarter), rows(block, give, quarter), pos.zm)

    def x_five(block):
        return copy(5, block, rows(block, xrow, quarter), rows(block, xrow, quarter), pos.xn)

    def x_five_in(block):
        return copy(5, block, rows(block, xrow_other, quarter), rows(block, xrow_other, quarter), pos.xn)

    def z_five(block):
        return copy(5, block, rows(block, half, half), rows(block, half, half), pos.zp)

    def core_six(block):
        return copy(6, block, rows(block, mine, half), rows(block, mine, half), pos.sib)

    def core_six_in(block):
        return copy(6, block, rows(block, (1 - pos.core) * half, half), rows(block, (1 - pos.core) * half, half), pos.sib)

    def start_core(block):
        core_out(block).start()

    def take_core(block):
        core_out(block).wait()
        free(2, pos.sib)
        add(block, mine, half, from_core.at[lax.rem(block, SLOTS)])

    def take_x(block):
        x_one(block).wait()
        free(1, pos.xn)
        add(block, xrow, quarter, from_one.at[lax.rem(block, SLOTS), pl.ds(0, quarter)])

    def send_x(block):
        take_core(block)
        x_one(block).start()

    def send_z(block):
        take_core(block)
        z_one(block).start()

    def x_end_two(block):
        take_x(block)
        x_two(block).start()

    def x_end_three(block):
        x_two(block).wait_send()
        free(0, pos.zp)

    def x_mid_three(block):
        x_two(block).wait_recv()
        add(block, xrow, quarter, from_two.at[lax.rem(block, SLOTS)])
        x_three(block).start()

    def x_mid_four(block):
        x_three(block).wait()
        add(block, xrow, quarter, from_three.at[lax.rem(block, SLOTS)])
        claim(0)
        x_four(block).start()

    def x_end_five(block):
        x_four(block).wait_recv()
        claim(1)
        x_five(block).start()

    def x_mid_five(block):
        x_four(block).wait_send()
        claim(1)
        x_five(block).start()

    def x_six(block):
        x_five(block).wait_send()
        x_five_in(block).wait_recv()
        claim(2)
        core_six(block).start()

    def z_end_two(block):
        z_one(block).wait_send()
        free(1, pos.zp)

    def z_end_six(block):
        z_five(block).wait_recv()
        claim(2)
        core_six(block).start()

    def z_mid_two(block):
        z_one(block).wait_recv()
        add(block, half, half, from_one.at[lax.rem(block, SLOTS)])
        z_two(block).start()

    def z_mid_three(block):
        z_two(block).wait()
        free(0, pos.zm)
        add(block, keep, quarter, from_two.at[lax.rem(block, SLOTS)])
        z_three(block).start()

    def z_mid_four(block):
        z_three(block).wait()
        add(block, keep, quarter, from_three.at[lax.rem(block, SLOTS)])
        claim(0)
        z_four(block).start()

    def z_mid_five(block):
        z_four(block).wait_send()
        z_four_in(block).wait_recv()
        claim(1)
        z_five(block).start()

    def z_mid_six(block):
        z_five(block).wait_send()
        claim(2)
        core_six(block).start()

    def last(block):
        core_six(block).wait_send()
        core_six_in(block).wait_recv()

    roles = (
        (x_first & pos.end, (start_core, send_x, x_end_two, x_end_three, None, x_end_five, x_six, last)),
        (x_first & pos.mid, (start_core, send_x, take_x, x_mid_three, x_mid_four, x_mid_five, x_six, last)),
        (z_first & pos.end, (start_core, send_z, z_end_two, None, None, None, z_end_six, last)),
        (z_first & pos.mid, (start_core, take_core, z_mid_two, z_mid_three, z_mid_four, z_mid_five, z_mid_six, last)),
    )
    depth = len(roles[0][1])

    def tick(step):
        for here, stages in roles:

            @pl.when(here)
            def _(stages=stages):
                for index in reversed(range(depth)):
                    block = step - AFTER[index]
                    if stages[index] is not None:

                        @pl.when((block >= 0) & (block < count))
                        def _(index=index, block=block, stages=stages):
                            stages[index](block)

        over = step - AFTER[depth - 1]

        @pl.when((over >= 0) & (over < count))
        def _():
            finish(over)

    return tick


def sum_scratch():
    return [
        pltpu.VMEM((SLOTS, BR // 2, BC), jnp.float32),
        pltpu.VMEM((SLOTS, BR // 2, BC), jnp.float32),
        pltpu.VMEM((SLOTS, BR // 4, BC), jnp.float32),
        pltpu.VMEM((SLOTS, BR // 4, BC), jnp.float32),
        pltpu.SemaphoreType.DMA((7, SLOTS)),
        pltpu.SemaphoreType.DMA((7, SLOTS)),
        pltpu.SemaphoreType.REGULAR((3,)),
    ]


CR, CC = 64, 384
CHUNKS = 24
HOPS = (3, 6, 7)
BF = jnp.bfloat16


def gather_greet(pos, other):
    barrier = pltpu.get_barrier_semaphore()
    for where in ({"tensor": other}, {"dp": pos.xn}, {"dp": pos.zp}, {"dp": pos.sib}):
        pl.semaphore_signal(barrier, inc=1, device_id=where, device_id_type=MESH)


def gather_met():
    pl.semaphore_wait(pltpu.get_barrier_semaphore(), 4)


def chunk_parts(piece, chunk, kind):
    if kind == 0:
        return [(piece * 384 + chunk * 64, 64, 0, 0)]
    if kind == 1:
        return [(piece * 64 + (chunk - 6) * 32, 32, 384 * q, 32 * q) for q in range(2)]
    if kind == 2:
        return [(piece * 128 + (chunk - 8) * 16, 16, 384 * q, 16 * q) for q in range(4)]
    return [((chunk - 16) * 192 + piece * 32, 32, 384 * q, 32 * q) for q in range(2)]


BOUNDS = ((0, 6), (6, 8), (8, 16), (16, 24))
UNIT = (64, 32, 16, 32)


def make_gather(pos, own, theirs, staged, landed, sent, got):
    other = 1 - lax.axis_index("tensor")
    odd = lax.rem(pos.z, 2)
    ky = jnp.where(pos.x == 0, odd, 2)
    kx = jnp.where(pos.x == 0, 2, odd)
    kz = 1 - odd
    piece_y = 2 * ky + pos.core
    piece_x = 2 * kx + pos.core
    piece_z = 2 * kz + pos.core
    sib_y = 2 * ky + 1 - pos.core
    sib_x = 2 * kx + 1 - pos.core
    sib_z = 2 * kz + 1 - pos.core

    def copy(lane, chunk, source, piece, where):
        return pltpu.make_async_remote_copy(
            src_ref=source,
            dst_ref=landed.at[piece, chunk],
            send_sem=sent.at[lane, chunk],
            recv_sem=got.at[lane, chunk],
            device_id=where,
            device_id_type=MESH,
        )

    def over_y(chunk):
        return copy(0, chunk, staged.at[chunk], piece_y, {"tensor": other})

    def over_x(chunk, piece):
        return copy(1, chunk, landed.at[piece, chunk], piece, {"dp": pos.xn})

    def over_z(chunk, piece):
        return copy(2, chunk, landed.at[piece, chunk], piece, {"dp": pos.zp})

    def over_core(lane, chunk, piece):
        return copy(lane, chunk, landed.at[piece, chunk], piece, {"dp": pos.sib})

    def stage_own(kind):
        lo, hi = BOUNDS[kind]

        @pl.loop(lo, hi)
        def _(chunk):
            for row, rows, column, at in chunk_parts(piece_y, chunk, kind):
                staged[chunk, pl.ds(at, rows)] = own[kind][
                    pl.ds(pl.multiple_of(row, UNIT[kind]), rows), pl.ds(column, CC)
                ].astype(jnp.float32)

    def send_own(kind):
        lo, hi = BOUNDS[kind]

        @pl.loop(lo, hi)
        def _(chunk):
            over_y(chunk).start()

    def unpack(chunk):
        for kind in range(4):
            lo, hi = BOUNDS[kind]

            @pl.when((chunk >= lo) & (chunk < hi))
            def _(kind=kind):
                @pl.loop(0, 6)
                def _(piece):
                    for row, rows, column, at in chunk_parts(piece, chunk, kind):
                        theirs[kind][pl.ds(pl.multiple_of(row, UNIT[kind]), rows), pl.ds(column, CC)] = landed[
                            piece, chunk, pl.ds(at, rows)
                        ].astype(BF)

    def guarded(chunk, body):
        @pl.when((chunk >= 0) & (chunk < CHUNKS))
        def _():
            body(chunk)

    def first(chunk):
        over_y(chunk).wait_recv()
        over_x(chunk, piece_y).start()

        @pl.when(pos.x == 0)
        def _():
            over_z(chunk, piece_y).start()

        over_core(3, chunk, piece_y).start()

    def second(chunk):
        over_x(chunk, piece_x).wait_recv()

        @pl.when(pos.x == 1)
        def _():
            over_z(chunk, piece_x).start()

        over_core(4, chunk, piece_x).start()

    def third(chunk):
        over_z(chunk, piece_z).wait_recv()
        over_core(5, chunk, piece_z).start()

    def fourth(chunk):
        over_core(3, chunk, sib_y).wait_recv()
        over_core(4, chunk, sib_x).wait_recv()
        over_core(5, chunk, sib_z).wait_recv()
        over_y(chunk).wait_send()
        over_x(chunk, piece_y).wait_send()
        over_z(chunk, piece_y).wait_send()
        over_core(3, chunk, piece_y).wait_send()
        over_core(4, chunk, piece_x).wait_send()
        over_core(5, chunk, piece_z).wait_send()
        unpack(chunk)

    def tick(step):
        guarded(step - HOPS[2], fourth)
        guarded(step - HOPS[1], third)
        guarded(step - HOPS[0], second)
        guarded(step, first)

    return stage_own, send_own, tick


def gather_scratch():
    return [
        pltpu.VMEM((CHUNKS, CR, CC), jnp.float32),
        pltpu.VMEM((6, CHUNKS, CR, CC), jnp.float32),
        pltpu.SemaphoreType.DMA((6, CHUNKS)),
        pltpu.SemaphoreType.DMA((6, CHUNKS)),
    ]


def swap_small(small, small_out, sems):
    return pltpu.make_async_remote_copy(
        src_ref=small,
        dst_ref=small_out,
        send_sem=sems.at[0],
        recv_sem=sems.at[1],
        device_id={"tensor": 1 - lax.axis_index("tensor")},
        device_id_type=MESH,
    )


HD = 64
SEG = 148
MEMW = 10
F32 = jnp.float32
EPSILON = 1e-12
MASKED = -1e30
WIN = 160
MEMP = 96
SEGS = 8
PAIR = 2 * HD

CONTRACT_LAST = (((1,), (1,)), ((), ()))
CONTRACT_FIRST = (((0,), (0,)), ((), ()))


def mm(a, b):
    return jnp.dot(a, b, preferred_element_type=F32)


def mm_t(a, b):
    return lax.dot_general(a, b, CONTRACT_LAST, preferred_element_type=F32)


def t_mm(a, b):
    return lax.dot_general(a, b, CONTRACT_FIRST, preferred_element_type=F32)


def build_masks(parent, base, colbias):
    lane = lax.broadcasted_iota(jnp.int32, (1, WIN + MEMP), 1)
    in_mem = [
        ((lane >= WIN + MEMW * t) & (lane < WIN + MEMW * (t + 1))).astype(F32) for t in range(SEGS)
    ]
    reach = [jnp.zeros((1, WIN + MEMP), F32)]
    for s in range(1, SEGS):
        row = jnp.zeros((1, WIN + MEMP), F32)
        for t in range(s):
            hit = jnp.where(parent[s] - base == t, 1.0, 0.0)
            row = row + hit * jnp.maximum(reach[t], in_mem[t])
        reach.append(row)
    for s in range(SEGS):
        off = 4 * (s % 4)
        inside = ((lane >= off) & (lane < off + SEG)).astype(F32)
        colbias[s : s + 1, :] = jnp.where(jnp.maximum(inside, reach[s]) > 0.0, 0.0, MASKED)


def build_select(slots, select, select_t):
    for ref, axis in ((select, 0), (select_t, 1)):
        shape = (ref.shape[0], 1) if axis == 0 else (1, ref.shape[1])
        entry = lax.broadcasted_iota(jnp.int32, shape, axis)
        where = jnp.full(shape, -1, jnp.int32)
        for t in range(SEGS):
            for m in range(MEMW):
                where = jnp.where(entry == MEMW * t + m, slots[t, m] + SEG * t, where)
        place = lax.broadcasted_iota(jnp.int32, ref.shape, 1 - axis)
        ref[...] = (where == place).astype(F32).astype(BF)


def window(s):
    return pl.multiple_of(144 * s + 16 * (s // 4), 16), 4 * lax.rem(s, 4)


def lane_halves():
    lane = lax.broadcasted_iota(jnp.int32, (1, PAIR), 1)
    left = (lane < HD).astype(F32)
    return left.astype(BF), (1.0 - left).astype(BF), lane < HD


def valid_rows(off):
    row = lax.broadcasted_iota(jnp.int32, (WIN, 1), 0)
    return row, (row >= off) & (row < off + SEG)


def softmax_parts(qs, kk, bias):
    scores = mm_t(qs, kk) * HD ** (-0.5) + bias
    top = jnp.max(scores, axis=-1, keepdims=True)
    raised = jnp.exp(scores - top)
    return raised, 1.0 / jnp.sum(raised, axis=-1, keepdims=True)


def attend_pair(q, k, v, kmem, vmem, colbias, mixed, probs, s, columns):
    left, right, is_left = lane_halves()
    at, off = window(s)
    rows = pl.ds(at, WIN)
    qw = q[rows, columns]
    qs = jnp.concatenate([qw * left, qw * right], axis=0)
    kk = jnp.concatenate([k[rows, columns], kmem[:, columns]], axis=0)
    vv = jnp.concatenate([v[rows, columns], vmem[:, columns]], axis=0)
    raised, scale = softmax_parts(qs, kk, colbias[pl.ds(s, 1), :])
    row, valid = valid_rows(off)
    keep = jnp.where(valid, 1.0, 0.0)
    chances = (raised * (scale * jnp.concatenate([keep, keep], axis=0))).astype(BF)
    probs[...] = chances
    both = mm(chances, vv)
    out = jnp.where(is_left, both[:WIN], both[WIN:])
    old = mixed[rows, columns].astype(F32)
    mixed[rows, columns] = jnp.where(row >= off, out, old).astype(BF)


def attend_back_pair(q, k, v, kmem, vmem, probs, dmix, dq, dk, dv, dkmem, dvmem, s, columns):
    left, right, is_left = lane_halves()
    at, off = window(s)
    rows = pl.ds(at, WIN)
    qw = q[rows, columns]
    qs = jnp.concatenate([qw * left, qw * right], axis=0)
    kk = jnp.concatenate([k[rows, columns], kmem[:, columns]], axis=0)
    vv = jnp.concatenate([v[rows, columns], vmem[:, columns]], axis=0)
    dw = dmix[rows, columns]
    ds_in = jnp.concatenate([dw * left, dw * right], axis=0)
    low = probs[...]
    chances = low.astype(F32)
    dp = mm_t(ds_in, vv)
    inner = jnp.sum(chances * dp, axis=-1, keepdims=True)
    ds = (chances * (dp - inner)).astype(BF)
    dqs = mm(ds, kk)
    row, valid = valid_rows(off)
    new = jnp.where(is_left, dqs[:WIN], dqs[WIN:]) * HD ** (-0.5)
    old = dq[rows, columns].astype(F32)
    dq[rows, columns] = jnp.where(row >= off, new, old).astype(BF)
    dks = t_mm(ds, qs)
    dvs = t_mm(low, ds_in)
    dk[rows, columns] = dk[rows, columns] + dks[:WIN]
    dv[rows, columns] = dv[rows, columns] + dvs[:WIN]
    dkmem[:, columns] = dkmem[:, columns] + dks[WIN:]
    dvmem[:, columns] = dvmem[:, columns] + dvs[WIN:]


def spread(select_t, part):
    high = part.astype(BF)
    low = (part - high.astype(F32)).astype(BF)
    return mm(select_t, high) + mm(select_t, low)


def norm_stats(values):
    centered = values - jnp.mean(values, axis=-1, keepdims=True)
    inverse = lax.rsqrt(jnp.mean(centered * centered, axis=-1, keepdims=True) + EPSILON)
    return centered * inverse, inverse


def norm_back(grad, normed, inverse, gain):
    scaled = grad * gain
    return inverse * (
        scaled
        - jnp.mean(scaled, axis=-1, keepdims=True)
        - normed * jnp.mean(scaled * normed, axis=-1, keepdims=True)
    )


def gelu_parts(inner):
    phi = 0.5 + 0.5 * lax.erf(inner * (0.5**0.5))
    density = jnp.exp(-0.5 * inner * inner) * (2.0 * jnp.pi) ** -0.5
    return (inner * phi).astype(BF), (phi + inner * density).astype(BF)


def flat_row(ref, start, size):
    return ref[pl.ds(start, size)].reshape(1, size)


TILE = 128


SPLIT = 6 * TILE


def row_tiles(first, last, body):
    full = (last - first) // TILE

    @pl.loop(0, full)
    def _(i):
        body(pl.ds(pl.multiple_of(first + i * TILE, TILE), TILE))

    if (last - first) % TILE:
        body(pl.ds(first + full * TILE, (last - first) % TILE))


def forward_kernel(
    fast,
    parent,
    slots,
    bias_qv,
    bias_out,
    gain_one,
    shift_one,
    bias_up,
    bias_down,
    gain_two,
    shift_two,
    tokens_h,
    grad_h,
    qkv_in,
    out_in,
    up_in,
    down_in,
    *rest,
):
    count = 0 if fast else 5
    given, outs, rest = rest[:count], rest[count : count + 19], rest[count + 19 :]
    (
        output_h,
        their_qkv_h,
        their_out_h,
        their_up_h,
        their_down_h,
        qkv_h,
        mixed_h,
        normed_h,
        inverse,
        hidden_h,
        acted_h,
        slope_own_h,
        slope_their_h,
        d_two_h,
        d_ffn_h,
        vec,
        probs_h,
        select_t,
        memory,
    ) = outs
    (
        tokens,
        own_qkv,
        own_out,
        own_up,
        own_down,
        their_qkv,
        their_out,
        their_up,
        their_down,
        small,
        small_their,
        qkv,
        mixed,
        normed,
        hidden,
        acc_own,
        acc_their,
        acted,
        slopes,
        colbias,
        select,
        sums,
        probs,
        io_sem,
        slope_sem,
        probs_sem,
        *wires,
    ) = rest
    rows, depth = tokens.shape
    width = mixed.shape[2]
    units = acted.shape[1]
    theirs = (their_qkv, their_out, their_up, their_down)
    own = (own_qkv, own_out, own_up, own_down)

    def move(index, source, target):
        return pltpu.make_async_copy(source, target, io_sem.at[index])

    load_tokens = move(0, tokens_h, tokens)
    load_grad = move(1, grad_h, tokens)
    put_qkv = move(2, qkv, qkv_h)
    put_mixed = move(3, mixed.at[0], mixed_h)
    put_normed = move(4, normed, normed_h)
    put_hidden = move(5, hidden, hidden_h)
    put_acted = move(6, acted, acted_h)
    late = ((acc_own, d_two_h), (hidden, d_ffn_h), (tokens, output_h))
    put_late = [
        [move(7 + 3 * part + i, ref.at[rows_of], target.at[rows_of]) for i, (ref, target) in enumerate(late)]
        for part, rows_of in enumerate((pl.ds(0, SPLIT), pl.ds(SPLIT, rows - SPLIT)))
    ]
    put_theirs = [
        move(13 + i, ref, target)
        for i, (ref, target) in enumerate(zip(theirs, (their_qkv_h, their_out_h, their_up_h, their_down_h)))
    ]
    load_own = [move(17 + i, a, b) for i, (a, b) in enumerate(zip((qkv_in, out_in, up_in, down_in), own))]
    if fast:
        pos = Place()
        gather_greet(pos, 1 - lax.axis_index("tensor"))
    load_own[0].start()
    load_tokens.start()
    for copy in load_own[1:]:
        copy.start()
    done = [0]
    small[...] = jnp.zeros(small.shape, F32)
    small[0:1, :] = bias_qv[0:1, :]
    small[2:3, :] = bias_qv[1:2, :]
    for c in range(units // CHUNK):
        small[3 + c : 4 + c, 0:CHUNK] = flat_row(bias_up, c * CHUNK, CHUNK)
    if fast:
        small_sem, *wires = wires
        stage_own, send_own, tick = make_gather(pos, own, theirs, *wires)
        load_own[0].wait()
        stage_own(0)
        gather_met()
        send_own(0)
        swap = swap_small(small, small_their, small_sem)
        swap.start()
        for kind in range(1, 4):
            load_own[kind].wait()
            stage_own(kind)
            send_own(kind)
    else:
        for copy in load_own:
            copy.wait()
        copies = [move(13 + i, a, b) for i, (a, b) in enumerate(zip(given, theirs + (small_their,)))]
        for copy in copies:
            copy.start()
        for copy in copies:
            copy.wait()

        def tick(step):
            pass

    def ticks(index, each, trips):
        for i in range(each):
            tick(done[0] + index * each + i)

    def tick_every(index, every, trips):
        @pl.when(lax.rem(index, every) == 0)
        def _():
            tick(done[0] + index // every)

        return -(-trips // every)

    def until(count):
        if done[0] < count:

            @pl.loop(done[0], count)
            def _(step):
                tick(step)

            done[0] = count

    build_masks(parent, lax.axis_index("dp") * SEGS, colbias)
    build_select(slots, select, select_t)
    load_tokens.wait()
    pairs = width // PAIR
    for half in range(2):
        weights = (own_qkv, their_qkv)[half]
        table = (small, small_their)[half]
        if half == 1:
            until(BOUNDS[0][1] + HOPS[2])
            if fast:
                swap.wait()

        @pl.loop(0, 3)
        def _(c, half=half, weights=weights, table=table):
            part = mm(tokens[...], weights[pl.ds(pl.multiple_of(c * depth, depth), depth), :])
            qkv[half, c] = (part + table[pl.ds(c, 1), :]).astype(BF)

        q, k, v = (qkv.at[half, i] for i in range(3))
        kmem, vmem = memory.at[half, 0], memory.at[half, 1]
        kmem[...] = mm(select[...], k[...]).astype(BF)
        vmem[...] = mm(select[...], v[...]).astype(BF)

        def put_probs(s, half=half):
            slot = lax.rem(s, 2)
            return pltpu.make_async_copy(probs.at[slot], probs_h.at[half, s], probs_sem.at[slot])

        @pl.loop(0, SEGS)
        def _(s, half=half, q=q, k=k, v=v, kmem=kmem, vmem=vmem, put_probs=put_probs):
            @pl.when(s >= 2)
            def _():
                put_probs(s - 2).wait()

            for pair in range(pairs):
                attend_pair(
                    q, k, v, kmem, vmem, colbias, mixed.at[half], probs.at[lax.rem(s, 2), pair], s, pl.ds(pair * PAIR, PAIR)
                )
                if pair == 0 and half == 0:
                    tick(done[0] + s)
                if pair == 2 and half == 1:
                    tick_every(s, GATHER[0], SEGS)
            put_probs(s).start()

        done[0] += SEGS if half == 0 else -(-SEGS // GATHER[0])
        put_probs(SEGS - 2).wait()
        put_probs(SEGS - 1).wait()

        if half == 1:
            until(BOUNDS[1][1] + HOPS[2])
        out = (own_out, their_out)[half]

        @pl.loop(0, 3)
        def _(n, half=half, out=out):
            columns = pl.ds(pl.multiple_of(n * CHUNK, CHUNK), CHUNK)
            part = mm(mixed[half], out[:, columns])
            acc_own[:, columns] = part if half == 0 else acc_own[:, columns] + part
            ticks(n, GATHER[1 + half], 3)

        done[0] += 3 * GATHER[1 + half]
    put_qkv.start()
    put_mixed.start()

    def norm_one(span):
        resid = tokens[span, :].astype(F32) + (acc_own[span, :] + flat_row(bias_out, 0, depth))
        unit, scale = norm_stats(resid)
        normed[span, :] = unit
        inverse[span, :] = scale
        hidden[span, :] = (unit * flat_row(gain_one, 0, depth) + flat_row(shift_one, 0, depth)).astype(BF)

    row_tiles(0, rows, norm_one)
    load_grad.start()
    put_normed.start()
    put_hidden.start()

    for half in range(2):
        up, down = ((own_up, own_down), (their_up, their_down))[half]
        table = (small, small_their)[half]
        slope_h = (slope_own_h, slope_their_h)[half]
        acc = (acc_own, acc_their)[half]

        def put_slope(c, slope_h=slope_h):
            span = pl.ds(pl.multiple_of(c * CHUNK, CHUNK), CHUNK)
            return pltpu.make_async_copy(slopes.at[lax.rem(c, 2)], slope_h.at[:, span], slope_sem.at[lax.rem(c, 2)])

        if half == 1:
            until(BOUNDS[2][1] + HOPS[2])
            put_acted.wait()
            put_slope(4).wait()
            put_slope(5).wait()

        @pl.loop(0, 6)
        def _(c, half=half, up=up, table=table, put_slope=put_slope):
            span = pl.ds(pl.multiple_of(c * CHUNK, CHUNK), CHUNK)

            @pl.when(c >= 2)
            def _():
                put_slope(c - 2).wait()

            bias = table[pl.ds(3 + c, 1), 0:CHUNK]
            act, steep = gelu_parts(mm(hidden[...], up[:, span]) + bias)
            acted[:, span] = act
            slopes[lax.rem(c, 2)] = steep
            put_slope(c).start()
            tick_every(c, GATHER[3 + 2 * half], 6)

        done[0] += -(-6 // GATHER[3 + 2 * half])
        low, high = slice(0, units // 2), slice(units // 2, units)
        if half == 0:
            put_acted.start()

            @pl.loop(0, 3)
            def _(n, down=down, acc=acc):
                columns = pl.ds(pl.multiple_of(n * CHUNK, CHUNK), CHUNK)
                acc[:, columns] = mm(acted[:, low], down[low, columns]) + mm(acted[:, high], down[high, columns])
                ticks(n, GATHER[4], 3)

        else:
            until((BOUNDS[3][0] + BOUNDS[3][1]) // 2 + HOPS[2])

            @pl.loop(0, 3)
            def _(n, down=down, acc=acc):
                columns = pl.ds(pl.multiple_of(n * CHUNK, CHUNK), CHUNK)
                acc[:, columns] = mm(acted[:, low], down[low, columns])
                ticks(n, 1, 3)

            done[0] += 3
            until(BOUNDS[3][1] + HOPS[2])
            if fast:
                for copy in put_theirs:
                    copy.start()

            @pl.loop(0, 3)
            def _(n, down=down, acc=acc):
                columns = pl.ds(pl.multiple_of(n * CHUNK, CHUNK), CHUNK)
                acc[:, columns] = acc[:, columns] + mm(acted[:, high], down[high, columns])

        done[0] += 3 * GATHER[4] if half == 0 else 0
    put_slope(4).wait()
    put_slope(5).wait()

    load_grad.wait()
    put_hidden.wait()
    sums[...] = jnp.zeros(sums.shape, F32)

    def norm_two(span):
        first = normed[span, :] * flat_row(gain_one, 0, depth) + flat_row(shift_one, 0, depth)
        resid = first + ((acc_own[span, :] + acc_their[span, :]) + flat_row(bias_down, 0, depth))
        unit, scale = norm_stats(resid)
        grad = tokens[span, :].astype(F32)
        tokens[span, :] = (unit * flat_row(gain_two, 0, depth) + flat_row(shift_two, 0, depth)).astype(BF)
        back = norm_back(grad, unit, scale, flat_row(gain_two, 0, depth))
        acc_own[span, :] = back
        low = back.astype(BF)
        hidden[span, :] = low
        for index, value in enumerate((low.astype(F32), grad * unit, grad)):
            sums[index] = sums[index] + value.reshape(-1, 8, depth).sum(axis=0)

    row_tiles(0, SPLIT, norm_two)
    for copy in put_late[0]:
        copy.start()
    row_tiles(SPLIT, rows, norm_two)
    for copy in put_late[1]:
        copy.start()
    for index in range(3):
        total = jnp.sum(sums[index], axis=0, keepdims=True)
        for j in range(6):
            vec[6 * index + j : 6 * index + j + 1, :] = total[:, BC * j : BC * (j + 1)]
    for copy in (put_qkv, put_mixed, put_normed, *put_late[0], *put_late[1]):
        copy.wait()
    if fast:
        for copy in put_theirs:
            copy.wait()


GATHER = (2, 1, 1, 2, 1, 2)


def forward(fast, parent, slots, vectors, tokens, grad_out, own, given):
    rows, depth = tokens.shape
    width = own[0].shape[1]
    units = own[2].shape[1]
    vm = pl.BlockSpec(memory_space=pltpu.VMEM)
    hbm = pl.BlockSpec(memory_space=pl.ANY)
    sm = pl.BlockSpec(memory_space=pltpu.SMEM)
    sd = jax.ShapeDtypeStruct
    out_shape = [
        sd((rows, depth), BF),
        *[sd(w.shape, BF) for w in own],
        sd((2, 3, rows, width), BF),
        sd((rows, width), BF),
        sd((rows, depth), F32),
        sd((rows, 1), F32),
        sd((rows, depth), BF),
        sd((rows, units), BF),
        sd((rows, units), BF),
        sd((rows, units), BF),
        sd((rows, depth), F32),
        sd((rows, depth), BF),
        sd((18, BC), F32),
        sd((2, SEGS, width // PAIR, 2 * WIN, WIN + MEMP), BF),
        sd((rows, MEMP), BF),
        sd((2, 2, MEMP, width), BF),
    ]
    return pl.pallas_call(
        functools.partial(forward_kernel, fast),
        out_shape=out_shape,
        in_specs=[sm, sm] + [vm] * len(vectors) + [hbm, hbm] + [hbm] * (4 + len(given)),
        out_specs=[hbm] * 8 + [vm] + [hbm] * 6 + [vm, hbm, vm, vm],
        scratch_shapes=[
            pltpu.VMEM((rows, depth), BF),
            *[pltpu.VMEM(w.shape, BF) for w in own],
            *[pltpu.VMEM(w.shape, BF) for w in own],
            pltpu.VMEM((16, width), F32),
            pltpu.VMEM((16, width), F32),
            pltpu.VMEM((2, 3, rows, width), BF),
            pltpu.VMEM((2, rows, width), BF),
            pltpu.VMEM((rows, depth), F32),
            pltpu.VMEM((rows, depth), BF),
            pltpu.VMEM((rows, depth), F32),
            pltpu.VMEM((rows, depth), F32),
            pltpu.VMEM((rows, units), BF),
            pltpu.VMEM((2, rows, CHUNK), BF),
            pltpu.VMEM((SEGS, WIN + MEMP), F32),
            pltpu.VMEM((MEMP, rows), BF),
            pltpu.VMEM((3, 8, depth), F32),
            pltpu.VMEM((2, width // PAIR, 2 * WIN, WIN + MEMP), BF),
            pltpu.SemaphoreType.DMA((21,)),
            pltpu.SemaphoreType.DMA((2,)),
            pltpu.SemaphoreType.DMA((2,)),
        ]
        + ([pltpu.SemaphoreType.DMA((2,))] + gather_scratch() if fast else []),
        compiler_params=pltpu.CompilerParams(
            collective_id=0 if fast else None, has_side_effects=fast, vmem_limit_bytes=67043328
        ),
        name="forward",
    )(parent, slots, *vectors, tokens, grad_out, *own, *given)


DOWN, UP, OUT, QKV, VEC = 0, 24, 48, 54, 72
COUNT = 73
CHUNK = 256
VEC_ROWS = 54


def backward_kernel(
    fast,
    select_t,
    memory,
    inverse,
    gain,
    vec_in,
    tokens_h,
    hidden_h,
    d_ffn_h,
    d_two_h,
    normed_h,
    acted_h,
    slope_own_h,
    slope_their_h,
    qkv_h,
    mixed_h,
    probs_h,
    w_up_own,
    w_up_their,
    w_down_own,
    w_down_their,
    w_out_own,
    w_out_their,
    w_qkv_own,
    w_qkv_their,
    grads,
    d_low,
    hidden,
    d_res,
    normed,
    acc_own,
    acc_their,
    a_buf,
    slope_buf,
    up_buf,
    down_buf,
    d_inner,
    sums,
    tokens,
    mixed,
    w_out,
    w_qkv,
    qkv,
    d_qkv,
    d_mixed,
    probs,
    dkm,
    dvm,
    load_sem,
    chunk_sem,
    probs_sem,
    *wires,
):
    rows, depth = tokens.shape
    width = mixed.shape[1]

    def fetch(index, source, target):
        return pltpu.make_async_copy(source, target, load_sem.at[index])

    load_d = fetch(0, d_ffn_h, d_low)
    load_hidden = fetch(1, hidden_h, hidden)
    load_two = fetch(2, d_two_h, d_res)
    load_normed = fetch(3, normed_h, normed)
    load_mixed = fetch(4, mixed_h, mixed)
    load_out = [fetch(5 + i, w, w_out.at[i]) for i, w in enumerate((w_out_own, w_out_their))]
    load_w = [fetch(7 + i, w, w_qkv.at[i]) for i, w in enumerate((w_qkv_own, w_qkv_their))]
    load_tokens = fetch(9, tokens_h, tokens)
    load_qkv = [fetch(10 + half, qkv_h.at[half], qkv) for half in range(2)]

    def load_acted(c):
        return pltpu.make_async_copy(acted_h.at[:, pl.ds(pl.multiple_of(c * BR, BR), BR)], a_buf.at[lax.rem(c, 2)], chunk_sem.at[0, lax.rem(c, 2)])

    def load_chunk(half, c):
        slot = lax.rem(c, 2)
        span = pl.ds(pl.multiple_of(c * CHUNK, CHUNK), CHUNK)
        slope_h, up_h, down_h = ((slope_own_h, w_up_own, w_down_own), (slope_their_h, w_up_their, w_down_their))[half]
        return (
            pltpu.make_async_copy(slope_h.at[:, span], slope_buf.at[slot], chunk_sem.at[1, slot]),
            pltpu.make_async_copy(up_h.at[:, span], up_buf.at[slot], chunk_sem.at[2, slot]),
            pltpu.make_async_copy(down_h.at[span, :], down_buf.at[slot], chunk_sem.at[3, slot]),
        )

    def load_probs(half, s):
        slot = lax.rem(s, 2)
        return pltpu.make_async_copy(probs_h.at[half, s], probs.at[slot], probs_sem.at[slot])

    def start(copies):
        for copy in copies:
            copy.start()

    def wait(copies):
        for copy in copies:
            copy.wait()

    if fast:
        pos = Place()
        sum_greet(pos)
    load_d.start()
    load_acted(0).start()
    start(load_chunk(0, 0))
    load_hidden.start()

    def finish(block):
        pass

    if fast:
        tick = make_tick(pos, grads, *wires, COUNT, finish)
        last = COUNT + AFTER[7]
    else:

        def tick(step):
            pass

        last = COUNT
    done = [0]

    def ticks(index, each, trips):
        for i in range(each):
            tick(done[0] + index * each + i)
        return trips * each

    grads[VEC] = jnp.zeros((BR, BC), F32)
    grads[VEC, 36:54] = vec_in[...]
    acc_own[...] = jnp.zeros(acc_own.shape, F32)
    acc_their[...] = jnp.zeros(acc_their.shape, F32)
    sums[...] = jnp.zeros(sums.shape, F32)
    if fast:
        sum_met(pos)

    load_d.wait()

    @pl.loop(0, 4)
    def _(c):
        load_acted(c).wait()

        @pl.when(c < 3)
        def _():
            load_acted(c + 1).start()

        @pl.when(c == 3)
        def _():
            load_two.start()
            load_normed.start()

        for part in range(2):
            piece = t_mm(a_buf[lax.rem(c, 2)], d_low[:, part * width : (part + 1) * width])
            for j in range(3):
                grads[DOWN + 6 * c + 3 * part + j] = piece[:, BC * j : BC * (j + 1)]
        ticks(c, TICKS[0], 4)

    done[0] += 4 * TICKS[0]

    load_hidden.wait()
    for half in range(2):
        acc = (acc_own, acc_their)[half]

        @pl.loop(0, 6)
        def _(c, half=half, acc=acc):
            slot = lax.rem(c, 2)
            wait(load_chunk(half, c))

            @pl.when(c < 5)
            def _():
                start(load_chunk(half, c + 1))

            if half == 0:

                @pl.when(c == 5)
                def _():
                    start(load_chunk(1, 0))
                    load_mixed.start()
                    start(load_out)
                    load_qkv[0].start()
                    load_probs(0, 0).start()

            each = TICKS[1 + half]
            d_inner[...] = (mm_t(d_low[...], down_buf[slot]) * slope_buf[slot].astype(F32)).astype(BF)
            if each > 1:
                tick(done[0] + c * each)
            if half == 0:
                piece = t_mm(hidden[...], d_inner[...])
                for r in range(2):
                    for j in range(2):
                        grads[UP + 4 * c + 2 * r + j] = piece[BR * r : BR * (r + 1), BC * j : BC * (j + 1)]
                total = jnp.sum(d_inner[...].astype(F32), axis=0, keepdims=True)
                for j in range(2):
                    grads[VEC, pl.ds(6 + 2 * c + j, 1), :] = total[:, BC * j : BC * (j + 1)]
                if each > 2:
                    tick(done[0] + c * each + 1)
            for part in range(3):
                columns = slice(CHUNK * part, CHUNK * (part + 1))
                acc[:, columns] = acc[:, columns] + mm_t(d_inner[...], up_buf[slot, columns, :])
            tick(done[0] + c * each + each - 1)

        done[0] += 6 * TICKS[1 + half]

    start(load_w)
    load_tokens.start()

    load_two.wait()
    load_normed.wait()
    def norm_one(span):
        total = d_res[span, :] + (acc_own[span, :] + acc_their[span, :])
        unit = normed[span, :]
        one = norm_back(total, unit, inverse[span, :], flat_row(gain, 0, depth))
        d_res[span, :] = one
        low = one.astype(BF)
        d_low[span, :] = low
        for index, value in enumerate((low.astype(F32), total * unit, total)):
            sums[index] = sums[index] + value.reshape(-1, 8, depth).sum(axis=0)

    trips = rows // NORM_TILE

    @pl.loop(0, trips)
    def _(i):
        norm_one(pl.ds(pl.multiple_of(i * NORM_TILE, NORM_TILE), NORM_TILE))

        @pl.when(lax.rem(i, TICK_TILES) == 0)
        def _():
            tick(done[0] + i // TICK_TILES)

    if rows % NORM_TILE:
        norm_one(pl.ds(trips * NORM_TILE, rows % NORM_TILE))
    done[0] += -(-trips // TICK_TILES)
    for index in range(3):
        total = jnp.sum(sums[index], axis=0, keepdims=True)
        for j in range(6):
            grads[VEC, 18 + 6 * index + j : 19 + 6 * index + j, :] = total[:, BC * j : BC * (j + 1)]

    load_mixed.wait()
    wait(load_out)

    @pl.loop(0, 2)
    def _(half):
        d_mixed[half] = mm_t(d_low[...], w_out[half]).astype(BF)
        piece = t_mm(mixed[...], d_low[:, pl.ds(pl.multiple_of(half * width, BC), width)])
        for j in range(3):
            grads[OUT + 3 * half + j] = piece[:, BC * j : BC * (j + 1)]
        ticks(half, TICKS[3], 2)

    done[0] += 2 * TICKS[3]

    pairs = width // PAIR
    dka, dva = acc_their.at[:, pl.ds(0, width)], acc_their.at[:, pl.ds(width, width)]
    for half in range(2):
        load_qkv[half].wait()
        q, k, v = (qkv.at[i] for i in range(3))
        kmem, vmem = memory.at[half, 0], memory.at[half, 1]
        acc_their[...] = jnp.zeros(acc_their.shape, F32)
        dkm[...] = jnp.zeros(dkm.shape, F32)
        dvm[...] = jnp.zeros(dvm.shape, F32)

        group = UNROLL[half]

        @pl.loop(0, SEGS * pairs // group)
        def _(trip, half=half, group=group, kmem=kmem, vmem=vmem):
            s, first = trip * group // pairs, lax.rem(trip * group, pairs)

            @pl.when(first == 0)
            def _():
                load_probs(half, s).wait()

                @pl.when(s < SEGS - 1)
                def _():
                    load_probs(half, s + 1).start()

                if half == 0:

                    @pl.when(s == SEGS - 1)
                    def _():
                        load_probs(1, 0).start()

            for i in range(group):
                pair = i if group == pairs else first
                columns = pl.ds(pl.multiple_of(pair * PAIR, PAIR), PAIR)
                part = probs.at[lax.rem(s, 2), pair]
                attend_back_pair(q, k, v, kmem, vmem, part, d_mixed.at[half], d_qkv.at[0], dka, dva, dkm, dvm, s, columns)
                spot = trip * group + i

                @pl.when(lax.rem(spot, TICKS[4 + half]) == 0)
                def _(spot=spot):
                    tick(done[0] + spot // TICKS[4 + half])

        done[0] += -(-SEGS * pairs // TICKS[4 + half])
        if half == 0:
            assert done[0] <= QKV
        if half == 0:
            load_qkv[1].start()
        d_qkv[1] = ((dka[...] + spread(select_t[...], dkm[...])) * HD ** (-0.5)).astype(BF)
        d_qkv[2] = (dva[...] + spread(select_t[...], dvm[...])).astype(BF)
        if half == 0:
            wait(load_w)
            load_tokens.wait()

            @pl.loop(0, 3)
            def _(c):
                piece = t_mm(tokens[...], d_qkv[c])
                for r in range(2):
                    for j in range(3):
                        grads[QKV + 6 * c + 3 * r + j] = piece[BR * r : BR * (r + 1), BC * j : BC * (j + 1)]
                columns = pl.ds(pl.multiple_of(c * CHUNK, CHUNK), CHUNK)
                part = mm_t(d_qkv[0], w_qkv[half, pl.ds(pl.multiple_of(c * CHUNK, CHUNK), CHUNK), :])
                for i in (1, 2):
                    part = part + mm_t(d_qkv[i], w_qkv[half, pl.ds(pl.multiple_of(i * depth + c * CHUNK, CHUNK), CHUNK), :])
                acc_own[:, columns] = part
                ticks(c, TICKS[6], 3)

            done[0] += 3 * TICKS[6]
            for index, row in ((0, 0), (2, 3)):
                total = jnp.sum(d_qkv[index].astype(F32), axis=0, keepdims=True)
                for j in range(3):
                    grads[VEC, row + j : row + j + 1, :] = total[:, BC * j : BC * (j + 1)]
        else:

            @pl.loop(0, 3)
            def _(c):
                columns = pl.ds(pl.multiple_of(c * CHUNK, CHUNK), CHUNK)
                part = mm_t(d_qkv[0], w_qkv[half, pl.ds(pl.multiple_of(c * CHUNK, CHUNK), CHUNK), :])
                for i in (1, 2):
                    part = part + mm_t(d_qkv[i], w_qkv[half, pl.ds(pl.multiple_of(i * depth + c * CHUNK, CHUNK), CHUNK), :])
                d_low[:, columns] = ((acc_own[:, columns] + part) + d_res[:, columns]).astype(BF)
                ticks(c, TICKS[7], 3)

            done[0] += 3 * TICKS[7]
    @pl.loop(min(done[0], last), last)
    def _(step):
        tick(step)


TICKS = (1, 3, 2, 1, 2, 1, 3, 1)
TICK_TILES = 2
NORM_TILE = 128
UNROLL = (3, 1)


def backward(fast, select_t, memory, inverse, gain, vec_in, arrays):
    tokens, acted, mixed = arrays[0], arrays[5], arrays[9]
    rows, depth = tokens.shape
    units = acted.shape[1]
    width = mixed.shape[1]
    vm = pl.BlockSpec(memory_space=pltpu.VMEM)
    hbm = pl.BlockSpec(memory_space=pl.ANY)
    kept = pltpu.VMEM if fast else jax.ShapeDtypeStruct
    return pl.pallas_call(
        functools.partial(backward_kernel, fast),
        out_shape=[kept((COUNT, BR, BC), F32), kept((rows, depth), BF)],
        in_specs=[vm, vm, vm, vm, vm] + [hbm] * len(arrays),
        out_specs=[vm, vm],
        scratch_shapes=[
            pltpu.VMEM((rows, depth), BF),
            pltpu.VMEM((rows, depth), F32),
            pltpu.VMEM((rows, depth), F32),
            pltpu.VMEM((rows, depth), F32),
            pltpu.VMEM((rows, depth), F32),
            pltpu.VMEM((2, rows, BR), BF),
            pltpu.VMEM((2, rows, CHUNK), BF),
            pltpu.VMEM((2, depth, CHUNK), BF),
            pltpu.VMEM((2, CHUNK, depth), BF),
            pltpu.VMEM((rows, CHUNK), BF),
            pltpu.VMEM((3, 8, depth), F32),
            pltpu.VMEM((rows, depth), BF),
            pltpu.VMEM((rows, width), BF),
            pltpu.VMEM((2, width, depth), BF),
            pltpu.VMEM((2, 3 * depth, width), BF),
            pltpu.VMEM((3, rows, width), BF),
            pltpu.VMEM((3, rows, width), BF),
            pltpu.VMEM((2, rows, width), BF),
            pltpu.VMEM((2, width // PAIR, 2 * WIN, WIN + MEMP), BF),
            pltpu.VMEM((MEMP, width), F32),
            pltpu.VMEM((MEMP, width), F32),
            pltpu.SemaphoreType.DMA((12,)),
            pltpu.SemaphoreType.DMA((4, 2)),
            pltpu.SemaphoreType.DMA((2,)),
        ]
        + (sum_scratch() if fast else []),
        compiler_params=pltpu.CompilerParams(
            collective_id=1 if fast else None, has_side_effects=fast, vmem_limit_bytes=47 * 2**20 if fast else 67043328
        ),
        name="backward",
    )(select_t, memory, inverse, gain, vec_in, *arrays)


def results_kernel(blocks, grad_tokens, output_h, g_qkv, g_out, g_up, g_down, tokens_h, output_out, *rest):
    vectors, (output, sems, out_sem) = rest[:8], rest[8:]
    load = pltpu.make_async_copy(output_h, output, out_sem.at[2])
    load.start()
    places = [(g_down, BR * (i // 6), BC * (i % 6)) for i in range(24)]
    places += [(g_up, BR * (i // 2 % 2), CHUNK * (i // 4) + BC * (i % 2)) for i in range(24)]
    places += [(g_out, 0, BC * i) for i in range(6)]
    places += [(g_qkv, BR * (i // 3), BC * (i % 3)) for i in range(18)]
    copies = [
        pltpu.make_async_copy(blocks.at[i], target.at[pl.ds(row, BR), pl.ds(column, BC)], sems.at[i])
        for i, (target, row, column) in enumerate(places)
    ]
    copies.append(pltpu.make_async_copy(grad_tokens, tokens_h, out_sem.at[0]))
    for copy in copies[:24]:
        copy.start()
    load.wait()
    copies.append(pltpu.make_async_copy(output, output_out, out_sem.at[1]))
    for copy in copies[24:]:
        copy.start()
    bias_qv, *flat = vectors
    for j in range(6):
        bias_qv[j // 3 : j // 3 + 1, BC * (j % 3) : BC * (j % 3 + 1)] = blocks[VEC, j : j + 1, :]
    row = 6
    for ref in flat:
        for j in range(ref.shape[0] // BC):
            ref[pl.ds(BC * j, BC)] = blocks[VEC, row, :]
            row += 1
    for copy in copies:
        copy.wait()


def results(fast, blocks, grad_tokens, output, width, units):
    vm = pl.BlockSpec(memory_space=pltpu.VMEM)
    hbm = pl.BlockSpec(memory_space=pl.ANY)
    sd = jax.ShapeDtypeStruct
    rows, depth = output.shape
    if fast:
        blocks, grad_tokens = (pltpu.with_memory_space_constraint(a, pltpu.VMEM) for a in (blocks, grad_tokens))
        output = pltpu.with_memory_space_constraint(output, pltpu.HBM)
    large = [sd((3 * depth, width), F32), sd((width, depth), F32), sd((depth, units), F32), sd((units, depth), F32)]
    large += [sd((rows, depth), BF)] * 2
    small = [sd((2, width), F32), sd((units,), F32)] + [sd((depth,), F32)] * 6
    return pl.pallas_call(
        results_kernel,
        out_shape=large + small,
        in_specs=[vm, vm, hbm],
        out_specs=[hbm] * 6 + [vm] * len(small),
        scratch_shapes=[
            pltpu.VMEM((rows, depth), BF),
            pltpu.SemaphoreType.DMA((VEC,)),
            pltpu.SemaphoreType.DMA((3,)),
        ],
        compiler_params=pltpu.CompilerParams(vmem_limit_bytes=(8 if fast else 40) * 2**20),
        name="results",
    )(blocks, grad_tokens, output)


def halves_swap(own, small):
    unit = (lax.axis_index("dp") >= 0).astype(F32)

    def other(array):
        arrived = lax.ppermute(array.astype(F32), "tensor", [(0, 1), (1, 0)])
        return (arrived * unit).astype(array.dtype)

    return tuple(other(array) for array in own) + (other(small),)


def shards(
    fast,
    tokens,
    w_qkv,
    bias_qv,
    w_out,
    bias_out,
    gain_one,
    shift_one,
    w_up,
    bias_up,
    w_down,
    bias_down,
    gain_two,
    shift_two,
    grad_out,
    parent,
    mem_slots,
):
    depth, width = w_qkv.shape[1:]
    hidden_units = w_up.shape[1]
    own = (w_qkv.reshape(3 * depth, width), w_out, w_up, w_down)
    if fast:
        given = ()
    else:
        table = jnp.pad(bias_up.reshape(-1, CHUNK), ((0, 0), (0, width - CHUNK)))
        small = jnp.concatenate([bias_qv[:1], jnp.zeros((1, width), F32), bias_qv[1:], table])
        given = halves_swap(own, jnp.pad(small, ((0, 16 - small.shape[0]), (0, 0))))
    vectors = (bias_qv, bias_out, gain_one, shift_one, bias_up, bias_down, gain_two, shift_two)
    (
        output,
        *theirs,
        qkv,
        mixed,
        normed,
        inverse,
        hidden_low,
        acted,
        slope_own,
        slope_their,
        d_two,
        d_ffn,
        vec,
        probs,
        select_t,
        memory,
    ) = forward(fast, parent, mem_slots, vectors, tokens, grad_out, own, given)
    if not fast:
        theirs = given[:4]
    arrays = (tokens, hidden_low, d_ffn, d_two, normed, acted, slope_own, slope_their, qkv, mixed, probs)
    weights = tuple(w[i] for i in (2, 3, 1, 0) for w in (own, theirs))
    blocks, grad_tokens = backward(fast, select_t, memory, inverse, gain_one, vec, arrays + weights)
    if not fast:
        blocks = lax.psum(blocks, "dp")
    (
        g_w_qkv,
        g_w_out,
        g_w_up,
        g_w_down,
        grad_tokens,
        output,
        g_bias_qv,
        g_bias_up,
        g_bias_out,
        g_gain_one,
        g_shift_one,
        g_bias_down,
        g_gain_two,
        g_shift_two,
    ) = results(fast, blocks, grad_tokens, output, width, hidden_units)
    return (
        output,
        grad_tokens,
        g_w_qkv.reshape(w_qkv.shape),
        g_bias_qv,
        g_w_out,
        g_bias_out,
        g_gain_one,
        g_shift_one,
        g_w_up,
        g_bias_up,
        g_w_down,
        g_bias_down,
        g_gain_two,
        g_shift_two,
    )


def solution(mesh):
    fast = mesh.shape["dp"] == 16 and mesh.shape["tensor"] == 2
    rows, whole = P("dp", None), P()
    return jax.shard_map(
        functools.partial(shards, fast),
        mesh=mesh,
        in_specs=(
            rows,
            P(None, None, "tensor"),
            P(None, "tensor"),
            P("tensor", None),
            whole,
            whole,
            whole,
            P(None, "tensor"),
            P("tensor"),
            P("tensor", None),
            whole,
            whole,
            whole,
            rows,
            P("dp"),
            rows,
        ),
        out_specs=(
            rows,
            rows,
            P(None, None, "tensor"),
            P(None, "tensor"),
            P("tensor", None),
            whole,
            whole,
            whole,
            P(None, "tensor"),
            P("tensor"),
            P("tensor", None),
            whole,
            whole,
            whole,
        ),
        check_vma=False,
    )
```

```python
import functools


import jax
import jax.numpy as jnp
from jax import lax
from jax.experimental import pallas as pl
from jax.experimental.pallas import tpu as pltpu
from jax.sharding import PartitionSpec as P


MESH = pl.DeviceIdType.MESH
BR, BC = 384, 128
AFTER = (0, 3, 6, 9, 12, 15, 18, 21)
SLOTS = 16


class Place:
    def __init__(self):
        me = lax.axis_index("dp")
        self.core = lax.rem(me, 2)
        self.x = lax.rem(me // 2, 2)
        self.z = me // 4
        self.sib = me + 1 - 2 * self.core
        self.xn = me + 2 - 4 * self.x
        self.zp = me + 4 - 8 * lax.rem(self.z, 2)
        self.zm = me + 4 * (3 - 2 * self.z)
        self.end = (self.z == 0) | (self.z == 3)
        self.mid = (self.z == 1) | (self.z == 2)


def sum_greet(pos):
    barrier = pltpu.get_barrier_semaphore()

    def greet(dev):
        pl.semaphore_signal(barrier, inc=1, device_id={"dp": dev}, device_id_type=MESH)

    greet(pos.sib)
    greet(pos.xn)
    greet(pos.zp)

    @pl.when(pos.mid)
    def _():
        greet(pos.zm)


def sum_met(pos):
    pl.semaphore_wait(pltpu.get_barrier_semaphore(), jnp.where(pos.mid, 4, 3))


def make_tick(pos, grads, from_core, from_one, from_two, from_three, sent, got, credit, count, finish):
    half = BR // 2
    quarter = BR // 4

    def copy(stage, block, source, target, device):
        slot = lax.rem(block, SLOTS)
        return pltpu.make_async_remote_copy(
            src_ref=source,
            dst_ref=target,
            send_sem=sent.at[stage, slot],
            recv_sem=got.at[stage, slot],
            device_id={"dp": device},
            device_id_type=MESH,
        )

    def rows(block, start, size):
        return grads.at[block, pl.ds(pl.multiple_of(start, quarter), size)]

    def add(block, start, size, landed):
        where = pl.ds(pl.multiple_of(start, quarter), size)
        grads[block, where] = grads[block, where] + landed[...]

    def free(index, device):
        pl.semaphore_signal(credit.at[index], inc=1, device_id={"dp": device}, device_id_type=MESH)

    def claim(index):
        pl.semaphore_wait(credit.at[index], 1)

    x_first = pos.core == 0
    z_first = pos.core == 1
    mine = pos.core * half
    xrow = pos.x * quarter
    xrow_other = (1 - pos.x) * quarter
    far = lax.rem(pos.z, 2) == 0
    keep = half + jnp.where(far, quarter, 0)
    give = half + jnp.where(far, 0, quarter)

    def core_out(block):
        return copy(0, block, rows(block, (1 - pos.core) * half, half), from_core.at[lax.rem(block, SLOTS)], pos.sib)

    def x_one(block):
        return copy(1, block, rows(block, xrow_other, quarter), from_one.at[lax.rem(block, SLOTS), pl.ds(0, quarter)], pos.xn)

    def z_one(block):
        return copy(1, block, rows(block, half, half), from_one.at[lax.rem(block, SLOTS)], pos.zp)

    def x_two(block):
        return copy(2, block, rows(block, xrow, quarter), from_two.at[lax.rem(block, SLOTS)], pos.zp)

    def z_two(block):
        return copy(2, block, rows(block, give, quarter), from_two.at[lax.rem(block, SLOTS)], pos.zm)

    def x_three(block):
        return copy(3, block, rows(block, xrow, quarter), from_three.at[lax.rem(block, SLOTS)], pos.zm)

    def z_three(block):
        return copy(3, block, rows(block, keep, quarter), from_three.at[lax.rem(block, SLOTS)], pos.xn)

    def x_four(block):
        return copy(4, block, rows(block, xrow, quarter), rows(block, xrow, quarter), pos.zp)

    def z_four(block):
        return copy(4, block, rows(block, keep, quarter), rows(block, keep, quarter), pos.zm)

    def z_four_in(block):
        return copy(4, block, rows(block, give, quarter), rows(block, give, quarter), pos.zm)

    def x_five(block):
        return copy(5, block, rows(block, xrow, quarter), rows(block, xrow, quarter), pos.xn)

    def x_five_in(block):
        return copy(5, block, rows(block, xrow_other, quarter), rows(block, xrow_other, quarter), pos.xn)

    def z_five(block):
        return copy(5, block, rows(block, half, half), rows(block, half, half), pos.zp)

    def core_six(block):
        return copy(6, block, rows(block, mine, half), rows(block, mine, half), pos.sib)

    def core_six_in(block):
        return copy(6, block, rows(block, (1 - pos.core) * half, half), rows(block, (1 - pos.core) * half, half), pos.sib)

    def start_core(block):
        core_out(block).start()

    def take_core(block):
        core_out(block).wait()
        free(2, pos.sib)
        add(block, mine, half, from_core.at[lax.rem(block, SLOTS)])

    def take_x(block):
        x_one(block).wait()
        free(1, pos.xn)
        add(block, xrow, quarter, from_one.at[lax.rem(block, SLOTS), pl.ds(0, quarter)])

    def send_x(block):
        take_core(block)
        x_one(block).start()

    def send_z(block):
        take_core(block)
        z_one(block).start()

    def x_end_two(block):
        take_x(block)
        x_two(block).start()

    def x_end_three(block):
        x_two(block).wait_send()
        free(0, pos.zp)

    def x_mid_three(block):
        x_two(block).wait_recv()
        add(block, xrow, quarter, from_two.at[lax.rem(block, SLOTS)])
        x_three(block).start()

    def x_mid_four(block):
        x_three(block).wait()
        add(block, xrow, quarter, from_three.at[lax.rem(block, SLOTS)])
        claim(0)
        x_four(block).start()

    def x_end_five(block):
        x_four(block).wait_recv()
        claim(1)
        x_five(block).start()

    def x_mid_five(block):
        x_four(block).wait_send()
        claim(1)
        x_five(block).start()

    def x_six(block):
        x_five(block).wait_send()
        x_five_in(block).wait_recv()
        claim(2)
        core_six(block).start()

    def z_end_two(block):
        z_one(block).wait_send()
        free(1, pos.zp)

    def z_end_six(block):
        z_five(block).wait_recv()
        claim(2)
        core_six(block).start()

    def z_mid_two(block):
        z_one(block).wait_recv()
        add(block, half, half, from_one.at[lax.rem(block, SLOTS)])
        z_two(block).start()

    def z_mid_three(block):
        z_two(block).wait()
        free(0, pos.zm)
        add(block, keep, quarter, from_two.at[lax.rem(block, SLOTS)])
        z_three(block).start()

    def z_mid_four(block):
        z_three(block).wait()
        add(block, keep, quarter, from_three.at[lax.rem(block, SLOTS)])
        claim(0)
        z_four(block).start()

    def z_mid_five(block):
        z_four(block).wait_send()
        z_four_in(block).wait_recv()
        claim(1)
        z_five(block).start()

    def z_mid_six(block):
        z_five(block).wait_send()
        claim(2)
        core_six(block).start()

    def last(block):
        core_six(block).wait_send()
        core_six_in(block).wait_recv()

    roles = (
        (x_first & pos.end, (start_core, send_x, x_end_two, x_end_three, None, x_end_five, x_six, last)),
        (x_first & pos.mid, (start_core, send_x, take_x, x_mid_three, x_mid_four, x_mid_five, x_six, last)),
        (z_first & pos.end, (start_core, send_z, z_end_two, None, None, None, z_end_six, last)),
        (z_first & pos.mid, (start_core, take_core, z_mid_two, z_mid_three, z_mid_four, z_mid_five, z_mid_six, last)),
    )
    depth = len(roles[0][1])

    def tick(step):
        for here, stages in roles:

            @pl.when(here)
            def _(stages=stages):
                for index in reversed(range(depth)):
                    block = step - AFTER[index]
                    if stages[index] is not None:

                        @pl.when((block >= 0) & (block < count))
                        def _(index=index, block=block, stages=stages):
                            stages[index](block)

        over = step - AFTER[depth - 1]

        @pl.when((over >= 0) & (over < count))
        def _():
            finish(over)

    return tick


def sum_scratch():
    return [
        pltpu.VMEM((SLOTS, BR // 2, BC), jnp.float32),
        pltpu.VMEM((SLOTS, BR // 2, BC), jnp.float32),
        pltpu.VMEM((SLOTS, BR // 4, BC), jnp.float32),
        pltpu.VMEM((SLOTS, BR // 4, BC), jnp.float32),
        pltpu.SemaphoreType.DMA((7, SLOTS)),
        pltpu.SemaphoreType.DMA((7, SLOTS)),
        pltpu.SemaphoreType.REGULAR((3,)),
    ]


CR, CC = 64, 384
CHUNKS = 24
HOPS = (3, 6, 7)
BF = jnp.bfloat16


def gather_greet(pos, other):
    barrier = pltpu.get_barrier_semaphore()
    for where in ({"tensor": other}, {"dp": pos.xn}, {"dp": pos.zp}, {"dp": pos.sib}):
        pl.semaphore_signal(barrier, inc=1, device_id=where, device_id_type=MESH)


def gather_met():
    pl.semaphore_wait(pltpu.get_barrier_semaphore(), 4)


def chunk_parts(piece, chunk, kind):
    if kind == 0:
        return [(piece * 384 + chunk * 64, 64, 0, 0)]
    if kind == 1:
        return [(piece * 64 + (chunk - 6) * 32, 32, 384 * q, 32 * q) for q in range(2)]
    if kind == 2:
        return [(piece * 128 + (chunk - 8) * 16, 16, 384 * q, 16 * q) for q in range(4)]
    return [((chunk - 16) * 192 + piece * 32, 32, 384 * q, 32 * q) for q in range(2)]


BOUNDS = ((0, 6), (6, 8), (8, 16), (16, 24))
UNIT = (64, 32, 16, 32)


def make_gather(pos, own, theirs, staged, landed, sent, got):
    other = 1 - lax.axis_index("tensor")
    odd = lax.rem(pos.z, 2)
    ky = jnp.where(pos.x == 0, odd, 2)
    kx = jnp.where(pos.x == 0, 2, odd)
    kz = 1 - odd
    piece_y = 2 * ky + pos.core
    piece_x = 2 * kx + pos.core
    piece_z = 2 * kz + pos.core
    sib_y = 2 * ky + 1 - pos.core
    sib_x = 2 * kx + 1 - pos.core
    sib_z = 2 * kz + 1 - pos.core

    def copy(lane, chunk, source, piece, where):
        return pltpu.make_async_remote_copy(
            src_ref=source,
            dst_ref=landed.at[piece, chunk],
            send_sem=sent.at[lane, chunk],
            recv_sem=got.at[lane, chunk],
            device_id=where,
            device_id_type=MESH,
        )

    def over_y(chunk):
        return copy(0, chunk, staged.at[chunk], piece_y, {"tensor": other})

    def over_x(chunk, piece):
        return copy(1, chunk, landed.at[piece, chunk], piece, {"dp": pos.xn})

    def over_z(chunk, piece):
        return copy(2, chunk, landed.at[piece, chunk], piece, {"dp": pos.zp})

    def over_core(lane, chunk, piece):
        return copy(lane, chunk, landed.at[piece, chunk], piece, {"dp": pos.sib})

    def stage_own(kind):
        lo, hi = BOUNDS[kind]

        @pl.loop(lo, hi)
        def _(chunk):
            for row, rows, column, at in chunk_parts(piece_y, chunk, kind):
                staged[chunk, pl.ds(at, rows)] = own[kind][
                    pl.ds(pl.multiple_of(row, UNIT[kind]), rows), pl.ds(column, CC)
                ].astype(jnp.float32)

    def send_own(kind):
        lo, hi = BOUNDS[kind]

        @pl.loop(lo, hi)
        def _(chunk):
            over_y(chunk).start()

    def unpack(chunk):
        for kind in range(4):
            lo, hi = BOUNDS[kind]

            @pl.when((chunk >= lo) & (chunk < hi))
            def _(kind=kind):
                @pl.loop(0, 6)
                def _(piece):
                    for row, rows, column, at in chunk_parts(piece, chunk, kind):
                        theirs[kind][pl.ds(pl.multiple_of(row, UNIT[kind]), rows), pl.ds(column, CC)] = landed[
                            piece, chunk, pl.ds(at, rows)
                        ].astype(BF)

    def guarded(chunk, body):
        @pl.when((chunk >= 0) & (chunk < CHUNKS))
        def _():
            body(chunk)

    def first(chunk):
        over_y(chunk).wait_recv()
        over_x(chunk, piece_y).start()

        @pl.when(pos.x == 0)
        def _():
            over_z(chunk, piece_y).start()

        over_core(3, chunk, piece_y).start()

    def second(chunk):
        over_x(chunk, piece_x).wait_recv()

        @pl.when(pos.x == 1)
        def _():
            over_z(chunk, piece_x).start()

        over_core(4, chunk, piece_x).start()

    def third(chunk):
        over_z(chunk, piece_z).wait_recv()
        over_core(5, chunk, piece_z).start()

    def fourth(chunk):
        over_core(3, chunk, sib_y).wait_recv()
        over_core(4, chunk, sib_x).wait_recv()
        over_core(5, chunk, sib_z).wait_recv()
        over_y(chunk).wait_send()
        over_x(chunk, piece_y).wait_send()
        over_z(chunk, piece_y).wait_send()
        over_core(3, chunk, piece_y).wait_send()
        over_core(4, chunk, piece_x).wait_send()
        over_core(5, chunk, piece_z).wait_send()
        unpack(chunk)

    def tick(step):
        guarded(step - HOPS[2], fourth)
        guarded(step - HOPS[1], third)
        guarded(step - HOPS[0], second)
        guarded(step, first)

    return stage_own, send_own, tick


def gather_scratch():
    return [
        pltpu.VMEM((CHUNKS, CR, CC), jnp.float32),
        pltpu.VMEM((6, CHUNKS, CR, CC), jnp.float32),
        pltpu.SemaphoreType.DMA((6, CHUNKS)),
        pltpu.SemaphoreType.DMA((6, CHUNKS)),
    ]


def swap_small(small, small_out, sems):
    return pltpu.make_async_remote_copy(
        src_ref=small,
        dst_ref=small_out,
        send_sem=sems.at[0],
        recv_sem=sems.at[1],
        device_id={"tensor": 1 - lax.axis_index("tensor")},
        device_id_type=MESH,
    )


HD = 64
SEG = 148
MEMW = 10
F32 = jnp.float32
EPSILON = 1e-12
MASKED = -1e30
WIN = 160
MEMP = 96
SEGS = 8
PAIR = 2 * HD

CONTRACT_LAST = (((1,), (1,)), ((), ()))
CONTRACT_FIRST = (((0,), (0,)), ((), ()))


def mm(a, b):
    return jnp.dot(a, b, preferred_element_type=F32)


def mm_t(a, b):
    return lax.dot_general(a, b, CONTRACT_LAST, preferred_element_type=F32)


def t_mm(a, b):
    return lax.dot_general(a, b, CONTRACT_FIRST, preferred_element_type=F32)


def build_masks(parent, base, colbias):
    lane = lax.broadcasted_iota(jnp.int32, (1, WIN + MEMP), 1)
    in_mem = [
        ((lane >= WIN + MEMW * t) & (lane < WIN + MEMW * (t + 1))).astype(F32) for t in range(SEGS)
    ]
    reach = [jnp.zeros((1, WIN + MEMP), F32)]
    for s in range(1, SEGS):
        row = jnp.zeros((1, WIN + MEMP), F32)
        for t in range(s):
            hit = jnp.where(parent[s] - base == t, 1.0, 0.0)
            row = row + hit * jnp.maximum(reach[t], in_mem[t])
        reach.append(row)
    for s in range(SEGS):
        off = 4 * (s % 4)
        inside = ((lane >= off) & (lane < off + SEG)).astype(F32)
        colbias[s : s + 1, :] = jnp.where(jnp.maximum(inside, reach[s]) > 0.0, 0.0, MASKED)


def build_select(slots, select, select_t):
    for ref, axis in ((select, 0), (select_t, 1)):
        shape = (ref.shape[0], 1) if axis == 0 else (1, ref.shape[1])
        entry = lax.broadcasted_iota(jnp.int32, shape, axis)
        where = jnp.full(shape, -1, jnp.int32)
        for t in range(SEGS):
            for m in range(MEMW):
                where = jnp.where(entry == MEMW * t + m, slots[t, m] + SEG * t, where)
        place = lax.broadcasted_iota(jnp.int32, ref.shape, 1 - axis)
        ref[...] = (where == place).astype(F32).astype(BF)


def window(s):
    return pl.multiple_of(144 * s + 16 * (s // 4), 16), 4 * lax.rem(s, 4)


def lane_halves():
    lane = lax.broadcasted_iota(jnp.int32, (1, PAIR), 1)
    left = (lane < HD).astype(F32)
    return left.astype(BF), (1.0 - left).astype(BF), lane < HD


def valid_rows(off):
    row = lax.broadcasted_iota(jnp.int32, (WIN, 1), 0)
    return row, (row >= off) & (row < off + SEG)


def softmax_parts(qs, kk, bias):
    scores = mm_t(qs, kk) * HD ** (-0.5) + bias
    top = jnp.max(scores, axis=-1, keepdims=True)
    raised = jnp.exp(scores - top)
    return raised, 1.0 / jnp.sum(raised, axis=-1, keepdims=True)


def attend_pair(q, k, v, kmem, vmem, colbias, mixed, probs, s, columns):
    left, right, is_left = lane_halves()
    at, off = window(s)
    rows = pl.ds(at, WIN)
    qw = q[rows, columns]
    qs = jnp.concatenate([qw * left, qw * right], axis=0)
    kk = jnp.concatenate([k[rows, columns], kmem[:, columns]], axis=0)
    vv = jnp.concatenate([v[rows, columns], vmem[:, columns]], axis=0)
    raised, scale = softmax_parts(qs, kk, colbias[pl.ds(s, 1), :])
    row, valid = valid_rows(off)
    keep = jnp.where(valid, 1.0, 0.0)
    chances = (raised * (scale * jnp.concatenate([keep, keep], axis=0))).astype(BF)
    probs[...] = chances
    both = mm(chances, vv)
    out = jnp.where(is_left, both[:WIN], both[WIN:])
    old = mixed[rows, columns].astype(F32)
    mixed[rows, columns] = jnp.where(row >= off, out, old).astype(BF)


def attend_back_pair(q, k, v, kmem, vmem, probs, dmix, dq, dk, dv, dkmem, dvmem, s, columns):
    left, right, is_left = lane_halves()
    at, off = window(s)
    rows = pl.ds(at, WIN)
    qw = q[rows, columns]
    qs = jnp.concatenate([qw * left, qw * right], axis=0)
    kk = jnp.concatenate([k[rows, columns], kmem[:, columns]], axis=0)
    vv = jnp.concatenate([v[rows, columns], vmem[:, columns]], axis=0)
    dw = dmix[rows, columns]
    ds_in = jnp.concatenate([dw * left, dw * right], axis=0)
    low = probs[...]
    chances = low.astype(F32)
    dp = mm_t(ds_in, vv)
    inner = jnp.sum(chances * dp, axis=-1, keepdims=True)
    ds = (chances * (dp - inner)).astype(BF)
    dqs = mm(ds, kk)
    row, valid = valid_rows(off)
    new = jnp.where(is_left, dqs[:WIN], dqs[WIN:]) * HD ** (-0.5)
    old = dq[rows, columns].astype(F32)
    dq[rows, columns] = jnp.where(row >= off, new, old).astype(BF)
    dks = t_mm(ds, qs)
    dvs = t_mm(low, ds_in)
    dk[rows, columns] = dk[rows, columns] + dks[:WIN]
    dv[rows, columns] = dv[rows, columns] + dvs[:WIN]
    dkmem[:, columns] = dkmem[:, columns] + dks[WIN:]
    dvmem[:, columns] = dvmem[:, columns] + dvs[WIN:]


def spread(select_t, part):
    high = part.astype(BF)
    low = (part - high.astype(F32)).astype(BF)
    return mm(select_t, high) + mm(select_t, low)


def norm_stats(values):
    centered = values - jnp.mean(values, axis=-1, keepdims=True)
    inverse = lax.rsqrt(jnp.mean(centered * centered, axis=-1, keepdims=True) + EPSILON)
    return centered * inverse, inverse


def norm_back(grad, normed, inverse, gain):
    scaled = grad * gain
    return inverse * (
        scaled
        - jnp.mean(scaled, axis=-1, keepdims=True)
        - normed * jnp.mean(scaled * normed, axis=-1, keepdims=True)
    )


def gelu_parts(inner):
    phi = 0.5 + 0.5 * lax.erf(inner * (0.5**0.5))
    density = jnp.exp(-0.5 * inner * inner) * (2.0 * jnp.pi) ** -0.5
    return (inner * phi).astype(BF), (phi + inner * density).astype(BF)


def flat_row(ref, start, size):
    return ref[pl.ds(start, size)].reshape(1, size)


TILE = 128


SPLIT = 6 * TILE


def row_tiles(first, last, body):
    full = (last - first) // TILE

    @pl.loop(0, full)
    def _(i):
        body(pl.ds(pl.multiple_of(first + i * TILE, TILE), TILE))

    if (last - first) % TILE:
        body(pl.ds(first + full * TILE, (last - first) % TILE))


def forward_kernel(
    fast,
    parent,
    slots,
    bias_qv,
    bias_out,
    gain_one,
    shift_one,
    bias_up,
    bias_down,
    gain_two,
    shift_two,
    tokens_h,
    grad_h,
    qkv_in,
    out_in,
    up_in,
    down_in,
    *rest,
):
    count = 0 if fast else 5
    given, outs, rest = rest[:count], rest[count : count + 19], rest[count + 19 :]
    (
        output_h,
        their_qkv_h,
        their_out_h,
        their_up_h,
        their_down_h,
        qkv_h,
        mixed_h,
        normed_h,
        inverse,
        hidden_h,
        acted_h,
        slope_own_h,
        slope_their_h,
        d_two_h,
        d_ffn,
        vec,
        probs_h,
        select_t,
        memory,
    ) = outs
    (
        tokens,
        own_qkv,
        own_out,
        own_up,
        own_down,
        their_qkv,
        their_out,
        their_up,
        their_down,
        small,
        small_their,
        qkv,
        mixed,
        normed,
        hidden,
        acc_own,
        acc_their,
        acted,
        slopes,
        colbias,
        select,
        sums,
        probs,
        io_sem,
        slope_sem,
        probs_sem,
        *wires,
    ) = rest
    rows, depth = tokens.shape
    width = mixed.shape[2]
    units = acted.shape[1]
    theirs = (their_qkv, their_out, their_up, their_down)
    own = (own_qkv, own_out, own_up, own_down)

    def move(index, source, target):
        return pltpu.make_async_copy(source, target, io_sem.at[index])

    load_tokens = move(0, tokens_h, tokens)
    load_grad = move(1, grad_h, tokens)
    put_qkv = move(2, qkv, qkv_h)
    put_mixed = move(3, mixed.at[0], mixed_h)
    put_normed = move(4, normed, normed_h)
    put_hidden = move(5, hidden, hidden_h)
    put_acted = move(6, acted, acted_h)
    late = ((acc_own, d_two_h), (tokens, output_h))
    put_late = [
        [move(7 + 3 * part + i, ref.at[rows_of], target.at[rows_of]) for i, (ref, target) in enumerate(late)]
        for part, rows_of in enumerate((pl.ds(0, SPLIT), pl.ds(SPLIT, rows - SPLIT)))
    ]
    put_theirs = [
        move(13 + i, ref, target)
        for i, (ref, target) in enumerate(zip(theirs, (their_qkv_h, their_out_h, their_up_h, their_down_h)))
    ]
    load_own = [move(17 + i, a, b) for i, (a, b) in enumerate(zip((qkv_in, out_in, up_in, down_in), own))]
    if fast:
        pos = Place()
        gather_greet(pos, 1 - lax.axis_index("tensor"))
    load_own[0].start()
    load_tokens.start()
    for copy in load_own[1:]:
        copy.start()
    done = [0]
    small[...] = jnp.zeros(small.shape, F32)
    small[0:1, :] = bias_qv[0:1, :]
    small[2:3, :] = bias_qv[1:2, :]
    for c in range(units // CHUNK):
        small[3 + c : 4 + c, 0:CHUNK] = flat_row(bias_up, c * CHUNK, CHUNK)
    if fast:
        small_sem, *wires = wires
        stage_own, send_own, tick = make_gather(pos, own, theirs, *wires)
        load_own[0].wait()
        stage_own(0)
        gather_met()
        send_own(0)
        swap = swap_small(small, small_their, small_sem)
        swap.start()
        for kind in range(1, 4):
            load_own[kind].wait()
            stage_own(kind)
            send_own(kind)
    else:
        for copy in load_own:
            copy.wait()
        copies = [move(13 + i, a, b) for i, (a, b) in enumerate(zip(given, theirs + (small_their,)))]
        for copy in copies:
            copy.start()
        for copy in copies:
            copy.wait()

        def tick(step):
            pass

    def ticks(index, each, trips):
        for i in range(each):
            tick(done[0] + index * each + i)

    def tick_every(index, every, trips):
        @pl.when(lax.rem(index, every) == 0)
        def _():
            tick(done[0] + index // every)

        return -(-trips // every)

    def until(count):
        if done[0] < count:

            @pl.loop(done[0], count)
            def _(step):
                tick(step)

            done[0] = count

    build_masks(parent, lax.axis_index("dp") * SEGS, colbias)
    build_select(slots, select, select_t)
    load_tokens.wait()
    pairs = width // PAIR
    for half in range(2):
        weights = (own_qkv, their_qkv)[half]
        table = (small, small_their)[half]
        if half == 1:
            until(BOUNDS[0][1] + HOPS[2])
            if fast:
                swap.wait()

        @pl.loop(0, 3)
        def _(c, half=half, weights=weights, table=table):
            part = mm(tokens[...], weights[pl.ds(pl.multiple_of(c * depth, depth), depth), :])
            qkv[half, c] = (part + table[pl.ds(c, 1), :]).astype(BF)

        q, k, v = (qkv.at[half, i] for i in range(3))
        kmem, vmem = memory.at[half, 0], memory.at[half, 1]
        kmem[...] = mm(select[...], k[...]).astype(BF)
        vmem[...] = mm(select[...], v[...]).astype(BF)

        def put_probs(s, half=half):
            slot = lax.rem(s, 2)
            return pltpu.make_async_copy(probs.at[slot], probs_h.at[half, s], probs_sem.at[slot])

        @pl.loop(0, SEGS)
        def _(s, half=half, q=q, k=k, v=v, kmem=kmem, vmem=vmem, put_probs=put_probs):
            @pl.when(s >= 2)
            def _():
                put_probs(s - 2).wait()

            for pair in range(pairs):
                attend_pair(
                    q, k, v, kmem, vmem, colbias, mixed.at[half], probs.at[lax.rem(s, 2), pair], s, pl.ds(pair * PAIR, PAIR)
                )
                if pair == 0 and half == 0:
                    tick(done[0] + s)
                if pair == 2 and half == 1:
                    tick_every(s, GATHER[0], SEGS)
            put_probs(s).start()

        done[0] += SEGS if half == 0 else -(-SEGS // GATHER[0])
        put_probs(SEGS - 2).wait()
        put_probs(SEGS - 1).wait()

        if half == 1:
            until(BOUNDS[1][1] + HOPS[2])
        out = (own_out, their_out)[half]

        @pl.loop(0, 3)
        def _(n, half=half, out=out):
            columns = pl.ds(pl.multiple_of(n * CHUNK, CHUNK), CHUNK)
            part = mm(mixed[half], out[:, columns])
            acc_own[:, columns] = part if half == 0 else acc_own[:, columns] + part
            ticks(n, GATHER[1 + half], 3)

        done[0] += 3 * GATHER[1 + half]
    put_qkv.start()
    put_mixed.start()

    def norm_one(span):
        resid = tokens[span, :].astype(F32) + (acc_own[span, :] + flat_row(bias_out, 0, depth))
        unit, scale = norm_stats(resid)
        normed[span, :] = unit
        inverse[span, :] = scale
        hidden[span, :] = (unit * flat_row(gain_one, 0, depth) + flat_row(shift_one, 0, depth)).astype(BF)

    row_tiles(0, rows, norm_one)
    load_grad.start()
    put_normed.start()
    put_hidden.start()

    for half in range(2):
        up, down = ((own_up, own_down), (their_up, their_down))[half]
        table = (small, small_their)[half]
        slope_h = (slope_own_h, slope_their_h)[half]
        acc = (acc_own, acc_their)[half]

        def put_slope(c, slope_h=slope_h):
            span = pl.ds(pl.multiple_of(c * CHUNK, CHUNK), CHUNK)
            return pltpu.make_async_copy(slopes.at[lax.rem(c, 2)], slope_h.at[:, span], slope_sem.at[lax.rem(c, 2)])

        if half == 1:
            until(BOUNDS[2][1] + HOPS[2])
            if fast:
                for copy in put_theirs[:3]:
                    copy.start()
            put_acted.wait()
            put_slope(4).wait()
            put_slope(5).wait()

        @pl.loop(0, 6)
        def _(c, half=half, up=up, table=table, put_slope=put_slope):
            span = pl.ds(pl.multiple_of(c * CHUNK, CHUNK), CHUNK)

            @pl.when(c >= 2)
            def _():
                put_slope(c - 2).wait()

            bias = table[pl.ds(3 + c, 1), 0:CHUNK]
            act, steep = gelu_parts(mm(hidden[...], up[:, span]) + bias)
            acted[:, span] = act
            slopes[lax.rem(c, 2)] = steep
            put_slope(c).start()
            tick_every(c, GATHER[3 + 2 * half], 6)

        done[0] += -(-6 // GATHER[3 + 2 * half])
        low, high = slice(0, units // 2), slice(units // 2, units)
        if half == 0:
            put_acted.start()

            @pl.loop(0, 3)
            def _(n, down=down, acc=acc):
                columns = pl.ds(pl.multiple_of(n * CHUNK, CHUNK), CHUNK)
                acc[:, columns] = mm(acted[:, low], down[low, columns]) + mm(acted[:, high], down[high, columns])
                ticks(n, GATHER[4], 3)

        else:
            until((BOUNDS[3][0] + BOUNDS[3][1]) // 2 + HOPS[2])

            @pl.loop(0, 3)
            def _(n, down=down, acc=acc):
                columns = pl.ds(pl.multiple_of(n * CHUNK, CHUNK), CHUNK)
                acc[:, columns] = mm(acted[:, low], down[low, columns])
                ticks(n, 1, 3)

            done[0] += 3
            until(BOUNDS[3][1] + HOPS[2])
            if fast:
                put_theirs[3].start()

            @pl.loop(0, 3)
            def _(n, down=down, acc=acc):
                columns = pl.ds(pl.multiple_of(n * CHUNK, CHUNK), CHUNK)
                acc[:, columns] = acc[:, columns] + mm(acted[:, high], down[high, columns])

        done[0] += 3 * GATHER[4] if half == 0 else 0
    put_slope(4).wait()
    put_slope(5).wait()

    load_grad.wait()
    sums[...] = jnp.zeros(sums.shape, F32)

    def norm_two(span):
        first = normed[span, :] * flat_row(gain_one, 0, depth) + flat_row(shift_one, 0, depth)
        resid = first + ((acc_own[span, :] + acc_their[span, :]) + flat_row(bias_down, 0, depth))
        unit, scale = norm_stats(resid)
        grad = tokens[span, :].astype(F32)
        tokens[span, :] = (unit * flat_row(gain_two, 0, depth) + flat_row(shift_two, 0, depth)).astype(BF)
        back = norm_back(grad, unit, scale, flat_row(gain_two, 0, depth))
        acc_own[span, :] = back
        low = back.astype(BF)
        d_ffn[span, :] = low
        for index, value in enumerate((low.astype(F32), grad * unit, grad)):
            sums[index] = sums[index] + value.reshape(-1, 8, depth).sum(axis=0)

    row_tiles(0, SPLIT, norm_two)
    for copy in put_late[0]:
        copy.start()
    row_tiles(SPLIT, rows, norm_two)
    for copy in put_late[1]:
        copy.start()
    for index in range(3):
        total = jnp.sum(sums[index], axis=0, keepdims=True)
        for j in range(6):
            vec[6 * index + j : 6 * index + j + 1, :] = total[:, BC * j : BC * (j + 1)]
    for copy in (put_qkv, put_mixed, put_normed, put_hidden, *put_late[0], *put_late[1]):
        copy.wait()
    if fast:
        for copy in put_theirs:
            copy.wait()


GATHER = (2, 1, 1, 2, 1, 2)


def forward(fast, parent, slots, vectors, tokens, grad_out, own, given):
    rows, depth = tokens.shape
    width = own[0].shape[1]
    units = own[2].shape[1]
    vm = pl.BlockSpec(memory_space=pltpu.VMEM)
    hbm = pl.BlockSpec(memory_space=pl.ANY)
    sm = pl.BlockSpec(memory_space=pltpu.SMEM)
    sd = jax.ShapeDtypeStruct
    kept = pltpu.VMEM if fast else sd
    out_shape = [
        sd((rows, depth), BF),
        *[sd(w.shape, BF) for w in own],
        sd((2, 3, rows, width), BF),
        sd((rows, width), BF),
        sd((rows, depth), F32),
        sd((rows, 1), F32),
        sd((rows, depth), BF),
        sd((rows, units), BF),
        sd((rows, units), BF),
        sd((rows, units), BF),
        sd((rows, depth), F32),
        kept((rows, depth), BF),
        sd((18, BC), F32),
        sd((2, SEGS, width // PAIR, 2 * WIN, WIN + MEMP), BF),
        sd((rows, MEMP), BF),
        sd((2, 2, MEMP, width), BF),
    ]
    return pl.pallas_call(
        functools.partial(forward_kernel, fast),
        out_shape=out_shape,
        in_specs=[sm, sm] + [vm] * len(vectors) + [hbm, hbm] + [hbm] * (4 + len(given)),
        out_specs=[hbm] * 8 + [vm] + [hbm] * 5 + [vm, vm, hbm, vm, vm],
        scratch_shapes=[
            pltpu.VMEM((rows, depth), BF),
            *[pltpu.VMEM(w.shape, BF) for w in own],
            *[pltpu.VMEM(w.shape, BF) for w in own],
            pltpu.VMEM((16, width), F32),
            pltpu.VMEM((16, width), F32),
            pltpu.VMEM((2, 3, rows, width), BF),
            pltpu.VMEM((2, rows, width), BF),
            pltpu.VMEM((rows, depth), F32),
            pltpu.VMEM((rows, depth), BF),
            pltpu.VMEM((rows, depth), F32),
            pltpu.VMEM((rows, depth), F32),
            pltpu.VMEM((rows, units), BF),
            pltpu.VMEM((2, rows, CHUNK), BF),
            pltpu.VMEM((SEGS, WIN + MEMP), F32),
            pltpu.VMEM((MEMP, rows), BF),
            pltpu.VMEM((3, 8, depth), F32),
            pltpu.VMEM((2, width // PAIR, 2 * WIN, WIN + MEMP), BF),
            pltpu.SemaphoreType.DMA((21,)),
            pltpu.SemaphoreType.DMA((2,)),
            pltpu.SemaphoreType.DMA((2,)),
        ]
        + ([pltpu.SemaphoreType.DMA((2,))] + gather_scratch() if fast else []),
        compiler_params=pltpu.CompilerParams(
            collective_id=0 if fast else None, has_side_effects=fast, vmem_limit_bytes=62000000 if fast else 67043328
        ),
        name="forward",
    )(parent, slots, *vectors, tokens, grad_out, *own, *given)


DOWN, UP, OUT, QKV, VEC = 0, 24, 48, 54, 72
COUNT = 73
CHUNK = 256
VEC_ROWS = 54


def backward_kernel(
    fast,
    select_t,
    memory,
    inverse,
    gain,
    vec_in,
    tokens_h,
    hidden_h,
    d_ffn,
    d_two_h,
    normed_h,
    acted_h,
    slope_own_h,
    slope_their_h,
    qkv_h,
    mixed_h,
    probs_h,
    w_up_own,
    w_up_their,
    w_down_own,
    w_down_their,
    w_out_own,
    w_out_their,
    w_qkv_own,
    w_qkv_their,
    grads,
    d_low,
    hidden,
    d_res,
    normed,
    acc_own,
    acc_their,
    a_buf,
    slope_buf,
    up_buf,
    down_buf,
    d_inner,
    sums,
    mixed,
    w_out,
    w_qkv,
    qkv,
    d_qkv,
    d_mixed,
    probs,
    dkm,
    dvm,
    load_sem,
    chunk_sem,
    probs_sem,
    *wires,
):
    rows, depth = hidden.shape
    width = mixed.shape[1]
    tokens = hidden

    def fetch(index, source, target):
        return pltpu.make_async_copy(source, target, load_sem.at[index])

    load_hidden = fetch(1, hidden_h, hidden)
    load_two = fetch(2, d_two_h, d_res)
    load_normed = fetch(3, normed_h, normed)
    load_mixed = fetch(4, mixed_h, mixed)
    load_out = [fetch(5 + i, w, w_out.at[i]) for i, w in enumerate((w_out_own, w_out_their))]
    load_w = [fetch(7 + i, w, w_qkv.at[i]) for i, w in enumerate((w_qkv_own, w_qkv_their))]
    load_tokens = fetch(9, tokens_h, tokens)
    load_qkv = [fetch(10 + half, qkv_h.at[half], qkv) for half in range(2)]

    def load_acted(c):
        return pltpu.make_async_copy(acted_h.at[:, pl.ds(pl.multiple_of(c * BR, BR), BR)], a_buf.at[lax.rem(c, 2)], chunk_sem.at[0, lax.rem(c, 2)])

    def load_chunk(half, c):
        slot = lax.rem(c, 2)
        span = pl.ds(pl.multiple_of(c * CHUNK, CHUNK), CHUNK)
        slope_h, up_h, down_h = ((slope_own_h, w_up_own, w_down_own), (slope_their_h, w_up_their, w_down_their))[half]
        return (
            pltpu.make_async_copy(slope_h.at[:, span], slope_buf.at[slot], chunk_sem.at[1, slot]),
            pltpu.make_async_copy(up_h.at[:, span], up_buf.at[slot], chunk_sem.at[2, slot]),
            pltpu.make_async_copy(down_h.at[span, :], down_buf.at[slot], chunk_sem.at[3, slot]),
        )

    def load_probs(half, s):
        slot = lax.rem(s, 2)
        return pltpu.make_async_copy(probs_h.at[half, s], probs.at[slot], probs_sem.at[slot])

    def start(copies):
        for copy in copies:
            copy.start()

    def wait(copies):
        for copy in copies:
            copy.wait()

    if fast:
        pos = Place()
        sum_greet(pos)
    load_acted(0).start()
    start(load_chunk(0, 0))
    load_hidden.start()

    def finish(block):
        pass

    if fast:
        tick = make_tick(pos, grads, *wires, COUNT, finish)
        last = COUNT + AFTER[7]
    else:

        def tick(step):
            pass

        last = COUNT
    done = [0]

    def ticks(index, each, trips):
        for i in range(each):
            tick(done[0] + index * each + i)
        return trips * each

    grads[VEC] = jnp.zeros((BR, BC), F32)
    grads[VEC, 36:54] = vec_in[...]
    acc_own[...] = jnp.zeros(acc_own.shape, F32)
    acc_their[...] = jnp.zeros(acc_their.shape, F32)
    sums[...] = jnp.zeros(sums.shape, F32)
    if fast:
        sum_met(pos)


    @pl.loop(0, 4)
    def _(c):
        load_acted(c).wait()

        @pl.when(c < 3)
        def _():
            load_acted(c + 1).start()

        @pl.when(c == 3)
        def _():
            load_two.start()
            load_normed.start()

        for part in range(2):
            piece = t_mm(a_buf[lax.rem(c, 2)], d_ffn[:, part * width : (part + 1) * width])
            for j in range(3):
                grads[DOWN + 6 * c + 3 * part + j] = piece[:, BC * j : BC * (j + 1)]
            if part >= 2 - TICKS[0]:
                tick(done[0] + c * TICKS[0] + part - 2 + TICKS[0])

    done[0] += 4 * TICKS[0]

    load_hidden.wait()
    for half in range(2):
        acc = (acc_own, acc_their)[half]

        @pl.loop(0, 6)
        def _(c, half=half, acc=acc):
            slot = lax.rem(c, 2)
            wait(load_chunk(half, c))

            @pl.when(c < 5)
            def _():
                start(load_chunk(half, c + 1))

            if half == 0:

                @pl.when(c == 5)
                def _():
                    start(load_chunk(1, 0))
                    load_mixed.start()
                    start(load_out)
                    load_qkv[0].start()
                    load_probs(0, 0).start()

            each = TICKS[1 + half]
            d_inner[...] = (mm_t(d_ffn[...], down_buf[slot]) * slope_buf[slot].astype(F32)).astype(BF)
            if each > 1:
                tick(done[0] + c * each)
            if half == 0:
                piece = t_mm(hidden[...], d_inner[...])
                for r in range(2):
                    for j in range(2):
                        grads[UP + 4 * c + 2 * r + j] = piece[BR * r : BR * (r + 1), BC * j : BC * (j + 1)]
                total = jnp.sum(d_inner[...].astype(F32), axis=0, keepdims=True)
                for j in range(2):
                    grads[VEC, pl.ds(6 + 2 * c + j, 1), :] = total[:, BC * j : BC * (j + 1)]
                if each > 2:
                    tick(done[0] + c * each + 1)
            for part in range(3):
                columns = slice(CHUNK * part, CHUNK * (part + 1))
                acc[:, columns] = acc[:, columns] + mm_t(d_inner[...], up_buf[slot, columns, :])
            tick(done[0] + c * each + each - 1)

        done[0] += 6 * TICKS[1 + half]

    start(load_w)
    load_tokens.start()

    load_two.wait()
    load_normed.wait()
    def norm_one(span):
        total = d_res[span, :] + (acc_own[span, :] + acc_their[span, :])
        unit = normed[span, :]
        one = norm_back(total, unit, inverse[span, :], flat_row(gain, 0, depth))
        d_res[span, :] = one
        low = one.astype(BF)
        d_low[span, :] = low
        for index, value in enumerate((low.astype(F32), total * unit, total)):
            sums[index] = sums[index] + value.reshape(-1, 8, depth).sum(axis=0)

    trips = rows // NORM_TILE

    @pl.loop(0, trips)
    def _(i):
        norm_one(pl.ds(pl.multiple_of(i * NORM_TILE, NORM_TILE), NORM_TILE))

        @pl.when(lax.rem(i, TICK_TILES) == 0)
        def _():
            tick(done[0] + i // TICK_TILES)

    if rows % NORM_TILE:
        norm_one(pl.ds(trips * NORM_TILE, rows % NORM_TILE))
    done[0] += -(-trips // TICK_TILES)
    for index in range(3):
        total = jnp.sum(sums[index], axis=0, keepdims=True)
        for j in range(6):
            grads[VEC, 18 + 6 * index + j : 19 + 6 * index + j, :] = total[:, BC * j : BC * (j + 1)]

    load_mixed.wait()
    wait(load_out)

    @pl.loop(0, 2)
    def _(half):
        d_mixed[half] = mm_t(d_low[...], w_out[half]).astype(BF)
        piece = t_mm(mixed[...], d_low[:, pl.ds(pl.multiple_of(half * width, BC), width)])
        for j in range(3):
            grads[OUT + 3 * half + j] = piece[:, BC * j : BC * (j + 1)]
        ticks(half, TICKS[3], 2)

    done[0] += 2 * TICKS[3]

    pairs = width // PAIR
    dka, dva = acc_their.at[:, pl.ds(0, width)], acc_their.at[:, pl.ds(width, width)]
    for half in range(2):
        load_qkv[half].wait()
        q, k, v = (qkv.at[i] for i in range(3))
        kmem, vmem = memory.at[half, 0], memory.at[half, 1]
        acc_their[...] = jnp.zeros(acc_their.shape, F32)
        dkm[...] = jnp.zeros(dkm.shape, F32)
        dvm[...] = jnp.zeros(dvm.shape, F32)

        group = UNROLL[half]

        @pl.loop(0, SEGS * pairs // group)
        def _(trip, half=half, group=group, kmem=kmem, vmem=vmem):
            s, first = trip * group // pairs, lax.rem(trip * group, pairs)

            @pl.when(first == 0)
            def _():
                load_probs(half, s).wait()

                @pl.when(s < SEGS - 1)
                def _():
                    load_probs(half, s + 1).start()

                if half == 0:

                    @pl.when(s == SEGS - 1)
                    def _():
                        load_probs(1, 0).start()

            for i in range(group):
                pair = i if group == pairs else first
                columns = pl.ds(pl.multiple_of(pair * PAIR, PAIR), PAIR)
                part = probs.at[lax.rem(s, 2), pair]
                attend_back_pair(q, k, v, kmem, vmem, part, d_mixed.at[half], d_qkv.at[0], dka, dva, dkm, dvm, s, columns)
                spot = trip * group + i

                @pl.when(lax.rem(spot, TICKS[4 + half]) == 0)
                def _(spot=spot):
                    tick(done[0] + spot // TICKS[4 + half])

        done[0] += -(-SEGS * pairs // TICKS[4 + half])
        if half == 0:
            assert done[0] <= QKV
        if half == 0:
            load_qkv[1].start()
        d_qkv[1] = ((dka[...] + spread(select_t[...], dkm[...])) * HD ** (-0.5)).astype(BF)
        d_qkv[2] = (dva[...] + spread(select_t[...], dvm[...])).astype(BF)
        if half == 0:
            wait(load_w)
            load_tokens.wait()

            @pl.loop(0, 3)
            def _(c):
                piece = t_mm(tokens[...], d_qkv[c])
                for r in range(2):
                    for j in range(3):
                        grads[QKV + 6 * c + 3 * r + j] = piece[BR * r : BR * (r + 1), BC * j : BC * (j + 1)]
                columns = pl.ds(pl.multiple_of(c * CHUNK, CHUNK), CHUNK)
                part = mm_t(d_qkv[0], w_qkv[half, pl.ds(pl.multiple_of(c * CHUNK, CHUNK), CHUNK), :])
                for i in (1, 2):
                    part = part + mm_t(d_qkv[i], w_qkv[half, pl.ds(pl.multiple_of(i * depth + c * CHUNK, CHUNK), CHUNK), :])
                acc_own[:, columns] = part
                ticks(c, TICKS[6], 3)

            done[0] += 3 * TICKS[6]
            for index, row in ((0, 0), (2, 3)):
                total = jnp.sum(d_qkv[index].astype(F32), axis=0, keepdims=True)
                for j in range(3):
                    grads[VEC, row + j : row + j + 1, :] = total[:, BC * j : BC * (j + 1)]
        else:

            @pl.loop(0, 3)
            def _(c):
                columns = pl.ds(pl.multiple_of(c * CHUNK, CHUNK), CHUNK)
                part = mm_t(d_qkv[0], w_qkv[half, pl.ds(pl.multiple_of(c * CHUNK, CHUNK), CHUNK), :])
                for i in (1, 2):
                    part = part + mm_t(d_qkv[i], w_qkv[half, pl.ds(pl.multiple_of(i * depth + c * CHUNK, CHUNK), CHUNK), :])
                d_low[:, columns] = ((acc_own[:, columns] + part) + d_res[:, columns]).astype(BF)
                ticks(c, TICKS[7], 3)

            done[0] += 3 * TICKS[7]
    @pl.loop(min(done[0], last), last)
    def _(step):
        tick(step)


TICKS = (1, 3, 2, 1, 2, 1, 3, 1)
TICK_TILES = 2
NORM_TILE = 128
UNROLL = (3, 1)


def backward(fast, select_t, memory, inverse, gain, vec_in, arrays):
    tokens, acted, mixed = arrays[0], arrays[5], arrays[9]
    rows, depth = tokens.shape
    units = acted.shape[1]
    width = mixed.shape[1]
    vm = pl.BlockSpec(memory_space=pltpu.VMEM)
    hbm = pl.BlockSpec(memory_space=pl.ANY)
    if fast:
        kept_in = pltpu.with_memory_space_constraint(arrays[2], pltpu.VMEM)
        arrays = (*arrays[:2], kept_in, *arrays[3:])
    kept = pltpu.VMEM if fast else jax.ShapeDtypeStruct
    return pl.pallas_call(
        functools.partial(backward_kernel, fast),
        out_shape=[kept((COUNT, BR, BC), F32), kept((rows, depth), BF)],
        in_specs=[vm, vm, vm, vm, vm, hbm, hbm, vm] + [hbm] * (len(arrays) - 3),
        out_specs=[vm, vm],
        scratch_shapes=[
            pltpu.VMEM((rows, depth), BF),
            pltpu.VMEM((rows, depth), F32),
            pltpu.VMEM((rows, depth), F32),
            pltpu.VMEM((rows, depth), F32),
            pltpu.VMEM((rows, depth), F32),
            pltpu.VMEM((2, rows, BR), BF),
            pltpu.VMEM((2, rows, CHUNK), BF),
            pltpu.VMEM((2, depth, CHUNK), BF),
            pltpu.VMEM((2, CHUNK, depth), BF),
            pltpu.VMEM((rows, CHUNK), BF),
            pltpu.VMEM((3, 8, depth), F32),
            pltpu.VMEM((rows, width), BF),
            pltpu.VMEM((2, width, depth), BF),
            pltpu.VMEM((2, 3 * depth, width), BF),
            pltpu.VMEM((3, rows, width), BF),
            pltpu.VMEM((3, rows, width), BF),
            pltpu.VMEM((2, rows, width), BF),
            pltpu.VMEM((2, width // PAIR, 2 * WIN, WIN + MEMP), BF),
            pltpu.VMEM((MEMP, width), F32),
            pltpu.VMEM((MEMP, width), F32),
            pltpu.SemaphoreType.DMA((12,)),
            pltpu.SemaphoreType.DMA((4, 2)),
            pltpu.SemaphoreType.DMA((2,)),
        ]
        + (sum_scratch() if fast else []),
        compiler_params=pltpu.CompilerParams(
            collective_id=1 if fast else None, has_side_effects=fast, vmem_limit_bytes=45100000 if fast else 67043328
        ),
        name="backward",
    )(select_t, memory, inverse, gain, vec_in, *arrays)


def results_kernel(blocks, grad_tokens, output, g_qkv, g_out, g_up, g_down, tokens_h, output_out, *rest):
    vectors, (sems, out_sem) = rest[:8], rest[8:]
    places = [(g_down, BR * (i // 6), BC * (i % 6)) for i in range(24)]
    places += [(g_up, BR * (i // 2 % 2), CHUNK * (i // 4) + BC * (i % 2)) for i in range(24)]
    places += [(g_out, 0, BC * i) for i in range(6)]
    places += [(g_qkv, BR * (i // 3), BC * (i % 3)) for i in range(18)]
    copies = [
        pltpu.make_async_copy(blocks.at[i], target.at[pl.ds(row, BR), pl.ds(column, BC)], sems.at[i])
        for i, (target, row, column) in enumerate(places)
    ]
    copies.append(pltpu.make_async_copy(grad_tokens, tokens_h, out_sem.at[0]))
    copies.append(pltpu.make_async_copy(output, output_out, out_sem.at[1]))
    for copy in copies:
        copy.start()
    bias_qv, *flat = vectors
    for j in range(6):
        bias_qv[j // 3 : j // 3 + 1, BC * (j % 3) : BC * (j % 3 + 1)] = blocks[VEC, j : j + 1, :]
    row = 6
    for ref in flat:
        for j in range(ref.shape[0] // BC):
            ref[pl.ds(BC * j, BC)] = blocks[VEC, row, :]
            row += 1
    for copy in copies:
        copy.wait()


def results(fast, blocks, grad_tokens, output, width, units):
    vm = pl.BlockSpec(memory_space=pltpu.VMEM)
    hbm = pl.BlockSpec(memory_space=pl.ANY)
    sd = jax.ShapeDtypeStruct
    rows, depth = output.shape
    if fast:
        blocks, grad_tokens, output = (
            pltpu.with_memory_space_constraint(a, pltpu.VMEM) for a in (blocks, grad_tokens, output)
        )
    large = [sd((3 * depth, width), F32), sd((width, depth), F32), sd((depth, units), F32), sd((units, depth), F32)]
    large += [sd((rows, depth), BF)] * 2
    small = [sd((2, width), F32), sd((units,), F32)] + [sd((depth,), F32)] * 6
    return pl.pallas_call(
        results_kernel,
        out_shape=large + small,
        in_specs=[vm, vm, vm],
        out_specs=[hbm] * 6 + [vm] * len(small),
        scratch_shapes=[
            pltpu.SemaphoreType.DMA((VEC,)),
            pltpu.SemaphoreType.DMA((2,)),
        ],
        compiler_params=pltpu.CompilerParams(vmem_limit_bytes=(8 if fast else 40) * 2**20),
        name="results",
    )(blocks, grad_tokens, output)


def halves_swap(own, small):
    unit = (lax.axis_index("dp") >= 0).astype(F32)

    def other(array):
        arrived = lax.ppermute(array.astype(F32), "tensor", [(0, 1), (1, 0)])
        return (arrived * unit).astype(array.dtype)

    return tuple(other(array) for array in own) + (other(small),)


def shards(
    fast,
    tokens,
    w_qkv,
    bias_qv,
    w_out,
    bias_out,
    gain_one,
    shift_one,
    w_up,
    bias_up,
    w_down,
    bias_down,
    gain_two,
    shift_two,
    grad_out,
    parent,
    mem_slots,
):
    depth, width = w_qkv.shape[1:]
    hidden_units = w_up.shape[1]
    own = (w_qkv.reshape(3 * depth, width), w_out, w_up, w_down)
    if fast:
        given = ()
    else:
        table = jnp.pad(bias_up.reshape(-1, CHUNK), ((0, 0), (0, width - CHUNK)))
        small = jnp.concatenate([bias_qv[:1], jnp.zeros((1, width), F32), bias_qv[1:], table])
        given = halves_swap(own, jnp.pad(small, ((0, 16 - small.shape[0]), (0, 0))))
    vectors = (bias_qv, bias_out, gain_one, shift_one, bias_up, bias_down, gain_two, shift_two)
    (
        output,
        *theirs,
        qkv,
        mixed,
        normed,
        inverse,
        hidden_low,
        acted,
        slope_own,
        slope_their,
        d_two,
        d_ffn,
        vec,
        probs,
        select_t,
        memory,
    ) = forward(fast, parent, mem_slots, vectors, tokens, grad_out, own, given)
    if not fast:
        theirs = given[:4]
    arrays = (tokens, hidden_low, d_ffn, d_two, normed, acted, slope_own, slope_their, qkv, mixed, probs)
    weights = tuple(w[i] for i in (2, 3, 1, 0) for w in (own, theirs))
    blocks, grad_tokens = backward(fast, select_t, memory, inverse, gain_one, vec, arrays + weights)
    if not fast:
        blocks = lax.psum(blocks, "dp")
    (
        g_w_qkv,
        g_w_out,
        g_w_up,
        g_w_down,
        grad_tokens,
        output,
        g_bias_qv,
        g_bias_up,
        g_bias_out,
        g_gain_one,
        g_shift_one,
        g_bias_down,
        g_gain_two,
        g_shift_two,
    ) = results(fast, blocks, grad_tokens, output, width, hidden_units)
    return (
        output,
        grad_tokens,
        g_w_qkv.reshape(w_qkv.shape),
        g_bias_qv,
        g_w_out,
        g_bias_out,
        g_gain_one,
        g_shift_one,
        g_w_up,
        g_bias_up,
        g_w_down,
        g_bias_down,
        g_gain_two,
        g_shift_two,
    )


def solution(mesh):
    fast = mesh.shape["dp"] == 16 and mesh.shape["tensor"] == 2
    rows, whole = P("dp", None), P()
    return jax.shard_map(
        functools.partial(shards, fast),
        mesh=mesh,
        in_specs=(
            rows,
            P(None, None, "tensor"),
            P(None, "tensor"),
            P("tensor", None),
            whole,
            whole,
            whole,
            P(None, "tensor"),
            P("tensor"),
            P("tensor", None),
            whole,
            whole,
            whole,
            rows,
            P("dp"),
            rows,
        ),
        out_specs=(
            rows,
            rows,
            P(None, None, "tensor"),
            P(None, "tensor"),
            P("tensor", None),
            whole,
            whole,
            whole,
            P(None, "tensor"),
            P("tensor"),
            P("tensor", None),
            whole,
            whole,
            whole,
        ),
        check_vma=False,
    )
```

```python
import functools


import jax
import jax.numpy as jnp
from jax import lax
from jax.experimental import pallas as pl
from jax.experimental.pallas import tpu as pltpu
from jax.sharding import PartitionSpec as P


MESH = pl.DeviceIdType.MESH
BR, BC = 384, 128
AFTER = (0, 3, 6, 9, 12, 15, 18, 21)
SLOTS = 16


class Place:
    def __init__(self):
        me = lax.axis_index("dp")
        self.core = lax.rem(me, 2)
        self.x = lax.rem(me // 2, 2)
        self.z = me // 4
        self.sib = me + 1 - 2 * self.core
        self.xn = me + 2 - 4 * self.x
        self.zp = me + 4 - 8 * lax.rem(self.z, 2)
        self.zm = me + 4 * (3 - 2 * self.z)
        self.end = (self.z == 0) | (self.z == 3)
        self.mid = (self.z == 1) | (self.z == 2)


def sum_greet(pos):
    barrier = pltpu.get_barrier_semaphore()

    def greet(dev):
        pl.semaphore_signal(barrier, inc=1, device_id={"dp": dev}, device_id_type=MESH)

    greet(pos.sib)
    greet(pos.xn)
    greet(pos.zp)

    @pl.when(pos.mid)
    def _():
        greet(pos.zm)


def sum_met(pos):
    pl.semaphore_wait(pltpu.get_barrier_semaphore(), jnp.where(pos.mid, 4, 3))


def make_tick(pos, grads, from_core, from_one, from_two, from_three, sent, got, credit, count, finish):
    half = BR // 2
    quarter = BR // 4

    def copy(stage, block, source, target, device):
        slot = lax.rem(block, SLOTS)
        return pltpu.make_async_remote_copy(
            src_ref=source,
            dst_ref=target,
            send_sem=sent.at[stage, slot],
            recv_sem=got.at[stage, slot],
            device_id={"dp": device},
            device_id_type=MESH,
        )

    def rows(block, start, size):
        return grads.at[block, pl.ds(pl.multiple_of(start, quarter), size)]

    def add(block, start, size, landed):
        where = pl.ds(pl.multiple_of(start, quarter), size)
        grads[block, where] = grads[block, where] + landed[...]

    def free(index, device):
        pl.semaphore_signal(credit.at[index], inc=1, device_id={"dp": device}, device_id_type=MESH)

    def claim(index):
        pl.semaphore_wait(credit.at[index], 1)

    x_first = pos.core == 0
    z_first = pos.core == 1
    mine = pos.core * half
    xrow = pos.x * quarter
    xrow_other = (1 - pos.x) * quarter
    far = lax.rem(pos.z, 2) == 0
    keep = half + jnp.where(far, quarter, 0)
    give = half + jnp.where(far, 0, quarter)

    def core_out(block):
        return copy(0, block, rows(block, (1 - pos.core) * half, half), from_core.at[lax.rem(block, SLOTS)], pos.sib)

    def x_one(block):
        return copy(1, block, rows(block, xrow_other, quarter), from_one.at[lax.rem(block, SLOTS), pl.ds(0, quarter)], pos.xn)

    def z_one(block):
        return copy(1, block, rows(block, half, half), from_one.at[lax.rem(block, SLOTS)], pos.zp)

    def x_two(block):
        return copy(2, block, rows(block, xrow, quarter), from_two.at[lax.rem(block, SLOTS)], pos.zp)

    def z_two(block):
        return copy(2, block, rows(block, give, quarter), from_two.at[lax.rem(block, SLOTS)], pos.zm)

    def x_three(block):
        return copy(3, block, rows(block, xrow, quarter), from_three.at[lax.rem(block, SLOTS)], pos.zm)

    def z_three(block):
        return copy(3, block, rows(block, keep, quarter), from_three.at[lax.rem(block, SLOTS)], pos.xn)

    def x_four(block):
        return copy(4, block, rows(block, xrow, quarter), rows(block, xrow, quarter), pos.zp)

    def z_four(block):
        return copy(4, block, rows(block, keep, quarter), rows(block, keep, quarter), pos.zm)

    def z_four_in(block):
        return copy(4, block, rows(block, give, quarter), rows(block, give, quarter), pos.zm)

    def x_five(block):
        return copy(5, block, rows(block, xrow, quarter), rows(block, xrow, quarter), pos.xn)

    def x_five_in(block):
        return copy(5, block, rows(block, xrow_other, quarter), rows(block, xrow_other, quarter), pos.xn)

    def z_five(block):
        return copy(5, block, rows(block, half, half), rows(block, half, half), pos.zp)

    def core_six(block):
        return copy(6, block, rows(block, mine, half), rows(block, mine, half), pos.sib)

    def core_six_in(block):
        return copy(6, block, rows(block, (1 - pos.core) * half, half), rows(block, (1 - pos.core) * half, half), pos.sib)

    def start_core(block):
        core_out(block).start()

    def take_core(block):
        core_out(block).wait()
        free(2, pos.sib)
        add(block, mine, half, from_core.at[lax.rem(block, SLOTS)])

    def take_x(block):
        x_one(block).wait()
        free(1, pos.xn)
        add(block, xrow, quarter, from_one.at[lax.rem(block, SLOTS), pl.ds(0, quarter)])

    def send_x(block):
        take_core(block)
        x_one(block).start()

    def send_z(block):
        take_core(block)
        z_one(block).start()

    def x_end_two(block):
        take_x(block)
        x_two(block).start()

    def x_end_three(block):
        x_two(block).wait_send()
        free(0, pos.zp)

    def x_mid_three(block):
        x_two(block).wait_recv()
        add(block, xrow, quarter, from_two.at[lax.rem(block, SLOTS)])
        x_three(block).start()

    def x_mid_four(block):
        x_three(block).wait()
        add(block, xrow, quarter, from_three.at[lax.rem(block, SLOTS)])
        claim(0)
        x_four(block).start()

    def x_end_five(block):
        x_four(block).wait_recv()
        claim(1)
        x_five(block).start()

    def x_mid_five(block):
        x_four(block).wait_send()
        claim(1)
        x_five(block).start()

    def x_six(block):
        x_five(block).wait_send()
        x_five_in(block).wait_recv()
        claim(2)
        core_six(block).start()

    def z_end_two(block):
        z_one(block).wait_send()
        free(1, pos.zp)

    def z_end_six(block):
        z_five(block).wait_recv()
        claim(2)
        core_six(block).start()

    def z_mid_two(block):
        z_one(block).wait_recv()
        add(block, half, half, from_one.at[lax.rem(block, SLOTS)])
        z_two(block).start()

    def z_mid_three(block):
        z_two(block).wait()
        free(0, pos.zm)
        add(block, keep, quarter, from_two.at[lax.rem(block, SLOTS)])
        z_three(block).start()

    def z_mid_four(block):
        z_three(block).wait()
        add(block, keep, quarter, from_three.at[lax.rem(block, SLOTS)])
        claim(0)
        z_four(block).start()

    def z_mid_five(block):
        z_four(block).wait_send()
        z_four_in(block).wait_recv()
        claim(1)
        z_five(block).start()

    def z_mid_six(block):
        z_five(block).wait_send()
        claim(2)
        core_six(block).start()

    def last(block):
        core_six(block).wait_send()
        core_six_in(block).wait_recv()

    roles = (
        (x_first & pos.end, (start_core, send_x, x_end_two, x_end_three, None, x_end_five, x_six, last)),
        (x_first & pos.mid, (start_core, send_x, take_x, x_mid_three, x_mid_four, x_mid_five, x_six, last)),
        (z_first & pos.end, (start_core, send_z, z_end_two, None, None, None, z_end_six, last)),
        (z_first & pos.mid, (start_core, take_core, z_mid_two, z_mid_three, z_mid_four, z_mid_five, z_mid_six, last)),
    )
    depth = len(roles[0][1])

    def tick(step):
        for here, stages in roles:

            @pl.when(here)
            def _(stages=stages):
                for index in reversed(range(depth)):
                    block = step - AFTER[index]
                    if stages[index] is not None:

                        @pl.when((block >= 0) & (block < count))
                        def _(index=index, block=block, stages=stages):
                            stages[index](block)

        over = step - AFTER[depth - 1]

        @pl.when((over >= 0) & (over < count))
        def _():
            finish(over)

    return tick


def sum_scratch():
    return [
        pltpu.VMEM((SLOTS, BR // 2, BC), jnp.float32),
        pltpu.VMEM((SLOTS, BR // 2, BC), jnp.float32),
        pltpu.VMEM((SLOTS, BR // 4, BC), jnp.float32),
        pltpu.VMEM((SLOTS, BR // 4, BC), jnp.float32),
        pltpu.SemaphoreType.DMA((7, SLOTS)),
        pltpu.SemaphoreType.DMA((7, SLOTS)),
        pltpu.SemaphoreType.REGULAR((3,)),
    ]


CR, CC = 64, 384
CHUNKS = 24
HOPS = (3, 6, 7)
BF = jnp.bfloat16


def gather_greet(pos, other):
    barrier = pltpu.get_barrier_semaphore()
    for where in ({"tensor": other}, {"dp": pos.xn}, {"dp": pos.zp}, {"dp": pos.sib}):
        pl.semaphore_signal(barrier, inc=1, device_id=where, device_id_type=MESH)


def gather_met():
    pl.semaphore_wait(pltpu.get_barrier_semaphore(), 4)


def chunk_parts(piece, chunk, kind):
    if kind == 0:
        return [(piece * 384 + chunk * 64, 64, 0, 0)]
    if kind == 1:
        return [(piece * 64 + (chunk - 6) * 32, 32, 384 * q, 32 * q) for q in range(2)]
    if kind == 2:
        return [(piece * 128 + (chunk - 8) * 16, 16, 384 * q, 16 * q) for q in range(4)]
    return [((chunk - 16) * 192 + piece * 32, 32, 384 * q, 32 * q) for q in range(2)]


BOUNDS = ((0, 6), (6, 8), (8, 16), (16, 24))
UNIT = (64, 32, 16, 32)


def make_gather(pos, own, theirs, staged, landed, sent, got):
    other = 1 - lax.axis_index("tensor")
    odd = lax.rem(pos.z, 2)
    ky = jnp.where(pos.x == 0, odd, 2)
    kx = jnp.where(pos.x == 0, 2, odd)
    kz = 1 - odd
    piece_y = 2 * ky + pos.core
    piece_x = 2 * kx + pos.core
    piece_z = 2 * kz + pos.core
    sib_y = 2 * ky + 1 - pos.core
    sib_x = 2 * kx + 1 - pos.core
    sib_z = 2 * kz + 1 - pos.core

    def copy(lane, chunk, source, piece, where):
        return pltpu.make_async_remote_copy(
            src_ref=source,
            dst_ref=landed.at[piece, chunk],
            send_sem=sent.at[lane, chunk],
            recv_sem=got.at[lane, chunk],
            device_id=where,
            device_id_type=MESH,
        )

    def over_y(chunk):
        return copy(0, chunk, staged.at[chunk], piece_y, {"tensor": other})

    def over_x(chunk, piece):
        return copy(1, chunk, landed.at[piece, chunk], piece, {"dp": pos.xn})

    def over_z(chunk, piece):
        return copy(2, chunk, landed.at[piece, chunk], piece, {"dp": pos.zp})

    def over_core(lane, chunk, piece):
        return copy(lane, chunk, landed.at[piece, chunk], piece, {"dp": pos.sib})

    def stage_own(kind):
        lo, hi = BOUNDS[kind]

        @pl.loop(lo, hi)
        def _(chunk):
            for row, rows, column, at in chunk_parts(piece_y, chunk, kind):
                staged[chunk, pl.ds(at, rows)] = own[kind][
                    pl.ds(pl.multiple_of(row, UNIT[kind]), rows), pl.ds(column, CC)
                ].astype(jnp.float32)

    def send_own(kind):
        lo, hi = BOUNDS[kind]

        @pl.loop(lo, hi)
        def _(chunk):
            over_y(chunk).start()

    def unpack(chunk):
        for kind in range(4):
            lo, hi = BOUNDS[kind]

            @pl.when((chunk >= lo) & (chunk < hi))
            def _(kind=kind):
                @pl.loop(0, 6)
                def _(piece):
                    for row, rows, column, at in chunk_parts(piece, chunk, kind):
                        theirs[kind][pl.ds(pl.multiple_of(row, UNIT[kind]), rows), pl.ds(column, CC)] = landed[
                            piece, chunk, pl.ds(at, rows)
                        ].astype(BF)

    def guarded(chunk, body):
        @pl.when((chunk >= 0) & (chunk < CHUNKS))
        def _():
            body(chunk)

    def first(chunk):
        over_y(chunk).wait_recv()
        over_x(chunk, piece_y).start()

        @pl.when(pos.x == 0)
        def _():
            over_z(chunk, piece_y).start()

        over_core(3, chunk, piece_y).start()

    def second(chunk):
        over_x(chunk, piece_x).wait_recv()

        @pl.when(pos.x == 1)
        def _():
            over_z(chunk, piece_x).start()

        over_core(4, chunk, piece_x).start()

    def third(chunk):
        over_z(chunk, piece_z).wait_recv()
        over_core(5, chunk, piece_z).start()

    def fourth(chunk):
        over_core(3, chunk, sib_y).wait_recv()
        over_core(4, chunk, sib_x).wait_recv()
        over_core(5, chunk, sib_z).wait_recv()
        over_y(chunk).wait_send()
        over_x(chunk, piece_y).wait_send()
        over_z(chunk, piece_y).wait_send()
        over_core(3, chunk, piece_y).wait_send()
        over_core(4, chunk, piece_x).wait_send()
        over_core(5, chunk, piece_z).wait_send()
        unpack(chunk)

    def tick(step):
        guarded(step - HOPS[2], fourth)
        guarded(step - HOPS[1], third)
        guarded(step - HOPS[0], second)
        guarded(step, first)

    return stage_own, send_own, tick


def gather_scratch():
    return [
        pltpu.VMEM((CHUNKS, CR, CC), jnp.float32),
        pltpu.VMEM((6, CHUNKS, CR, CC), jnp.float32),
        pltpu.SemaphoreType.DMA((6, CHUNKS)),
        pltpu.SemaphoreType.DMA((6, CHUNKS)),
    ]


def swap_small(small, small_out, sems):
    return pltpu.make_async_remote_copy(
        src_ref=small,
        dst_ref=small_out,
        send_sem=sems.at[0],
        recv_sem=sems.at[1],
        device_id={"tensor": 1 - lax.axis_index("tensor")},
        device_id_type=MESH,
    )


HD = 64
SEG = 148
MEMW = 10
F32 = jnp.float32
EPSILON = 1e-12
MASKED = -1e30
WIN = 160
MEMP = 96
SEGS = 8
PAIR = 2 * HD

CONTRACT_LAST = (((1,), (1,)), ((), ()))
CONTRACT_FIRST = (((0,), (0,)), ((), ()))


def mm(a, b):
    return jnp.dot(a, b, preferred_element_type=F32)


def mm_t(a, b):
    return lax.dot_general(a, b, CONTRACT_LAST, preferred_element_type=F32)


def t_mm(a, b):
    return lax.dot_general(a, b, CONTRACT_FIRST, preferred_element_type=F32)


def build_masks(parent, base, colbias):
    lane = lax.broadcasted_iota(jnp.int32, (1, WIN + MEMP), 1)
    in_mem = [
        ((lane >= WIN + MEMW * t) & (lane < WIN + MEMW * (t + 1))).astype(F32) for t in range(SEGS)
    ]
    reach = [jnp.zeros((1, WIN + MEMP), F32)]
    for s in range(1, SEGS):
        row = jnp.zeros((1, WIN + MEMP), F32)
        for t in range(s):
            hit = jnp.where(parent[s] - base == t, 1.0, 0.0)
            row = row + hit * jnp.maximum(reach[t], in_mem[t])
        reach.append(row)
    for s in range(SEGS):
        off = 4 * (s % 4)
        inside = ((lane >= off) & (lane < off + SEG)).astype(F32)
        colbias[s : s + 1, :] = jnp.where(jnp.maximum(inside, reach[s]) > 0.0, 0.0, MASKED)


def build_select(slots, select, select_t):
    for ref, axis in ((select, 0), (select_t, 1)):
        shape = (ref.shape[0], 1) if axis == 0 else (1, ref.shape[1])
        entry = lax.broadcasted_iota(jnp.int32, shape, axis)
        where = jnp.full(shape, -1, jnp.int32)
        for t in range(SEGS):
            for m in range(MEMW):
                where = jnp.where(entry == MEMW * t + m, slots[t, m] + SEG * t, where)
        place = lax.broadcasted_iota(jnp.int32, ref.shape, 1 - axis)
        ref[...] = (where == place).astype(F32).astype(BF)


def window(s):
    return pl.multiple_of(144 * s + 16 * (s // 4), 16), 4 * lax.rem(s, 4)


def lane_halves():
    lane = lax.broadcasted_iota(jnp.int32, (1, PAIR), 1)
    left = (lane < HD).astype(F32)
    return left.astype(BF), (1.0 - left).astype(BF), lane < HD


def valid_rows(off):
    row = lax.broadcasted_iota(jnp.int32, (WIN, 1), 0)
    return row, (row >= off) & (row < off + SEG)


def softmax_parts(qs, kk, bias):
    scores = mm_t(qs, kk) * HD ** (-0.5) + bias
    top = jnp.max(scores, axis=-1, keepdims=True)
    raised = jnp.exp(scores - top)
    return raised, 1.0 / jnp.sum(raised, axis=-1, keepdims=True)


def attend_pair(q, k, v, kmem, vmem, colbias, mixed, probs, s, columns):
    left, right, is_left = lane_halves()
    at, off = window(s)
    rows = pl.ds(at, WIN)
    qw = q[rows, columns]
    qs = jnp.concatenate([qw * left, qw * right], axis=0)
    kk = jnp.concatenate([k[rows, columns], kmem[:, columns]], axis=0)
    vv = jnp.concatenate([v[rows, columns], vmem[:, columns]], axis=0)
    raised, scale = softmax_parts(qs, kk, colbias[pl.ds(s, 1), :])
    row, valid = valid_rows(off)
    keep = jnp.where(valid, 1.0, 0.0)
    chances = (raised * (scale * jnp.concatenate([keep, keep], axis=0))).astype(BF)
    probs[...] = chances
    both = mm(chances, vv)
    out = jnp.where(is_left, both[:WIN], both[WIN:])
    old = mixed[rows, columns].astype(F32)
    mixed[rows, columns] = jnp.where(row >= off, out, old).astype(BF)


def attend_back_pair(q, k, v, kmem, vmem, probs, dmix, dq, dk, dv, dkmem, dvmem, s, columns):
    left, right, is_left = lane_halves()
    at, off = window(s)
    rows = pl.ds(at, WIN)
    qw = q[rows, columns]
    qs = jnp.concatenate([qw * left, qw * right], axis=0)
    kk = jnp.concatenate([k[rows, columns], kmem[:, columns]], axis=0)
    vv = jnp.concatenate([v[rows, columns], vmem[:, columns]], axis=0)
    dw = dmix[rows, columns]
    ds_in = jnp.concatenate([dw * left, dw * right], axis=0)
    low = probs[...]
    chances = low.astype(F32)
    dp = mm_t(ds_in, vv)
    inner = jnp.sum(chances * dp, axis=-1, keepdims=True)
    ds = (chances * (dp - inner)).astype(BF)
    dqs = mm(ds, kk)
    row, valid = valid_rows(off)
    new = jnp.where(is_left, dqs[:WIN], dqs[WIN:]) * HD ** (-0.5)
    old = dq[rows, columns].astype(F32)
    dq[rows, columns] = jnp.where(row >= off, new, old).astype(BF)
    dks = t_mm(ds, qs)
    dvs = t_mm(low, ds_in)
    dk[rows, columns] = dk[rows, columns] + dks[:WIN]
    dv[rows, columns] = dv[rows, columns] + dvs[:WIN]
    dkmem[:, columns] = dkmem[:, columns] + dks[WIN:]
    dvmem[:, columns] = dvmem[:, columns] + dvs[WIN:]


def spread(select_t, part):
    high = part.astype(BF)
    low = (part - high.astype(F32)).astype(BF)
    return mm(select_t, high) + mm(select_t, low)


def norm_stats(values):
    centered = values - jnp.mean(values, axis=-1, keepdims=True)
    inverse = lax.rsqrt(jnp.mean(centered * centered, axis=-1, keepdims=True) + EPSILON)
    return centered * inverse, inverse


def norm_back(grad, normed, inverse, gain):
    scaled = grad * gain
    return inverse * (
        scaled
        - jnp.mean(scaled, axis=-1, keepdims=True)
        - normed * jnp.mean(scaled * normed, axis=-1, keepdims=True)
    )


def gelu_parts(inner):
    phi = 0.5 + 0.5 * lax.erf(inner * (0.5**0.5))
    density = jnp.exp(-0.5 * inner * inner) * (2.0 * jnp.pi) ** -0.5
    return (inner * phi).astype(BF), (phi + inner * density).astype(BF)


def flat_row(ref, start, size):
    return ref[pl.ds(start, size)].reshape(1, size)


TILE = 128


SPLIT = 6 * TILE


def row_tiles(first, last, body):
    full = (last - first) // TILE

    @pl.loop(0, full)
    def _(i):
        body(pl.ds(pl.multiple_of(first + i * TILE, TILE), TILE))

    if (last - first) % TILE:
        body(pl.ds(first + full * TILE, (last - first) % TILE))


def forward_kernel(
    fast,
    parent,
    slots,
    bias_qv,
    bias_out,
    gain_one,
    shift_one,
    bias_up,
    bias_down,
    gain_two,
    shift_two,
    tokens_h,
    grad_h,
    qkv_in,
    out_in,
    up_in,
    down_in,
    *rest,
):
    count = 0 if fast else 5
    given, outs, rest = rest[:count], rest[count : count + 19], rest[count + 19 :]
    (
        output_h,
        their_qkv_h,
        their_out_h,
        their_up_h,
        their_down_h,
        qkv_h,
        mixed_h,
        normed_h,
        inverse,
        hidden_h,
        acted_h,
        slope_own_h,
        slope_their_h,
        d_two_h,
        d_ffn,
        vec,
        probs_h,
        select_t,
        memory,
    ) = outs
    (
        tokens,
        own_qkv,
        own_out,
        own_up,
        own_down,
        their_qkv,
        their_out,
        their_up,
        their_down,
        small,
        small_their,
        qkv,
        mixed,
        normed,
        hidden,
        acc_own,
        acc_their,
        acted,
        slopes,
        colbias,
        select,
        sums,
        probs,
        io_sem,
        slope_sem,
        probs_sem,
        *wires,
    ) = rest
    rows, depth = tokens.shape
    width = mixed.shape[2]
    units = acted.shape[1]
    theirs = (their_qkv, their_out, their_up, their_down)
    own = (own_qkv, own_out, own_up, own_down)

    def move(index, source, target):
        return pltpu.make_async_copy(source, target, io_sem.at[index])

    load_tokens = move(0, tokens_h, tokens)
    load_grad = move(1, grad_h, tokens)
    put_qkv = move(2, qkv, qkv_h)
    put_mixed = move(3, mixed.at[0], mixed_h)
    put_normed = move(4, normed, normed_h)
    put_hidden = move(5, hidden, hidden_h)
    put_acted = move(6, acted, acted_h)
    late = ((acc_own, d_two_h), (tokens, output_h))
    put_late = [
        [move(7 + 3 * part + i, ref.at[rows_of], target.at[rows_of]) for i, (ref, target) in enumerate(late)]
        for part, rows_of in enumerate((pl.ds(0, SPLIT), pl.ds(SPLIT, rows - SPLIT)))
    ]
    put_theirs = [
        move(13 + i, ref, target)
        for i, (ref, target) in enumerate(zip(theirs, (their_qkv_h, their_out_h, their_up_h, their_down_h)))
    ]
    load_own = [move(17 + i, a, b) for i, (a, b) in enumerate(zip((qkv_in, out_in, up_in, down_in), own))]
    if fast:
        pos = Place()
        gather_greet(pos, 1 - lax.axis_index("tensor"))
    load_own[0].start()
    load_tokens.start()
    for copy in load_own[1:]:
        copy.start()
    done = [0]
    small[...] = jnp.zeros(small.shape, F32)
    small[0:1, :] = bias_qv[0:1, :]
    small[2:3, :] = bias_qv[1:2, :]
    for c in range(units // CHUNK):
        small[3 + c : 4 + c, 0:CHUNK] = flat_row(bias_up, c * CHUNK, CHUNK)
    if fast:
        small_sem, *wires = wires
        stage_own, send_own, tick = make_gather(pos, own, theirs, *wires)
        load_own[0].wait()
        stage_own(0)
        gather_met()
        send_own(0)
        swap = swap_small(small, small_their, small_sem)
        swap.start()
        for kind in range(1, 4):
            load_own[kind].wait()
            stage_own(kind)
            send_own(kind)
    else:
        for copy in load_own:
            copy.wait()
        copies = [move(13 + i, a, b) for i, (a, b) in enumerate(zip(given, theirs + (small_their,)))]
        for copy in copies:
            copy.start()
        for copy in copies:
            copy.wait()

        def tick(step):
            pass

    def ticks(index, each, trips):
        for i in range(each):
            tick(done[0] + index * each + i)

    def tick_every(index, every, trips):
        @pl.when(lax.rem(index, every) == 0)
        def _():
            tick(done[0] + index // every)

        return -(-trips // every)

    def until(count):
        if done[0] < count:

            @pl.loop(done[0], count)
            def _(step):
                tick(step)

            done[0] = count

    build_masks(parent, lax.axis_index("dp") * SEGS, colbias)
    build_select(slots, select, select_t)
    load_tokens.wait()
    pairs = width // PAIR
    for half in range(2):
        weights = (own_qkv, their_qkv)[half]
        table = (small, small_their)[half]
        if half == 1:
            until(BOUNDS[0][1] + HOPS[2])
            if fast:
                swap.wait()

        @pl.loop(0, 3)
        def _(c, half=half, weights=weights, table=table):
            part = mm(tokens[...], weights[pl.ds(pl.multiple_of(c * depth, depth), depth), :])
            qkv[half, c] = (part + table[pl.ds(c, 1), :]).astype(BF)

        q, k, v = (qkv.at[half, i] for i in range(3))
        kmem, vmem = memory.at[half, 0], memory.at[half, 1]
        kmem[...] = mm(select[...], k[...]).astype(BF)
        vmem[...] = mm(select[...], v[...]).astype(BF)

        def put_probs(s, half=half):
            slot = lax.rem(s, 2)
            return pltpu.make_async_copy(probs.at[slot], probs_h.at[half, s], probs_sem.at[slot])

        @pl.loop(0, SEGS)
        def _(s, half=half, q=q, k=k, v=v, kmem=kmem, vmem=vmem, put_probs=put_probs):
            @pl.when(s >= 2)
            def _():
                put_probs(s - 2).wait()

            for pair in range(pairs):
                attend_pair(
                    q, k, v, kmem, vmem, colbias, mixed.at[half], probs.at[lax.rem(s, 2), pair], s, pl.ds(pair * PAIR, PAIR)
                )
                if pair == 0 and half == 0:
                    tick(done[0] + s)
                if pair == 2 and half == 1:
                    tick_every(s, GATHER[0], SEGS)
            put_probs(s).start()

        done[0] += SEGS if half == 0 else -(-SEGS // GATHER[0])
        put_probs(SEGS - 2).wait()
        put_probs(SEGS - 1).wait()

        if half == 1:
            until(BOUNDS[1][1] + HOPS[2])
        out = (own_out, their_out)[half]

        @pl.loop(0, 3)
        def _(n, half=half, out=out):
            columns = pl.ds(pl.multiple_of(n * CHUNK, CHUNK), CHUNK)
            part = mm(mixed[half], out[:, columns])
            acc_own[:, columns] = part if half == 0 else acc_own[:, columns] + part
            ticks(n, GATHER[1 + half], 3)

        done[0] += 3 * GATHER[1 + half]
    put_qkv.start()
    put_mixed.start()

    def norm_one(span):
        resid = tokens[span, :].astype(F32) + (acc_own[span, :] + flat_row(bias_out, 0, depth))
        unit, scale = norm_stats(resid)
        normed[span, :] = unit
        inverse[span, :] = scale
        hidden[span, :] = (unit * flat_row(gain_one, 0, depth) + flat_row(shift_one, 0, depth)).astype(BF)

    row_tiles(0, rows, norm_one)
    load_grad.start()
    put_normed.start()
    put_hidden.start()

    for half in range(2):
        up, down = ((own_up, own_down), (their_up, their_down))[half]
        table = (small, small_their)[half]
        slope_h = (slope_own_h, slope_their_h)[half]
        acc = (acc_own, acc_their)[half]

        def put_slope(c, slope_h=slope_h):
            span = pl.ds(pl.multiple_of(c * CHUNK, CHUNK), CHUNK)
            return pltpu.make_async_copy(slopes.at[lax.rem(c, 2)], slope_h.at[:, span], slope_sem.at[lax.rem(c, 2)])

        if half == 1:
            until(BOUNDS[2][1] + HOPS[2])
            if fast:
                for copy in put_theirs[:3]:
                    copy.start()
            put_acted.wait()
            put_slope(4).wait()
            put_slope(5).wait()

        @pl.loop(0, 6)
        def _(c, half=half, up=up, table=table, put_slope=put_slope):
            span = pl.ds(pl.multiple_of(c * CHUNK, CHUNK), CHUNK)

            @pl.when(c >= 2)
            def _():
                put_slope(c - 2).wait()

            bias = table[pl.ds(3 + c, 1), 0:CHUNK]
            act, steep = gelu_parts(mm(hidden[...], up[:, span]) + bias)
            acted[:, span] = act
            slopes[lax.rem(c, 2)] = steep
            put_slope(c).start()
            tick_every(c, GATHER[3 + 2 * half], 6)

        done[0] += -(-6 // GATHER[3 + 2 * half])
        low, high = slice(0, units // 2), slice(units // 2, units)
        if half == 0:
            put_acted.start()

            @pl.loop(0, 3)
            def _(n, down=down, acc=acc):
                columns = pl.ds(pl.multiple_of(n * CHUNK, CHUNK), CHUNK)
                acc[:, columns] = mm(acted[:, low], down[low, columns]) + mm(acted[:, high], down[high, columns])
                ticks(n, GATHER[4], 3)

        else:
            until((BOUNDS[3][0] + BOUNDS[3][1]) // 2 + HOPS[2])

            @pl.loop(0, 3)
            def _(n, down=down, acc=acc):
                columns = pl.ds(pl.multiple_of(n * CHUNK, CHUNK), CHUNK)
                acc[:, columns] = mm(acted[:, low], down[low, columns])
                ticks(n, 1, 3)

            done[0] += 3
            until(BOUNDS[3][1] + HOPS[2])
            if fast:
                put_theirs[3].start()

            @pl.loop(0, 3)
            def _(n, down=down, acc=acc):
                columns = pl.ds(pl.multiple_of(n * CHUNK, CHUNK), CHUNK)
                acc[:, columns] = acc[:, columns] + mm(acted[:, high], down[high, columns])

        done[0] += 3 * GATHER[4] if half == 0 else 0
    put_slope(4).wait()
    put_slope(5).wait()

    load_grad.wait()
    sums[...] = jnp.zeros(sums.shape, F32)

    def norm_two(span):
        first = normed[span, :] * flat_row(gain_one, 0, depth) + flat_row(shift_one, 0, depth)
        resid = first + ((acc_own[span, :] + acc_their[span, :]) + flat_row(bias_down, 0, depth))
        unit, scale = norm_stats(resid)
        grad = tokens[span, :].astype(F32)
        tokens[span, :] = (unit * flat_row(gain_two, 0, depth) + flat_row(shift_two, 0, depth)).astype(BF)
        back = norm_back(grad, unit, scale, flat_row(gain_two, 0, depth))
        acc_own[span, :] = back
        low = back.astype(BF)
        d_ffn[span, :] = low
        for index, value in enumerate((low.astype(F32), grad * unit, grad)):
            sums[index] = sums[index] + value.reshape(-1, 8, depth).sum(axis=0)

    row_tiles(0, SPLIT, norm_two)
    for copy in put_late[0]:
        copy.start()
    row_tiles(SPLIT, rows, norm_two)
    for copy in put_late[1]:
        copy.start()
    for index in range(3):
        total = jnp.sum(sums[index], axis=0, keepdims=True)
        for j in range(6):
            vec[6 * index + j : 6 * index + j + 1, :] = total[:, BC * j : BC * (j + 1)]
    for copy in (put_qkv, put_mixed, put_normed, put_hidden, *put_late[0], *put_late[1]):
        copy.wait()
    if fast:
        for copy in put_theirs:
            copy.wait()


GATHER = (2, 1, 1, 2, 1, 2)


def forward(fast, parent, slots, vectors, tokens, grad_out, own, given):
    rows, depth = tokens.shape
    width = own[0].shape[1]
    units = own[2].shape[1]
    vm = pl.BlockSpec(memory_space=pltpu.VMEM)
    hbm = pl.BlockSpec(memory_space=pl.ANY)
    sm = pl.BlockSpec(memory_space=pltpu.SMEM)
    sd = jax.ShapeDtypeStruct
    kept = pltpu.VMEM if fast else sd
    out_shape = [
        sd((rows, depth), BF),
        *[sd(w.shape, BF) for w in own],
        sd((2, 3, rows, width), BF),
        sd((rows, width), BF),
        sd((rows, depth), F32),
        sd((rows, 1), F32),
        sd((rows, depth), BF),
        sd((rows, units), BF),
        sd((rows, units), BF),
        sd((rows, units), BF),
        sd((rows, depth), F32),
        kept((rows, depth), BF),
        sd((18, BC), F32),
        sd((2, SEGS, width // PAIR, 2 * WIN, WIN + MEMP), BF),
        sd((rows, MEMP), BF),
        sd((2, 2, MEMP, width), BF),
    ]
    return pl.pallas_call(
        functools.partial(forward_kernel, fast),
        out_shape=out_shape,
        in_specs=[sm, sm] + [vm] * len(vectors) + [hbm, hbm] + [hbm] * (4 + len(given)),
        out_specs=[hbm] * 8 + [vm] + [hbm] * 5 + [vm, vm, hbm, vm, vm],
        scratch_shapes=[
            pltpu.VMEM((rows, depth), BF),
            *[pltpu.VMEM(w.shape, BF) for w in own],
            *[pltpu.VMEM(w.shape, BF) for w in own],
            pltpu.VMEM((16, width), F32),
            pltpu.VMEM((16, width), F32),
            pltpu.VMEM((2, 3, rows, width), BF),
            pltpu.VMEM((2, rows, width), BF),
            pltpu.VMEM((rows, depth), F32),
            pltpu.VMEM((rows, depth), BF),
            pltpu.VMEM((rows, depth), F32),
            pltpu.VMEM((rows, depth), F32),
            pltpu.VMEM((rows, units), BF),
            pltpu.VMEM((2, rows, CHUNK), BF),
            pltpu.VMEM((SEGS, WIN + MEMP), F32),
            pltpu.VMEM((MEMP, rows), BF),
            pltpu.VMEM((3, 8, depth), F32),
            pltpu.VMEM((2, width // PAIR, 2 * WIN, WIN + MEMP), BF),
            pltpu.SemaphoreType.DMA((21,)),
            pltpu.SemaphoreType.DMA((2,)),
            pltpu.SemaphoreType.DMA((2,)),
        ]
        + ([pltpu.SemaphoreType.DMA((2,))] + gather_scratch() if fast else []),
        compiler_params=pltpu.CompilerParams(
            collective_id=0 if fast else None, has_side_effects=fast, vmem_limit_bytes=62000000 if fast else 67043328
        ),
        name="forward",
    )(parent, slots, *vectors, tokens, grad_out, *own, *given)


DOWN, UP, OUT, QKV, VEC = 0, 24, 48, 54, 72
COUNT = 73
CHUNK = 256
VEC_ROWS = 54


def backward_kernel(
    fast,
    select_t,
    memory,
    inverse,
    gain,
    vec_in,
    tokens_h,
    hidden_h,
    d_ffn,
    d_two_h,
    normed_h,
    acted_h,
    slope_own_h,
    slope_their_h,
    qkv_h,
    mixed_h,
    probs_h,
    w_up_own,
    w_up_their,
    w_down_own,
    w_down_their,
    w_out_own,
    w_out_their,
    w_qkv_own,
    w_qkv_their,
    grads,
    d_low,
    hidden,
    d_res,
    normed,
    acc_own,
    acc_their,
    a_buf,
    slope_buf,
    up_buf,
    down_buf,
    d_inner,
    sums,
    mixed,
    w_out,
    w_qkv,
    qkv,
    d_qkv,
    d_mixed,
    probs,
    dkm,
    dvm,
    load_sem,
    chunk_sem,
    probs_sem,
    *wires,
):
    rows, depth = hidden.shape
    width = mixed.shape[1]
    tokens = hidden

    def fetch(index, source, target):
        return pltpu.make_async_copy(source, target, load_sem.at[index])

    load_hidden = fetch(1, hidden_h, hidden)
    load_two = fetch(2, d_two_h, d_res)
    load_normed = fetch(3, normed_h, normed)
    load_mixed = fetch(4, mixed_h, mixed)
    load_out = [fetch(5 + i, w, w_out.at[i]) for i, w in enumerate((w_out_own, w_out_their))]
    load_w = [fetch(7 + i, w, w_qkv.at[i]) for i, w in enumerate((w_qkv_own, w_qkv_their))]
    load_tokens = fetch(9, tokens_h, tokens)
    load_qkv = [fetch(10 + half, qkv_h.at[half], qkv) for half in range(2)]

    def load_acted(c):
        return pltpu.make_async_copy(acted_h.at[:, pl.ds(pl.multiple_of(c * BR, BR), BR)], a_buf.at[lax.rem(c, 2)], chunk_sem.at[0, lax.rem(c, 2)])

    def load_chunk(half, c):
        slot = lax.rem(c, 2)
        span = pl.ds(pl.multiple_of(c * CHUNK, CHUNK), CHUNK)
        slope_h, up_h, down_h = ((slope_own_h, w_up_own, w_down_own), (slope_their_h, w_up_their, w_down_their))[half]
        return (
            pltpu.make_async_copy(slope_h.at[:, span], slope_buf.at[slot], chunk_sem.at[1, slot]),
            pltpu.make_async_copy(up_h.at[:, span], up_buf.at[slot], chunk_sem.at[2, slot]),
            pltpu.make_async_copy(down_h.at[span, :], down_buf.at[slot], chunk_sem.at[3, slot]),
        )

    def load_probs(half, s):
        slot = lax.rem(s, 2)
        return pltpu.make_async_copy(probs_h.at[half, s], probs.at[slot], probs_sem.at[slot])

    def start(copies):
        for copy in copies:
            copy.start()

    def wait(copies):
        for copy in copies:
            copy.wait()

    if fast:
        pos = Place()
        sum_greet(pos)
    load_acted(0).start()
    start(load_chunk(0, 0))
    load_hidden.start()

    def finish(block):
        pass

    if fast:
        tick = make_tick(pos, grads, *wires, COUNT, finish)
        last = COUNT + AFTER[7]
    else:

        def tick(step):
            pass

        last = COUNT
    done = [0]

    def ticks(index, each, trips):
        for i in range(each):
            tick(done[0] + index * each + i)
        return trips * each

    grads[VEC] = jnp.zeros((BR, BC), F32)
    grads[VEC, 36:54] = vec_in[...]
    acc_own[...] = jnp.zeros(acc_own.shape, F32)
    acc_their[...] = jnp.zeros(acc_their.shape, F32)
    sums[...] = jnp.zeros(sums.shape, F32)
    if fast:
        sum_met(pos)


    @pl.loop(0, 4)
    def _(c):
        load_acted(c).wait()

        @pl.when(c < 3)
        def _():
            load_acted(c + 1).start()

        @pl.when(c == 3)
        def _():
            load_two.start()
            load_normed.start()

        for part in range(2):
            piece = t_mm(a_buf[lax.rem(c, 2)], d_ffn[:, part * width : (part + 1) * width])
            for j in range(3):
                grads[DOWN + 6 * c + 3 * part + j] = piece[:, BC * j : BC * (j + 1)]
            if part >= 2 - TICKS[0]:
                tick(done[0] + c * TICKS[0] + part - 2 + TICKS[0])

    done[0] += 4 * TICKS[0]

    load_hidden.wait()
    for half in range(2):
        acc = (acc_own, acc_their)[half]

        @pl.loop(0, 6)
        def _(c, half=half, acc=acc):
            slot = lax.rem(c, 2)
            wait(load_chunk(half, c))

            @pl.when(c < 5)
            def _():
                start(load_chunk(half, c + 1))

            if half == 0:

                @pl.when(c == 5)
                def _():
                    start(load_chunk(1, 0))
                    load_mixed.start()
                    start(load_out)
                    load_qkv[0].start()
                    load_probs(0, 0).start()

            each = TICKS[1 + half]
            d_inner[...] = (mm_t(d_ffn[...], down_buf[slot]) * slope_buf[slot].astype(F32)).astype(BF)
            if each > 1:
                tick(done[0] + c * each)
            if half == 0:
                piece = t_mm(hidden[...], d_inner[...])
                for r in range(2):
                    for j in range(2):
                        grads[UP + 4 * c + 2 * r + j] = piece[BR * r : BR * (r + 1), BC * j : BC * (j + 1)]
                total = jnp.sum(d_inner[...].astype(F32), axis=0, keepdims=True)
                for j in range(2):
                    grads[VEC, pl.ds(6 + 2 * c + j, 1), :] = total[:, BC * j : BC * (j + 1)]
                if each > 2:
                    tick(done[0] + c * each + 1)
            for part in range(3):
                columns = slice(CHUNK * part, CHUNK * (part + 1))
                acc[:, columns] = acc[:, columns] + mm_t(d_inner[...], up_buf[slot, columns, :])
            tick(done[0] + c * each + each - 1)

        done[0] += 6 * TICKS[1 + half]

    start(load_w)
    load_tokens.start()

    load_two.wait()
    load_normed.wait()
    def norm_one(span):
        total = d_res[span, :] + (acc_own[span, :] + acc_their[span, :])
        unit = normed[span, :]
        one = norm_back(total, unit, inverse[span, :], flat_row(gain, 0, depth))
        d_res[span, :] = one
        low = one.astype(BF)
        d_low[span, :] = low
        for index, value in enumerate((low.astype(F32), total * unit, total)):
            sums[index] = sums[index] + value.reshape(-1, 8, depth).sum(axis=0)

    trips = rows // NORM_TILE

    @pl.loop(0, trips)
    def _(i):
        norm_one(pl.ds(pl.multiple_of(i * NORM_TILE, NORM_TILE), NORM_TILE))

        @pl.when(lax.rem(i, TICK_TILES) == 0)
        def _():
            tick(done[0] + i // TICK_TILES)

    if rows % NORM_TILE:
        norm_one(pl.ds(trips * NORM_TILE, rows % NORM_TILE))
    done[0] += -(-trips // TICK_TILES)
    for index in range(3):
        total = jnp.sum(sums[index], axis=0, keepdims=True)
        for j in range(6):
            grads[VEC, 18 + 6 * index + j : 19 + 6 * index + j, :] = total[:, BC * j : BC * (j + 1)]

    load_mixed.wait()
    wait(load_out)

    @pl.loop(0, 2)
    def _(half):
        d_mixed[half] = mm_t(d_low[...], w_out[half]).astype(BF)
        piece = t_mm(mixed[...], d_low[:, pl.ds(pl.multiple_of(half * width, BC), width)])
        for j in range(3):
            grads[OUT + 3 * half + j] = piece[:, BC * j : BC * (j + 1)]
        ticks(half, TICKS[3], 2)

    done[0] += 2 * TICKS[3]

    pairs = width // PAIR
    dka, dva = acc_their.at[:, pl.ds(0, width)], acc_their.at[:, pl.ds(width, width)]
    for half in range(2):
        load_qkv[half].wait()
        q, k, v = (qkv.at[i] for i in range(3))
        kmem, vmem = memory.at[half, 0], memory.at[half, 1]
        acc_their[...] = jnp.zeros(acc_their.shape, F32)
        dkm[...] = jnp.zeros(dkm.shape, F32)
        dvm[...] = jnp.zeros(dvm.shape, F32)

        group = UNROLL[half]

        @pl.loop(0, SEGS * pairs // group)
        def _(trip, half=half, group=group, kmem=kmem, vmem=vmem):
            s, first = trip * group // pairs, lax.rem(trip * group, pairs)

            @pl.when(first == 0)
            def _():
                load_probs(half, s).wait()

                @pl.when(s < SEGS - 1)
                def _():
                    load_probs(half, s + 1).start()

                if half == 0:

                    @pl.when(s == SEGS - 1)
                    def _():
                        load_probs(1, 0).start()

            for i in range(group):
                pair = i if group == pairs else first
                columns = pl.ds(pl.multiple_of(pair * PAIR, PAIR), PAIR)
                part = probs.at[lax.rem(s, 2), pair]
                attend_back_pair(q, k, v, kmem, vmem, part, d_mixed.at[half], d_qkv.at[0], dka, dva, dkm, dvm, s, columns)
                spot = trip * group + i

                @pl.when(lax.rem(spot, TICKS[4 + half]) == 0)
                def _(spot=spot):
                    tick(done[0] + spot // TICKS[4 + half])

        done[0] += -(-SEGS * pairs // TICKS[4 + half])
        if half == 0:
            assert done[0] <= QKV
        if half == 0:
            load_qkv[1].start()
        d_qkv[1] = ((dka[...] + spread(select_t[...], dkm[...])) * HD ** (-0.5)).astype(BF)
        d_qkv[2] = (dva[...] + spread(select_t[...], dvm[...])).astype(BF)
        if half == 0:
            wait(load_w)
            load_tokens.wait()

            @pl.loop(0, 3)
            def _(c):
                piece = t_mm(tokens[...], d_qkv[c])
                for r in range(2):
                    for j in range(3):
                        grads[QKV + 6 * c + 3 * r + j] = piece[BR * r : BR * (r + 1), BC * j : BC * (j + 1)]
                columns = pl.ds(pl.multiple_of(c * CHUNK, CHUNK), CHUNK)
                part = mm_t(d_qkv[0], w_qkv[half, pl.ds(pl.multiple_of(c * CHUNK, CHUNK), CHUNK), :])
                for i in (1, 2):
                    part = part + mm_t(d_qkv[i], w_qkv[half, pl.ds(pl.multiple_of(i * depth + c * CHUNK, CHUNK), CHUNK), :])
                acc_own[:, columns] = part
                ticks(c, TICKS[6], 3)

            done[0] += 3 * TICKS[6]
            for index, row in ((0, 0), (2, 3)):
                total = jnp.sum(d_qkv[index].astype(F32), axis=0, keepdims=True)
                for j in range(3):
                    grads[VEC, row + j : row + j + 1, :] = total[:, BC * j : BC * (j + 1)]
        else:

            @pl.loop(0, 3)
            def _(c):
                columns = pl.ds(pl.multiple_of(c * CHUNK, CHUNK), CHUNK)
                part = mm_t(d_qkv[0], w_qkv[half, pl.ds(pl.multiple_of(c * CHUNK, CHUNK), CHUNK), :])
                for i in (1, 2):
                    part = part + mm_t(d_qkv[i], w_qkv[half, pl.ds(pl.multiple_of(i * depth + c * CHUNK, CHUNK), CHUNK), :])
                d_low[:, columns] = ((acc_own[:, columns] + part) + d_res[:, columns]).astype(BF)
                ticks(c, TICKS[7], 3)

            done[0] += 3 * TICKS[7]
    @pl.loop(min(done[0], last), last)
    def _(step):
        tick(step)


TICKS = (2, 3, 1, 1, 2, 1, 2, 2)
TICK_TILES = 2
NORM_TILE = 128
UNROLL = (3, 1)


def backward(fast, select_t, memory, inverse, gain, vec_in, arrays):
    tokens, acted, mixed = arrays[0], arrays[5], arrays[9]
    rows, depth = tokens.shape
    units = acted.shape[1]
    width = mixed.shape[1]
    vm = pl.BlockSpec(memory_space=pltpu.VMEM)
    hbm = pl.BlockSpec(memory_space=pl.ANY)
    if fast:
        kept_in = pltpu.with_memory_space_constraint(arrays[2], pltpu.VMEM)
        arrays = (*arrays[:2], kept_in, *arrays[3:])
    kept = pltpu.VMEM if fast else jax.ShapeDtypeStruct
    return pl.pallas_call(
        functools.partial(backward_kernel, fast),
        out_shape=[kept((COUNT, BR, BC), F32), kept((rows, depth), BF)],
        in_specs=[vm, vm, vm, vm, vm, hbm, hbm, vm] + [hbm] * (len(arrays) - 3),
        out_specs=[vm, vm],
        scratch_shapes=[
            pltpu.VMEM((rows, depth), BF),
            pltpu.VMEM((rows, depth), F32),
            pltpu.VMEM((rows, depth), F32),
            pltpu.VMEM((rows, depth), F32),
            pltpu.VMEM((rows, depth), F32),
            pltpu.VMEM((2, rows, BR), BF),
            pltpu.VMEM((2, rows, CHUNK), BF),
            pltpu.VMEM((2, depth, CHUNK), BF),
            pltpu.VMEM((2, CHUNK, depth), BF),
            pltpu.VMEM((rows, CHUNK), BF),
            pltpu.VMEM((3, 8, depth), F32),
            pltpu.VMEM((rows, width), BF),
            pltpu.VMEM((2, width, depth), BF),
            pltpu.VMEM((2, 3 * depth, width), BF),
            pltpu.VMEM((3, rows, width), BF),
            pltpu.VMEM((3, rows, width), BF),
            pltpu.VMEM((2, rows, width), BF),
            pltpu.VMEM((2, width // PAIR, 2 * WIN, WIN + MEMP), BF),
            pltpu.VMEM((MEMP, width), F32),
            pltpu.VMEM((MEMP, width), F32),
            pltpu.SemaphoreType.DMA((12,)),
            pltpu.SemaphoreType.DMA((4, 2)),
            pltpu.SemaphoreType.DMA((2,)),
        ]
        + (sum_scratch() if fast else []),
        compiler_params=pltpu.CompilerParams(
            collective_id=1 if fast else None, has_side_effects=fast, vmem_limit_bytes=45100000 if fast else 67043328
        ),
        name="backward",
    )(select_t, memory, inverse, gain, vec_in, *arrays)


def results_kernel(blocks, grad_tokens, output, g_qkv, g_out, g_up, g_down, tokens_h, output_out, *rest):
    vectors, (sems, out_sem) = rest[:8], rest[8:]
    places = [(g_down, BR * (i // 6), BC * (i % 6)) for i in range(24)]
    places += [(g_up, BR * (i // 2 % 2), CHUNK * (i // 4) + BC * (i % 2)) for i in range(24)]
    places += [(g_out, 0, BC * i) for i in range(6)]
    places += [(g_qkv, BR * (i // 3), BC * (i % 3)) for i in range(18)]
    copies = [
        pltpu.make_async_copy(blocks.at[i], target.at[pl.ds(row, BR), pl.ds(column, BC)], sems.at[i])
        for i, (target, row, column) in enumerate(places)
    ]
    copies.append(pltpu.make_async_copy(grad_tokens, tokens_h, out_sem.at[0]))
    copies.append(pltpu.make_async_copy(output, output_out, out_sem.at[1]))
    for copy in copies:
        copy.start()
    bias_qv, *flat = vectors
    for j in range(6):
        bias_qv[j // 3 : j // 3 + 1, BC * (j % 3) : BC * (j % 3 + 1)] = blocks[VEC, j : j + 1, :]
    row = 6
    for ref in flat:
        for j in range(ref.shape[0] // BC):
            ref[pl.ds(BC * j, BC)] = blocks[VEC, row, :]
            row += 1
    for copy in copies:
        copy.wait()


def results(fast, blocks, grad_tokens, output, width, units):
    vm = pl.BlockSpec(memory_space=pltpu.VMEM)
    hbm = pl.BlockSpec(memory_space=pl.ANY)
    sd = jax.ShapeDtypeStruct
    rows, depth = output.shape
    if fast:
        blocks, grad_tokens, output = (
            pltpu.with_memory_space_constraint(a, pltpu.VMEM) for a in (blocks, grad_tokens, output)
        )
    large = [sd((3 * depth, width), F32), sd((width, depth), F32), sd((depth, units), F32), sd((units, depth), F32)]
    large += [sd((rows, depth), BF)] * 2
    small = [sd((2, width), F32), sd((units,), F32)] + [sd((depth,), F32)] * 6
    return pl.pallas_call(
        results_kernel,
        out_shape=large + small,
        in_specs=[vm, vm, vm],
        out_specs=[hbm] * 6 + [vm] * len(small),
        scratch_shapes=[
            pltpu.SemaphoreType.DMA((VEC,)),
            pltpu.SemaphoreType.DMA((2,)),
        ],
        compiler_params=pltpu.CompilerParams(vmem_limit_bytes=(8 if fast else 40) * 2**20),
        name="results",
    )(blocks, grad_tokens, output)


def halves_swap(own, small):
    unit = (lax.axis_index("dp") >= 0).astype(F32)

    def other(array):
        arrived = lax.ppermute(array.astype(F32), "tensor", [(0, 1), (1, 0)])
        return (arrived * unit).astype(array.dtype)

    return tuple(other(array) for array in own) + (other(small),)


def shards(
    fast,
    tokens,
    w_qkv,
    bias_qv,
    w_out,
    bias_out,
    gain_one,
    shift_one,
    w_up,
    bias_up,
    w_down,
    bias_down,
    gain_two,
    shift_two,
    grad_out,
    parent,
    mem_slots,
):
    depth, width = w_qkv.shape[1:]
    hidden_units = w_up.shape[1]
    own = (w_qkv.reshape(3 * depth, width), w_out, w_up, w_down)
    if fast:
        given = ()
    else:
        table = jnp.pad(bias_up.reshape(-1, CHUNK), ((0, 0), (0, width - CHUNK)))
        small = jnp.concatenate([bias_qv[:1], jnp.zeros((1, width), F32), bias_qv[1:], table])
        given = halves_swap(own, jnp.pad(small, ((0, 16 - small.shape[0]), (0, 0))))
    vectors = (bias_qv, bias_out, gain_one, shift_one, bias_up, bias_down, gain_two, shift_two)
    (
        output,
        *theirs,
        qkv,
        mixed,
        normed,
        inverse,
        hidden_low,
        acted,
        slope_own,
        slope_their,
        d_two,
        d_ffn,
        vec,
        probs,
        select_t,
        memory,
    ) = forward(fast, parent, mem_slots, vectors, tokens, grad_out, own, given)
    if not fast:
        theirs = given[:4]
    arrays = (tokens, hidden_low, d_ffn, d_two, normed, acted, slope_own, slope_their, qkv, mixed, probs)
    weights = tuple(w[i] for i in (2, 3, 1, 0) for w in (own, theirs))
    blocks, grad_tokens = backward(fast, select_t, memory, inverse, gain_one, vec, arrays + weights)
    if not fast:
        blocks = lax.psum(blocks, "dp")
    (
        g_w_qkv,
        g_w_out,
        g_w_up,
        g_w_down,
        grad_tokens,
        output,
        g_bias_qv,
        g_bias_up,
        g_bias_out,
        g_gain_one,
        g_shift_one,
        g_bias_down,
        g_gain_two,
        g_shift_two,
    ) = results(fast, blocks, grad_tokens, output, width, hidden_units)
    return (
        output,
        grad_tokens,
        g_w_qkv.reshape(w_qkv.shape),
        g_bias_qv,
        g_w_out,
        g_bias_out,
        g_gain_one,
        g_shift_one,
        g_w_up,
        g_bias_up,
        g_w_down,
        g_bias_down,
        g_gain_two,
        g_shift_two,
    )


def solution(mesh):
    fast = mesh.shape["dp"] == 16 and mesh.shape["tensor"] == 2
    rows, whole = P("dp", None), P()
    return jax.shard_map(
        functools.partial(shards, fast),
        mesh=mesh,
        in_specs=(
            rows,
            P(None, None, "tensor"),
            P(None, "tensor"),
            P("tensor", None),
            whole,
            whole,
            whole,
            P(None, "tensor"),
            P("tensor"),
            P("tensor", None),
            whole,
            whole,
            whole,
            rows,
            P("dp"),
            rows,
        ),
        out_specs=(
            rows,
            rows,
            P(None, None, "tensor"),
            P(None, "tensor"),
            P("tensor", None),
            whole,
            whole,
            whole,
            P(None, "tensor"),
            P("tensor"),
            P("tensor", None),
            whole,
            whole,
            whole,
        ),
        check_vma=False,
    )
```
